512 devices in a mesh: grp: 16 (over y, x), tp: 32 (over z, core).
Axes of the slice: x: 4, y: 4, z: 16, core: 2. Of those that a mesh axis runs over, the one named last changes fastest.
Arguments:
- tokens: bfloat16 [6144, 5120], P('grp'), may hold values from -36 to 36
- trainer_panels: bfloat16 [64, 5120, 128], P('tp', 'grp'), may hold values from -0.078125 to 0.078125
- panel_home: int32 [48], replicated, may hold values from 0 to 63, as said below
- lengths: int32 [16, 4], P('grp'), may hold values from 1 to 192, 384 in all within a row
Outputs:
- context: float32 [6144, 4096], P(('grp', 'tp'))
The draws below stay inside these ranges and needn't reach their ends.
Inputs may be any that keep to these rules, and one draw needn't show every extreme that they name: `panel_home`: entries are distinct; entry p is 2 times the tp index of the trainer device that holds panel p, plus the panel's slot on that device. Panels 0 to 31 are query heads, the next 8 key heads, the last 8 value heads. Some trainer device holds 2 panels.
All inputs are finite; a program needn't handle non-finite values.
Results may differ from the reference program's by a relative error of at most 0.012.
Values may be sent and summed in bfloat16 or wider, within the bound.
A program may use at most 64 MiB of HBM per device.

```python
import math
import jax
import jax.numpy as jnp
import numpy as np
from jax import lax

D = 5120
HEAD_DIM = 128
KV_HEADS = 8
RESP = 4
HEADS = 32
TOKENS = 384
ALL_TOKENS = 6144
MOST_LEN = 192
PANELS = 48
SLOTS = 2
SLOTS_ALL = 64
N_GRP = 16


def draw_tokens(key, part):
    normal_base = jnp.clip(jax.random.normal(key, (ALL_TOKENS, D), jnp.float32), -6.0, 6.0)
    return normal_base.astype(jnp.bfloat16)


def draw_panel_home(key, part):
    panel_order = jax.random.permutation(jax.random.fold_in(key, 11), PANELS)
    full_owner = jax.random.randint(jax.random.fold_in(key, 12), (), 0, SLOTS_ALL // SLOTS)
    free_spots = jax.random.permutation(jax.random.fold_in(key, 13), SLOTS_ALL - SLOTS).astype(jnp.int32)
    free_spots = jnp.where(free_spots >= full_owner * SLOTS, free_spots + SLOTS, free_spots)
    panel_rank = jnp.arange(PANELS, dtype=jnp.int32)
    slot_spot = jnp.where(panel_rank < SLOTS, full_owner * SLOTS + panel_rank, free_spots[jnp.maximum(panel_rank - SLOTS, 0)])
    home_slots = jnp.zeros((PANELS,), jnp.int32).at[panel_order].set(slot_spot.astype(jnp.int32))
    return home_slots


def block_levels(stream_key, extent, pieces, least, high):
    loudness, own = 1.0, jax.random.fold_in(stream_key, 6)
    for axis_at, blocks in pieces:
        heights = jnp.exp(jax.random.uniform(jax.random.fold_in(own, axis_at), (blocks,), jnp.float32, least / len(pieces), high / len(pieces)))
        loudness = loudness * jnp.repeat(heights, extent[axis_at] // blocks).reshape([-1 if axis == axis_at else 1 for axis in range(len(extent))])
    return loudness


def split_up(amount, total, bound, lean):
    loads = [(1 << 20) // math.isqrt(standing ** lean) + 1 for standing in range(2, amount + 1)]
    rest, counts = total - bound - (amount - 1), [1] * (amount - 1)
    while rest > 0:
        free = [i for i in range(amount - 1) if counts[i] < bound]
        pool, budget = sum([loads[i] for i in free]), rest
        for i in free:
            more = min(bound - counts[i], max(1, budget * loads[i] // pool), rest)
            counts[i] = counts[i] + more
            rest = rest - more
    return np.array([bound] + counts)


def ragged_sizes(rng, number_of, total, limit, slope):
    if number_of == 2:
        one = jax.random.randint(rng, (), max(1, total - limit), min(limit, total - 1) + 1)
        return jnp.stack([one, total - one])
    sizes = jnp.asarray(split_up(number_of, total, limit, slope), jnp.int32)
    couples = (number_of - 1) // 2
    source_of, sink = sizes[1:1 + 2 * couples:2], sizes[2:2 + 2 * couples:2]
    margin = jnp.minimum(source_of - 1, limit - sink)
    moved = jax.random.randint(jax.random.fold_in(rng, 1), (couples,), 0, 1 << 20) % (margin + 1)
    sizes = sizes.at[1:1 + 2 * couples:2].set(source_of - moved).at[2:2 + 2 * couples:2].set(sink + moved)
    return sizes[jax.random.permutation(jax.random.fold_in(rng, 2), number_of)]


def normal_values(rng, dims, scale, most, shards=(), held_as=jnp.bfloat16):
    level = block_levels(rng, dims, shards, -0.22, 0.18) if shards else 1.0
    values = jax.random.normal(rng, dims, jnp.float32) * scale * level
    return jnp.minimum(jnp.maximum(values, -most), most).astype(held_as)


def setup_inputs(seed: int = 0) -> dict:
    keys = jax.random.split(jax.random.key(seed), 5)
    tokens = draw_tokens(jax.random.fold_in(keys[4], 71), 0)
    trainer_panels = normal_values(keys[1], (SLOTS_ALL, D, HEAD_DIM), D ** -0.5, 0.078125, ((0, 32), (1, 16)))
    panel_home = draw_panel_home(jax.random.fold_in(keys[4], 71), 0)
    lengths = jax.vmap(lambda own: ragged_sizes(own, RESP, TOKENS, MOST_LEN, 2))(jax.random.split(keys[3], N_GRP)).reshape((N_GRP, RESP)).astype(jnp.int32)
    return dict(tokens=tokens, trainer_panels=trainer_panels, panel_home=panel_home, lengths=lengths)


def reference(tokens, trainer_panels, panel_home, lengths):
    group_size = HEADS // KV_HEADS
    stacked = trainer_panels[panel_home]
    weights = jnp.transpose(stacked, (1, 0, 2)).reshape(D, PANELS * HEAD_DIM)
    score_scale = HEAD_DIM ** -0.5
    head_ids = jnp.arange(HEADS, dtype=jnp.int32)
    kv_panel = HEADS + head_ids // group_size
    position = jnp.arange(TOKENS, dtype=jnp.int32)
    outputs = []
    for group_id in range(N_GRP):
        group_rows = tokens[group_id * TOKENS:(group_id + 1) * TOKENS]
        projected = jnp.dot(group_rows, weights, preferred_element_type=jnp.float32).astype(jnp.bfloat16)
        projected = lax.optimization_barrier(projected)
        projected = projected.astype(jnp.float32).reshape(TOKENS, PANELS, HEAD_DIM)
        projected = jnp.transpose(projected, (1, 0, 2))
        query_rows = projected[:HEADS]
        key_rows = projected[kv_panel]
        value_rows = projected[kv_panel + KV_HEADS]
        bounds = jnp.cumsum(lengths[group_id])
        segment = jnp.sum((position[:, None] >= bounds[None, :]).astype(jnp.int32), axis=1)
        allowed = (segment[:, None] == segment[None, :]) & (position[None, :] <= position[:, None])
        scores = jnp.einsum('hqe,hke->hqk', query_rows, key_rows) * score_scale
        masked = jnp.where(allowed[None], scores, -jnp.inf)
        row_peak = jnp.max(masked, axis=2, keepdims=True)
        row_exp = jnp.exp(masked - row_peak)
        attn_probs = (row_exp / jnp.sum(row_exp, axis=2, keepdims=True)).astype(jnp.bfloat16)
        attn_probs = lax.optimization_barrier(attn_probs).astype(jnp.float32)
        context = jnp.einsum('hqk,hke->hqe', attn_probs, value_rows)
        outputs.append(jnp.transpose(context, (1, 0, 2)).reshape(TOKENS, HEADS * HEAD_DIM))
    return jnp.concatenate(outputs, axis=0)
```

```python
import jax
import jax.numpy as jnp
from jax import lax
from jax.sharding import PartitionSpec as P


def on_device(tokens, trainer_panels, panel_home, lengths):
    tp_count = lax.axis_size("tp")
    grp_count = lax.axis_size("grp")
    member_id = lax.axis_index("tp")
    kv_count = (panel_home.shape[0] - tp_count) // 2
    group_size = tp_count // kv_count
    head_dim = trainer_panels.shape[2]
    block_rows = trainer_panels.shape[1]
    half_rows = block_rows // 2
    seq_total = tokens.shape[0]

    all_slots = lax.all_gather(trainer_panels, "tp", axis=0, tiled=True)
    kv_id = member_id // group_size
    quarter = member_id % group_size
    kv_panel = tp_count + kv_id + kv_count * (quarter // 2)
    half = quarter % 2
    q_block = all_slots[panel_home[member_id]]
    kv_block = all_slots[panel_home[kv_panel]]
    kv_half = lax.dynamic_slice_in_dim(kv_block, half * half_rows, half_rows, axis=0)
    piece = jnp.concatenate([q_block, kv_half], axis=0)
    gathered = lax.all_gather(piece, "grp", axis=0, tiled=False)
    q_weights = gathered[:, :block_rows].reshape(grp_count * block_rows, head_dim)
    kv_weights = gathered[:, block_rows:]

    query_rows = jnp.dot(tokens, q_weights, preferred_element_type=jnp.float32).astype(jnp.bfloat16)
    token_halves = tokens.reshape(seq_total, grp_count, 2, half_rows)
    token_half = lax.dynamic_index_in_dim(token_halves, half, axis=2, keepdims=False)
    kv_part = jnp.einsum(
        "sgi,gic->sc", token_half, kv_weights, preferred_element_type=jnp.float32
    )
    pair_perm = [(i, i ^ 1) for i in range(tp_count)]
    kv_full = (kv_part + lax.ppermute(kv_part, "tp", pair_perm)).astype(jnp.bfloat16)
    swap_perm = [(i, i ^ 2) for i in range(tp_count)]
    kv_other = lax.ppermute(kv_full, "tp", swap_perm)
    holds_k = quarter < 2
    key_rows = jnp.where(holds_k, kv_full, kv_other)
    value_rows = jnp.where(holds_k, kv_other, kv_full)

    position = jnp.arange(seq_total, dtype=jnp.int32)
    bounds = jnp.cumsum(lengths[0])
    segment = jnp.sum((position[:, None] >= bounds[None, :]).astype(jnp.int32), axis=1)
    allowed = (segment[:, None] == segment[None, :]) & (position[None, :] <= position[:, None])
    score_scale = head_dim ** (-0.5)
    scores = (
        lax.dot_general(
            query_rows, key_rows, (((1,), (1,)), ((), ())), preferred_element_type=jnp.float32
        )
        * score_scale
    )
    masked = jnp.where(allowed, scores, -jnp.inf)
    row_peak = jnp.max(masked, axis=1, keepdims=True)
    row_exp = jnp.exp(masked - row_peak)
    attn_probs = (row_exp / jnp.sum(row_exp, axis=1, keepdims=True)).astype(jnp.bfloat16)
    context = jnp.dot(attn_probs, value_rows, preferred_element_type=jnp.float32)
    return lax.all_to_all(context, "tp", split_axis=0, concat_axis=1, tiled=True)


def solution(mesh):
    placed = (P("grp", None), P("tp", "grp", None), P(), P("grp", None))
    return jax.shard_map(
        on_device, mesh=mesh, in_specs=placed, out_specs=P(("grp", "tp"), None), check_vma=False
    )
```

```python
import jax
import jax.numpy as jnp
from jax import lax
from jax.sharding import PartitionSpec as P


def on_device(tokens, trainer_panels, panel_home, lengths):
    tp_count = lax.axis_size("tp")
    grp_count = lax.axis_size("grp")
    member_id = lax.axis_index("tp")
    kv_count = (panel_home.shape[0] - tp_count) // 2
    group_size = tp_count // kv_count
    head_dim = trainer_panels.shape[2]
    block_rows = trainer_panels.shape[1]
    half_rows = block_rows // 2
    seq_total = tokens.shape[0]

    core = member_id % 2
    partner_perm = [(i, i ^ 1) for i in range(tp_count)]
    mine = lax.dynamic_slice_in_dim(trainer_panels, core * half_rows, half_rows, axis=1)
    other = lax.dynamic_slice_in_dim(trainer_panels, (1 - core) * half_rows, half_rows, axis=1)
    from_partner = lax.ppermute(other, "tp", partner_perm)
    chip_slots = jnp.where(core == 0, jnp.concatenate([mine, from_partner], axis=0),
                           jnp.concatenate([from_partner, mine], axis=0))
    same_core = [list(range(c, tp_count, 2)) for c in range(2)]
    all_halves = lax.all_gather(chip_slots, "tp", axis=0, tiled=True, axis_index_groups=same_core)
    kv_id = member_id // group_size
    quarter = member_id % group_size
    kv_panel = tp_count + kv_id + kv_count * (quarter // 2)
    half = core
    partner_id = member_id ^ 1
    q_mine = all_halves[panel_home[member_id]]
    q_theirs = lax.ppermute(all_halves[panel_home[partner_id]], "tp", partner_perm)
    q_block = jnp.where(core == 0, jnp.concatenate([q_mine, q_theirs], axis=0),
                        jnp.concatenate([q_theirs, q_mine], axis=0))
    kv_half = all_halves[panel_home[kv_panel]]
    piece = jnp.concatenate([q_block, kv_half], axis=0)
    gathered = lax.all_gather(piece, "grp", axis=0, tiled=False)
    q_weights = gathered[:, :block_rows].reshape(grp_count * block_rows, head_dim)
    kv_weights = gathered[:, block_rows:]

    query_rows = jnp.dot(tokens, q_weights, preferred_element_type=jnp.float32).astype(jnp.bfloat16)
    token_halves = tokens.reshape(seq_total, grp_count, 2, half_rows)
    token_half = lax.dynamic_index_in_dim(token_halves, half, axis=2, keepdims=False)
    kv_part = jnp.einsum(
        "sgi,gic->sc", token_half, kv_weights, preferred_element_type=jnp.float32
    )
    pair_perm = [(i, i ^ 1) for i in range(tp_count)]
    kv_full = (kv_part + lax.ppermute(kv_part, "tp", pair_perm)).astype(jnp.bfloat16)
    swap_perm = [(i, i ^ 2) for i in range(tp_count)]
    kv_other = lax.ppermute(kv_full, "tp", swap_perm)
    holds_k = quarter < 2
    key_rows = jnp.where(holds_k, kv_full, kv_other)
    value_rows = jnp.where(holds_k, kv_other, kv_full)

    position = jnp.arange(seq_total, dtype=jnp.int32)
    bounds = jnp.cumsum(lengths[0])
    segment = jnp.sum((position[:, None] >= bounds[None, :]).astype(jnp.int32), axis=1)
    allowed = (segment[:, None] == segment[None, :]) & (position[None, :] <= position[:, None])
    score_scale = head_dim ** (-0.5)
    scores = (
        lax.dot_general(
            query_rows, key_rows, (((1,), (1,)), ((), ())), preferred_element_type=jnp.float32
        )
        * score_scale
    )
    masked = jnp.where(allowed, scores, -jnp.inf)
    row_peak = jnp.max(masked, axis=1, keepdims=True)
    row_exp = jnp.exp(masked - row_peak)
    attn_probs = (row_exp / jnp.sum(row_exp, axis=1, keepdims=True)).astype(jnp.bfloat16)
    context = jnp.dot(attn_probs, value_rows, preferred_element_type=jnp.float32)
    sent = lax.all_to_all(context.astype(jnp.bfloat16), "tp", split_axis=0, concat_axis=1, tiled=True)
    return sent.astype(jnp.float32)


def solution(mesh):
    placed = (P("grp", None), P("tp", "grp", None), P(), P("grp", None))
    return jax.shard_map(
        on_device, mesh=mesh, in_specs=placed, out_specs=P(("grp", "tp"), None), check_vma=False
    )
```

```python
import functools

import jax
import jax.numpy as jnp
from jax import lax
from jax.experimental import pallas as pl
from jax.experimental.pallas import tpu as pltpu
from jax.sharding import PartitionSpec as P

MESH = pl.DeviceIdType.MESH


def exchange_kernel(axis, count, scatter, send_ref, out_ref, landed, send_sems, recv_sems):
    me = lax.axis_index(axis)
    barrier = pltpu.get_barrier_semaphore()
    for step in range(1, count):
        peer = lax.rem(me + step, count)
        pl.semaphore_signal(barrier, inc=1, device_id={axis: peer}, device_id_type=MESH)
    pl.semaphore_wait(barrier, count - 1)
    copies = []
    for step in range(1, count):
        peer = lax.rem(me + step, count)
        source = send_ref.at[peer] if scatter else send_ref
        copy = pltpu.make_async_remote_copy(
            src_ref=source,
            dst_ref=landed.at[me],
            send_sem=send_sems.at[step],
            recv_sem=recv_sems.at[step],
            device_id={axis: peer},
            device_id_type=MESH,
        )
        copy.start()
        copies.append(copy)
    landed[me] = send_ref[me] if scatter else send_ref[...]
    for copy in copies:
        copy.wait()
    out_ref[...] = landed[...]


def exchange(x, axis, count, scatter, collective_id):
    piece = x.shape[1:] if scatter else x.shape
    return pl.pallas_call(
        functools.partial(exchange_kernel, axis, count, scatter),
        out_shape=jax.ShapeDtypeStruct((count,) + piece, x.dtype),
        in_specs=[pl.BlockSpec(memory_space=pltpu.VMEM)],
        out_specs=pl.BlockSpec(memory_space=pltpu.VMEM),
        scratch_shapes=[
            pltpu.VMEM((count,) + piece, x.dtype),
            pltpu.SemaphoreType.DMA((count,)),
            pltpu.SemaphoreType.DMA((count,)),
        ],
        compiler_params=pltpu.CompilerParams(collective_id=collective_id, has_side_effects=True),
    )(x)


def on_device(tokens, trainer_panels, panel_home, lengths):
    tp_count = lax.axis_size("tp")
    grp_count = lax.axis_size("grp")
    member_id = lax.axis_index("tp")
    kv_count = (panel_home.shape[0] - tp_count) // 2
    group_size = tp_count // kv_count
    head_dim = trainer_panels.shape[2]
    block_rows = trainer_panels.shape[1]
    half_rows = block_rows // 2
    seq_total = tokens.shape[0]

    core = member_id % 2
    partner_perm = [(i, i ^ 1) for i in range(tp_count)]
    mine = lax.dynamic_slice_in_dim(trainer_panels, core * half_rows, half_rows, axis=1)
    other = lax.dynamic_slice_in_dim(trainer_panels, (1 - core) * half_rows, half_rows, axis=1)
    from_partner = lax.ppermute(other, "tp", partner_perm)
    chip_slots = jnp.where(core == 0, jnp.concatenate([mine, from_partner], axis=0),
                           jnp.concatenate([from_partner, mine], axis=0))
    same_core = [list(range(c, tp_count, 2)) for c in range(2)]
    all_halves = lax.all_gather(chip_slots, "tp", axis=0, tiled=True, axis_index_groups=same_core)
    kv_id = member_id // group_size
    quarter = member_id % group_size
    kv_panel = tp_count + kv_id + kv_count * (quarter // 2)
    half = core
    partner_id = member_id ^ 1
    q_mine = all_halves[panel_home[member_id]]
    q_theirs = lax.ppermute(all_halves[panel_home[partner_id]], "tp", partner_perm)
    q_block = jnp.where(core == 0, jnp.concatenate([q_mine, q_theirs], axis=0),
                        jnp.concatenate([q_theirs, q_mine], axis=0))
    kv_half = all_halves[panel_home[kv_panel]]
    piece = jnp.concatenate([q_block, kv_half], axis=0)
    gathered = exchange(piece, "grp", grp_count, False, 0)
    q_weights = gathered[:, :block_rows].reshape(grp_count * block_rows, head_dim)
    kv_weights = gathered[:, block_rows:]

    query_rows = jnp.dot(tokens, q_weights, preferred_element_type=jnp.float32).astype(jnp.bfloat16)
    token_halves = tokens.reshape(seq_total, grp_count, 2, half_rows)
    token_half = lax.dynamic_index_in_dim(token_halves, half, axis=2, keepdims=False)
    kv_part = jnp.einsum(
        "sgi,gic->sc", token_half, kv_weights, preferred_element_type=jnp.float32
    )
    pair_perm = [(i, i ^ 1) for i in range(tp_count)]
    kv_full = (kv_part + lax.ppermute(kv_part, "tp", pair_perm)).astype(jnp.bfloat16)
    swap_perm = [(i, i ^ 2) for i in range(tp_count)]
    kv_other = lax.ppermute(kv_full, "tp", swap_perm)
    holds_k = quarter < 2
    key_rows = jnp.where(holds_k, kv_full, kv_other)
    value_rows = jnp.where(holds_k, kv_other, kv_full)

    position = jnp.arange(seq_total, dtype=jnp.int32)
    bounds = jnp.cumsum(lengths[0])
    segment = jnp.sum((position[:, None] >= bounds[None, :]).astype(jnp.int32), axis=1)
    allowed = (segment[:, None] == segment[None, :]) & (position[None, :] <= position[:, None])
    score_scale = head_dim ** (-0.5)
    scores = (
        lax.dot_general(
            query_rows, key_rows, (((1,), (1,)), ((), ())), preferred_element_type=jnp.float32
        )
        * score_scale
    )
    masked = jnp.where(allowed, scores, -jnp.inf)
    row_peak = jnp.max(masked, axis=1, keepdims=True)
    row_exp = jnp.exp(masked - row_peak)
    attn_probs = (row_exp / jnp.sum(row_exp, axis=1, keepdims=True)).astype(jnp.bfloat16)
    context = jnp.dot(attn_probs, value_rows, preferred_element_type=jnp.float32)
    outgoing = context.reshape(tp_count, seq_total // tp_count, head_dim)
    arrived = exchange(outgoing, "tp", tp_count, True, 1)
    return jnp.transpose(arrived, (1, 0, 2)).reshape(seq_total // tp_count, tp_count * head_dim)


def solution(mesh):
    placed = (P("grp", None), P("tp", "grp", None), P(), P("grp", None))
    return jax.shard_map(
        on_device, mesh=mesh, in_specs=placed, out_specs=P(("grp", "tp"), None), check_vma=False
    )
```

```python
import functools

import jax
import jax.numpy as jnp
from jax import lax
from jax.experimental import pallas as pl
from jax.experimental.pallas import tpu as pltpu
from jax.sharding import PartitionSpec as P

MESH = pl.DeviceIdType.MESH


def exchange_kernel(axis, count, scatter, send_ref, out_ref, landed, send_sems, recv_sems):
    me = lax.axis_index(axis)
    barrier = pltpu.get_barrier_semaphore()
    for step in range(1, count):
        peer = lax.rem(me + step, count)
        pl.semaphore_signal(barrier, inc=1, device_id={axis: peer}, device_id_type=MESH)
    pl.semaphore_wait(barrier, count - 1)
    copies = []
    for step in range(1, count):
        peer = lax.rem(me + step, count)
        source = send_ref.at[peer] if scatter else send_ref
        copy = pltpu.make_async_remote_copy(
            src_ref=source,
            dst_ref=landed.at[me],
            send_sem=send_sems.at[step],
            recv_sem=recv_sems.at[step],
            device_id={axis: peer},
            device_id_type=MESH,
        )
        copy.start()
        copies.append(copy)
    landed[me] = send_ref[me] if scatter else send_ref[...]
    for copy in copies:
        copy.wait()
    out_ref[...] = landed[...]


def ring_kernel(count, stride, send_ref, out_ref, landed, send_sems, recv_sems):
    me = lax.axis_index("tp")
    total = count * stride
    right, left = lax.rem(me + stride, total), lax.rem(me + total - stride, total)
    spot = me // stride
    barrier = pltpu.get_barrier_semaphore()
    for neighbour in (left, right):
        pl.semaphore_signal(barrier, inc=1, device_id={"tp": neighbour}, device_id_type=MESH)
    pl.semaphore_wait(barrier, 2)

    def incoming(origin):
        return pltpu.make_async_remote_copy(
            src_ref=send_ref,
            dst_ref=landed.at[origin],
            send_sem=send_sems.at[0, 0],
            recv_sem=recv_sems.at[origin],
            device_id={"tp": right},
            device_id_type=MESH,
        )

    landed[spot] = send_ref[...]
    sends = []
    far_right, far_left = count // 2, (count - 1) // 2
    for step in range(1, far_right + 1):
        streams = [(0, right, lax.rem(spot + count - (step - 1), count))]
        if step <= far_left:
            streams.append((1, left, lax.rem(spot + step - 1, count)))
        for way, target, origin in streams:
            if step > 1:
                incoming(origin).wait_recv()
            source = send_ref if step == 1 else landed.at[origin]
            copy = pltpu.make_async_remote_copy(
                src_ref=source,
                dst_ref=landed.at[origin],
                send_sem=send_sems.at[way, step],
                recv_sem=recv_sems.at[origin],
                device_id={"tp": target},
                device_id_type=MESH,
            )
            copy.start()
            sends.append(copy)
    incoming(lax.rem(spot + count - far_right, count)).wait_recv()
    incoming(lax.rem(spot + far_left, count)).wait_recv()
    for copy in sends:
        copy.wait_send()
    out_ref[...] = landed[...]


def ring_gather(x, count, stride, collective_id):
    return pl.pallas_call(
        functools.partial(ring_kernel, count, stride),
        out_shape=jax.ShapeDtypeStruct((count,) + x.shape, x.dtype),
        in_specs=[pl.BlockSpec(memory_space=pltpu.VMEM)],
        out_specs=pl.BlockSpec(memory_space=pltpu.VMEM),
        scratch_shapes=[
            pltpu.VMEM((count,) + x.shape, x.dtype),
            pltpu.SemaphoreType.DMA((2, count // 2 + 1)),
            pltpu.SemaphoreType.DMA((count,)),
        ],
        compiler_params=pltpu.CompilerParams(collective_id=collective_id, has_side_effects=True),
    )(x)


def exchange(x, axis, count, scatter, collective_id):
    piece = x.shape[1:] if scatter else x.shape
    return pl.pallas_call(
        functools.partial(exchange_kernel, axis, count, scatter),
        out_shape=jax.ShapeDtypeStruct((count,) + piece, x.dtype),
        in_specs=[pl.BlockSpec(memory_space=pltpu.VMEM)],
        out_specs=pl.BlockSpec(memory_space=pltpu.VMEM),
        scratch_shapes=[
            pltpu.VMEM((count,) + piece, x.dtype),
            pltpu.SemaphoreType.DMA((count,)),
            pltpu.SemaphoreType.DMA((count,)),
        ],
        compiler_params=pltpu.CompilerParams(collective_id=collective_id, has_side_effects=True),
    )(x)


def on_device(tokens, trainer_panels, panel_home, lengths):
    tp_count = lax.axis_size("tp")
    grp_count = lax.axis_size("grp")
    member_id = lax.axis_index("tp")
    kv_count = (panel_home.shape[0] - tp_count) // 2
    group_size = tp_count // kv_count
    head_dim = trainer_panels.shape[2]
    block_rows = trainer_panels.shape[1]
    half_rows = block_rows // 2
    seq_total = tokens.shape[0]

    core = member_id % 2
    partner_perm = [(i, i ^ 1) for i in range(tp_count)]
    mine = lax.dynamic_slice_in_dim(trainer_panels, core * half_rows, half_rows, axis=1)
    other = lax.dynamic_slice_in_dim(trainer_panels, (1 - core) * half_rows, half_rows, axis=1)
    from_partner = lax.ppermute(other, "tp", partner_perm)
    chip_slots = jnp.where(core == 0, jnp.concatenate([mine, from_partner], axis=0),
                           jnp.concatenate([from_partner, mine], axis=0))
    ring_slots = ring_gather(chip_slots, tp_count // 2, 2, 2)
    all_halves = ring_slots.reshape((-1,) + chip_slots.shape[1:])
    kv_id = member_id // group_size
    quarter = member_id % group_size
    kv_panel = tp_count + kv_id + kv_count * (quarter // 2)
    half = core
    partner_id = member_id ^ 1
    q_mine = all_halves[panel_home[member_id]]
    q_theirs = lax.ppermute(all_halves[panel_home[partner_id]], "tp", partner_perm)
    q_block = jnp.where(core == 0, jnp.concatenate([q_mine, q_theirs], axis=0),
                        jnp.concatenate([q_theirs, q_mine], axis=0))
    kv_half = all_halves[panel_home[kv_panel]]
    piece = jnp.concatenate([q_block, kv_half], axis=0)
    gathered = exchange(piece, "grp", grp_count, False, 0)
    q_weights = gathered[:, :block_rows].reshape(grp_count * block_rows, head_dim)
    kv_weights = gathered[:, block_rows:]

    query_rows = jnp.dot(tokens, q_weights, preferred_element_type=jnp.float32).astype(jnp.bfloat16)
    token_halves = tokens.reshape(seq_total, grp_count, 2, half_rows)
    token_half = lax.dynamic_index_in_dim(token_halves, half, axis=2, keepdims=False)
    kv_part = jnp.einsum(
        "sgi,gic->sc", token_half, kv_weights, preferred_element_type=jnp.float32
    )
    pair_perm = [(i, i ^ 1) for i in range(tp_count)]
    kv_full = (kv_part + lax.ppermute(kv_part, "tp", pair_perm)).astype(jnp.bfloat16)
    swap_perm = [(i, i ^ 2) for i in range(tp_count)]
    kv_other = lax.ppermute(kv_full, "tp", swap_perm)
    holds_k = quarter < 2
    key_rows = jnp.where(holds_k, kv_full, kv_other)
    value_rows = jnp.where(holds_k, kv_other, kv_full)

    position = jnp.arange(seq_total, dtype=jnp.int32)
    bounds = jnp.cumsum(lengths[0])
    segment = jnp.sum((position[:, None] >= bounds[None, :]).astype(jnp.int32), axis=1)
    allowed = (segment[:, None] == segment[None, :]) & (position[None, :] <= position[:, None])
    score_scale = head_dim ** (-0.5)
    scores = (
        lax.dot_general(
            query_rows, key_rows, (((1,), (1,)), ((), ())), preferred_element_type=jnp.float32
        )
        * score_scale
    )
    masked = jnp.where(allowed, scores, -jnp.inf)
    row_peak = jnp.max(masked, axis=1, keepdims=True)
    row_exp = jnp.exp(masked - row_peak)
    attn_probs = (row_exp / jnp.sum(row_exp, axis=1, keepdims=True)).astype(jnp.bfloat16)
    context = jnp.dot(attn_probs, value_rows, preferred_element_type=jnp.float32)
    outgoing = context.reshape(tp_count, seq_total // tp_count, head_dim)
    arrived = exchange(outgoing, "tp", tp_count, True, 1)
    return jnp.transpose(arrived, (1, 0, 2)).reshape(seq_total // tp_count, tp_count * head_dim)


def solution(mesh):
    placed = (P("grp", None), P("tp", "grp", None), P(), P("grp", None))
    return jax.shard_map(
        on_device, mesh=mesh, in_specs=placed, out_specs=P(("grp", "tp"), None), check_vma=False
    )
```

```python
import functools

import jax
import jax.numpy as jnp
from jax import lax
from jax.experimental import pallas as pl
from jax.experimental.pallas import tpu as pltpu
from jax.sharding import PartitionSpec as P

MESH = pl.DeviceIdType.MESH


def ring_kernel(count, stride, chunks, send_ref, out_ref, landed, send_sems, recv_sems):
    me = lax.axis_index("tp")
    total = count * stride
    right, left = lax.rem(me + stride, total), lax.rem(me + total - stride, total)
    spot = me // stride
    barrier = pltpu.get_barrier_semaphore()
    for neighbour in (left, right):
        pl.semaphore_signal(barrier, inc=1, device_id={"tp": neighbour}, device_id_type=MESH)
    pl.semaphore_wait(barrier, 2)

    def incoming(origin, chunk):
        return pltpu.make_async_remote_copy(
            src_ref=send_ref.at[chunk],
            dst_ref=landed.at[origin, chunk],
            send_sem=send_sems.at[0, 0, 0],
            recv_sem=recv_sems.at[origin, chunk],
            device_id={"tp": right},
            device_id_type=MESH,
        )

    landed[spot] = send_ref[...]
    sends = []
    far_right, far_left = count // 2, (count - 1) // 2
    for step in range(1, far_right + 1):
        for chunk in range(chunks):
            streams = [(0, right, lax.rem(spot + count - (step - 1), count))]
            if step <= far_left:
                streams.append((1, left, lax.rem(spot + step - 1, count)))
            for way, target, origin in streams:
                if step > 1:
                    incoming(origin, chunk).wait_recv()
                source = send_ref.at[chunk] if step == 1 else landed.at[origin, chunk]
                copy = pltpu.make_async_remote_copy(
                    src_ref=source,
                    dst_ref=landed.at[origin, chunk],
                    send_sem=send_sems.at[way, step, chunk],
                    recv_sem=recv_sems.at[origin, chunk],
                    device_id={"tp": target},
                    device_id_type=MESH,
                )
                copy.start()
                sends.append(copy)
    for chunk in range(chunks):
        incoming(lax.rem(spot + count - far_right, count), chunk).wait_recv()
        incoming(lax.rem(spot + far_left, count), chunk).wait_recv()
    for copy in sends:
        copy.wait_send()
    out_ref[...] = landed[...]


def ring_gather(x, count, stride, chunks, collective_id):
    x = x.reshape((chunks, x.shape[0] // chunks) + x.shape[1:])
    gathered = pl.pallas_call(
        functools.partial(ring_kernel, count, stride, chunks),
        out_shape=jax.ShapeDtypeStruct((count,) + x.shape, x.dtype),
        in_specs=[pl.BlockSpec(memory_space=pltpu.VMEM)],
        out_specs=pl.BlockSpec(memory_space=pltpu.VMEM),
        scratch_shapes=[
            pltpu.VMEM((count,) + x.shape, x.dtype),
            pltpu.SemaphoreType.DMA((2, count // 2 + 1, chunks)),
            pltpu.SemaphoreType.DMA((count, chunks)),
        ],
        compiler_params=pltpu.CompilerParams(collective_id=collective_id, has_side_effects=True),
    )(x)
    return gathered.reshape((count * x.shape[0] * x.shape[1],) + x.shape[2:])


def exchange_kernel(axis, count, scatter, send_ref, out_ref, landed, send_sems, recv_sems):
    me = lax.axis_index(axis)
    barrier = pltpu.get_barrier_semaphore()
    for step in range(1, count):
        peer = lax.rem(me + step, count)
        pl.semaphore_signal(barrier, inc=1, device_id={axis: peer}, device_id_type=MESH)
    pl.semaphore_wait(barrier, count - 1)
    copies = []
    for step in range(1, count):
        peer = lax.rem(me + step, count)
        source = send_ref.at[peer] if scatter else send_ref
        copy = pltpu.make_async_remote_copy(
            src_ref=source,
            dst_ref=landed.at[me],
            send_sem=send_sems.at[step],
            recv_sem=recv_sems.at[step],
            device_id={axis: peer},
            device_id_type=MESH,
        )
        copy.start()
        copies.append(copy)
    landed[me] = send_ref[me] if scatter else send_ref[...]
    for copy in copies:
        copy.wait()
    if scatter:
        width = landed.shape[-1]
        for source in range(count):
            out_ref[:, source * width:(source + 1) * width] = landed[source]
    else:
        out_ref[...] = landed[...]


def exchange(x, axis, count, scatter, collective_id):
    piece = x.shape[1:] if scatter else x.shape
    result = (piece[0], count * piece[1]) if scatter else (count,) + piece
    return pl.pallas_call(
        functools.partial(exchange_kernel, axis, count, scatter),
        out_shape=jax.ShapeDtypeStruct(result, x.dtype),
        in_specs=[pl.BlockSpec(memory_space=pltpu.VMEM)],
        out_specs=pl.BlockSpec(memory_space=pltpu.VMEM),
        scratch_shapes=[
            pltpu.VMEM((count,) + piece, x.dtype),
            pltpu.SemaphoreType.DMA((count,)),
            pltpu.SemaphoreType.DMA((count,)),
        ],
        compiler_params=pltpu.CompilerParams(collective_id=collective_id, has_side_effects=True),
    )(x)


def on_device(tokens, trainer_panels, panel_home, lengths):
    tp_count = lax.axis_size("tp")
    grp_count = lax.axis_size("grp")
    member_id = lax.axis_index("tp")
    kv_count = (panel_home.shape[0] - tp_count) // 2
    group_size = tp_count // kv_count
    head_dim = trainer_panels.shape[2]
    block_rows = trainer_panels.shape[1]
    half_rows = block_rows // 2
    seq_total = tokens.shape[0]

    core = member_id % 2
    partner_perm = [(i, i ^ 1) for i in range(tp_count)]
    mine = lax.dynamic_slice_in_dim(trainer_panels, core * half_rows, half_rows, axis=1)
    other = lax.dynamic_slice_in_dim(trainer_panels, (1 - core) * half_rows, half_rows, axis=1)
    from_partner = lax.ppermute(other, "tp", partner_perm)
    chip_slots = jnp.where(core == 0, jnp.concatenate([mine, from_partner], axis=0),
                           jnp.concatenate([from_partner, mine], axis=0))
    all_halves = ring_gather(chip_slots, tp_count // 2, 2, 2, 2)
    kv_id = member_id // group_size
    quarter = member_id % group_size
    kv_panel = tp_count + kv_id + kv_count * (quarter // 2)
    half = core
    partner_id = member_id ^ 1
    q_mine = all_halves[panel_home[member_id]]
    q_theirs = lax.ppermute(all_halves[panel_home[partner_id]], "tp", partner_perm)
    q_block = jnp.where(core == 0, jnp.concatenate([q_mine, q_theirs], axis=0),
                        jnp.concatenate([q_theirs, q_mine], axis=0))
    kv_half = all_halves[panel_home[kv_panel]]
    piece = jnp.concatenate([q_block, kv_half], axis=0)
    gathered = exchange(piece, "grp", grp_count, False, 0)
    q_weights = gathered[:, :block_rows].reshape(grp_count * block_rows, head_dim)
    kv_weights = gathered[:, block_rows:]

    use_half = lax.broadcasted_iota(jnp.int32, (1, 2, 1, 1), 1) == half
    kv_rows = jnp.where(use_half, kv_weights[:, None], jnp.zeros_like(kv_weights[:, None]))
    both_weights = jnp.concatenate(
        [q_weights, kv_rows.reshape(grp_count * block_rows, head_dim)], axis=1
    )
    projected = jnp.dot(tokens, both_weights, preferred_element_type=jnp.float32)
    query_rows = projected[:, :head_dim].astype(jnp.bfloat16)
    kv_part = projected[:, head_dim:]
    pair_perm = [(i, i ^ 1) for i in range(tp_count)]
    kv_full = (kv_part + lax.ppermute(kv_part, "tp", pair_perm)).astype(jnp.bfloat16)
    swap_perm = [(i, i ^ 2) for i in range(tp_count)]
    kv_other = lax.ppermute(kv_full, "tp", swap_perm)
    holds_k = quarter < 2
    key_rows = jnp.where(holds_k, kv_full, kv_other)
    value_rows = jnp.where(holds_k, kv_other, kv_full)

    position = jnp.arange(seq_total, dtype=jnp.int32)
    bounds = jnp.cumsum(lengths[0])
    segment = jnp.sum((position[:, None] >= bounds[None, :]).astype(jnp.int32), axis=1)
    allowed = (segment[:, None] == segment[None, :]) & (position[None, :] <= position[:, None])
    score_scale = head_dim ** (-0.5)
    scores = (
        lax.dot_general(
            query_rows, key_rows, (((1,), (1,)), ((), ())), preferred_element_type=jnp.float32
        )
        * score_scale
    )
    masked = jnp.where(allowed, scores, -jnp.inf)
    row_peak = jnp.max(masked, axis=1, keepdims=True)
    row_exp = jnp.exp(masked - row_peak)
    attn_probs = (row_exp / jnp.sum(row_exp, axis=1, keepdims=True)).astype(jnp.bfloat16)
    context = jnp.dot(attn_probs, value_rows, preferred_element_type=jnp.float32)
    outgoing = context.reshape(tp_count, seq_total // tp_count, head_dim)
    return exchange(outgoing, "tp", tp_count, True, 1)


def solution(mesh):
    placed = (P("grp", None), P("tp", "grp", None), P(), P("grp", None))
    return jax.shard_map(
        on_device, mesh=mesh, in_specs=placed, out_specs=P(("grp", "tp"), None), check_vma=False
    )
```

```python
import functools

import jax
import jax.numpy as jnp
from jax import lax
from jax.experimental import pallas as pl
from jax.experimental.pallas import tpu as pltpu
from jax.sharding import PartitionSpec as P

MESH = pl.DeviceIdType.MESH


def ring_kernel(count, stride, chunks, send_ref, out_ref, landed, send_sems, recv_sems):
    me = lax.axis_index("tp")
    total = count * stride
    right, left = lax.rem(me + stride, total), lax.rem(me + total - stride, total)
    spot = me // stride
    barrier = pltpu.get_barrier_semaphore()
    for neighbour in (left, right):
        pl.semaphore_signal(barrier, inc=1, device_id={"tp": neighbour}, device_id_type=MESH)
    pl.semaphore_wait(barrier, 2)

    def incoming(origin, chunk):
        return pltpu.make_async_remote_copy(
            src_ref=send_ref.at[chunk],
            dst_ref=landed.at[origin, chunk],
            send_sem=send_sems.at[0, 0, 0],
            recv_sem=recv_sems.at[origin, chunk],
            device_id={"tp": right},
            device_id_type=MESH,
        )

    landed[spot] = send_ref[...]
    sends = []
    far_right, far_left = count // 2, (count - 1) // 2
    for step in range(1, far_right + 1):
        for chunk in range(chunks):
            streams = [(0, right, lax.rem(spot + count - (step - 1), count))]
            if step <= far_left:
                streams.append((1, left, lax.rem(spot + step - 1, count)))
            for way, target, origin in streams:
                if step > 1:
                    incoming(origin, chunk).wait_recv()
                source = send_ref.at[chunk] if step == 1 else landed.at[origin, chunk]
                copy = pltpu.make_async_remote_copy(
                    src_ref=source,
                    dst_ref=landed.at[origin, chunk],
                    send_sem=send_sems.at[way, step, chunk],
                    recv_sem=recv_sems.at[origin, chunk],
                    device_id={"tp": target},
                    device_id_type=MESH,
                )
                copy.start()
                sends.append(copy)
    for chunk in range(chunks):
        incoming(lax.rem(spot + count - far_right, count), chunk).wait_recv()
        incoming(lax.rem(spot + far_left, count), chunk).wait_recv()
    for copy in sends:
        copy.wait_send()
    out_ref[...] = landed[...]


def ring_gather(x, count, stride, chunks, collective_id):
    x = x.reshape((chunks, x.shape[0] // chunks) + x.shape[1:])
    gathered = pl.pallas_call(
        functools.partial(ring_kernel, count, stride, chunks),
        out_shape=jax.ShapeDtypeStruct((count,) + x.shape, x.dtype),
        in_specs=[pl.BlockSpec(memory_space=pltpu.VMEM)],
        out_specs=pl.BlockSpec(memory_space=pltpu.VMEM),
        scratch_shapes=[
            pltpu.VMEM((count,) + x.shape, x.dtype),
            pltpu.SemaphoreType.DMA((2, count // 2 + 1, chunks)),
            pltpu.SemaphoreType.DMA((count, chunks)),
        ],
        compiler_params=pltpu.CompilerParams(collective_id=collective_id, has_side_effects=True),
    )(x)
    return gathered.reshape((count * x.shape[0] * x.shape[1],) + x.shape[2:])


def grid_kernel(width, send_ref, out_ref, landed, send_sems, recv_sems):
    me = lax.axis_index("grp")
    core = lax.axis_index("tp") % 2
    col, row = me % width, me // width

    def node(c, r):
        return lax.rem(r + width, width) * width + lax.rem(c + width, width)

    def along(dim, c, r, k):
        return node(c + k, r) if dim == 0 else node(c, r + k)

    barrier = pltpu.get_barrier_semaphore()
    neighbours = [node(col + 1, row), node(col - 1, row), node(col, row + 1), node(col, row - 1)]
    for neighbour in neighbours:
        pl.semaphore_signal(barrier, inc=1, device_id={"grp": neighbour}, device_id_type=MESH)
    pl.semaphore_wait(barrier, 4)

    landed[me] = send_ref[...]
    sends = []

    def send(source, origin, half, target):
        copy = pltpu.make_async_remote_copy(
            src_ref=source,
            dst_ref=landed.at[origin, half],
            send_sem=send_sems.at[len(sends)],
            recv_sem=recv_sems.at[origin, half],
            device_id={"grp": target},
            device_id_type=MESH,
        )
        copy.start()
        sends.append(copy)

    def arrive(origin, half):
        pltpu.make_async_remote_copy(
            src_ref=send_ref.at[half],
            dst_ref=landed.at[origin, half],
            send_sem=send_sems.at[0],
            recv_sem=recv_sems.at[origin, half],
            device_id={"grp": neighbours[0]},
            device_id_type=MESH,
        ).wait_recv()

    ahead = 1 - 2 * core

    def phase(lines, half, dim):
        for k in (1, -1):
            for line in lines:
                origin = along(1 - dim, col, row, line)
                source = send_ref.at[half] if line == 0 else landed.at[origin, half]
                send(source, origin, half, along(dim, col, row, k))
        for line in lines:
            for k in (1, -1):
                arrive(along(dim, along(1 - dim, col, row, line) % width, along(1 - dim, col, row, line) // width, k), half)
        for line in lines:
            base = along(1 - dim, col, row, line)
            bc, br = base % width, base // width
            send(landed.at[along(dim, bc, br, -ahead), half], along(dim, bc, br, -ahead), half,
                 along(dim, col, row, ahead))
        for line in lines:
            base = along(1 - dim, col, row, line)
            arrive(along(dim, base % width, base // width, 2), half)

    phase([0], 0, 0)
    phase([0], 1, 1)
    phase([0, 1, -1, 2], 0, 1)
    phase([0, 1, -1, 2], 1, 0)
    for copy in sends:
        copy.wait_send()
    out_ref[...] = landed[...]


def grid_gather(x, width, collective_id):
    count = width * width
    x = x.reshape((2, x.shape[0] // 2) + x.shape[1:])
    gathered = pl.pallas_call(
        functools.partial(grid_kernel, width),
        out_shape=jax.ShapeDtypeStruct((count,) + x.shape, x.dtype),
        in_specs=[pl.BlockSpec(memory_space=pltpu.VMEM)],
        out_specs=pl.BlockSpec(memory_space=pltpu.VMEM),
        scratch_shapes=[
            pltpu.VMEM((count,) + x.shape, x.dtype),
            pltpu.SemaphoreType.DMA((2 * (count - 1),)),
            pltpu.SemaphoreType.DMA((count, 2)),
        ],
        compiler_params=pltpu.CompilerParams(collective_id=collective_id, has_side_effects=True),
    )(x)
    return gathered.reshape((count, x.shape[0] * x.shape[1]) + x.shape[2:])


def exchange_kernel(axis, count, scatter, send_ref, out_ref, landed, send_sems, recv_sems):
    me = lax.axis_index(axis)
    barrier = pltpu.get_barrier_semaphore()
    for step in range(1, count):
        peer = lax.rem(me + step, count)
        pl.semaphore_signal(barrier, inc=1, device_id={axis: peer}, device_id_type=MESH)
    pl.semaphore_wait(barrier, count - 1)
    copies = []
    for step in range(1, count):
        peer = lax.rem(me + step, count)
        source = send_ref.at[peer] if scatter else send_ref
        copy = pltpu.make_async_remote_copy(
            src_ref=source,
            dst_ref=landed.at[me],
            send_sem=send_sems.at[step],
            recv_sem=recv_sems.at[step],
            device_id={axis: peer},
            device_id_type=MESH,
        )
        copy.start()
        copies.append(copy)
    landed[me] = send_ref[me] if scatter else send_ref[...]
    for copy in copies:
        copy.wait()
    if scatter:
        width = landed.shape[-1]
        for source in range(count):
            out_ref[:, source * width:(source + 1) * width] = landed[source]
    else:
        out_ref[...] = landed[...]


def exchange(x, axis, count, scatter, collective_id):
    piece = x.shape[1:] if scatter else x.shape
    result = (piece[0], count * piece[1]) if scatter else (count,) + piece
    return pl.pallas_call(
        functools.partial(exchange_kernel, axis, count, scatter),
        out_shape=jax.ShapeDtypeStruct(result, x.dtype),
        in_specs=[pl.BlockSpec(memory_space=pltpu.VMEM)],
        out_specs=pl.BlockSpec(memory_space=pltpu.VMEM),
        scratch_shapes=[
            pltpu.VMEM((count,) + piece, x.dtype),
            pltpu.SemaphoreType.DMA((count,)),
            pltpu.SemaphoreType.DMA((count,)),
        ],
        compiler_params=pltpu.CompilerParams(collective_id=collective_id, has_side_effects=True),
    )(x)


def on_device(tokens, trainer_panels, panel_home, lengths):
    tp_count = lax.axis_size("tp")
    grp_count = lax.axis_size("grp")
    member_id = lax.axis_index("tp")
    kv_count = (panel_home.shape[0] - tp_count) // 2
    group_size = tp_count // kv_count
    head_dim = trainer_panels.shape[2]
    block_rows = trainer_panels.shape[1]
    half_rows = block_rows // 2
    seq_total = tokens.shape[0]

    core = member_id % 2
    partner_perm = [(i, i ^ 1) for i in range(tp_count)]
    mine = lax.dynamic_slice_in_dim(trainer_panels, core * half_rows, half_rows, axis=1)
    other = lax.dynamic_slice_in_dim(trainer_panels, (1 - core) * half_rows, half_rows, axis=1)
    from_partner = lax.ppermute(other, "tp", partner_perm)
    chip_slots = jnp.where(core == 0, jnp.concatenate([mine, from_partner], axis=0),
                           jnp.concatenate([from_partner, mine], axis=0))
    all_halves = ring_gather(chip_slots, tp_count // 2, 2, 4, 2)
    kv_id = member_id // group_size
    quarter = member_id % group_size
    kv_panel = tp_count + kv_id + kv_count * (quarter // 2)
    half = core
    partner_id = member_id ^ 1
    q_mine = all_halves[panel_home[member_id]]
    q_theirs = lax.ppermute(all_halves[panel_home[partner_id]], "tp", partner_perm)
    q_block = jnp.where(core == 0, jnp.concatenate([q_mine, q_theirs], axis=0),
                        jnp.concatenate([q_theirs, q_mine], axis=0))
    kv_half = all_halves[panel_home[kv_panel]]
    piece = jnp.concatenate([q_block, kv_half], axis=0)
    gathered = grid_gather(piece, 4, 0)
    q_weights = gathered[:, :block_rows].reshape(grp_count * block_rows, head_dim)
    kv_weights = gathered[:, block_rows:]

    use_half = lax.broadcasted_iota(jnp.int32, (1, 2, 1, 1), 1) == half
    kv_rows = jnp.where(use_half, kv_weights[:, None], jnp.zeros_like(kv_weights[:, None]))
    both_weights = jnp.concatenate(
        [q_weights, kv_rows.reshape(grp_count * block_rows, head_dim)], axis=1
    )
    projected = jnp.dot(tokens, both_weights, preferred_element_type=jnp.float32)
    query_rows = projected[:, :head_dim].astype(jnp.bfloat16)
    kv_part = projected[:, head_dim:]
    pair_perm = [(i, i ^ 1) for i in range(tp_count)]
    kv_full = (kv_part + lax.ppermute(kv_part, "tp", pair_perm)).astype(jnp.bfloat16)
    swap_perm = [(i, i ^ 2) for i in range(tp_count)]
    kv_other = lax.ppermute(kv_full, "tp", swap_perm)
    holds_k = quarter < 2
    key_rows = jnp.where(holds_k, kv_full, kv_other)
    value_rows = jnp.where(holds_k, kv_other, kv_full)

    position = jnp.arange(seq_total, dtype=jnp.int32)
    bounds = jnp.cumsum(lengths[0])
    segment = jnp.sum((position[:, None] >= bounds[None, :]).astype(jnp.int32), axis=1)
    allowed = (segment[:, None] == segment[None, :]) & (position[None, :] <= position[:, None])
    score_scale = head_dim ** (-0.5)
    scores = (
        lax.dot_general(
            query_rows, key_rows, (((1,), (1,)), ((), ())), preferred_element_type=jnp.float32
        )
        * score_scale
    )
    masked = jnp.where(allowed, scores, -jnp.inf)
    row_peak = jnp.max(masked, axis=1, keepdims=True)
    row_exp = jnp.exp(masked - row_peak)
    attn_probs = (row_exp / jnp.sum(row_exp, axis=1, keepdims=True)).astype(jnp.bfloat16)
    context = jnp.dot(attn_probs, value_rows, preferred_element_type=jnp.float32)
    outgoing = context.reshape(tp_count, seq_total // tp_count, head_dim)
    return exchange(outgoing, "tp", tp_count, True, 1)


def solution(mesh):
    placed = (P("grp", None), P("tp", "grp", None), P(), P("grp", None))
    return jax.shard_map(
        on_device, mesh=mesh, in_specs=placed, out_specs=P(("grp", "tp"), None), check_vma=False
    )
```

```python
import functools

import jax
import jax.numpy as jnp
from jax import lax
from jax.experimental import pallas as pl
from jax.experimental.pallas import tpu as pltpu
from jax.sharding import PartitionSpec as P

MESH = pl.DeviceIdType.MESH


def ring_kernel(count, stride, chunks, send_ref, out_ref, landed, send_sems, recv_sems):
    me = lax.axis_index("tp")
    total = count * stride
    right, left = lax.rem(me + stride, total), lax.rem(me + total - stride, total)
    spot = me // stride
    barrier = pltpu.get_barrier_semaphore()
    for neighbour in (left, right):
        pl.semaphore_signal(barrier, inc=1, device_id={"tp": neighbour}, device_id_type=MESH)
    pl.semaphore_wait(barrier, 2)

    def incoming(origin, chunk):
        return pltpu.make_async_remote_copy(
            src_ref=send_ref.at[chunk],
            dst_ref=landed.at[origin, chunk],
            send_sem=send_sems.at[0, 0, 0],
            recv_sem=recv_sems.at[origin, chunk],
            device_id={"tp": right},
            device_id_type=MESH,
        )

    landed[spot] = send_ref[...]
    sends = []
    far_right, far_left = count // 2, (count - 1) // 2
    for step in range(1, far_right + 1):
        for chunk in range(chunks):
            streams = [(0, right, lax.rem(spot + count - (step - 1), count))]
            if step <= far_left:
                streams.append((1, left, lax.rem(spot + step - 1, count)))
            for way, target, origin in streams:
                if step > 1:
                    incoming(origin, chunk).wait_recv()
                source = send_ref.at[chunk] if step == 1 else landed.at[origin, chunk]
                copy = pltpu.make_async_remote_copy(
                    src_ref=source,
                    dst_ref=landed.at[origin, chunk],
                    send_sem=send_sems.at[way, step, chunk],
                    recv_sem=recv_sems.at[origin, chunk],
                    device_id={"tp": target},
                    device_id_type=MESH,
                )
                copy.start()
                sends.append(copy)
    for chunk in range(chunks):
        incoming(lax.rem(spot + count - far_right, count), chunk).wait_recv()
        incoming(lax.rem(spot + far_left, count), chunk).wait_recv()
    for copy in sends:
        copy.wait_send()
    out_ref[...] = landed[...]


def ring_gather(x, count, stride, chunks, collective_id):
    x = x.reshape((chunks, x.shape[0] // chunks) + x.shape[1:])
    gathered = pl.pallas_call(
        functools.partial(ring_kernel, count, stride, chunks),
        out_shape=jax.ShapeDtypeStruct((count,) + x.shape, x.dtype),
        in_specs=[pl.BlockSpec(memory_space=pltpu.VMEM)],
        out_specs=pl.BlockSpec(memory_space=pltpu.VMEM),
        scratch_shapes=[
            pltpu.VMEM((count,) + x.shape, x.dtype),
            pltpu.SemaphoreType.DMA((2, count // 2 + 1, chunks)),
            pltpu.SemaphoreType.DMA((count, chunks)),
        ],
        compiler_params=pltpu.CompilerParams(collective_id=collective_id, has_side_effects=True),
    )(x)
    return gathered.reshape((count * x.shape[0] * x.shape[1],) + x.shape[2:])


def chip_ring_kernel(count, panels_ref, out_ref, landed, send_sems, recv_sems):
    me = lax.axis_index("tp")
    total = 2 * count
    core = me % 2
    partner = me + 1 - 2 * core
    right, left = lax.rem(me + 2, total), lax.rem(me + total - 2, total)
    spot = me // 2
    half = panels_ref.shape[1] // 2
    barrier = pltpu.get_barrier_semaphore()
    for neighbour in (left, right, partner):
        pl.semaphore_signal(barrier, inc=1, device_id={"tp": neighbour}, device_id_type=MESH)
    pl.semaphore_wait(barrier, 3)

    def rows_of(slot, which):
        return panels_ref.at[slot, pl.ds(pl.multiple_of(which * half, 16), half)]

    def incoming(origin, chunk):
        return pltpu.make_async_remote_copy(
            src_ref=rows_of(0, 0),
            dst_ref=landed.at[origin, chunk],
            send_sem=send_sems.at[0, 0, 0],
            recv_sem=recv_sems.at[origin, chunk],
            device_id={"tp": right},
            device_id_type=MESH,
        )

    sends = []

    def send(source, origin, chunk, sem, target):
        copy = pltpu.make_async_remote_copy(
            src_ref=source,
            dst_ref=landed.at[origin, chunk],
            send_sem=sem,
            recv_sem=recv_sems.at[origin, chunk],
            device_id={"tp": target},
            device_id_type=MESH,
        )
        copy.start()
        sends.append(copy)

    own = [2 * core + j for j in range(2)]
    theirs = [2 * (1 - core) + j for j in range(2)]
    for j in range(2):
        send(rows_of(j, 1 - core), spot, own[j], send_sems.at[0, 0, 1 + j], partner)
        landed[spot, own[j]] = rows_of(j, core)[...]
    far_right, far_left = count // 2, (count - 1) // 2
    first = [(rows_of(j, core), own[j]) for j in range(2)] + [(None, theirs[j]) for j in range(2)]
    for position, (source, chunk) in enumerate(first):
        if source is None:
            incoming(spot, chunk).wait_recv()
            source = landed.at[spot, chunk]
        send(source, spot, chunk, send_sems.at[0, 1, position], right)
        if far_left >= 1:
            send(source, spot, chunk, send_sems.at[1, 1, position], left)
    for step in range(2, far_right + 1):
        for chunk in range(4):
            streams = [(0, right, lax.rem(spot + count - (step - 1), count))]
            if step <= far_left:
                streams.append((1, left, lax.rem(spot + step - 1, count)))
            for way, target, origin in streams:
                incoming(origin, chunk).wait_recv()
                send(landed.at[origin, chunk], origin, chunk, send_sems.at[way, step, chunk], target)
    for chunk in range(4):
        incoming(lax.rem(spot + count - far_right, count), chunk).wait_recv()
        incoming(lax.rem(spot + far_left, count), chunk).wait_recv()
    for copy in sends:
        copy.wait_send()
    out_ref[...] = landed[...]


def chip_ring_gather(panels, count, collective_id):
    slots, rows, width = panels.shape
    return pl.pallas_call(
        functools.partial(chip_ring_kernel, count),
        out_shape=jax.ShapeDtypeStruct((count, 2 * slots, rows // 2, width), panels.dtype),
        in_specs=[pl.BlockSpec(memory_space=pltpu.VMEM)],
        out_specs=pl.BlockSpec(memory_space=pltpu.VMEM),
        scratch_shapes=[
            pltpu.VMEM((count, 2 * slots, rows // 2, width), panels.dtype),
            pltpu.SemaphoreType.DMA((2, count // 2 + 1, 2 * slots)),
            pltpu.SemaphoreType.DMA((count, 2 * slots)),
        ],
        compiler_params=pltpu.CompilerParams(collective_id=collective_id, has_side_effects=True),
    )(panels)


def grid_kernel(width, send_ref, out_ref, landed, send_sems, recv_sems):
    me = lax.axis_index("grp")
    core = lax.axis_index("tp") % 2
    col, row = me % width, me // width

    def node(c, r):
        return lax.rem(r + width, width) * width + lax.rem(c + width, width)

    def along(dim, c, r, k):
        return node(c + k, r) if dim == 0 else node(c, r + k)

    barrier = pltpu.get_barrier_semaphore()
    neighbours = [node(col + 1, row), node(col - 1, row), node(col, row + 1), node(col, row - 1)]
    for neighbour in neighbours:
        pl.semaphore_signal(barrier, inc=1, device_id={"grp": neighbour}, device_id_type=MESH)
    pl.semaphore_wait(barrier, 4)

    landed[me] = send_ref[...]
    sends = []

    def send(source, origin, half, target):
        copy = pltpu.make_async_remote_copy(
            src_ref=source,
            dst_ref=landed.at[origin, half],
            send_sem=send_sems.at[len(sends)],
            recv_sem=recv_sems.at[origin, half],
            device_id={"grp": target},
            device_id_type=MESH,
        )
        copy.start()
        sends.append(copy)

    def arrive(origin, half):
        pltpu.make_async_remote_copy(
            src_ref=send_ref.at[half],
            dst_ref=landed.at[origin, half],
            send_sem=send_sems.at[0],
            recv_sem=recv_sems.at[origin, half],
            device_id={"grp": neighbours[0]},
            device_id_type=MESH,
        ).wait_recv()

    ahead = 1 - 2 * core

    def phase(lines, half, dim):
        for k in (1, -1):
            for line in lines:
                origin = along(1 - dim, col, row, line)
                source = send_ref.at[half] if line == 0 else landed.at[origin, half]
                send(source, origin, half, along(dim, col, row, k))
        for line in lines:
            for k in (1, -1):
                arrive(along(dim, along(1 - dim, col, row, line) % width, along(1 - dim, col, row, line) // width, k), half)
        for line in lines:
            base = along(1 - dim, col, row, line)
            bc, br = base % width, base // width
            send(landed.at[along(dim, bc, br, -ahead), half], along(dim, bc, br, -ahead), half,
                 along(dim, col, row, ahead))
        for line in lines:
            base = along(1 - dim, col, row, line)
            arrive(along(dim, base % width, base // width, 2), half)

    phase([0], 0, 0)
    phase([0], 1, 1)
    phase([0, 1, -1, 2], 0, 1)
    phase([0, 1, -1, 2], 1, 0)
    for copy in sends:
        copy.wait_send()
    out_ref[...] = landed[...]


def grid_gather(x, width, collective_id):
    count = width * width
    x = x.reshape((2, x.shape[0] // 2) + x.shape[1:])
    gathered = pl.pallas_call(
        functools.partial(grid_kernel, width),
        out_shape=jax.ShapeDtypeStruct((count,) + x.shape, x.dtype),
        in_specs=[pl.BlockSpec(memory_space=pltpu.VMEM)],
        out_specs=pl.BlockSpec(memory_space=pltpu.VMEM),
        scratch_shapes=[
            pltpu.VMEM((count,) + x.shape, x.dtype),
            pltpu.SemaphoreType.DMA((2 * (count - 1),)),
            pltpu.SemaphoreType.DMA((count, 2)),
        ],
        compiler_params=pltpu.CompilerParams(collective_id=collective_id, has_side_effects=True),
    )(x)
    return gathered.reshape((count, x.shape[0] * x.shape[1]) + x.shape[2:])


def exchange_kernel(axis, count, scatter, send_ref, out_ref, landed, send_sems, recv_sems):
    me = lax.axis_index(axis)
    barrier = pltpu.get_barrier_semaphore()
    for step in range(1, count):
        peer = lax.rem(me + step, count)
        pl.semaphore_signal(barrier, inc=1, device_id={axis: peer}, device_id_type=MESH)
    pl.semaphore_wait(barrier, count - 1)
    copies = []
    for step in range(1, count):
        peer = lax.rem(me + step, count)
        source = send_ref.at[peer] if scatter else send_ref
        copy = pltpu.make_async_remote_copy(
            src_ref=source,
            dst_ref=landed.at[me],
            send_sem=send_sems.at[step],
            recv_sem=recv_sems.at[step],
            device_id={axis: peer},
            device_id_type=MESH,
        )
        copy.start()
        copies.append(copy)
    landed[me] = send_ref[me] if scatter else send_ref[...]
    for copy in copies:
        copy.wait()
    if scatter:
        width = landed.shape[-1]
        for source in range(count):
            out_ref[:, source * width:(source + 1) * width] = landed[source]
    else:
        out_ref[...] = landed[...]


def exchange(x, axis, count, scatter, collective_id):
    piece = x.shape[1:] if scatter else x.shape
    result = (piece[0], count * piece[1]) if scatter else (count,) + piece
    return pl.pallas_call(
        functools.partial(exchange_kernel, axis, count, scatter),
        out_shape=jax.ShapeDtypeStruct(result, x.dtype),
        in_specs=[pl.BlockSpec(memory_space=pltpu.VMEM)],
        out_specs=pl.BlockSpec(memory_space=pltpu.VMEM),
        scratch_shapes=[
            pltpu.VMEM((count,) + piece, x.dtype),
            pltpu.SemaphoreType.DMA((count,)),
            pltpu.SemaphoreType.DMA((count,)),
        ],
        compiler_params=pltpu.CompilerParams(collective_id=collective_id, has_side_effects=True),
    )(x)


def on_device(tokens, trainer_panels, panel_home, lengths):
    tp_count = lax.axis_size("tp")
    grp_count = lax.axis_size("grp")
    member_id = lax.axis_index("tp")
    kv_count = (panel_home.shape[0] - tp_count) // 2
    group_size = tp_count // kv_count
    head_dim = trainer_panels.shape[2]
    block_rows = trainer_panels.shape[1]
    half_rows = block_rows // 2
    seq_total = tokens.shape[0]

    core = member_id % 2
    partner_perm = [(i, i ^ 1) for i in range(tp_count)]
    all_halves = chip_ring_gather(trainer_panels, tp_count // 2, 2)
    all_halves = all_halves.reshape((-1,) + all_halves.shape[2:])
    kv_id = member_id // group_size
    quarter = member_id % group_size
    kv_panel = tp_count + kv_id + kv_count * (quarter // 2)
    half = core
    partner_id = member_id ^ 1
    q_mine = all_halves[panel_home[member_id]]
    q_theirs = lax.ppermute(all_halves[panel_home[partner_id]], "tp", partner_perm)
    q_block = jnp.where(core == 0, jnp.concatenate([q_mine, q_theirs], axis=0),
                        jnp.concatenate([q_theirs, q_mine], axis=0))
    kv_half = all_halves[panel_home[kv_panel]]
    piece = jnp.concatenate([q_block, kv_half], axis=0)
    gathered = exchange(piece, "grp", grp_count, False, 0)
    q_weights = gathered[:, :block_rows].reshape(grp_count * block_rows, head_dim)
    kv_weights = gathered[:, block_rows:]

    use_half = lax.broadcasted_iota(jnp.int32, (1, 2, 1, 1), 1) == half
    kv_rows = jnp.where(use_half, kv_weights[:, None], jnp.zeros_like(kv_weights[:, None]))
    both_weights = jnp.concatenate(
        [q_weights, kv_rows.reshape(grp_count * block_rows, head_dim)], axis=1
    )
    projected = jnp.dot(tokens, both_weights, preferred_element_type=jnp.float32)
    query_rows = projected[:, :head_dim].astype(jnp.bfloat16)
    kv_part = projected[:, head_dim:]
    pair_perm = [(i, i ^ 1) for i in range(tp_count)]
    kv_full = (kv_part + lax.ppermute(kv_part, "tp", pair_perm)).astype(jnp.bfloat16)
    swap_perm = [(i, i ^ 2) for i in range(tp_count)]
    kv_other = lax.ppermute(kv_full, "tp", swap_perm)
    holds_k = quarter < 2
    key_rows = jnp.where(holds_k, kv_full, kv_other)
    value_rows = jnp.where(holds_k, kv_other, kv_full)

    position = jnp.arange(seq_total, dtype=jnp.int32)
    bounds = jnp.cumsum(lengths[0])
    segment = jnp.sum((position[:, None] >= bounds[None, :]).astype(jnp.int32), axis=1)
    allowed = (segment[:, None] == segment[None, :]) & (position[None, :] <= position[:, None])
    score_scale = head_dim ** (-0.5)
    scores = (
        lax.dot_general(
            query_rows, key_rows, (((1,), (1,)), ((), ())), preferred_element_type=jnp.float32
        )
        * score_scale
    )
    masked = jnp.where(allowed, scores, -jnp.inf)
    row_peak = jnp.max(masked, axis=1, keepdims=True)
    row_exp = jnp.exp(masked - row_peak)
    attn_probs = (row_exp / jnp.sum(row_exp, axis=1, keepdims=True)).astype(jnp.bfloat16)
    context = jnp.dot(attn_probs, value_rows, preferred_element_type=jnp.float32)
    outgoing = context.reshape(tp_count, seq_total // tp_count, head_dim)
    return exchange(outgoing, "tp", tp_count, True, 1)


def solution(mesh):
    placed = (P("grp", None), P("tp", "grp", None), P(), P("grp", None))
    return jax.shard_map(
        on_device, mesh=mesh, in_specs=placed, out_specs=P(("grp", "tp"), None), check_vma=False
    )
```

```python
import functools

import jax
import jax.numpy as jnp
from jax import lax
from jax.experimental import pallas as pl
from jax.experimental.pallas import tpu as pltpu
from jax.sharding import PartitionSpec as P

MESH = pl.DeviceIdType.MESH


def ring_kernel(count, stride, chunks, send_ref, out_ref, landed, send_sems, recv_sems):
    me = lax.axis_index("tp")
    total = count * stride
    right, left = lax.rem(me + stride, total), lax.rem(me + total - stride, total)
    spot = me // stride
    barrier = pltpu.get_barrier_semaphore()
    for neighbour in (left, right):
        pl.semaphore_signal(barrier, inc=1, device_id={"tp": neighbour}, device_id_type=MESH)
    pl.semaphore_wait(barrier, 2)

    def incoming(origin, chunk):
        return pltpu.make_async_remote_copy(
            src_ref=send_ref.at[chunk],
            dst_ref=landed.at[origin, chunk],
            send_sem=send_sems.at[0, 0, 0],
            recv_sem=recv_sems.at[origin, chunk],
            device_id={"tp": right},
            device_id_type=MESH,
        )

    landed[spot] = send_ref[...]
    sends = []
    far_right, far_left = count // 2, (count - 1) // 2
    for step in range(1, far_right + 1):
        for chunk in range(chunks):
            streams = [(0, right, lax.rem(spot + count - (step - 1), count))]
            if step <= far_left:
                streams.append((1, left, lax.rem(spot + step - 1, count)))
            for way, target, origin in streams:
                if step > 1:
                    incoming(origin, chunk).wait_recv()
                source = send_ref.at[chunk] if step == 1 else landed.at[origin, chunk]
                copy = pltpu.make_async_remote_copy(
                    src_ref=source,
                    dst_ref=landed.at[origin, chunk],
                    send_sem=send_sems.at[way, step, chunk],
                    recv_sem=recv_sems.at[origin, chunk],
                    device_id={"tp": target},
                    device_id_type=MESH,
                )
                copy.start()
                sends.append(copy)
    for chunk in range(chunks):
        incoming(lax.rem(spot + count - far_right, count), chunk).wait_recv()
        incoming(lax.rem(spot + far_left, count), chunk).wait_recv()
    for copy in sends:
        copy.wait_send()
    out_ref[...] = landed[...]


def ring_gather(x, count, stride, chunks, collective_id):
    x = x.reshape((chunks, x.shape[0] // chunks) + x.shape[1:])
    gathered = pl.pallas_call(
        functools.partial(ring_kernel, count, stride, chunks),
        out_shape=jax.ShapeDtypeStruct((count,) + x.shape, x.dtype),
        in_specs=[pl.BlockSpec(memory_space=pltpu.VMEM)],
        out_specs=pl.BlockSpec(memory_space=pltpu.VMEM),
        scratch_shapes=[
            pltpu.VMEM((count,) + x.shape, x.dtype),
            pltpu.SemaphoreType.DMA((2, count // 2 + 1, chunks)),
            pltpu.SemaphoreType.DMA((count, chunks)),
        ],
        compiler_params=pltpu.CompilerParams(collective_id=collective_id, has_side_effects=True),
    )(x)
    return gathered.reshape((count * x.shape[0] * x.shape[1],) + x.shape[2:])


def chip_ring_kernel(count, panels_ref, out_ref, landed, send_sems, recv_sems):
    me = lax.axis_index("tp")
    total = 2 * count
    core = me % 2
    partner = me + 1 - 2 * core
    right, left = lax.rem(me + 2, total), lax.rem(me + total - 2, total)
    spot = me // 2
    half = panels_ref.shape[1] // 2
    barrier = pltpu.get_barrier_semaphore()
    for neighbour in (left, right, partner):
        pl.semaphore_signal(barrier, inc=1, device_id={"tp": neighbour}, device_id_type=MESH)
    pl.semaphore_wait(barrier, 3)

    def rows_of(slot, which):
        return panels_ref.at[slot, pl.ds(pl.multiple_of(which * half, 16), half)]

    def incoming(origin, chunk):
        return pltpu.make_async_remote_copy(
            src_ref=rows_of(0, 0),
            dst_ref=landed.at[origin, chunk],
            send_sem=send_sems.at[0, 0, 0],
            recv_sem=recv_sems.at[origin, chunk],
            device_id={"tp": right},
            device_id_type=MESH,
        )

    sends = []

    def send(source, origin, chunk, sem, target):
        copy = pltpu.make_async_remote_copy(
            src_ref=source,
            dst_ref=landed.at[origin, chunk],
            send_sem=sem,
            recv_sem=recv_sems.at[origin, chunk],
            device_id={"tp": target},
            device_id_type=MESH,
        )
        copy.start()
        sends.append(copy)

    own = [2 * core + j for j in range(2)]
    theirs = [2 * (1 - core) + j for j in range(2)]
    for j in range(2):
        send(rows_of(j, 1 - core), spot, own[j], send_sems.at[0, 0, 1 + j], partner)
        landed[spot, own[j]] = rows_of(j, core)[...]
    far_right, far_left = count // 2, (count - 1) // 2
    first = [(rows_of(j, core), own[j]) for j in range(2)] + [(None, theirs[j]) for j in range(2)]
    for position, (source, chunk) in enumerate(first):
        if source is None:
            incoming(spot, chunk).wait_recv()
            source = landed.at[spot, chunk]
        send(source, spot, chunk, send_sems.at[0, 1, position], right)
        if far_left >= 1:
            send(source, spot, chunk, send_sems.at[1, 1, position], left)
    for step in range(2, far_right + 1):
        for chunk in range(4):
            streams = [(0, right, lax.rem(spot + count - (step - 1), count))]
            if step <= far_left:
                streams.append((1, left, lax.rem(spot + step - 1, count)))
            for way, target, origin in streams:
                incoming(origin, chunk).wait_recv()
                send(landed.at[origin, chunk], origin, chunk, send_sems.at[way, step, chunk], target)
    for chunk in range(4):
        incoming(lax.rem(spot + count - far_right, count), chunk).wait_recv()
        incoming(lax.rem(spot + far_left, count), chunk).wait_recv()
    for copy in sends:
        copy.wait_send()
    out_ref[...] = landed[...]


def chip_ring_gather(panels, count, collective_id):
    slots, rows, width = panels.shape
    return pl.pallas_call(
        functools.partial(chip_ring_kernel, count),
        out_shape=jax.ShapeDtypeStruct((count, 2 * slots, rows // 2, width), panels.dtype),
        in_specs=[pl.BlockSpec(memory_space=pltpu.VMEM)],
        out_specs=pl.BlockSpec(memory_space=pltpu.VMEM),
        scratch_shapes=[
            pltpu.VMEM((count, 2 * slots, rows // 2, width), panels.dtype),
            pltpu.SemaphoreType.DMA((2, count // 2 + 1, 2 * slots)),
            pltpu.SemaphoreType.DMA((count, 2 * slots)),
        ],
        compiler_params=pltpu.CompilerParams(collective_id=collective_id, has_side_effects=True),
    )(panels)


def grid_kernel(width, send_ref, out_ref, landed, send_sems, recv_sems):
    me = lax.axis_index("grp")
    core = lax.axis_index("tp") % 2
    col, row = me % width, me // width

    def node(c, r):
        return lax.rem(r + width, width) * width + lax.rem(c + width, width)

    def along(dim, c, r, k):
        return node(c + k, r) if dim == 0 else node(c, r + k)

    barrier = pltpu.get_barrier_semaphore()
    neighbours = [node(col + 1, row), node(col - 1, row), node(col, row + 1), node(col, row - 1)]
    for neighbour in neighbours:
        pl.semaphore_signal(barrier, inc=1, device_id={"grp": neighbour}, device_id_type=MESH)
    pl.semaphore_wait(barrier, 4)

    landed[me] = send_ref[...]
    sends = []

    def send(source, origin, half, target):
        copy = pltpu.make_async_remote_copy(
            src_ref=source,
            dst_ref=landed.at[origin, half],
            send_sem=send_sems.at[len(sends)],
            recv_sem=recv_sems.at[origin, half],
            device_id={"grp": target},
            device_id_type=MESH,
        )
        copy.start()
        sends.append(copy)

    def arrive(origin, half):
        pltpu.make_async_remote_copy(
            src_ref=send_ref.at[half],
            dst_ref=landed.at[origin, half],
            send_sem=send_sems.at[0],
            recv_sem=recv_sems.at[origin, half],
            device_id={"grp": neighbours[0]},
            device_id_type=MESH,
        ).wait_recv()

    ahead = 1 - 2 * core

    def phase(lines, half, dim):
        for k in (1, -1):
            for line in lines:
                origin = along(1 - dim, col, row, line)
                source = send_ref.at[half] if line == 0 else landed.at[origin, half]
                send(source, origin, half, along(dim, col, row, k))
        for line in lines:
            for k in (1, -1):
                arrive(along(dim, along(1 - dim, col, row, line) % width, along(1 - dim, col, row, line) // width, k), half)
        for line in lines:
            base = along(1 - dim, col, row, line)
            bc, br = base % width, base // width
            send(landed.at[along(dim, bc, br, -ahead), half], along(dim, bc, br, -ahead), half,
                 along(dim, col, row, ahead))
        for line in lines:
            base = along(1 - dim, col, row, line)
            arrive(along(dim, base % width, base // width, 2), half)

    phase([0], 0, 0)
    phase([0], 1, 1)
    phase([0, 1, -1, 2], 0, 1)
    phase([0, 1, -1, 2], 1, 0)
    for copy in sends:
        copy.wait_send()
    out_ref[...] = landed[...]


def grid_gather(x, width, collective_id):
    count = width * width
    x = x.reshape((2, x.shape[0] // 2) + x.shape[1:])
    gathered = pl.pallas_call(
        functools.partial(grid_kernel, width),
        out_shape=jax.ShapeDtypeStruct((count,) + x.shape, x.dtype),
        in_specs=[pl.BlockSpec(memory_space=pltpu.VMEM)],
        out_specs=pl.BlockSpec(memory_space=pltpu.VMEM),
        scratch_shapes=[
            pltpu.VMEM((count,) + x.shape, x.dtype),
            pltpu.SemaphoreType.DMA((2 * (count - 1),)),
            pltpu.SemaphoreType.DMA((count, 2)),
        ],
        compiler_params=pltpu.CompilerParams(collective_id=collective_id, has_side_effects=True),
    )(x)
    return gathered.reshape((count, x.shape[0] * x.shape[1]) + x.shape[2:])


def exchange_kernel(axis, count, scatter, own_barrier, send_ref, out_ref, landed, send_sems, recv_sems):
    me = lax.axis_index(axis)
    if own_barrier:
        barrier = pltpu.get_barrier_semaphore()
        for step in range(1, count):
            peer = lax.rem(me + step, count)
            pl.semaphore_signal(barrier, inc=1, device_id={axis: peer}, device_id_type=MESH)
        pl.semaphore_wait(barrier, count - 1)
    copies = []
    for step in range(1, count):
        peer = lax.rem(me + step, count)
        source = send_ref.at[peer] if scatter else send_ref
        copy = pltpu.make_async_remote_copy(
            src_ref=source,
            dst_ref=landed.at[me],
            send_sem=send_sems.at[step],
            recv_sem=recv_sems.at[step],
            device_id={axis: peer},
            device_id_type=MESH,
        )
        copy.start()
        copies.append(copy)
    landed[me] = send_ref[me] if scatter else send_ref[...]
    for copy in copies:
        copy.wait()
    if scatter:
        width = landed.shape[-1]
        for source in range(count):
            out_ref[:, source * width:(source + 1) * width] = landed[source]
    else:
        out_ref[...] = landed[...]


def exchange(x, axis, count, scatter, collective_id):
    piece = x.shape[1:] if scatter else x.shape
    result = (piece[0], count * piece[1]) if scatter else (count,) + piece
    own_barrier = collective_id is not None
    params = dict(collective_id=collective_id) if own_barrier else {}
    return pl.pallas_call(
        functools.partial(exchange_kernel, axis, count, scatter, own_barrier),
        out_shape=jax.ShapeDtypeStruct(result, x.dtype),
        in_specs=[pl.BlockSpec(memory_space=pltpu.VMEM)],
        out_specs=pl.BlockSpec(memory_space=pltpu.VMEM),
        scratch_shapes=[
            pltpu.VMEM((count,) + piece, x.dtype),
            pltpu.SemaphoreType.DMA((count,)),
            pltpu.SemaphoreType.DMA((count,)),
        ],
        compiler_params=pltpu.CompilerParams(has_side_effects=True, **params),
    )(x)


def on_device(tokens, trainer_panels, panel_home, lengths):
    tp_count = lax.axis_size("tp")
    grp_count = lax.axis_size("grp")
    member_id = lax.axis_index("tp")
    kv_count = (panel_home.shape[0] - tp_count) // 2
    group_size = tp_count // kv_count
    head_dim = trainer_panels.shape[2]
    block_rows = trainer_panels.shape[1]
    half_rows = block_rows // 2
    seq_total = tokens.shape[0]

    core = member_id % 2
    partner_perm = [(i, i ^ 1) for i in range(tp_count)]
    all_halves = chip_ring_gather(trainer_panels, tp_count // 2, 2)
    all_halves = all_halves.reshape((-1,) + all_halves.shape[2:])
    kv_id = member_id // group_size
    quarter = member_id % group_size
    kv_panel = tp_count + kv_id + kv_count * (quarter // 2)
    half = core
    partner_id = member_id ^ 1
    q_mine = all_halves[panel_home[member_id]]
    q_theirs = lax.ppermute(all_halves[panel_home[partner_id]], "tp", partner_perm)
    q_block = jnp.where(core == 0, jnp.concatenate([q_mine, q_theirs], axis=0),
                        jnp.concatenate([q_theirs, q_mine], axis=0))
    kv_half = all_halves[panel_home[kv_panel]]
    piece = jnp.concatenate([q_block, kv_half], axis=0)
    gathered = exchange(piece, "grp", grp_count, False, 0)
    q_weights = gathered[:, :block_rows].reshape(grp_count * block_rows, head_dim)
    kv_weights = gathered[:, block_rows:]

    use_half = lax.broadcasted_iota(jnp.int32, (1, 2, 1, 1), 1) == half
    kv_rows = jnp.where(use_half, kv_weights[:, None], jnp.zeros_like(kv_weights[:, None]))
    both_weights = jnp.concatenate(
        [q_weights, kv_rows.reshape(grp_count * block_rows, head_dim)], axis=1
    )
    projected = jnp.dot(tokens, both_weights, preferred_element_type=jnp.float32)
    query_rows = projected[:, :head_dim].astype(jnp.bfloat16)
    kv_part = projected[:, head_dim:]
    pair_perm = [(i, i ^ 1) for i in range(tp_count)]
    kv_full = (kv_part + lax.ppermute(kv_part, "tp", pair_perm)).astype(jnp.bfloat16)
    swap_perm = [(i, i ^ 2) for i in range(tp_count)]
    kv_other = lax.ppermute(kv_full, "tp", swap_perm)
    holds_k = quarter < 2
    key_rows = jnp.where(holds_k, kv_full, kv_other)
    value_rows = jnp.where(holds_k, kv_other, kv_full)

    position = jnp.arange(seq_total, dtype=jnp.int32)
    bounds = jnp.cumsum(lengths[0])
    segment = jnp.sum((position[:, None] >= bounds[None, :]).astype(jnp.int32), axis=1)
    allowed = (segment[:, None] == segment[None, :]) & (position[None, :] <= position[:, None])
    score_scale = head_dim ** (-0.5)
    scores = (
        lax.dot_general(
            query_rows, key_rows, (((1,), (1,)), ((), ())), preferred_element_type=jnp.float32
        )
        * score_scale
    )
    masked = jnp.where(allowed, scores, -jnp.inf)
    row_peak = jnp.max(masked, axis=1, keepdims=True)
    row_exp = jnp.exp(masked - row_peak)
    attn_probs = (row_exp / jnp.sum(row_exp, axis=1, keepdims=True)).astype(jnp.bfloat16)
    context = jnp.dot(attn_probs, value_rows, preferred_element_type=jnp.float32)
    outgoing = context.reshape(tp_count, seq_total // tp_count, head_dim)
    return exchange(outgoing, "tp", tp_count, True, None)


def solution(mesh):
    placed = (P("grp", None), P("tp", "grp", None), P(), P("grp", None))
    return jax.shard_map(
        on_device, mesh=mesh, in_specs=placed, out_specs=P(("grp", "tp"), None), check_vma=False
    )
```

```python
import functools

import jax
import jax.numpy as jnp
from jax import lax
from jax.experimental import pallas as pl
from jax.experimental.pallas import tpu as pltpu
from jax.sharding import PartitionSpec as P

MESH = pl.DeviceIdType.MESH


def ring_kernel(count, stride, chunks, send_ref, out_ref, landed, send_sems, recv_sems):
    me = lax.axis_index("tp")
    total = count * stride
    right, left = lax.rem(me + stride, total), lax.rem(me + total - stride, total)
    spot = me // stride
    barrier = pltpu.get_barrier_semaphore()
    for neighbour in (left, right):
        pl.semaphore_signal(barrier, inc=1, device_id={"tp": neighbour}, device_id_type=MESH)
    pl.semaphore_wait(barrier, 2)

    def incoming(origin, chunk):
        return pltpu.make_async_remote_copy(
            src_ref=send_ref.at[chunk],
            dst_ref=landed.at[origin, chunk],
            send_sem=send_sems.at[0, 0, 0],
            recv_sem=recv_sems.at[origin, chunk],
            device_id={"tp": right},
            device_id_type=MESH,
        )

    landed[spot] = send_ref[...]
    sends = []
    far_right, far_left = count // 2, (count - 1) // 2
    for step in range(1, far_right + 1):
        for chunk in range(chunks):
            streams = [(0, right, lax.rem(spot + count - (step - 1), count))]
            if step <= far_left:
                streams.append((1, left, lax.rem(spot + step - 1, count)))
            for way, target, origin in streams:
                if step > 1:
                    incoming(origin, chunk).wait_recv()
                source = send_ref.at[chunk] if step == 1 else landed.at[origin, chunk]
                copy = pltpu.make_async_remote_copy(
                    src_ref=source,
                    dst_ref=landed.at[origin, chunk],
                    send_sem=send_sems.at[way, step, chunk],
                    recv_sem=recv_sems.at[origin, chunk],
                    device_id={"tp": target},
                    device_id_type=MESH,
                )
                copy.start()
                sends.append(copy)
    for chunk in range(chunks):
        incoming(lax.rem(spot + count - far_right, count), chunk).wait_recv()
        incoming(lax.rem(spot + far_left, count), chunk).wait_recv()
    for copy in sends:
        copy.wait_send()
    out_ref[...] = landed[...]


def ring_gather(x, count, stride, chunks, collective_id):
    x = x.reshape((chunks, x.shape[0] // chunks) + x.shape[1:])
    gathered = pl.pallas_call(
        functools.partial(ring_kernel, count, stride, chunks),
        out_shape=jax.ShapeDtypeStruct((count,) + x.shape, x.dtype),
        in_specs=[pl.BlockSpec(memory_space=pltpu.VMEM)],
        out_specs=pl.BlockSpec(memory_space=pltpu.VMEM),
        scratch_shapes=[
            pltpu.VMEM((count,) + x.shape, x.dtype),
            pltpu.SemaphoreType.DMA((2, count // 2 + 1, chunks)),
            pltpu.SemaphoreType.DMA((count, chunks)),
        ],
        compiler_params=pltpu.CompilerParams(collective_id=collective_id, has_side_effects=True),
    )(x)
    return gathered.reshape((count * x.shape[0] * x.shape[1],) + x.shape[2:])


def chip_ring_kernel(count, panels_ref, out_ref, landed, send_sems, recv_sems):
    me = lax.axis_index("tp")
    total = 2 * count
    core = me % 2
    partner = me + 1 - 2 * core
    right, left = lax.rem(me + 2, total), lax.rem(me + total - 2, total)
    spot = me // 2
    half = panels_ref.shape[1] // 2
    barrier = pltpu.get_barrier_semaphore()
    for neighbour in (left, right, partner):
        pl.semaphore_signal(barrier, inc=1, device_id={"tp": neighbour}, device_id_type=MESH)
    pl.semaphore_wait(barrier, 3)

    def rows_of(slot, which):
        return panels_ref.at[slot, pl.ds(pl.multiple_of(which * half, 16), half)]

    def incoming(origin, chunk):
        return pltpu.make_async_remote_copy(
            src_ref=rows_of(0, 0),
            dst_ref=landed.at[origin, chunk],
            send_sem=send_sems.at[0, 0, 0],
            recv_sem=recv_sems.at[origin, chunk],
            device_id={"tp": right},
            device_id_type=MESH,
        )

    sends = []

    def send(source, origin, chunk, sem, target):
        copy = pltpu.make_async_remote_copy(
            src_ref=source,
            dst_ref=landed.at[origin, chunk],
            send_sem=sem,
            recv_sem=recv_sems.at[origin, chunk],
            device_id={"tp": target},
            device_id_type=MESH,
        )
        copy.start()
        sends.append(copy)

    own = [2 * core + j for j in range(2)]
    theirs = [2 * (1 - core) + j for j in range(2)]
    for j in range(2):
        send(rows_of(j, 1 - core), spot, own[j], send_sems.at[0, 0, 1 + j], partner)
        landed[spot, own[j]] = rows_of(j, core)[...]
    far_right, far_left = count // 2, (count - 1) // 2
    first = [(rows_of(j, core), own[j]) for j in range(2)] + [(None, theirs[j]) for j in range(2)]
    for position, (source, chunk) in enumerate(first):
        if source is None:
            incoming(spot, chunk).wait_recv()
            source = landed.at[spot, chunk]
        send(source, spot, chunk, send_sems.at[0, 1, position], right)
        if far_left >= 1:
            send(source, spot, chunk, send_sems.at[1, 1, position], left)
    for step in range(2, far_right + 1):
        for chunk in range(4):
            streams = [(0, right, lax.rem(spot + count - (step - 1), count))]
            if step <= far_left:
                streams.append((1, left, lax.rem(spot + step - 1, count)))
            for way, target, origin in streams:
                incoming(origin, chunk).wait_recv()
                send(landed.at[origin, chunk], origin, chunk, send_sems.at[way, step, chunk], target)
    for chunk in range(4):
        incoming(lax.rem(spot + count - far_right, count), chunk).wait_recv()
        incoming(lax.rem(spot + far_left, count), chunk).wait_recv()
    for copy in sends:
        copy.wait_send()
    out_ref[...] = landed[...]


def chip_ring_gather(panels, count, collective_id):
    slots, rows, width = panels.shape
    return pl.pallas_call(
        functools.partial(chip_ring_kernel, count),
        out_shape=jax.ShapeDtypeStruct((count, 2 * slots, rows // 2, width), panels.dtype),
        in_specs=[pl.BlockSpec(memory_space=pltpu.VMEM)],
        out_specs=pl.BlockSpec(memory_space=pltpu.VMEM),
        scratch_shapes=[
            pltpu.VMEM((count, 2 * slots, rows // 2, width), panels.dtype),
            pltpu.SemaphoreType.DMA((2, count // 2 + 1, 2 * slots)),
            pltpu.SemaphoreType.DMA((count, 2 * slots)),
        ],
        compiler_params=pltpu.CompilerParams(collective_id=collective_id, has_side_effects=True),
    )(panels)


def kv_share_kernel(part_ref, out_ref, partner_part, mine, theirs, send_sems, recv_sems):
    me = lax.axis_index("tp")
    partner = me + 1 - 2 * (me % 2)
    across = me + 2 - 4 * ((me // 2) % 2)
    barrier = pltpu.get_barrier_semaphore()
    for neighbour in (partner, across):
        pl.semaphore_signal(barrier, inc=1, device_id={"tp": neighbour}, device_id_type=MESH)
    pl.semaphore_wait(barrier, 2)
    first = pltpu.make_async_remote_copy(
        src_ref=part_ref, dst_ref=partner_part, send_sem=send_sems.at[0], recv_sem=recv_sems.at[0],
        device_id={"tp": partner}, device_id_type=MESH,
    )
    first.start()
    first.wait()
    mine[...] = (part_ref[...] + partner_part[...]).astype(mine.dtype)
    second = pltpu.make_async_remote_copy(
        src_ref=mine, dst_ref=theirs, send_sem=send_sems.at[1], recv_sem=recv_sems.at[1],
        device_id={"tp": across}, device_id_type=MESH,
    )
    second.start()
    second.wait()
    holds_k = (me % 4) < 2
    out_ref[0] = jnp.where(holds_k, mine[...], theirs[...])
    out_ref[1] = jnp.where(holds_k, theirs[...], mine[...])


def kv_share(part, collective_id):
    return pl.pallas_call(
        kv_share_kernel,
        out_shape=jax.ShapeDtypeStruct((2,) + part.shape, jnp.bfloat16),
        in_specs=[pl.BlockSpec(memory_space=pltpu.VMEM)],
        out_specs=pl.BlockSpec(memory_space=pltpu.VMEM),
        scratch_shapes=[
            pltpu.VMEM(part.shape, part.dtype),
            pltpu.VMEM(part.shape, jnp.bfloat16),
            pltpu.VMEM(part.shape, jnp.bfloat16),
            pltpu.SemaphoreType.DMA((2,)),
            pltpu.SemaphoreType.DMA((2,)),
        ],
        compiler_params=pltpu.CompilerParams(collective_id=collective_id, has_side_effects=True),
    )(part)


def grid_kernel(width, send_ref, out_ref, landed, send_sems, recv_sems):
    me = lax.axis_index("grp")
    core = lax.axis_index("tp") % 2
    col, row = me % width, me // width

    def node(c, r):
        return lax.rem(r + width, width) * width + lax.rem(c + width, width)

    def along(dim, c, r, k):
        return node(c + k, r) if dim == 0 else node(c, r + k)

    barrier = pltpu.get_barrier_semaphore()
    neighbours = [node(col + 1, row), node(col - 1, row), node(col, row + 1), node(col, row - 1)]
    for neighbour in neighbours:
        pl.semaphore_signal(barrier, inc=1, device_id={"grp": neighbour}, device_id_type=MESH)
    pl.semaphore_wait(barrier, 4)

    landed[me] = send_ref[...]
    sends = []

    def send(source, origin, half, target):
        copy = pltpu.make_async_remote_copy(
            src_ref=source,
            dst_ref=landed.at[origin, half],
            send_sem=send_sems.at[len(sends)],
            recv_sem=recv_sems.at[origin, half],
            device_id={"grp": target},
            device_id_type=MESH,
        )
        copy.start()
        sends.append(copy)

    def arrive(origin, half):
        pltpu.make_async_remote_copy(
            src_ref=send_ref.at[half],
            dst_ref=landed.at[origin, half],
            send_sem=send_sems.at[0],
            recv_sem=recv_sems.at[origin, half],
            device_id={"grp": neighbours[0]},
            device_id_type=MESH,
        ).wait_recv()

    ahead = 1 - 2 * core

    def phase(lines, half, dim):
        for k in (1, -1):
            for line in lines:
                origin = along(1 - dim, col, row, line)
                source = send_ref.at[half] if line == 0 else landed.at[origin, half]
                send(source, origin, half, along(dim, col, row, k))
        for line in lines:
            for k in (1, -1):
                arrive(along(dim, along(1 - dim, col, row, line) % width, along(1 - dim, col, row, line) // width, k), half)
        for line in lines:
            base = along(1 - dim, col, row, line)
            bc, br = base % width, base // width
            send(landed.at[along(dim, bc, br, -ahead), half], along(dim, bc, br, -ahead), half,
                 along(dim, col, row, ahead))
        for line in lines:
            base = along(1 - dim, col, row, line)
            arrive(along(dim, base % width, base // width, 2), half)

    phase([0], 0, 0)
    phase([0], 1, 1)
    phase([0, 1, -1, 2], 0, 1)
    phase([0, 1, -1, 2], 1, 0)
    for copy in sends:
        copy.wait_send()
    out_ref[...] = landed[...]


def grid_gather(x, width, collective_id):
    count = width * width
    x = x.reshape((2, x.shape[0] // 2) + x.shape[1:])
    gathered = pl.pallas_call(
        functools.partial(grid_kernel, width),
        out_shape=jax.ShapeDtypeStruct((count,) + x.shape, x.dtype),
        in_specs=[pl.BlockSpec(memory_space=pltpu.VMEM)],
        out_specs=pl.BlockSpec(memory_space=pltpu.VMEM),
        scratch_shapes=[
            pltpu.VMEM((count,) + x.shape, x.dtype),
            pltpu.SemaphoreType.DMA((2 * (count - 1),)),
            pltpu.SemaphoreType.DMA((count, 2)),
        ],
        compiler_params=pltpu.CompilerParams(collective_id=collective_id, has_side_effects=True),
    )(x)
    return gathered.reshape((count, x.shape[0] * x.shape[1]) + x.shape[2:])


def exchange_kernel(axis, count, scatter, send_ref, out_ref, landed, send_sems, recv_sems):
    me = lax.axis_index(axis)
    barrier = pltpu.get_barrier_semaphore()
    for step in range(1, count):
        peer = lax.rem(me + step, count)
        pl.semaphore_signal(barrier, inc=1, device_id={axis: peer}, device_id_type=MESH)
    pl.semaphore_wait(barrier, count - 1)
    copies = []
    for step in range(1, count):
        peer = lax.rem(me + step, count)
        source = send_ref.at[peer] if scatter else send_ref
        copy = pltpu.make_async_remote_copy(
            src_ref=source,
            dst_ref=landed.at[me],
            send_sem=send_sems.at[step],
            recv_sem=recv_sems.at[step],
            device_id={axis: peer},
            device_id_type=MESH,
        )
        copy.start()
        copies.append(copy)
    landed[me] = send_ref[me] if scatter else send_ref[...]
    for copy in copies:
        copy.wait()
    if scatter:
        width = landed.shape[-1]
        for source in range(count):
            out_ref[:, source * width:(source + 1) * width] = landed[source]
    else:
        out_ref[...] = landed[...]


def exchange(x, axis, count, scatter, collective_id):
    piece = x.shape[1:] if scatter else x.shape
    result = (piece[0], count * piece[1]) if scatter else (count,) + piece
    return pl.pallas_call(
        functools.partial(exchange_kernel, axis, count, scatter),
        out_shape=jax.ShapeDtypeStruct(result, x.dtype),
        in_specs=[pl.BlockSpec(memory_space=pltpu.VMEM)],
        out_specs=pl.BlockSpec(memory_space=pltpu.VMEM),
        scratch_shapes=[
            pltpu.VMEM((count,) + piece, x.dtype),
            pltpu.SemaphoreType.DMA((count,)),
            pltpu.SemaphoreType.DMA((count,)),
        ],
        compiler_params=pltpu.CompilerParams(collective_id=collective_id, has_side_effects=True),
    )(x)


def on_device(tokens, trainer_panels, panel_home, lengths):
    tp_count = lax.axis_size("tp")
    grp_count = lax.axis_size("grp")
    member_id = lax.axis_index("tp")
    kv_count = (panel_home.shape[0] - tp_count) // 2
    group_size = tp_count // kv_count
    head_dim = trainer_panels.shape[2]
    block_rows = trainer_panels.shape[1]
    half_rows = block_rows // 2
    seq_total = tokens.shape[0]

    core = member_id % 2
    partner_perm = [(i, i ^ 1) for i in range(tp_count)]
    all_halves = chip_ring_gather(trainer_panels, tp_count // 2, 2)
    all_halves = all_halves.reshape((-1,) + all_halves.shape[2:])
    kv_id = member_id // group_size
    quarter = member_id % group_size
    kv_panel = tp_count + kv_id + kv_count * (quarter // 2)
    half = core
    partner_id = member_id ^ 1
    q_mine = all_halves[panel_home[member_id]]
    q_theirs = lax.ppermute(all_halves[panel_home[partner_id]], "tp", partner_perm)
    q_block = jnp.where(core == 0, jnp.concatenate([q_mine, q_theirs], axis=0),
                        jnp.concatenate([q_theirs, q_mine], axis=0))
    kv_half = all_halves[panel_home[kv_panel]]
    piece = jnp.concatenate([q_block, kv_half], axis=0)
    gathered = exchange(piece, "grp", grp_count, False, 0)
    q_weights = gathered[:, :block_rows].reshape(grp_count * block_rows, head_dim)
    kv_weights = gathered[:, block_rows:]

    use_half = lax.broadcasted_iota(jnp.int32, (1, 2, 1, 1), 1) == half
    kv_rows = jnp.where(use_half, kv_weights[:, None], jnp.zeros_like(kv_weights[:, None]))
    both_weights = jnp.concatenate(
        [q_weights, kv_rows.reshape(grp_count * block_rows, head_dim)], axis=1
    )
    projected = jnp.dot(tokens, both_weights, preferred_element_type=jnp.float32)
    query_rows = projected[:, :head_dim].astype(jnp.bfloat16)
    kv_part = projected[:, head_dim:]
    key_rows, value_rows = kv_share(kv_part, 3)

    position = jnp.arange(seq_total, dtype=jnp.int32)
    bounds = jnp.cumsum(lengths[0])
    segment = jnp.sum((position[:, None] >= bounds[None, :]).astype(jnp.int32), axis=1)
    allowed = (segment[:, None] == segment[None, :]) & (position[None, :] <= position[:, None])
    score_scale = head_dim ** (-0.5)
    scores = (
        lax.dot_general(
            query_rows, key_rows, (((1,), (1,)), ((), ())), preferred_element_type=jnp.float32
        )
        * score_scale
    )
    masked = jnp.where(allowed, scores, -jnp.inf)
    row_peak = jnp.max(masked, axis=1, keepdims=True)
    row_exp = jnp.exp(masked - row_peak)
    attn_probs = (row_exp / jnp.sum(row_exp, axis=1, keepdims=True)).astype(jnp.bfloat16)
    context = jnp.dot(attn_probs, value_rows, preferred_element_type=jnp.float32)
    outgoing = context.reshape(tp_count, seq_total // tp_count, head_dim)
    return exchange(outgoing, "tp", tp_count, True, 1)


def solution(mesh):
    placed = (P("grp", None), P("tp", "grp", None), P(), P("grp", None))
    return jax.shard_map(
        on_device, mesh=mesh, in_specs=placed, out_specs=P(("grp", "tp"), None), check_vma=False
    )
```

```python
import functools

import jax
import jax.numpy as jnp
from jax import lax
from jax.experimental import pallas as pl
from jax.experimental.pallas import tpu as pltpu
from jax.sharding import PartitionSpec as P

MESH = pl.DeviceIdType.MESH


def ring_kernel(count, stride, chunks, send_ref, out_ref, landed, send_sems, recv_sems):
    me = lax.axis_index("tp")
    total = count * stride
    right, left = lax.rem(me + stride, total), lax.rem(me + total - stride, total)
    spot = me // stride
    barrier = pltpu.get_barrier_semaphore()
    for neighbour in (left, right):
        pl.semaphore_signal(barrier, inc=1, device_id={"tp": neighbour}, device_id_type=MESH)
    pl.semaphore_wait(barrier, 2)

    def incoming(origin, chunk):
        return pltpu.make_async_remote_copy(
            src_ref=send_ref.at[chunk],
            dst_ref=landed.at[origin, chunk],
            send_sem=send_sems.at[0, 0, 0],
            recv_sem=recv_sems.at[origin, chunk],
            device_id={"tp": right},
            device_id_type=MESH,
        )

    landed[spot] = send_ref[...]
    sends = []
    far_right, far_left = count // 2, (count - 1) // 2
    for step in range(1, far_right + 1):
        for chunk in range(chunks):
            streams = [(0, right, lax.rem(spot + count - (step - 1), count))]
            if step <= far_left:
                streams.append((1, left, lax.rem(spot + step - 1, count)))
            for way, target, origin in streams:
                if step > 1:
                    incoming(origin, chunk).wait_recv()
                source = send_ref.at[chunk] if step == 1 else landed.at[origin, chunk]
                copy = pltpu.make_async_remote_copy(
                    src_ref=source,
                    dst_ref=landed.at[origin, chunk],
                    send_sem=send_sems.at[way, step, chunk],
                    recv_sem=recv_sems.at[origin, chunk],
                    device_id={"tp": target},
                    device_id_type=MESH,
                )
                copy.start()
                sends.append(copy)
    for chunk in range(chunks):
        incoming(lax.rem(spot + count - far_right, count), chunk).wait_recv()
        incoming(lax.rem(spot + far_left, count), chunk).wait_recv()
    for copy in sends:
        copy.wait_send()
    out_ref[...] = landed[...]


def ring_gather(x, count, stride, chunks, collective_id):
    x = x.reshape((chunks, x.shape[0] // chunks) + x.shape[1:])
    gathered = pl.pallas_call(
        functools.partial(ring_kernel, count, stride, chunks),
        out_shape=jax.ShapeDtypeStruct((count,) + x.shape, x.dtype),
        in_specs=[pl.BlockSpec(memory_space=pltpu.VMEM)],
        out_specs=pl.BlockSpec(memory_space=pltpu.VMEM),
        scratch_shapes=[
            pltpu.VMEM((count,) + x.shape, x.dtype),
            pltpu.SemaphoreType.DMA((2, count // 2 + 1, chunks)),
            pltpu.SemaphoreType.DMA((count, chunks)),
        ],
        compiler_params=pltpu.CompilerParams(collective_id=collective_id, has_side_effects=True),
    )(x)
    return gathered.reshape((count * x.shape[0] * x.shape[1],) + x.shape[2:])


def chip_ring_kernel(count, panels_ref, out_ref, landed, send_sems, recv_sems):
    me = lax.axis_index("tp")
    total = 2 * count
    core = me % 2
    partner = me + 1 - 2 * core
    right, left = lax.rem(me + 2, total), lax.rem(me + total - 2, total)
    spot = me // 2
    half = panels_ref.shape[1] // 2
    barrier = pltpu.get_barrier_semaphore()
    for neighbour in (left, right, partner):
        pl.semaphore_signal(barrier, inc=1, device_id={"tp": neighbour}, device_id_type=MESH)
    pl.semaphore_wait(barrier, 3)

    def rows_of(slot, which):
        return panels_ref.at[slot, pl.ds(pl.multiple_of(which * half, 16), half)]

    def incoming(origin, chunk):
        return pltpu.make_async_remote_copy(
            src_ref=rows_of(0, 0),
            dst_ref=landed.at[origin, chunk],
            send_sem=send_sems.at[0, 0, 0],
            recv_sem=recv_sems.at[origin, chunk],
            device_id={"tp": right},
            device_id_type=MESH,
        )

    sends = []

    def send(source, origin, chunk, sem, target):
        copy = pltpu.make_async_remote_copy(
            src_ref=source,
            dst_ref=landed.at[origin, chunk],
            send_sem=sem,
            recv_sem=recv_sems.at[origin, chunk],
            device_id={"tp": target},
            device_id_type=MESH,
        )
        copy.start()
        sends.append(copy)

    own = [2 * core + j for j in range(2)]
    theirs = [2 * (1 - core) + j for j in range(2)]
    for j in range(2):
        send(rows_of(j, 1 - core), spot, own[j], send_sems.at[0, 0, 1 + j], partner)
        landed[spot, own[j]] = rows_of(j, core)[...]
    far_right, far_left = count // 2, (count - 1) // 2
    first = [(rows_of(j, core), own[j]) for j in range(2)] + [(None, theirs[j]) for j in range(2)]
    for position, (source, chunk) in enumerate(first):
        if source is None:
            incoming(spot, chunk).wait_recv()
            source = landed.at[spot, chunk]
        send(source, spot, chunk, send_sems.at[0, 1, position], right)
        if far_left >= 1:
            send(source, spot, chunk, send_sems.at[1, 1, position], left)
    for step in range(2, far_right + 1):
        for chunk in range(4):
            streams = [(0, right, lax.rem(spot + count - (step - 1), count))]
            if step <= far_left:
                streams.append((1, left, lax.rem(spot + step - 1, count)))
            for way, target, origin in streams:
                incoming(origin, chunk).wait_recv()
                send(landed.at[origin, chunk], origin, chunk, send_sems.at[way, step, chunk], target)
    for chunk in range(4):
        incoming(lax.rem(spot + count - far_right, count), chunk).wait_recv()
        incoming(lax.rem(spot + far_left, count), chunk).wait_recv()
    for copy in sends:
        copy.wait_send()
    out_ref[...] = landed[...]


def chip_ring_gather(panels, count, collective_id):
    slots, rows, width = panels.shape
    return pl.pallas_call(
        functools.partial(chip_ring_kernel, count),
        out_shape=jax.ShapeDtypeStruct((count, 2 * slots, rows // 2, width), panels.dtype),
        in_specs=[pl.BlockSpec(memory_space=pltpu.VMEM)],
        out_specs=pl.BlockSpec(memory_space=pltpu.VMEM),
        scratch_shapes=[
            pltpu.VMEM((count, 2 * slots, rows // 2, width), panels.dtype),
            pltpu.SemaphoreType.DMA((2, count // 2 + 1, 2 * slots)),
            pltpu.SemaphoreType.DMA((count, 2 * slots)),
        ],
        compiler_params=pltpu.CompilerParams(collective_id=collective_id, has_side_effects=True),
    )(panels)


def kv_share_kernel(part_ref, out_ref, partner_part, mine, theirs, send_sems, recv_sems):
    me = lax.axis_index("tp")
    partner = me + 1 - 2 * (me % 2)
    across = me + 2 - 4 * ((me // 2) % 2)
    barrier = pltpu.get_barrier_semaphore()
    for neighbour in (partner, across):
        pl.semaphore_signal(barrier, inc=1, device_id={"tp": neighbour}, device_id_type=MESH)
    pl.semaphore_wait(barrier, 2)
    first = pltpu.make_async_remote_copy(
        src_ref=part_ref, dst_ref=partner_part, send_sem=send_sems.at[0], recv_sem=recv_sems.at[0],
        device_id={"tp": partner}, device_id_type=MESH,
    )
    first.start()
    first.wait()
    mine[...] = (part_ref[...] + partner_part[...]).astype(mine.dtype)
    second = pltpu.make_async_remote_copy(
        src_ref=mine, dst_ref=theirs, send_sem=send_sems.at[1], recv_sem=recv_sems.at[1],
        device_id={"tp": across}, device_id_type=MESH,
    )
    second.start()
    second.wait()
    holds_k = (me % 4) < 2
    out_ref[0] = jnp.where(holds_k, mine[...], theirs[...])
    out_ref[1] = jnp.where(holds_k, theirs[...], mine[...])


def kv_share(part, collective_id):
    return pl.pallas_call(
        kv_share_kernel,
        out_shape=jax.ShapeDtypeStruct((2,) + part.shape, jnp.bfloat16),
        in_specs=[pl.BlockSpec(memory_space=pltpu.VMEM)],
        out_specs=pl.BlockSpec(memory_space=pltpu.VMEM),
        scratch_shapes=[
            pltpu.VMEM(part.shape, part.dtype),
            pltpu.VMEM(part.shape, jnp.bfloat16),
            pltpu.VMEM(part.shape, jnp.bfloat16),
            pltpu.SemaphoreType.DMA((2,)),
            pltpu.SemaphoreType.DMA((2,)),
        ],
        compiler_params=pltpu.CompilerParams(collective_id=collective_id, has_side_effects=True),
    )(part)


def grid_kernel(width, send_ref, out_ref, landed, send_sems, recv_sems):
    me = lax.axis_index("grp")
    core = lax.axis_index("tp") % 2
    col, row = me % width, me // width

    def node(c, r):
        return lax.rem(r + width, width) * width + lax.rem(c + width, width)

    def along(dim, c, r, k):
        return node(c + k, r) if dim == 0 else node(c, r + k)

    barrier = pltpu.get_barrier_semaphore()
    neighbours = [node(col + 1, row), node(col - 1, row), node(col, row + 1), node(col, row - 1)]
    for neighbour in neighbours:
        pl.semaphore_signal(barrier, inc=1, device_id={"grp": neighbour}, device_id_type=MESH)
    pl.semaphore_wait(barrier, 4)

    landed[me] = send_ref[...]
    sends = []

    def send(source, origin, half, target):
        copy = pltpu.make_async_remote_copy(
            src_ref=source,
            dst_ref=landed.at[origin, half],
            send_sem=send_sems.at[len(sends)],
            recv_sem=recv_sems.at[origin, half],
            device_id={"grp": target},
            device_id_type=MESH,
        )
        copy.start()
        sends.append(copy)

    def arrive(origin, half):
        pltpu.make_async_remote_copy(
            src_ref=send_ref.at[half],
            dst_ref=landed.at[origin, half],
            send_sem=send_sems.at[0],
            recv_sem=recv_sems.at[origin, half],
            device_id={"grp": neighbours[0]},
            device_id_type=MESH,
        ).wait_recv()

    ahead = 1 - 2 * core

    def phase(lines, half, dim):
        for k in (1, -1):
            for line in lines:
                origin = along(1 - dim, col, row, line)
                source = send_ref.at[half] if line == 0 else landed.at[origin, half]
                send(source, origin, half, along(dim, col, row, k))
        for line in lines:
            for k in (1, -1):
                arrive(along(dim, along(1 - dim, col, row, line) % width, along(1 - dim, col, row, line) // width, k), half)
        for line in lines:
            base = along(1 - dim, col, row, line)
            bc, br = base % width, base // width
            send(landed.at[along(dim, bc, br, -ahead), half], along(dim, bc, br, -ahead), half,
                 along(dim, col, row, ahead))
        for line in lines:
            base = along(1 - dim, col, row, line)
            arrive(along(dim, base % width, base // width, 2), half)

    phase([0], 0, 0)
    phase([0], 1, 1)
    phase([0, 1, -1, 2], 0, 1)
    phase([0, 1, -1, 2], 1, 0)
    for copy in sends:
        copy.wait_send()
    out_ref[...] = landed[...]


def grid_gather(x, width, collective_id):
    count = width * width
    x = x.reshape((2, x.shape[0] // 2) + x.shape[1:])
    gathered = pl.pallas_call(
        functools.partial(grid_kernel, width),
        out_shape=jax.ShapeDtypeStruct((count,) + x.shape, x.dtype),
        in_specs=[pl.BlockSpec(memory_space=pltpu.VMEM)],
        out_specs=pl.BlockSpec(memory_space=pltpu.VMEM),
        scratch_shapes=[
            pltpu.VMEM((count,) + x.shape, x.dtype),
            pltpu.SemaphoreType.DMA((2 * (count - 1),)),
            pltpu.SemaphoreType.DMA((count, 2)),
        ],
        compiler_params=pltpu.CompilerParams(collective_id=collective_id, has_side_effects=True),
    )(x)
    return gathered.reshape((count, x.shape[0] * x.shape[1]) + x.shape[2:])


def gather_hbm_kernel(axis, count, send_ref, out_ref, send_sems, recv_sems, local_sem):
    me = lax.axis_index(axis)
    barrier = pltpu.get_barrier_semaphore()
    for step in range(1, count):
        peer = lax.rem(me + step, count)
        pl.semaphore_signal(barrier, inc=1, device_id={axis: peer}, device_id_type=MESH)
    pl.semaphore_wait(barrier, count - 1)
    copies = []
    for step in range(1, count):
        peer = lax.rem(me + step, count)
        copy = pltpu.make_async_remote_copy(
            src_ref=send_ref,
            dst_ref=out_ref.at[me],
            send_sem=send_sems.at[step],
            recv_sem=recv_sems.at[step],
            device_id={axis: peer},
            device_id_type=MESH,
        )
        copy.start()
        copies.append(copy)
    local = pltpu.make_async_copy(send_ref, out_ref.at[me], local_sem)
    local.start()
    for copy in copies:
        copy.wait()
    local.wait()


def gather_hbm(x, axis, count, collective_id):
    return pl.pallas_call(
        functools.partial(gather_hbm_kernel, axis, count),
        out_shape=jax.ShapeDtypeStruct((count,) + x.shape, x.dtype),
        in_specs=[pl.BlockSpec(memory_space=pltpu.VMEM)],
        out_specs=pl.BlockSpec(memory_space=pl.ANY),
        scratch_shapes=[
            pltpu.SemaphoreType.DMA((count,)),
            pltpu.SemaphoreType.DMA((count,)),
            pltpu.SemaphoreType.DMA(()),
        ],
        compiler_params=pltpu.CompilerParams(collective_id=collective_id, has_side_effects=True),
    )(x)


def exchange_kernel(axis, count, scatter, send_ref, out_ref, landed, send_sems, recv_sems):
    me = lax.axis_index(axis)
    barrier = pltpu.get_barrier_semaphore()
    for step in range(1, count):
        peer = lax.rem(me + step, count)
        pl.semaphore_signal(barrier, inc=1, device_id={axis: peer}, device_id_type=MESH)
    pl.semaphore_wait(barrier, count - 1)
    copies = []
    for step in range(1, count):
        peer = lax.rem(me + step, count)
        source = send_ref.at[peer] if scatter else send_ref
        copy = pltpu.make_async_remote_copy(
            src_ref=source,
            dst_ref=landed.at[me],
            send_sem=send_sems.at[step],
            recv_sem=recv_sems.at[step],
            device_id={axis: peer},
            device_id_type=MESH,
        )
        copy.start()
        copies.append(copy)
    landed[me] = send_ref[me] if scatter else send_ref[...]
    for copy in copies:
        copy.wait()
    if scatter:
        width = landed.shape[-1]
        for source in range(count):
            out_ref[:, source * width:(source + 1) * width] = landed[source]
    else:
        out_ref[...] = landed[...]


def exchange(x, axis, count, scatter, collective_id):
    piece = x.shape[1:] if scatter else x.shape
    result = (piece[0], count * piece[1]) if scatter else (count,) + piece
    return pl.pallas_call(
        functools.partial(exchange_kernel, axis, count, scatter),
        out_shape=jax.ShapeDtypeStruct(result, x.dtype),
        in_specs=[pl.BlockSpec(memory_space=pltpu.VMEM)],
        out_specs=pl.BlockSpec(memory_space=pltpu.VMEM),
        scratch_shapes=[
            pltpu.VMEM((count,) + piece, x.dtype),
            pltpu.SemaphoreType.DMA((count,)),
            pltpu.SemaphoreType.DMA((count,)),
        ],
        compiler_params=pltpu.CompilerParams(collective_id=collective_id, has_side_effects=True),
    )(x)


def on_device(tokens, trainer_panels, panel_home, lengths):
    tp_count = lax.axis_size("tp")
    grp_count = lax.axis_size("grp")
    member_id = lax.axis_index("tp")
    kv_count = (panel_home.shape[0] - tp_count) // 2
    group_size = tp_count // kv_count
    head_dim = trainer_panels.shape[2]
    block_rows = trainer_panels.shape[1]
    half_rows = block_rows // 2
    seq_total = tokens.shape[0]

    core = member_id % 2
    partner_perm = [(i, i ^ 1) for i in range(tp_count)]
    all_halves = chip_ring_gather(trainer_panels, tp_count // 2, 2)
    all_halves = all_halves.reshape((-1,) + all_halves.shape[2:])
    kv_id = member_id // group_size
    quarter = member_id % group_size
    kv_panel = tp_count + kv_id + kv_count * (quarter // 2)
    half = core
    partner_id = member_id ^ 1
    q_mine = all_halves[panel_home[member_id]]
    q_theirs = lax.ppermute(all_halves[panel_home[partner_id]], "tp", partner_perm)
    q_block = jnp.where(core == 0, jnp.concatenate([q_mine, q_theirs], axis=0),
                        jnp.concatenate([q_theirs, q_mine], axis=0))
    kv_half = all_halves[panel_home[kv_panel]]
    piece = jnp.concatenate([q_block, kv_half], axis=0)
    gathered = gather_hbm(piece, "grp", grp_count, 0)
    q_weights = gathered[:, :block_rows].reshape(grp_count * block_rows, head_dim)
    kv_weights = gathered[:, block_rows:]

    use_half = lax.broadcasted_iota(jnp.int32, (1, 2, 1, 1), 1) == half
    kv_rows = jnp.where(use_half, kv_weights[:, None], jnp.zeros_like(kv_weights[:, None]))
    both_weights = jnp.concatenate(
        [q_weights, kv_rows.reshape(grp_count * block_rows, head_dim)], axis=1
    )
    projected = jnp.dot(tokens, both_weights, preferred_element_type=jnp.float32)
    query_rows = projected[:, :head_dim].astype(jnp.bfloat16)
    kv_part = projected[:, head_dim:]
    key_rows, value_rows = kv_share(kv_part, 3)

    position = jnp.arange(seq_total, dtype=jnp.int32)
    bounds = jnp.cumsum(lengths[0])
    segment = jnp.sum((position[:, None] >= bounds[None, :]).astype(jnp.int32), axis=1)
    allowed = (segment[:, None] == segment[None, :]) & (position[None, :] <= position[:, None])
    score_scale = head_dim ** (-0.5)
    scores = (
        lax.dot_general(
            query_rows, key_rows, (((1,), (1,)), ((), ())), preferred_element_type=jnp.float32
        )
        * score_scale
    )
    masked = jnp.where(allowed, scores, -jnp.inf)
    row_peak = jnp.max(masked, axis=1, keepdims=True)
    row_exp = jnp.exp(masked - row_peak)
    attn_probs = (row_exp / jnp.sum(row_exp, axis=1, keepdims=True)).astype(jnp.bfloat16)
    context = jnp.dot(attn_probs, value_rows, preferred_element_type=jnp.float32)
    outgoing = context.reshape(tp_count, seq_total // tp_count, head_dim)
    return exchange(outgoing, "tp", tp_count, True, 1)


def solution(mesh):
    placed = (P("grp", None), P("tp", "grp", None), P(), P("grp", None))
    return jax.shard_map(
        on_device, mesh=mesh, in_specs=placed, out_specs=P(("grp", "tp"), None), check_vma=False
    )
```

```python
import functools

import jax
import jax.numpy as jnp
from jax import lax
from jax.experimental import pallas as pl
from jax.experimental.pallas import tpu as pltpu
from jax.sharding import PartitionSpec as P

MESH = pl.DeviceIdType.MESH


def ring_kernel(count, stride, chunks, send_ref, out_ref, landed, send_sems, recv_sems):
    me = lax.axis_index("tp")
    total = count * stride
    right, left = lax.rem(me + stride, total), lax.rem(me + total - stride, total)
    spot = me // stride
    barrier = pltpu.get_barrier_semaphore()
    for neighbour in (left, right):
        pl.semaphore_signal(barrier, inc=1, device_id={"tp": neighbour}, device_id_type=MESH)
    pl.semaphore_wait(barrier, 2)

    def incoming(origin, chunk):
        return pltpu.make_async_remote_copy(
            src_ref=send_ref.at[chunk],
            dst_ref=landed.at[origin, chunk],
            send_sem=send_sems.at[0, 0, 0],
            recv_sem=recv_sems.at[origin, chunk],
            device_id={"tp": right},
            device_id_type=MESH,
        )

    landed[spot] = send_ref[...]
    sends = []
    far_right, far_left = count // 2, (count - 1) // 2
    for step in range(1, far_right + 1):
        for chunk in range(chunks):
            streams = [(0, right, lax.rem(spot + count - (step - 1), count))]
            if step <= far_left:
                streams.append((1, left, lax.rem(spot + step - 1, count)))
            for way, target, origin in streams:
                if step > 1:
                    incoming(origin, chunk).wait_recv()
                source = send_ref.at[chunk] if step == 1 else landed.at[origin, chunk]
                copy = pltpu.make_async_remote_copy(
                    src_ref=source,
                    dst_ref=landed.at[origin, chunk],
                    send_sem=send_sems.at[way, step, chunk],
                    recv_sem=recv_sems.at[origin, chunk],
                    device_id={"tp": target},
                    device_id_type=MESH,
                )
                copy.start()
                sends.append(copy)
    for chunk in range(chunks):
        incoming(lax.rem(spot + count - far_right, count), chunk).wait_recv()
        incoming(lax.rem(spot + far_left, count), chunk).wait_recv()
    for copy in sends:
        copy.wait_send()
    out_ref[...] = landed[...]


def ring_gather(x, count, stride, chunks, collective_id):
    x = x.reshape((chunks, x.shape[0] // chunks) + x.shape[1:])
    gathered = pl.pallas_call(
        functools.partial(ring_kernel, count, stride, chunks),
        out_shape=jax.ShapeDtypeStruct((count,) + x.shape, x.dtype),
        in_specs=[pl.BlockSpec(memory_space=pltpu.VMEM)],
        out_specs=pl.BlockSpec(memory_space=pltpu.VMEM),
        scratch_shapes=[
            pltpu.VMEM((count,) + x.shape, x.dtype),
            pltpu.SemaphoreType.DMA((2, count // 2 + 1, chunks)),
            pltpu.SemaphoreType.DMA((count, chunks)),
        ],
        compiler_params=pltpu.CompilerParams(collective_id=collective_id, has_side_effects=True),
    )(x)
    return gathered.reshape((count * x.shape[0] * x.shape[1],) + x.shape[2:])


def chip_ring_kernel(count, panels_ref, out_ref, landed, send_sems, recv_sems):
    me = lax.axis_index("tp")
    total = 2 * count
    core = me % 2
    partner = me + 1 - 2 * core
    right, left = lax.rem(me + 2, total), lax.rem(me + total - 2, total)
    spot = me // 2
    half = panels_ref.shape[1] // 2
    barrier = pltpu.get_barrier_semaphore()
    for neighbour in (left, right, partner):
        pl.semaphore_signal(barrier, inc=1, device_id={"tp": neighbour}, device_id_type=MESH)
    pl.semaphore_wait(barrier, 3)

    def rows_of(slot, which):
        return panels_ref.at[slot, pl.ds(pl.multiple_of(which * half, 16), half)]

    def incoming(origin, chunk):
        return pltpu.make_async_remote_copy(
            src_ref=rows_of(0, 0),
            dst_ref=landed.at[origin, chunk],
            send_sem=send_sems.at[0, 0, 0],
            recv_sem=recv_sems.at[origin, chunk],
            device_id={"tp": right},
            device_id_type=MESH,
        )

    sends = []

    def send(source, origin, chunk, sem, target):
        copy = pltpu.make_async_remote_copy(
            src_ref=source,
            dst_ref=landed.at[origin, chunk],
            send_sem=sem,
            recv_sem=recv_sems.at[origin, chunk],
            device_id={"tp": target},
            device_id_type=MESH,
        )
        copy.start()
        sends.append(copy)

    own = [2 * core + j for j in range(2)]
    theirs = [2 * (1 - core) + j for j in range(2)]
    for j in range(2):
        send(rows_of(j, 1 - core), spot, own[j], send_sems.at[0, 0, 1 + j], partner)
        landed[spot, own[j]] = rows_of(j, core)[...]
    far_right, far_left = count // 2, (count - 1) // 2
    first = [(rows_of(j, core), own[j]) for j in range(2)] + [(None, theirs[j]) for j in range(2)]
    for position, (source, chunk) in enumerate(first):
        if source is None:
            incoming(spot, chunk).wait_recv()
            source = landed.at[spot, chunk]
        send(source, spot, chunk, send_sems.at[0, 1, position], right)
        if far_left >= 1:
            send(source, spot, chunk, send_sems.at[1, 1, position], left)
    for step in range(2, far_right + 1):
        for chunk in range(4):
            streams = [(0, right, lax.rem(spot + count - (step - 1), count))]
            if step <= far_left:
                streams.append((1, left, lax.rem(spot + step - 1, count)))
            for way, target, origin in streams:
                incoming(origin, chunk).wait_recv()
                send(landed.at[origin, chunk], origin, chunk, send_sems.at[way, step, chunk], target)
    for chunk in range(4):
        incoming(lax.rem(spot + count - far_right, count), chunk).wait_recv()
        incoming(lax.rem(spot + far_left, count), chunk).wait_recv()
    for copy in sends:
        copy.wait_send()
    out_ref[...] = landed[...]


def chip_ring_gather(panels, count, collective_id):
    slots, rows, width = panels.shape
    return pl.pallas_call(
        functools.partial(chip_ring_kernel, count),
        out_shape=jax.ShapeDtypeStruct((count, 2 * slots, rows // 2, width), panels.dtype),
        in_specs=[pl.BlockSpec(memory_space=pltpu.VMEM)],
        out_specs=pl.BlockSpec(memory_space=pltpu.VMEM),
        scratch_shapes=[
            pltpu.VMEM((count, 2 * slots, rows // 2, width), panels.dtype),
            pltpu.SemaphoreType.DMA((2, count // 2 + 1, 2 * slots)),
            pltpu.SemaphoreType.DMA((count, 2 * slots)),
        ],
        compiler_params=pltpu.CompilerParams(collective_id=collective_id, has_side_effects=True),
    )(panels)


def kv_share_kernel(part_ref, out_ref, partner_part, mine, theirs, send_sems, recv_sems):
    me = lax.axis_index("tp")
    partner = me + 1 - 2 * (me % 2)
    across = me + 2 - 4 * ((me // 2) % 2)
    barrier = pltpu.get_barrier_semaphore()
    for neighbour in (partner, across):
        pl.semaphore_signal(barrier, inc=1, device_id={"tp": neighbour}, device_id_type=MESH)
    pl.semaphore_wait(barrier, 2)
    first = pltpu.make_async_remote_copy(
        src_ref=part_ref, dst_ref=partner_part, send_sem=send_sems.at[0], recv_sem=recv_sems.at[0],
        device_id={"tp": partner}, device_id_type=MESH,
    )
    first.start()
    first.wait()
    mine[...] = (part_ref[...] + partner_part[...]).astype(mine.dtype)
    second = pltpu.make_async_remote_copy(
        src_ref=mine, dst_ref=theirs, send_sem=send_sems.at[1], recv_sem=recv_sems.at[1],
        device_id={"tp": across}, device_id_type=MESH,
    )
    second.start()
    second.wait()
    holds_k = (me % 4) < 2
    out_ref[0] = jnp.where(holds_k, mine[...], theirs[...])
    out_ref[1] = jnp.where(holds_k, theirs[...], mine[...])


def kv_share(part, collective_id):
    return pl.pallas_call(
        kv_share_kernel,
        out_shape=jax.ShapeDtypeStruct((2,) + part.shape, jnp.bfloat16),
        in_specs=[pl.BlockSpec(memory_space=pltpu.VMEM)],
        out_specs=pl.BlockSpec(memory_space=pltpu.VMEM),
        scratch_shapes=[
            pltpu.VMEM(part.shape, part.dtype),
            pltpu.VMEM(part.shape, jnp.bfloat16),
            pltpu.VMEM(part.shape, jnp.bfloat16),
            pltpu.SemaphoreType.DMA((2,)),
            pltpu.SemaphoreType.DMA((2,)),
        ],
        compiler_params=pltpu.CompilerParams(collective_id=collective_id, has_side_effects=True),
    )(part)


def tail_kernel(count, scale, part_ref, q_ref, segq_ref, segk_ref, out_ref,
                partner_part, mine, theirs, staged, landed, send_sems, recv_sems):
    me = lax.axis_index("tp")
    partner = me + 1 - 2 * (me % 2)
    across = me + 2 - 4 * ((me // 2) % 2)
    barrier = pltpu.get_barrier_semaphore()
    for step in range(1, count):
        peer = lax.rem(me + step, count)
        pl.semaphore_signal(barrier, inc=1, device_id={"tp": peer}, device_id_type=MESH)
    pl.semaphore_wait(barrier, count - 1)
    first = pltpu.make_async_remote_copy(
        src_ref=part_ref, dst_ref=partner_part, send_sem=send_sems.at[0], recv_sem=recv_sems.at[0],
        device_id={"tp": partner}, device_id_type=MESH,
    )
    first.start()
    first.wait()
    mine[...] = (part_ref[...] + partner_part[...]).astype(mine.dtype)
    second = pltpu.make_async_remote_copy(
        src_ref=mine, dst_ref=theirs, send_sem=send_sems.at[1], recv_sem=recv_sems.at[1],
        device_id={"tp": across}, device_id_type=MESH,
    )
    second.start()
    second.wait()
    holds_k = (me % 4) < 2
    keys = jnp.where(holds_k, mine[...], theirs[...])
    values = jnp.where(holds_k, theirs[...], mine[...])

    scores = lax.dot_general(
        q_ref[...], keys, (((1,), (1,)), ((), ())), preferred_element_type=jnp.float32
    ) * scale
    seq = scores.shape[0]
    row = lax.broadcasted_iota(jnp.int32, (seq, seq), 0)
    col = lax.broadcasted_iota(jnp.int32, (seq, seq), 1)
    allowed = (segq_ref[...] == segk_ref[...]) & (col <= row)
    masked = jnp.where(allowed, scores, -jnp.inf)
    peak = jnp.max(masked, axis=1, keepdims=True)
    weights = jnp.exp(masked - peak)
    probs = (weights / jnp.sum(weights, axis=1, keepdims=True)).astype(jnp.bfloat16)
    context = jnp.dot(probs, values, preferred_element_type=jnp.float32)
    rows = seq // count
    for target in range(count):
        staged[target] = context[target * rows:(target + 1) * rows]

    copies = []
    for step in range(1, count):
        peer = lax.rem(me + step, count)
        copy = pltpu.make_async_remote_copy(
            src_ref=staged.at[peer],
            dst_ref=landed.at[me],
            send_sem=send_sems.at[1 + step],
            recv_sem=recv_sems.at[1 + step],
            device_id={"tp": peer},
            device_id_type=MESH,
        )
        copy.start()
        copies.append(copy)
    landed[me] = staged[me]
    for copy in copies:
        copy.wait()
    width = landed.shape[-1]
    for source in range(count):
        out_ref[:, source * width:(source + 1) * width] = landed[source]


def tail(part, query, segment, count, collective_id):
    seq, width = query.shape
    rows = seq // count
    vmem = pl.BlockSpec(memory_space=pltpu.VMEM)
    return pl.pallas_call(
        functools.partial(tail_kernel, count, width ** (-0.5)),
        out_shape=jax.ShapeDtypeStruct((rows, count * width), jnp.float32),
        in_specs=[vmem] * 4,
        out_specs=vmem,
        scratch_shapes=[
            pltpu.VMEM(part.shape, part.dtype),
            pltpu.VMEM(part.shape, jnp.bfloat16),
            pltpu.VMEM(part.shape, jnp.bfloat16),
            pltpu.VMEM((count, rows, width), jnp.float32),
            pltpu.VMEM((count, rows, width), jnp.float32),
            pltpu.SemaphoreType.DMA((count + 1,)),
            pltpu.SemaphoreType.DMA((count + 1,)),
        ],
        compiler_params=pltpu.CompilerParams(collective_id=collective_id, has_side_effects=True),
    )(part, query, segment[:, None], segment[None, :])


def grid_kernel(width, send_ref, out_ref, landed, send_sems, recv_sems):
    me = lax.axis_index("grp")
    core = lax.axis_index("tp") % 2
    col, row = me % width, me // width

    def node(c, r):
        return lax.rem(r + width, width) * width + lax.rem(c + width, width)

    def along(dim, c, r, k):
        return node(c + k, r) if dim == 0 else node(c, r + k)

    barrier = pltpu.get_barrier_semaphore()
    neighbours = [node(col + 1, row), node(col - 1, row), node(col, row + 1), node(col, row - 1)]
    for neighbour in neighbours:
        pl.semaphore_signal(barrier, inc=1, device_id={"grp": neighbour}, device_id_type=MESH)
    pl.semaphore_wait(barrier, 4)

    landed[me] = send_ref[...]
    sends = []

    def send(source, origin, half, target):
        copy = pltpu.make_async_remote_copy(
            src_ref=source,
            dst_ref=landed.at[origin, half],
            send_sem=send_sems.at[len(sends)],
            recv_sem=recv_sems.at[origin, half],
            device_id={"grp": target},
            device_id_type=MESH,
        )
        copy.start()
        sends.append(copy)

    def arrive(origin, half):
        pltpu.make_async_remote_copy(
            src_ref=send_ref.at[half],
            dst_ref=landed.at[origin, half],
            send_sem=send_sems.at[0],
            recv_sem=recv_sems.at[origin, half],
            device_id={"grp": neighbours[0]},
            device_id_type=MESH,
        ).wait_recv()

    ahead = 1 - 2 * core

    def phase(lines, half, dim):
        for k in (1, -1):
            for line in lines:
                origin = along(1 - dim, col, row, line)
                source = send_ref.at[half] if line == 0 else landed.at[origin, half]
                send(source, origin, half, along(dim, col, row, k))
        for line in lines:
            for k in (1, -1):
                arrive(along(dim, along(1 - dim, col, row, line) % width, along(1 - dim, col, row, line) // width, k), half)
        for line in lines:
            base = along(1 - dim, col, row, line)
            bc, br = base % width, base // width
            send(landed.at[along(dim, bc, br, -ahead), half], along(dim, bc, br, -ahead), half,
                 along(dim, col, row, ahead))
        for line in lines:
            base = along(1 - dim, col, row, line)
            arrive(along(dim, base % width, base // width, 2), half)

    phase([0], 0, 0)
    phase([0], 1, 1)
    phase([0, 1, -1, 2], 0, 1)
    phase([0, 1, -1, 2], 1, 0)
    for copy in sends:
        copy.wait_send()
    out_ref[...] = landed[...]


def grid_gather(x, width, collective_id):
    count = width * width
    x = x.reshape((2, x.shape[0] // 2) + x.shape[1:])
    gathered = pl.pallas_call(
        functools.partial(grid_kernel, width),
        out_shape=jax.ShapeDtypeStruct((count,) + x.shape, x.dtype),
        in_specs=[pl.BlockSpec(memory_space=pltpu.VMEM)],
        out_specs=pl.BlockSpec(memory_space=pltpu.VMEM),
        scratch_shapes=[
            pltpu.VMEM((count,) + x.shape, x.dtype),
            pltpu.SemaphoreType.DMA((2 * (count - 1),)),
            pltpu.SemaphoreType.DMA((count, 2)),
        ],
        compiler_params=pltpu.CompilerParams(collective_id=collective_id, has_side_effects=True),
    )(x)
    return gathered.reshape((count, x.shape[0] * x.shape[1]) + x.shape[2:])


def gather_hbm_kernel(axis, count, send_ref, out_ref, send_sems, recv_sems, local_sem):
    me = lax.axis_index(axis)
    barrier = pltpu.get_barrier_semaphore()
    for step in range(1, count):
        peer = lax.rem(me + step, count)
        pl.semaphore_signal(barrier, inc=1, device_id={axis: peer}, device_id_type=MESH)
    pl.semaphore_wait(barrier, count - 1)
    copies = []
    for step in range(1, count):
        peer = lax.rem(me + step, count)
        copy = pltpu.make_async_remote_copy(
            src_ref=send_ref,
            dst_ref=out_ref.at[me],
            send_sem=send_sems.at[step],
            recv_sem=recv_sems.at[step],
            device_id={axis: peer},
            device_id_type=MESH,
        )
        copy.start()
        copies.append(copy)
    local = pltpu.make_async_copy(send_ref, out_ref.at[me], local_sem)
    local.start()
    for copy in copies:
        copy.wait()
    local.wait()


def gather_hbm(x, axis, count, collective_id):
    return pl.pallas_call(
        functools.partial(gather_hbm_kernel, axis, count),
        out_shape=jax.ShapeDtypeStruct((count,) + x.shape, x.dtype),
        in_specs=[pl.BlockSpec(memory_space=pltpu.VMEM)],
        out_specs=pl.BlockSpec(memory_space=pl.ANY),
        scratch_shapes=[
            pltpu.SemaphoreType.DMA((count,)),
            pltpu.SemaphoreType.DMA((count,)),
            pltpu.SemaphoreType.DMA(()),
        ],
        compiler_params=pltpu.CompilerParams(collective_id=collective_id, has_side_effects=True),
    )(x)


def exchange_kernel(axis, count, scatter, send_ref, out_ref, landed, send_sems, recv_sems):
    me = lax.axis_index(axis)
    barrier = pltpu.get_barrier_semaphore()
    for step in range(1, count):
        peer = lax.rem(me + step, count)
        pl.semaphore_signal(barrier, inc=1, device_id={axis: peer}, device_id_type=MESH)
    pl.semaphore_wait(barrier, count - 1)
    copies = []
    for step in range(1, count):
        peer = lax.rem(me + step, count)
        source = send_ref.at[peer] if scatter else send_ref
        copy = pltpu.make_async_remote_copy(
            src_ref=source,
            dst_ref=landed.at[me],
            send_sem=send_sems.at[step],
            recv_sem=recv_sems.at[step],
            device_id={axis: peer},
            device_id_type=MESH,
        )
        copy.start()
        copies.append(copy)
    landed[me] = send_ref[me] if scatter else send_ref[...]
    for copy in copies:
        copy.wait()
    if scatter:
        width = landed.shape[-1]
        for source in range(count):
            out_ref[:, source * width:(source + 1) * width] = landed[source]
    else:
        out_ref[...] = landed[...]


def exchange(x, axis, count, scatter, collective_id):
    piece = x.shape[1:] if scatter else x.shape
    result = (piece[0], count * piece[1]) if scatter else (count,) + piece
    return pl.pallas_call(
        functools.partial(exchange_kernel, axis, count, scatter),
        out_shape=jax.ShapeDtypeStruct(result, x.dtype),
        in_specs=[pl.BlockSpec(memory_space=pltpu.VMEM)],
        out_specs=pl.BlockSpec(memory_space=pltpu.VMEM),
        scratch_shapes=[
            pltpu.VMEM((count,) + piece, x.dtype),
            pltpu.SemaphoreType.DMA((count,)),
            pltpu.SemaphoreType.DMA((count,)),
        ],
        compiler_params=pltpu.CompilerParams(collective_id=collective_id, has_side_effects=True),
    )(x)


def on_device(tokens, trainer_panels, panel_home, lengths):
    tp_count = lax.axis_size("tp")
    grp_count = lax.axis_size("grp")
    member_id = lax.axis_index("tp")
    kv_count = (panel_home.shape[0] - tp_count) // 2
    group_size = tp_count // kv_count
    head_dim = trainer_panels.shape[2]
    block_rows = trainer_panels.shape[1]
    half_rows = block_rows // 2
    seq_total = tokens.shape[0]

    core = member_id % 2
    partner_perm = [(i, i ^ 1) for i in range(tp_count)]
    all_halves = chip_ring_gather(trainer_panels, tp_count // 2, 2)
    all_halves = all_halves.reshape((-1,) + all_halves.shape[2:])
    kv_id = member_id // group_size
    quarter = member_id % group_size
    kv_panel = tp_count + kv_id + kv_count * (quarter // 2)
    half = core
    partner_id = member_id ^ 1
    q_mine = all_halves[panel_home[member_id]]
    q_theirs = lax.ppermute(all_halves[panel_home[partner_id]], "tp", partner_perm)
    q_block = jnp.where(core == 0, jnp.concatenate([q_mine, q_theirs], axis=0),
                        jnp.concatenate([q_theirs, q_mine], axis=0))
    kv_half = all_halves[panel_home[kv_panel]]
    piece = jnp.concatenate([q_block, kv_half], axis=0)
    gathered = gather_hbm(piece, "grp", grp_count, 0)
    q_weights = gathered[:, :block_rows].reshape(grp_count * block_rows, head_dim)
    kv_weights = gathered[:, block_rows:]

    use_half = lax.broadcasted_iota(jnp.int32, (1, 2, 1, 1), 1) == half
    kv_rows = jnp.where(use_half, kv_weights[:, None], jnp.zeros_like(kv_weights[:, None]))
    both_weights = jnp.concatenate(
        [q_weights, kv_rows.reshape(grp_count * block_rows, head_dim)], axis=1
    )
    projected = jnp.dot(tokens, both_weights, preferred_element_type=jnp.float32)
    query_rows = projected[:, :head_dim].astype(jnp.bfloat16)
    kv_part = projected[:, head_dim:]
    position = jnp.arange(seq_total, dtype=jnp.int32)
    bounds = jnp.cumsum(lengths[0])
    segment = jnp.sum((position[:, None] >= bounds[None, :]).astype(jnp.int32), axis=1)
    return tail(kv_part, query_rows, segment, tp_count, 1)


def solution(mesh):
    placed = (P("grp", None), P("tp", "grp", None), P(), P("grp", None))
    return jax.shard_map(
        on_device, mesh=mesh, in_specs=placed, out_specs=P(("grp", "tp"), None), check_vma=False
    )
```

```python
import functools

import jax
import jax.numpy as jnp
from jax import lax
from jax.experimental import pallas as pl
from jax.experimental.pallas import tpu as pltpu
from jax.sharding import PartitionSpec as P

MESH = pl.DeviceIdType.MESH


def ring_kernel(count, stride, chunks, send_ref, out_ref, landed, send_sems, recv_sems):
    me = lax.axis_index("tp")
    total = count * stride
    right, left = lax.rem(me + stride, total), lax.rem(me + total - stride, total)
    spot = me // stride
    barrier = pltpu.get_barrier_semaphore()
    for neighbour in (left, right):
        pl.semaphore_signal(barrier, inc=1, device_id={"tp": neighbour}, device_id_type=MESH)
    pl.semaphore_wait(barrier, 2)

    def incoming(origin, chunk):
        return pltpu.make_async_remote_copy(
            src_ref=send_ref.at[chunk],
            dst_ref=landed.at[origin, chunk],
            send_sem=send_sems.at[0, 0, 0],
            recv_sem=recv_sems.at[origin, chunk],
            device_id={"tp": right},
            device_id_type=MESH,
        )

    landed[spot] = send_ref[...]
    sends = []
    far_right, far_left = count // 2, (count - 1) // 2
    for step in range(1, far_right + 1):
        for chunk in range(chunks):
            streams = [(0, right, lax.rem(spot + count - (step - 1), count))]
            if step <= far_left:
                streams.append((1, left, lax.rem(spot + step - 1, count)))
            for way, target, origin in streams:
                if step > 1:
                    incoming(origin, chunk).wait_recv()
                source = send_ref.at[chunk] if step == 1 else landed.at[origin, chunk]
                copy = pltpu.make_async_remote_copy(
                    src_ref=source,
                    dst_ref=landed.at[origin, chunk],
                    send_sem=send_sems.at[way, step, chunk],
                    recv_sem=recv_sems.at[origin, chunk],
                    device_id={"tp": target},
                    device_id_type=MESH,
                )
                copy.start()
                sends.append(copy)
    for chunk in range(chunks):
        incoming(lax.rem(spot + count - far_right, count), chunk).wait_recv()
        incoming(lax.rem(spot + far_left, count), chunk).wait_recv()
    for copy in sends:
        copy.wait_send()
    out_ref[...] = landed[...]


def ring_gather(x, count, stride, chunks, collective_id):
    x = x.reshape((chunks, x.shape[0] // chunks) + x.shape[1:])
    gathered = pl.pallas_call(
        functools.partial(ring_kernel, count, stride, chunks),
        out_shape=jax.ShapeDtypeStruct((count,) + x.shape, x.dtype),
        in_specs=[pl.BlockSpec(memory_space=pltpu.VMEM)],
        out_specs=pl.BlockSpec(memory_space=pltpu.VMEM),
        scratch_shapes=[
            pltpu.VMEM((count,) + x.shape, x.dtype),
            pltpu.SemaphoreType.DMA((2, count // 2 + 1, chunks)),
            pltpu.SemaphoreType.DMA((count, chunks)),
        ],
        compiler_params=pltpu.CompilerParams(collective_id=collective_id, has_side_effects=True),
    )(x)
    return gathered.reshape((count * x.shape[0] * x.shape[1],) + x.shape[2:])


def chip_ring_kernel(count, panels_ref, out_ref, landed, send_sems, recv_sems):
    me = lax.axis_index("tp")
    total = 2 * count
    core = me % 2
    partner = me + 1 - 2 * core
    right, left = lax.rem(me + 2, total), lax.rem(me + total - 2, total)
    spot = me // 2
    half = panels_ref.shape[1] // 2
    barrier = pltpu.get_barrier_semaphore()
    for neighbour in (left, right, partner):
        pl.semaphore_signal(barrier, inc=1, device_id={"tp": neighbour}, device_id_type=MESH)
    pl.semaphore_wait(barrier, 3)

    def rows_of(slot, which):
        return panels_ref.at[slot, pl.ds(pl.multiple_of(which * half, 16), half)]

    def incoming(origin, chunk):
        return pltpu.make_async_remote_copy(
            src_ref=rows_of(0, 0),
            dst_ref=landed.at[origin, chunk],
            send_sem=send_sems.at[0, 0, 0],
            recv_sem=recv_sems.at[origin, chunk],
            device_id={"tp": right},
            device_id_type=MESH,
        )

    sends = []

    def send(source, origin, chunk, sem, target):
        copy = pltpu.make_async_remote_copy(
            src_ref=source,
            dst_ref=landed.at[origin, chunk],
            send_sem=sem,
            recv_sem=recv_sems.at[origin, chunk],
            device_id={"tp": target},
            device_id_type=MESH,
        )
        copy.start()
        sends.append(copy)

    own = [2 * core + j for j in range(2)]
    theirs = [2 * (1 - core) + j for j in range(2)]
    for j in range(2):
        send(rows_of(j, 1 - core), spot, own[j], send_sems.at[0, 0, 1 + j], partner)
        landed[spot, own[j]] = rows_of(j, core)[...]
    far_right, far_left = count // 2, (count - 1) // 2
    first = [(rows_of(j, core), own[j]) for j in range(2)] + [(None, theirs[j]) for j in range(2)]
    for position, (source, chunk) in enumerate(first):
        if source is None:
            incoming(spot, chunk).wait_recv()
            source = landed.at[spot, chunk]
        send(source, spot, chunk, send_sems.at[0, 1, position], right)
        if far_left >= 1:
            send(source, spot, chunk, send_sems.at[1, 1, position], left)
    for step in range(2, far_right + 1):
        for chunk in range(4):
            streams = [(0, right, lax.rem(spot + count - (step - 1), count))]
            if step <= far_left:
                streams.append((1, left, lax.rem(spot + step - 1, count)))
            for way, target, origin in streams:
                incoming(origin, chunk).wait_recv()
                send(landed.at[origin, chunk], origin, chunk, send_sems.at[way, step, chunk], target)
    for chunk in range(4):
        incoming(lax.rem(spot + count - far_right, count), chunk).wait_recv()
        incoming(lax.rem(spot + far_left, count), chunk).wait_recv()
    for copy in sends:
        copy.wait_send()
    out_ref[...] = landed[...]


def chip_ring_gather(panels, count, collective_id):
    slots, rows, width = panels.shape
    return pl.pallas_call(
        functools.partial(chip_ring_kernel, count),
        out_shape=jax.ShapeDtypeStruct((count, 2 * slots, rows // 2, width), panels.dtype),
        in_specs=[pl.BlockSpec(memory_space=pltpu.VMEM)],
        out_specs=pl.BlockSpec(memory_space=pltpu.VMEM),
        scratch_shapes=[
            pltpu.VMEM((count, 2 * slots, rows // 2, width), panels.dtype),
            pltpu.SemaphoreType.DMA((2, count // 2 + 1, 2 * slots)),
            pltpu.SemaphoreType.DMA((count, 2 * slots)),
        ],
        compiler_params=pltpu.CompilerParams(collective_id=collective_id, has_side_effects=True),
    )(panels)


def kv_share_kernel(part_ref, out_ref, partner_part, mine, theirs, send_sems, recv_sems):
    me = lax.axis_index("tp")
    partner = me + 1 - 2 * (me % 2)
    across = me + 2 - 4 * ((me // 2) % 2)
    barrier = pltpu.get_barrier_semaphore()
    for neighbour in (partner, across):
        pl.semaphore_signal(barrier, inc=1, device_id={"tp": neighbour}, device_id_type=MESH)
    pl.semaphore_wait(barrier, 2)
    first = pltpu.make_async_remote_copy(
        src_ref=part_ref, dst_ref=partner_part, send_sem=send_sems.at[0], recv_sem=recv_sems.at[0],
        device_id={"tp": partner}, device_id_type=MESH,
    )
    first.start()
    first.wait()
    mine[...] = (part_ref[...] + partner_part[...]).astype(mine.dtype)
    second = pltpu.make_async_remote_copy(
        src_ref=mine, dst_ref=theirs, send_sem=send_sems.at[1], recv_sem=recv_sems.at[1],
        device_id={"tp": across}, device_id_type=MESH,
    )
    second.start()
    second.wait()
    holds_k = (me % 4) < 2
    out_ref[0] = jnp.where(holds_k, mine[...], theirs[...])
    out_ref[1] = jnp.where(holds_k, theirs[...], mine[...])


def kv_share(part, collective_id):
    return pl.pallas_call(
        kv_share_kernel,
        out_shape=jax.ShapeDtypeStruct((2,) + part.shape, jnp.bfloat16),
        in_specs=[pl.BlockSpec(memory_space=pltpu.VMEM)],
        out_specs=pl.BlockSpec(memory_space=pltpu.VMEM),
        scratch_shapes=[
            pltpu.VMEM(part.shape, part.dtype),
            pltpu.VMEM(part.shape, jnp.bfloat16),
            pltpu.VMEM(part.shape, jnp.bfloat16),
            pltpu.SemaphoreType.DMA((2,)),
            pltpu.SemaphoreType.DMA((2,)),
        ],
        compiler_params=pltpu.CompilerParams(collective_id=collective_id, has_side_effects=True),
    )(part)


def tail_kernel(count, scale, projected_ref, segq_ref, segk_ref, out_ref,
                part_ref, partner_part, mine, theirs, staged, landed, send_sems, recv_sems):
    width = landed.shape[-1]
    part_ref[...] = projected_ref[:, width:]
    me = lax.axis_index("tp")
    partner = me + 1 - 2 * (me % 2)
    across = me + 2 - 4 * ((me // 2) % 2)
    barrier = pltpu.get_barrier_semaphore()
    for step in range(1, count):
        peer = lax.rem(me + step, count)
        pl.semaphore_signal(barrier, inc=1, device_id={"tp": peer}, device_id_type=MESH)
    pl.semaphore_wait(barrier, count - 1)
    first = pltpu.make_async_remote_copy(
        src_ref=part_ref, dst_ref=partner_part, send_sem=send_sems.at[0], recv_sem=recv_sems.at[0],
        device_id={"tp": partner}, device_id_type=MESH,
    )
    first.start()
    first.wait()
    mine[...] = (part_ref[...] + partner_part[...]).astype(mine.dtype)
    second = pltpu.make_async_remote_copy(
        src_ref=mine, dst_ref=theirs, send_sem=send_sems.at[1], recv_sem=recv_sems.at[1],
        device_id={"tp": across}, device_id_type=MESH,
    )
    second.start()
    second.wait()
    holds_k = (me % 4) < 2
    keys = jnp.where(holds_k, mine[...], theirs[...])
    values = jnp.where(holds_k, theirs[...], mine[...])

    scores = lax.dot_general(
        projected_ref[:, :width].astype(jnp.bfloat16), keys, (((1,), (1,)), ((), ())), preferred_element_type=jnp.float32
    ) * scale
    seq = scores.shape[0]
    row = lax.broadcasted_iota(jnp.int32, (seq, seq), 0)
    col = lax.broadcasted_iota(jnp.int32, (seq, seq), 1)
    allowed = (segq_ref[...] == segk_ref[...]) & (col <= row)
    masked = jnp.where(allowed, scores, -jnp.inf)
    peak = jnp.max(masked, axis=1, keepdims=True)
    weights = jnp.exp(masked - peak)
    probs = (weights / jnp.sum(weights, axis=1, keepdims=True)).astype(jnp.bfloat16)
    context = jnp.dot(probs, values, preferred_element_type=jnp.float32)
    rows = seq // count
    for target in range(count):
        staged[target] = context[target * rows:(target + 1) * rows]

    copies = []
    for step in range(1, count):
        peer = lax.rem(me + step, count)
        copy = pltpu.make_async_remote_copy(
            src_ref=staged.at[peer],
            dst_ref=landed.at[me],
            send_sem=send_sems.at[1 + step],
            recv_sem=recv_sems.at[1 + step],
            device_id={"tp": peer},
            device_id_type=MESH,
        )
        copy.start()
        copies.append(copy)
    landed[me] = staged[me]
    for copy in copies:
        copy.wait()
    for source in range(count):
        out_ref[:, source * width:(source + 1) * width] = landed[source]


def tail(projected, segment, count, collective_id):
    seq, width = projected.shape[0], projected.shape[1] // 2
    part = jax.ShapeDtypeStruct((seq, width), jnp.float32)
    rows = seq // count
    vmem = pl.BlockSpec(memory_space=pltpu.VMEM)
    return pl.pallas_call(
        functools.partial(tail_kernel, count, width ** (-0.5)),
        out_shape=jax.ShapeDtypeStruct((rows, count * width), jnp.float32),
        in_specs=[vmem] * 3,
        out_specs=vmem,
        scratch_shapes=[
            pltpu.VMEM(part.shape, part.dtype),
            pltpu.VMEM(part.shape, part.dtype),
            pltpu.VMEM(part.shape, jnp.bfloat16),
            pltpu.VMEM(part.shape, jnp.bfloat16),
            pltpu.VMEM((count, rows, width), jnp.float32),
            pltpu.VMEM((count, rows, width), jnp.float32),
            pltpu.SemaphoreType.DMA((count + 1,)),
            pltpu.SemaphoreType.DMA((count + 1,)),
        ],
        compiler_params=pltpu.CompilerParams(collective_id=collective_id, has_side_effects=True),
    )(projected, segment[:, None], segment[None, :])


def grid_kernel(width, send_ref, out_ref, landed, send_sems, recv_sems):
    me = lax.axis_index("grp")
    core = lax.axis_index("tp") % 2
    col, row = me % width, me // width

    def node(c, r):
        return lax.rem(r + width, width) * width + lax.rem(c + width, width)

    def along(dim, c, r, k):
        return node(c + k, r) if dim == 0 else node(c, r + k)

    barrier = pltpu.get_barrier_semaphore()
    neighbours = [node(col + 1, row), node(col - 1, row), node(col, row + 1), node(col, row - 1)]
    for neighbour in neighbours:
        pl.semaphore_signal(barrier, inc=1, device_id={"grp": neighbour}, device_id_type=MESH)
    pl.semaphore_wait(barrier, 4)

    landed[me] = send_ref[...]
    sends = []

    def send(source, origin, half, target):
        copy = pltpu.make_async_remote_copy(
            src_ref=source,
            dst_ref=landed.at[origin, half],
            send_sem=send_sems.at[len(sends)],
            recv_sem=recv_sems.at[origin, half],
            device_id={"grp": target},
            device_id_type=MESH,
        )
        copy.start()
        sends.append(copy)

    def arrive(origin, half):
        pltpu.make_async_remote_copy(
            src_ref=send_ref.at[half],
            dst_ref=landed.at[origin, half],
            send_sem=send_sems.at[0],
            recv_sem=recv_sems.at[origin, half],
            device_id={"grp": neighbours[0]},
            device_id_type=MESH,
        ).wait_recv()

    ahead = 1 - 2 * core

    def phase(lines, half, dim):
        for k in (1, -1):
            for line in lines:
                origin = along(1 - dim, col, row, line)
                source = send_ref.at[half] if line == 0 else landed.at[origin, half]
                send(source, origin, half, along(dim, col, row, k))
        for line in lines:
            for k in (1, -1):
                arrive(along(dim, along(1 - dim, col, row, line) % width, along(1 - dim, col, row, line) // width, k), half)
        for line in lines:
            base = along(1 - dim, col, row, line)
            bc, br = base % width, base // width
            send(landed.at[along(dim, bc, br, -ahead), half], along(dim, bc, br, -ahead), half,
                 along(dim, col, row, ahead))
        for line in lines:
            base = along(1 - dim, col, row, line)
            arrive(along(dim, base % width, base // width, 2), half)

    phase([0], 0, 0)
    phase([0], 1, 1)
    phase([0, 1, -1, 2], 0, 1)
    phase([0, 1, -1, 2], 1, 0)
    for copy in sends:
        copy.wait_send()
    out_ref[...] = landed[...]


def grid_gather(x, width, collective_id):
    count = width * width
    x = x.reshape((2, x.shape[0] // 2) + x.shape[1:])
    gathered = pl.pallas_call(
        functools.partial(grid_kernel, width),
        out_shape=jax.ShapeDtypeStruct((count,) + x.shape, x.dtype),
        in_specs=[pl.BlockSpec(memory_space=pltpu.VMEM)],
        out_specs=pl.BlockSpec(memory_space=pltpu.VMEM),
        scratch_shapes=[
            pltpu.VMEM((count,) + x.shape, x.dtype),
            pltpu.SemaphoreType.DMA((2 * (count - 1),)),
            pltpu.SemaphoreType.DMA((count, 2)),
        ],
        compiler_params=pltpu.CompilerParams(collective_id=collective_id, has_side_effects=True),
    )(x)
    return gathered.reshape((count, x.shape[0] * x.shape[1]) + x.shape[2:])


def gather_hbm_kernel(axis, count, send_ref, out_ref, send_sems, recv_sems, local_sem):
    me = lax.axis_index(axis)
    barrier = pltpu.get_barrier_semaphore()
    for step in range(1, count):
        peer = lax.rem(me + step, count)
        pl.semaphore_signal(barrier, inc=1, device_id={axis: peer}, device_id_type=MESH)
    pl.semaphore_wait(barrier, count - 1)
    copies = []
    for step in range(1, count):
        peer = lax.rem(me + step, count)
        copy = pltpu.make_async_remote_copy(
            src_ref=send_ref,
            dst_ref=out_ref.at[me],
            send_sem=send_sems.at[step],
            recv_sem=recv_sems.at[step],
            device_id={axis: peer},
            device_id_type=MESH,
        )
        copy.start()
        copies.append(copy)
    local = pltpu.make_async_copy(send_ref, out_ref.at[me], local_sem)
    local.start()
    for copy in copies:
        copy.wait()
    local.wait()


def gather_hbm(x, axis, count, collective_id):
    return pl.pallas_call(
        functools.partial(gather_hbm_kernel, axis, count),
        out_shape=jax.ShapeDtypeStruct((count,) + x.shape, x.dtype),
        in_specs=[pl.BlockSpec(memory_space=pltpu.VMEM)],
        out_specs=pl.BlockSpec(memory_space=pl.ANY),
        scratch_shapes=[
            pltpu.SemaphoreType.DMA((count,)),
            pltpu.SemaphoreType.DMA((count,)),
            pltpu.SemaphoreType.DMA(()),
        ],
        compiler_params=pltpu.CompilerParams(collective_id=collective_id, has_side_effects=True),
    )(x)


def exchange_kernel(axis, count, scatter, send_ref, out_ref, landed, send_sems, recv_sems):
    me = lax.axis_index(axis)
    barrier = pltpu.get_barrier_semaphore()
    for step in range(1, count):
        peer = lax.rem(me + step, count)
        pl.semaphore_signal(barrier, inc=1, device_id={axis: peer}, device_id_type=MESH)
    pl.semaphore_wait(barrier, count - 1)
    copies = []
    for step in range(1, count):
        peer = lax.rem(me + step, count)
        source = send_ref.at[peer] if scatter else send_ref
        copy = pltpu.make_async_remote_copy(
            src_ref=source,
            dst_ref=landed.at[me],
            send_sem=send_sems.at[step],
            recv_sem=recv_sems.at[step],
            device_id={axis: peer},
            device_id_type=MESH,
        )
        copy.start()
        copies.append(copy)
    landed[me] = send_ref[me] if scatter else send_ref[...]
    for copy in copies:
        copy.wait()
    if scatter:
        width = landed.shape[-1]
        for source in range(count):
            out_ref[:, source * width:(source + 1) * width] = landed[source]
    else:
        out_ref[...] = landed[...]


def exchange(x, axis, count, scatter, collective_id):
    piece = x.shape[1:] if scatter else x.shape
    result = (piece[0], count * piece[1]) if scatter else (count,) + piece
    return pl.pallas_call(
        functools.partial(exchange_kernel, axis, count, scatter),
        out_shape=jax.ShapeDtypeStruct(result, x.dtype),
        in_specs=[pl.BlockSpec(memory_space=pltpu.VMEM)],
        out_specs=pl.BlockSpec(memory_space=pltpu.VMEM),
        scratch_shapes=[
            pltpu.VMEM((count,) + piece, x.dtype),
            pltpu.SemaphoreType.DMA((count,)),
            pltpu.SemaphoreType.DMA((count,)),
        ],
        compiler_params=pltpu.CompilerParams(collective_id=collective_id, has_side_effects=True),
    )(x)


def on_device(tokens, trainer_panels, panel_home, lengths):
    tp_count = lax.axis_size("tp")
    grp_count = lax.axis_size("grp")
    member_id = lax.axis_index("tp")
    kv_count = (panel_home.shape[0] - tp_count) // 2
    group_size = tp_count // kv_count
    head_dim = trainer_panels.shape[2]
    block_rows = trainer_panels.shape[1]
    half_rows = block_rows // 2
    seq_total = tokens.shape[0]

    core = member_id % 2
    partner_perm = [(i, i ^ 1) for i in range(tp_count)]
    all_halves = chip_ring_gather(trainer_panels, tp_count // 2, 2)
    all_halves = all_halves.reshape((-1,) + all_halves.shape[2:])
    kv_id = member_id // group_size
    quarter = member_id % group_size
    kv_panel = tp_count + kv_id + kv_count * (quarter // 2)
    half = core
    partner_id = member_id ^ 1
    q_mine = all_halves[panel_home[member_id]]
    q_theirs = lax.ppermute(all_halves[panel_home[partner_id]], "tp", partner_perm)
    q_block = jnp.where(core == 0, jnp.concatenate([q_mine, q_theirs], axis=0),
                        jnp.concatenate([q_theirs, q_mine], axis=0))
    kv_half = all_halves[panel_home[kv_panel]]
    piece = jnp.concatenate([q_block, kv_half], axis=0)
    gathered = gather_hbm(piece, "grp", grp_count, 0)
    q_weights = gathered[:, :block_rows].reshape(grp_count * block_rows, head_dim)
    kv_weights = gathered[:, block_rows:]

    use_half = lax.broadcasted_iota(jnp.int32, (1, 2, 1, 1), 1) == half
    kv_rows = jnp.where(use_half, kv_weights[:, None], jnp.zeros_like(kv_weights[:, None]))
    both_weights = jnp.concatenate(
        [q_weights, kv_rows.reshape(grp_count * block_rows, head_dim)], axis=1
    )
    projected = jnp.dot(tokens, both_weights, preferred_element_type=jnp.float32)
    position = jnp.arange(seq_total, dtype=jnp.int32)
    bounds = jnp.cumsum(lengths[0])
    segment = jnp.sum((position[:, None] >= bounds[None, :]).astype(jnp.int32), axis=1)
    return tail(projected, segment, tp_count, 1)


def solution(mesh):
    placed = (P("grp", None), P("tp", "grp", None), P(), P("grp", None))
    return jax.shard_map(
        on_device, mesh=mesh, in_specs=placed, out_specs=P(("grp", "tp"), None), check_vma=False
    )
```

```python
import functools

import jax
import jax.numpy as jnp
from jax import lax
from jax.experimental import pallas as pl
from jax.experimental.pallas import tpu as pltpu
from jax.sharding import PartitionSpec as P

MESH = pl.DeviceIdType.MESH


def ring_kernel(count, stride, chunks, send_ref, out_ref, landed, send_sems, recv_sems):
    me = lax.axis_index("tp")
    total = count * stride
    right, left = lax.rem(me + stride, total), lax.rem(me + total - stride, total)
    spot = me // stride
    barrier = pltpu.get_barrier_semaphore()
    for neighbour in (left, right):
        pl.semaphore_signal(barrier, inc=1, device_id={"tp": neighbour}, device_id_type=MESH)
    pl.semaphore_wait(barrier, 2)

    def incoming(origin, chunk):
        return pltpu.make_async_remote_copy(
            src_ref=send_ref.at[chunk],
            dst_ref=landed.at[origin, chunk],
            send_sem=send_sems.at[0, 0, 0],
            recv_sem=recv_sems.at[origin, chunk],
            device_id={"tp": right},
            device_id_type=MESH,
        )

    landed[spot] = send_ref[...]
    sends = []
    far_right, far_left = count // 2, (count - 1) // 2
    for step in range(1, far_right + 1):
        for chunk in range(chunks):
            streams = [(0, right, lax.rem(spot + count - (step - 1), count))]
            if step <= far_left:
                streams.append((1, left, lax.rem(spot + step - 1, count)))
            for way, target, origin in streams:
                if step > 1:
                    incoming(origin, chunk).wait_recv()
                source = send_ref.at[chunk] if step == 1 else landed.at[origin, chunk]
                copy = pltpu.make_async_remote_copy(
                    src_ref=source,
                    dst_ref=landed.at[origin, chunk],
                    send_sem=send_sems.at[way, step, chunk],
                    recv_sem=recv_sems.at[origin, chunk],
                    device_id={"tp": target},
                    device_id_type=MESH,
                )
                copy.start()
                sends.append(copy)
    for chunk in range(chunks):
        incoming(lax.rem(spot + count - far_right, count), chunk).wait_recv()
        incoming(lax.rem(spot + far_left, count), chunk).wait_recv()
    for copy in sends:
        copy.wait_send()
    out_ref[...] = landed[...]


def ring_gather(x, count, stride, chunks, collective_id):
    x = x.reshape((chunks, x.shape[0] // chunks) + x.shape[1:])
    gathered = pl.pallas_call(
        functools.partial(ring_kernel, count, stride, chunks),
        out_shape=jax.ShapeDtypeStruct((count,) + x.shape, x.dtype),
        in_specs=[pl.BlockSpec(memory_space=pltpu.VMEM)],
        out_specs=pl.BlockSpec(memory_space=pltpu.VMEM),
        scratch_shapes=[
            pltpu.VMEM((count,) + x.shape, x.dtype),
            pltpu.SemaphoreType.DMA((2, count // 2 + 1, chunks)),
            pltpu.SemaphoreType.DMA((count, chunks)),
        ],
        compiler_params=pltpu.CompilerParams(collective_id=collective_id, has_side_effects=True),
    )(x)
    return gathered.reshape((count * x.shape[0] * x.shape[1],) + x.shape[2:])


def chip_ring_kernel(count, panels_ref, out_ref, landed, send_sems, recv_sems):
    me = lax.axis_index("tp")
    total = 2 * count
    core = me % 2
    partner = me + 1 - 2 * core
    right, left = lax.rem(me + 2, total), lax.rem(me + total - 2, total)
    spot = me // 2
    half = panels_ref.shape[1] // 2
    barrier = pltpu.get_barrier_semaphore()
    for neighbour in (left, right, partner):
        pl.semaphore_signal(barrier, inc=1, device_id={"tp": neighbour}, device_id_type=MESH)
    pl.semaphore_wait(barrier, 3)

    def rows_of(slot, which):
        return panels_ref.at[slot, pl.ds(pl.multiple_of(which * half, 16), half)]

    def incoming(origin, chunk):
        return pltpu.make_async_remote_copy(
            src_ref=rows_of(0, 0),
            dst_ref=landed.at[origin, chunk],
            send_sem=send_sems.at[0, 0, 0],
            recv_sem=recv_sems.at[origin, chunk],
            device_id={"tp": right},
            device_id_type=MESH,
        )

    sends = []

    def send(source, origin, chunk, sem, target):
        copy = pltpu.make_async_remote_copy(
            src_ref=source,
            dst_ref=landed.at[origin, chunk],
            send_sem=sem,
            recv_sem=recv_sems.at[origin, chunk],
            device_id={"tp": target},
            device_id_type=MESH,
        )
        copy.start()
        sends.append(copy)

    own = [2 * core + j for j in range(2)]
    theirs = [2 * (1 - core) + j for j in range(2)]
    for j in range(2):
        send(rows_of(j, 1 - core), spot, own[j], send_sems.at[0, 0, 1 + j], partner)
        landed[spot, own[j]] = rows_of(j, core)[...]
    far_right, far_left = count // 2, (count - 1) // 2
    first = [(rows_of(j, core), own[j]) for j in range(2)] + [(None, theirs[j]) for j in range(2)]
    for position, (source, chunk) in enumerate(first):
        if source is None:
            incoming(spot, chunk).wait_recv()
            source = landed.at[spot, chunk]
        send(source, spot, chunk, send_sems.at[0, 1, position], right)
        if far_left >= 1:
            send(source, spot, chunk, send_sems.at[1, 1, position], left)
    for step in range(2, far_right + 1):
        for chunk in range(4):
            streams = [(0, right, lax.rem(spot + count - (step - 1), count))]
            if step <= far_left:
                streams.append((1, left, lax.rem(spot + step - 1, count)))
            for way, target, origin in streams:
                incoming(origin, chunk).wait_recv()
                send(landed.at[origin, chunk], origin, chunk, send_sems.at[way, step, chunk], target)
    for chunk in range(4):
        incoming(lax.rem(spot + count - far_right, count), chunk).wait_recv()
        incoming(lax.rem(spot + far_left, count), chunk).wait_recv()
    for copy in sends:
        copy.wait_send()
    out_ref[...] = landed[...]


def chip_ring_gather(panels, count, collective_id):
    slots, rows, width = panels.shape
    return pl.pallas_call(
        functools.partial(chip_ring_kernel, count),
        out_shape=jax.ShapeDtypeStruct((count, 2 * slots, rows // 2, width), panels.dtype),
        in_specs=[pl.BlockSpec(memory_space=pltpu.VMEM)],
        out_specs=pl.BlockSpec(memory_space=pltpu.VMEM),
        scratch_shapes=[
            pltpu.VMEM((count, 2 * slots, rows // 2, width), panels.dtype),
            pltpu.SemaphoreType.DMA((2, count // 2 + 1, 2 * slots)),
            pltpu.SemaphoreType.DMA((count, 2 * slots)),
        ],
        compiler_params=pltpu.CompilerParams(collective_id=collective_id, has_side_effects=True),
    )(panels)


def kv_share_kernel(part_ref, out_ref, partner_part, mine, theirs, send_sems, recv_sems):
    me = lax.axis_index("tp")
    partner = me + 1 - 2 * (me % 2)
    across = me + 2 - 4 * ((me // 2) % 2)
    barrier = pltpu.get_barrier_semaphore()
    for neighbour in (partner, across):
        pl.semaphore_signal(barrier, inc=1, device_id={"tp": neighbour}, device_id_type=MESH)
    pl.semaphore_wait(barrier, 2)
    first = pltpu.make_async_remote_copy(
        src_ref=part_ref, dst_ref=partner_part, send_sem=send_sems.at[0], recv_sem=recv_sems.at[0],
        device_id={"tp": partner}, device_id_type=MESH,
    )
    first.start()
    first.wait()
    mine[...] = (part_ref[...] + partner_part[...]).astype(mine.dtype)
    second = pltpu.make_async_remote_copy(
        src_ref=mine, dst_ref=theirs, send_sem=send_sems.at[1], recv_sem=recv_sems.at[1],
        device_id={"tp": across}, device_id_type=MESH,
    )
    second.start()
    second.wait()
    holds_k = (me % 4) < 2
    out_ref[0] = jnp.where(holds_k, mine[...], theirs[...])
    out_ref[1] = jnp.where(holds_k, theirs[...], mine[...])


def kv_share(part, collective_id):
    return pl.pallas_call(
        kv_share_kernel,
        out_shape=jax.ShapeDtypeStruct((2,) + part.shape, jnp.bfloat16),
        in_specs=[pl.BlockSpec(memory_space=pltpu.VMEM)],
        out_specs=pl.BlockSpec(memory_space=pltpu.VMEM),
        scratch_shapes=[
            pltpu.VMEM(part.shape, part.dtype),
            pltpu.VMEM(part.shape, jnp.bfloat16),
            pltpu.VMEM(part.shape, jnp.bfloat16),
            pltpu.SemaphoreType.DMA((2,)),
            pltpu.SemaphoreType.DMA((2,)),
        ],
        compiler_params=pltpu.CompilerParams(collective_id=collective_id, has_side_effects=True),
    )(part)


def tail_kernel(count, scale, projected_ref, lengths_ref, out_ref,
                part_ref, partner_part, mine, theirs, staged, landed, send_sems, recv_sems):
    width = landed.shape[-1]
    part_ref[...] = projected_ref[:, width:]
    me = lax.axis_index("tp")
    partner = me + 1 - 2 * (me % 2)
    across = me + 2 - 4 * ((me // 2) % 2)
    barrier = pltpu.get_barrier_semaphore()
    for step in range(1, count):
        peer = lax.rem(me + step, count)
        pl.semaphore_signal(barrier, inc=1, device_id={"tp": peer}, device_id_type=MESH)
    pl.semaphore_wait(barrier, count - 1)
    first = pltpu.make_async_remote_copy(
        src_ref=part_ref, dst_ref=partner_part, send_sem=send_sems.at[0], recv_sem=recv_sems.at[0],
        device_id={"tp": partner}, device_id_type=MESH,
    )
    first.start()
    first.wait()
    mine[...] = (part_ref[...] + partner_part[...]).astype(mine.dtype)
    second = pltpu.make_async_remote_copy(
        src_ref=mine, dst_ref=theirs, send_sem=send_sems.at[1], recv_sem=recv_sems.at[1],
        device_id={"tp": across}, device_id_type=MESH,
    )
    second.start()
    second.wait()
    holds_k = (me % 4) < 2
    keys = jnp.where(holds_k, mine[...], theirs[...])
    values = jnp.where(holds_k, theirs[...], mine[...])

    scores = lax.dot_general(
        projected_ref[:, :width].astype(jnp.bfloat16), keys, (((1,), (1,)), ((), ())), preferred_element_type=jnp.float32
    ) * scale
    seq = scores.shape[0]
    row = lax.broadcasted_iota(jnp.int32, (seq, seq), 0)
    col = lax.broadcasted_iota(jnp.int32, (seq, seq), 1)
    row_segment = jnp.zeros((seq, seq), jnp.int32)
    col_segment = jnp.zeros((seq, seq), jnp.int32)
    bound = lengths_ref[0, 0] * 0
    for response in range(lengths_ref.shape[1]):
        bound = bound + lengths_ref[0, response]
        row_segment = row_segment + (row >= bound).astype(jnp.int32)
        col_segment = col_segment + (col >= bound).astype(jnp.int32)
    allowed = (row_segment == col_segment) & (col <= row)
    masked = jnp.where(allowed, scores, -jnp.inf)
    peak = jnp.max(masked, axis=1, keepdims=True)
    weights = jnp.exp(masked - peak)
    probs = (weights / jnp.sum(weights, axis=1, keepdims=True)).astype(jnp.bfloat16)
    context = jnp.dot(probs, values, preferred_element_type=jnp.float32)
    rows = seq // count
    for target in range(count):
        staged[target] = context[target * rows:(target + 1) * rows]

    copies = []
    for step in range(1, count):
        peer = lax.rem(me + step, count)
        copy = pltpu.make_async_remote_copy(
            src_ref=staged.at[peer],
            dst_ref=landed.at[me],
            send_sem=send_sems.at[1 + step],
            recv_sem=recv_sems.at[1 + step],
            device_id={"tp": peer},
            device_id_type=MESH,
        )
        copy.start()
        copies.append(copy)
    landed[me] = staged[me]
    for copy in copies:
        copy.wait()
    for source in range(count):
        out_ref[:, source * width:(source + 1) * width] = landed[source]


def tail(projected, lengths, count, collective_id):
    seq, width = projected.shape[0], projected.shape[1] // 2
    part = jax.ShapeDtypeStruct((seq, width), jnp.float32)
    rows = seq // count
    vmem = pl.BlockSpec(memory_space=pltpu.VMEM)
    return pl.pallas_call(
        functools.partial(tail_kernel, count, width ** (-0.5)),
        out_shape=jax.ShapeDtypeStruct((rows, count * width), jnp.float32),
        in_specs=[vmem, pl.BlockSpec(memory_space=pltpu.SMEM)],
        out_specs=vmem,
        scratch_shapes=[
            pltpu.VMEM(part.shape, part.dtype),
            pltpu.VMEM(part.shape, part.dtype),
            pltpu.VMEM(part.shape, jnp.bfloat16),
            pltpu.VMEM(part.shape, jnp.bfloat16),
            pltpu.VMEM((count, rows, width), jnp.float32),
            pltpu.VMEM((count, rows, width), jnp.float32),
            pltpu.SemaphoreType.DMA((count + 1,)),
            pltpu.SemaphoreType.DMA((count + 1,)),
        ],
        compiler_params=pltpu.CompilerParams(collective_id=collective_id, has_side_effects=True),
    )(projected, lengths)


def grid_kernel(width, send_ref, out_ref, landed, send_sems, recv_sems):
    me = lax.axis_index("grp")
    core = lax.axis_index("tp") % 2
    col, row = me % width, me // width

    def node(c, r):
        return lax.rem(r + width, width) * width + lax.rem(c + width, width)

    def along(dim, c, r, k):
        return node(c + k, r) if dim == 0 else node(c, r + k)

    barrier = pltpu.get_barrier_semaphore()
    neighbours = [node(col + 1, row), node(col - 1, row), node(col, row + 1), node(col, row - 1)]
    for neighbour in neighbours:
        pl.semaphore_signal(barrier, inc=1, device_id={"grp": neighbour}, device_id_type=MESH)
    pl.semaphore_wait(barrier, 4)

    landed[me] = send_ref[...]
    sends = []

    def send(source, origin, half, target):
        copy = pltpu.make_async_remote_copy(
            src_ref=source,
            dst_ref=landed.at[origin, half],
            send_sem=send_sems.at[len(sends)],
            recv_sem=recv_sems.at[origin, half],
            device_id={"grp": target},
            device_id_type=MESH,
        )
        copy.start()
        sends.append(copy)

    def arrive(origin, half):
        pltpu.make_async_remote_copy(
            src_ref=send_ref.at[half],
            dst_ref=landed.at[origin, half],
            send_sem=send_sems.at[0],
            recv_sem=recv_sems.at[origin, half],
            device_id={"grp": neighbours[0]},
            device_id_type=MESH,
        ).wait_recv()

    ahead = 1 - 2 * core

    def phase(lines, half, dim):
        for k in (1, -1):
            for line in lines:
                origin = along(1 - dim, col, row, line)
                source = send_ref.at[half] if line == 0 else landed.at[origin, half]
                send(source, origin, half, along(dim, col, row, k))
        for line in lines:
            for k in (1, -1):
                arrive(along(dim, along(1 - dim, col, row, line) % width, along(1 - dim, col, row, line) // width, k), half)
        for line in lines:
            base = along(1 - dim, col, row, line)
            bc, br = base % width, base // width
            send(landed.at[along(dim, bc, br, -ahead), half], along(dim, bc, br, -ahead), half,
                 along(dim, col, row, ahead))
        for line in lines:
            base = along(1 - dim, col, row, line)
            arrive(along(dim, base % width, base // width, 2), half)

    phase([0], 0, 0)
    phase([0], 1, 1)
    phase([0, 1, -1, 2], 0, 1)
    phase([0, 1, -1, 2], 1, 0)
    for copy in sends:
        copy.wait_send()
    out_ref[...] = landed[...]


def grid_gather(x, width, collective_id):
    count = width * width
    x = x.reshape((2, x.shape[0] // 2) + x.shape[1:])
    gathered = pl.pallas_call(
        functools.partial(grid_kernel, width),
        out_shape=jax.ShapeDtypeStruct((count,) + x.shape, x.dtype),
        in_specs=[pl.BlockSpec(memory_space=pltpu.VMEM)],
        out_specs=pl.BlockSpec(memory_space=pltpu.VMEM),
        scratch_shapes=[
            pltpu.VMEM((count,) + x.shape, x.dtype),
            pltpu.SemaphoreType.DMA((2 * (count - 1),)),
            pltpu.SemaphoreType.DMA((count, 2)),
        ],
        compiler_params=pltpu.CompilerParams(collective_id=collective_id, has_side_effects=True),
    )(x)
    return gathered.reshape((count, x.shape[0] * x.shape[1]) + x.shape[2:])


def gather_hbm_kernel(axis, count, send_ref, out_ref, send_sems, recv_sems, local_sem):
    me = lax.axis_index(axis)
    barrier = pltpu.get_barrier_semaphore()
    for step in range(1, count):
        peer = lax.rem(me + step, count)
        pl.semaphore_signal(barrier, inc=1, device_id={axis: peer}, device_id_type=MESH)
    pl.semaphore_wait(barrier, count - 1)
    copies = []
    for step in range(1, count):
        peer = lax.rem(me + step, count)
        copy = pltpu.make_async_remote_copy(
            src_ref=send_ref,
            dst_ref=out_ref.at[me],
            send_sem=send_sems.at[step],
            recv_sem=recv_sems.at[step],
            device_id={axis: peer},
            device_id_type=MESH,
        )
        copy.start()
        copies.append(copy)
    local = pltpu.make_async_copy(send_ref, out_ref.at[me], local_sem)
    local.start()
    for copy in copies:
        copy.wait()
    local.wait()


def gather_hbm(x, axis, count, collective_id):
    return pl.pallas_call(
        functools.partial(gather_hbm_kernel, axis, count),
        out_shape=jax.ShapeDtypeStruct((count,) + x.shape, x.dtype),
        in_specs=[pl.BlockSpec(memory_space=pltpu.VMEM)],
        out_specs=pl.BlockSpec(memory_space=pl.ANY),
        scratch_shapes=[
            pltpu.SemaphoreType.DMA((count,)),
            pltpu.SemaphoreType.DMA((count,)),
            pltpu.SemaphoreType.DMA(()),
        ],
        compiler_params=pltpu.CompilerParams(collective_id=collective_id, has_side_effects=True),
    )(x)


def exchange_kernel(axis, count, scatter, send_ref, out_ref, landed, send_sems, recv_sems):
    me = lax.axis_index(axis)
    barrier = pltpu.get_barrier_semaphore()
    for step in range(1, count):
        peer = lax.rem(me + step, count)
        pl.semaphore_signal(barrier, inc=1, device_id={axis: peer}, device_id_type=MESH)
    pl.semaphore_wait(barrier, count - 1)
    copies = []
    for step in range(1, count):
        peer = lax.rem(me + step, count)
        source = send_ref.at[peer] if scatter else send_ref
        copy = pltpu.make_async_remote_copy(
            src_ref=source,
            dst_ref=landed.at[me],
            send_sem=send_sems.at[step],
            recv_sem=recv_sems.at[step],
            device_id={axis: peer},
            device_id_type=MESH,
        )
        copy.start()
        copies.append(copy)
    landed[me] = send_ref[me] if scatter else send_ref[...]
    for copy in copies:
        copy.wait()
    if scatter:
        width = landed.shape[-1]
        for source in range(count):
            out_ref[:, source * width:(source + 1) * width] = landed[source]
    else:
        out_ref[...] = landed[...]


def exchange(x, axis, count, scatter, collective_id):
    piece = x.shape[1:] if scatter else x.shape
    result = (piece[0], count * piece[1]) if scatter else (count,) + piece
    return pl.pallas_call(
        functools.partial(exchange_kernel, axis, count, scatter),
        out_shape=jax.ShapeDtypeStruct(result, x.dtype),
        in_specs=[pl.BlockSpec(memory_space=pltpu.VMEM)],
        out_specs=pl.BlockSpec(memory_space=pltpu.VMEM),
        scratch_shapes=[
            pltpu.VMEM((count,) + piece, x.dtype),
            pltpu.SemaphoreType.DMA((count,)),
            pltpu.SemaphoreType.DMA((count,)),
        ],
        compiler_params=pltpu.CompilerParams(collective_id=collective_id, has_side_effects=True),
    )(x)


def on_device(tokens, trainer_panels, panel_home, lengths):
    tp_count = lax.axis_size("tp")
    grp_count = lax.axis_size("grp")
    member_id = lax.axis_index("tp")
    kv_count = (panel_home.shape[0] - tp_count) // 2
    group_size = tp_count // kv_count
    head_dim = trainer_panels.shape[2]
    block_rows = trainer_panels.shape[1]
    half_rows = block_rows // 2
    seq_total = tokens.shape[0]

    core = member_id % 2
    partner_perm = [(i, i ^ 1) for i in range(tp_count)]
    all_halves = chip_ring_gather(trainer_panels, tp_count // 2, 2)
    all_halves = all_halves.reshape((-1,) + all_halves.shape[2:])
    kv_id = member_id // group_size
    quarter = member_id % group_size
    kv_panel = tp_count + kv_id + kv_count * (quarter // 2)
    half = core
    partner_id = member_id ^ 1
    q_mine = all_halves[panel_home[member_id]]
    q_theirs = lax.ppermute(all_halves[panel_home[partner_id]], "tp", partner_perm)
    q_block = jnp.where(core == 0, jnp.concatenate([q_mine, q_theirs], axis=0),
                        jnp.concatenate([q_theirs, q_mine], axis=0))
    kv_half = all_halves[panel_home[kv_panel]]
    piece = jnp.concatenate([q_block, kv_half], axis=0)
    gathered = gather_hbm(piece, "grp", grp_count, 0)
    q_weights = gathered[:, :block_rows].reshape(grp_count * block_rows, head_dim)
    kv_weights = gathered[:, block_rows:]

    use_half = lax.broadcasted_iota(jnp.int32, (1, 2, 1, 1), 1) == half
    kv_rows = jnp.where(use_half, kv_weights[:, None], jnp.zeros_like(kv_weights[:, None]))
    both_weights = jnp.concatenate(
        [q_weights, kv_rows.reshape(grp_count * block_rows, head_dim)], axis=1
    )
    projected = jnp.dot(tokens, both_weights, preferred_element_type=jnp.float32)
    return tail(projected, lengths, tp_count, 1)


def solution(mesh):
    placed = (P("grp", None), P("tp", "grp", None), P(), P("grp", None))
    return jax.shard_map(
        on_device, mesh=mesh, in_specs=placed, out_specs=P(("grp", "tp"), None), check_vma=False
    )
```

```python
import functools

import jax
import jax.numpy as jnp
from jax import lax
from jax.experimental import pallas as pl
from jax.experimental.pallas import tpu as pltpu
from jax.sharding import PartitionSpec as P

MESH = pl.DeviceIdType.MESH


def ring_kernel(count, stride, chunks, send_ref, out_ref, landed, send_sems, recv_sems):
    me = lax.axis_index("tp")
    total = count * stride
    right, left = lax.rem(me + stride, total), lax.rem(me + total - stride, total)
    spot = me // stride
    barrier = pltpu.get_barrier_semaphore()
    for neighbour in (left, right):
        pl.semaphore_signal(barrier, inc=1, device_id={"tp": neighbour}, device_id_type=MESH)
    pl.semaphore_wait(barrier, 2)

    def incoming(origin, chunk):
        return pltpu.make_async_remote_copy(
            src_ref=send_ref.at[chunk],
            dst_ref=landed.at[origin, chunk],
            send_sem=send_sems.at[0, 0, 0],
            recv_sem=recv_sems.at[origin, chunk],
            device_id={"tp": right},
            device_id_type=MESH,
        )

    landed[spot] = send_ref[...]
    sends = []
    far_right, far_left = count // 2, (count - 1) // 2
    for step in range(1, far_right + 1):
        for chunk in range(chunks):
            streams = [(0, right, lax.rem(spot + count - (step - 1), count))]
            if step <= far_left:
                streams.append((1, left, lax.rem(spot + step - 1, count)))
            for way, target, origin in streams:
                if step > 1:
                    incoming(origin, chunk).wait_recv()
                source = send_ref.at[chunk] if step == 1 else landed.at[origin, chunk]
                copy = pltpu.make_async_remote_copy(
                    src_ref=source,
                    dst_ref=landed.at[origin, chunk],
                    send_sem=send_sems.at[way, step, chunk],
                    recv_sem=recv_sems.at[origin, chunk],
                    device_id={"tp": target},
                    device_id_type=MESH,
                )
                copy.start()
                sends.append(copy)
    for chunk in range(chunks):
        incoming(lax.rem(spot + count - far_right, count), chunk).wait_recv()
        incoming(lax.rem(spot + far_left, count), chunk).wait_recv()
    for copy in sends:
        copy.wait_send()
    out_ref[...] = landed[...]


def ring_gather(x, count, stride, chunks, collective_id):
    x = x.reshape((chunks, x.shape[0] // chunks) + x.shape[1:])
    gathered = pl.pallas_call(
        functools.partial(ring_kernel, count, stride, chunks),
        out_shape=jax.ShapeDtypeStruct((count,) + x.shape, x.dtype),
        in_specs=[pl.BlockSpec(memory_space=pltpu.VMEM)],
        out_specs=pl.BlockSpec(memory_space=pltpu.VMEM),
        scratch_shapes=[
            pltpu.VMEM((count,) + x.shape, x.dtype),
            pltpu.SemaphoreType.DMA((2, count // 2 + 1, chunks)),
            pltpu.SemaphoreType.DMA((count, chunks)),
        ],
        compiler_params=pltpu.CompilerParams(collective_id=collective_id, has_side_effects=True),
    )(x)
    return gathered.reshape((count * x.shape[0] * x.shape[1],) + x.shape[2:])


def chip_ring_kernel(count, panels_ref, out_ref, landed, send_sems, recv_sems):
    me = lax.axis_index("tp")
    total = 2 * count
    core = me % 2
    partner = me + 1 - 2 * core
    right, left = lax.rem(me + 2, total), lax.rem(me + total - 2, total)
    spot = me // 2
    half = panels_ref.shape[1] // 2
    barrier = pltpu.get_barrier_semaphore()
    for neighbour in (left, right, partner):
        pl.semaphore_signal(barrier, inc=1, device_id={"tp": neighbour}, device_id_type=MESH)
    pl.semaphore_wait(barrier, 3)

    def rows_of(slot, which):
        return panels_ref.at[slot, pl.ds(pl.multiple_of(which * half, 16), half)]

    def incoming(origin, chunk):
        return pltpu.make_async_remote_copy(
            src_ref=rows_of(0, 0),
            dst_ref=landed.at[origin, chunk],
            send_sem=send_sems.at[0, 0, 0],
            recv_sem=recv_sems.at[origin, chunk],
            device_id={"tp": right},
            device_id_type=MESH,
        )

    sends = []

    def send(source, origin, chunk, sem, target):
        copy = pltpu.make_async_remote_copy(
            src_ref=source,
            dst_ref=landed.at[origin, chunk],
            send_sem=sem,
            recv_sem=recv_sems.at[origin, chunk],
            device_id={"tp": target},
            device_id_type=MESH,
        )
        copy.start()
        sends.append(copy)

    own = [2 * core + j for j in range(2)]
    theirs = [2 * (1 - core) + j for j in range(2)]
    for j in range(2):
        send(rows_of(j, 1 - core), spot, own[j], send_sems.at[0, 0, 1 + j], partner)
        landed[spot, own[j]] = rows_of(j, core)[...]
    far_right, far_left = count // 2, (count - 1) // 2
    first = [(rows_of(j, core), own[j]) for j in range(2)] + [(None, theirs[j]) for j in range(2)]
    for position, (source, chunk) in enumerate(first):
        if source is None:
            incoming(spot, chunk).wait_recv()
            source = landed.at[spot, chunk]
        send(source, spot, chunk, send_sems.at[0, 1, position], right)
        if far_left >= 1:
            send(source, spot, chunk, send_sems.at[1, 1, position], left)
    for step in range(2, far_right + 1):
        for chunk in range(4):
            streams = [(0, right, lax.rem(spot + count - (step - 1), count))]
            if step <= far_left:
                streams.append((1, left, lax.rem(spot + step - 1, count)))
            for way, target, origin in streams:
                incoming(origin, chunk).wait_recv()
                send(landed.at[origin, chunk], origin, chunk, send_sems.at[way, step, chunk], target)
    for chunk in range(4):
        incoming(lax.rem(spot + count - far_right, count), chunk).wait_recv()
        incoming(lax.rem(spot + far_left, count), chunk).wait_recv()
    for copy in sends:
        copy.wait_send()
    out_ref[...] = landed[...]


def chip_ring_gather(panels, count, collective_id):
    slots, rows, width = panels.shape
    return pl.pallas_call(
        functools.partial(chip_ring_kernel, count),
        out_shape=jax.ShapeDtypeStruct((count, 2 * slots, rows // 2, width), panels.dtype),
        in_specs=[pl.BlockSpec(memory_space=pltpu.VMEM)],
        out_specs=pl.BlockSpec(memory_space=pltpu.VMEM),
        scratch_shapes=[
            pltpu.VMEM((count, 2 * slots, rows // 2, width), panels.dtype),
            pltpu.SemaphoreType.DMA((2, count // 2 + 1, 2 * slots)),
            pltpu.SemaphoreType.DMA((count, 2 * slots)),
        ],
        compiler_params=pltpu.CompilerParams(collective_id=collective_id, has_side_effects=True),
    )(panels)


def kv_share_kernel(part_ref, out_ref, partner_part, mine, theirs, send_sems, recv_sems):
    me = lax.axis_index("tp")
    partner = me + 1 - 2 * (me % 2)
    across = me + 2 - 4 * ((me // 2) % 2)
    barrier = pltpu.get_barrier_semaphore()
    for neighbour in (partner, across):
        pl.semaphore_signal(barrier, inc=1, device_id={"tp": neighbour}, device_id_type=MESH)
    pl.semaphore_wait(barrier, 2)
    first = pltpu.make_async_remote_copy(
        src_ref=part_ref, dst_ref=partner_part, send_sem=send_sems.at[0], recv_sem=recv_sems.at[0],
        device_id={"tp": partner}, device_id_type=MESH,
    )
    first.start()
    first.wait()
    mine[...] = (part_ref[...] + partner_part[...]).astype(mine.dtype)
    second = pltpu.make_async_remote_copy(
        src_ref=mine, dst_ref=theirs, send_sem=send_sems.at[1], recv_sem=recv_sems.at[1],
        device_id={"tp": across}, device_id_type=MESH,
    )
    second.start()
    second.wait()
    holds_k = (me % 4) < 2
    out_ref[0] = jnp.where(holds_k, mine[...], theirs[...])
    out_ref[1] = jnp.where(holds_k, theirs[...], mine[...])


def kv_share(part, collective_id):
    return pl.pallas_call(
        kv_share_kernel,
        out_shape=jax.ShapeDtypeStruct((2,) + part.shape, jnp.bfloat16),
        in_specs=[pl.BlockSpec(memory_space=pltpu.VMEM)],
        out_specs=pl.BlockSpec(memory_space=pltpu.VMEM),
        scratch_shapes=[
            pltpu.VMEM(part.shape, part.dtype),
            pltpu.VMEM(part.shape, jnp.bfloat16),
            pltpu.VMEM(part.shape, jnp.bfloat16),
            pltpu.SemaphoreType.DMA((2,)),
            pltpu.SemaphoreType.DMA((2,)),
        ],
        compiler_params=pltpu.CompilerParams(collective_id=collective_id, has_side_effects=True),
    )(part)


def tail_kernel(count, scale, projected_ref, lengths_ref, out_ref,
                part_ref, partner_part, mine, theirs, staged, landed, send_sems, recv_sems):
    width = landed.shape[-1]
    part_ref[...] = projected_ref[:, width:]
    me = lax.axis_index("tp")
    partner = me + 1 - 2 * (me % 2)
    across = me + 2 - 4 * ((me // 2) % 2)
    barrier = pltpu.get_barrier_semaphore()
    for step in range(1, count):
        peer = lax.rem(me + step, count)
        pl.semaphore_signal(barrier, inc=1, device_id={"tp": peer}, device_id_type=MESH)
    pl.semaphore_wait(barrier, count - 1)
    first = pltpu.make_async_remote_copy(
        src_ref=part_ref, dst_ref=partner_part, send_sem=send_sems.at[0], recv_sem=recv_sems.at[0],
        device_id={"tp": partner}, device_id_type=MESH,
    )
    first.start()
    first.wait()
    mine[...] = (part_ref[...] + partner_part[...]).astype(mine.dtype)
    second = pltpu.make_async_remote_copy(
        src_ref=mine, dst_ref=theirs, send_sem=send_sems.at[1], recv_sem=recv_sems.at[1],
        device_id={"tp": across}, device_id_type=MESH,
    )
    second.start()
    second.wait()
    holds_k = (me % 4) < 2
    keys = jnp.where(holds_k, mine[...], theirs[...])
    values = jnp.where(holds_k, theirs[...], mine[...])

    scores = lax.dot_general(
        projected_ref[:, :width].astype(jnp.bfloat16), keys, (((1,), (1,)), ((), ())), preferred_element_type=jnp.float32
    ) * scale
    seq = scores.shape[0]
    row = lax.broadcasted_iota(jnp.int32, (seq, seq), 0)
    col = lax.broadcasted_iota(jnp.int32, (seq, seq), 1)
    row_segment = jnp.zeros((seq, seq), jnp.int32)
    col_segment = jnp.zeros((seq, seq), jnp.int32)
    bound = lengths_ref[0, 0] * 0
    for response in range(lengths_ref.shape[1]):
        bound = bound + lengths_ref[0, response]
        row_segment = row_segment + (row >= bound).astype(jnp.int32)
        col_segment = col_segment + (col >= bound).astype(jnp.int32)
    allowed = (row_segment == col_segment) & (col <= row)
    masked = jnp.where(allowed, scores, -jnp.inf)
    peak = jnp.max(masked, axis=1, keepdims=True)
    weights = jnp.exp(masked - peak)
    probs = (weights / jnp.sum(weights, axis=1, keepdims=True)).astype(jnp.bfloat16)
    context = jnp.dot(probs, values, preferred_element_type=jnp.float32)
    rows = seq // count
    for target in range(count):
        staged[target] = context[target * rows:(target + 1) * rows]

    copies = []
    for step in range(1, count):
        peer = lax.rem(me + step, count)
        copy = pltpu.make_async_remote_copy(
            src_ref=staged.at[peer],
            dst_ref=landed.at[me],
            send_sem=send_sems.at[1 + step],
            recv_sem=recv_sems.at[1 + step],
            device_id={"tp": peer},
            device_id_type=MESH,
        )
        copy.start()
        copies.append(copy)
    landed[me] = staged[me]
    for copy in copies:
        copy.wait()
    for source in range(count):
        out_ref[:, source * width:(source + 1) * width] = landed[source]


def tail(projected, lengths, count, collective_id):
    seq, width = projected.shape[0], projected.shape[1] // 2
    part = jax.ShapeDtypeStruct((seq, width), jnp.float32)
    rows = seq // count
    vmem = pl.BlockSpec(memory_space=pltpu.VMEM)
    return pl.pallas_call(
        functools.partial(tail_kernel, count, width ** (-0.5)),
        out_shape=jax.ShapeDtypeStruct((rows, count * width), jnp.float32),
        in_specs=[vmem, pl.BlockSpec(memory_space=pltpu.SMEM)],
        out_specs=vmem,
        scratch_shapes=[
            pltpu.VMEM(part.shape, part.dtype),
            pltpu.VMEM(part.shape, part.dtype),
            pltpu.VMEM(part.shape, jnp.bfloat16),
            pltpu.VMEM(part.shape, jnp.bfloat16),
            pltpu.VMEM((count, rows, width), jnp.float32),
            pltpu.VMEM((count, rows, width), jnp.float32),
            pltpu.SemaphoreType.DMA((count + 1,)),
            pltpu.SemaphoreType.DMA((count + 1,)),
        ],
        compiler_params=pltpu.CompilerParams(collective_id=collective_id, has_side_effects=True),
    )(projected, lengths)


def grid_kernel(width, send_ref, out_ref, landed, send_sems, recv_sems):
    me = lax.axis_index("grp")
    core = lax.axis_index("tp") % 2
    col, row = me % width, me // width

    def node(c, r):
        return lax.rem(r + width, width) * width + lax.rem(c + width, width)

    def along(dim, c, r, k):
        return node(c + k, r) if dim == 0 else node(c, r + k)

    barrier = pltpu.get_barrier_semaphore()
    neighbours = [node(col + 1, row), node(col - 1, row), node(col, row + 1), node(col, row - 1)]
    for neighbour in neighbours:
        pl.semaphore_signal(barrier, inc=1, device_id={"grp": neighbour}, device_id_type=MESH)
    pl.semaphore_wait(barrier, 4)

    landed[me] = send_ref[...]
    sends = []

    def send(source, origin, half, target):
        copy = pltpu.make_async_remote_copy(
            src_ref=source,
            dst_ref=landed.at[origin, half],
            send_sem=send_sems.at[len(sends)],
            recv_sem=recv_sems.at[origin, half],
            device_id={"grp": target},
            device_id_type=MESH,
        )
        copy.start()
        sends.append(copy)

    def arrive(origin, half):
        pltpu.make_async_remote_copy(
            src_ref=send_ref.at[half],
            dst_ref=landed.at[origin, half],
            send_sem=send_sems.at[0],
            recv_sem=recv_sems.at[origin, half],
            device_id={"grp": neighbours[0]},
            device_id_type=MESH,
        ).wait_recv()

    ahead = 1 - 2 * core

    def phase(lines, half, dim):
        for k in (1, -1):
            for line in lines:
                origin = along(1 - dim, col, row, line)
                source = send_ref.at[half] if line == 0 else landed.at[origin, half]
                send(source, origin, half, along(dim, col, row, k))
        for line in lines:
            for k in (1, -1):
                arrive(along(dim, along(1 - dim, col, row, line) % width, along(1 - dim, col, row, line) // width, k), half)
        for line in lines:
            base = along(1 - dim, col, row, line)
            bc, br = base % width, base // width
            send(landed.at[along(dim, bc, br, -ahead), half], along(dim, bc, br, -ahead), half,
                 along(dim, col, row, ahead))
        for line in lines:
            base = along(1 - dim, col, row, line)
            arrive(along(dim, base % width, base // width, 2), half)

    phase([0], 0, 0)
    phase([0], 1, 1)
    phase([0, 1, -1, 2], 0, 1)
    phase([0, 1, -1, 2], 1, 0)
    for copy in sends:
        copy.wait_send()
    out_ref[...] = landed[...]


def grid_gather(x, width, collective_id):
    count = width * width
    x = x.reshape((2, x.shape[0] // 2) + x.shape[1:])
    gathered = pl.pallas_call(
        functools.partial(grid_kernel, width),
        out_shape=jax.ShapeDtypeStruct((count,) + x.shape, x.dtype),
        in_specs=[pl.BlockSpec(memory_space=pltpu.VMEM)],
        out_specs=pl.BlockSpec(memory_space=pltpu.VMEM),
        scratch_shapes=[
            pltpu.VMEM((count,) + x.shape, x.dtype),
            pltpu.SemaphoreType.DMA((2 * (count - 1),)),
            pltpu.SemaphoreType.DMA((count, 2)),
        ],
        compiler_params=pltpu.CompilerParams(collective_id=collective_id, has_side_effects=True),
    )(x)
    return gathered.reshape((count, x.shape[0] * x.shape[1]) + x.shape[2:])


def gather_hbm_kernel(axis, count, send_ref, out_ref, send_sems, recv_sems, local_sem):
    me = lax.axis_index(axis)
    barrier = pltpu.get_barrier_semaphore()
    for step in range(1, count):
        peer = lax.rem(me + step, count)
        pl.semaphore_signal(barrier, inc=1, device_id={axis: peer}, device_id_type=MESH)
    pl.semaphore_wait(barrier, count - 1)
    copies = []
    for step in range(1, count):
        peer = lax.rem(me + step, count)
        copy = pltpu.make_async_remote_copy(
            src_ref=send_ref,
            dst_ref=out_ref.at[me],
            send_sem=send_sems.at[step],
            recv_sem=recv_sems.at[step],
            device_id={axis: peer},
            device_id_type=MESH,
        )
        copy.start()
        copies.append(copy)
    local = pltpu.make_async_copy(send_ref, out_ref.at[me], local_sem)
    local.start()
    for copy in copies:
        copy.wait()
    local.wait()


def gather_hbm(x, axis, count, collective_id):
    return pl.pallas_call(
        functools.partial(gather_hbm_kernel, axis, count),
        out_shape=jax.ShapeDtypeStruct((count,) + x.shape, x.dtype),
        in_specs=[pl.BlockSpec(memory_space=pltpu.VMEM)],
        out_specs=pl.BlockSpec(memory_space=pl.ANY),
        scratch_shapes=[
            pltpu.SemaphoreType.DMA((count,)),
            pltpu.SemaphoreType.DMA((count,)),
            pltpu.SemaphoreType.DMA(()),
        ],
        compiler_params=pltpu.CompilerParams(collective_id=collective_id, has_side_effects=True),
    )(x)


def weights_gather_kernel(count, own_ref, for_partner_ref, out_ref, partner_rows,
                          send_sems, recv_sems, partner_sems, local_sems):
    me = lax.axis_index("grp")
    member = lax.axis_index("tp")
    partner = member + 1 - 2 * (member % 2)
    rows = own_ref.shape[0]
    barrier = pltpu.get_barrier_semaphore()
    pl.semaphore_signal(barrier, inc=1, device_id={"tp": partner}, device_id_type=MESH)
    for step in range(1, count):
        peer = lax.rem(me + step, count)
        pl.semaphore_signal(barrier, inc=1, device_id={"grp": peer}, device_id_type=MESH)
    pl.semaphore_wait(barrier, count)
    to_partner = pltpu.make_async_remote_copy(
        src_ref=for_partner_ref, dst_ref=partner_rows, send_sem=partner_sems.at[0],
        recv_sem=partner_sems.at[1], device_id={"tp": partner}, device_id_type=MESH,
    )
    to_partner.start()
    copies = []

    def spread(part, source, window):
        for step in range(1, count):
            peer = lax.rem(me + step, count)
            copy = pltpu.make_async_remote_copy(
                src_ref=source,
                dst_ref=out_ref.at[me, window],
                send_sem=send_sems.at[part, step],
                recv_sem=recv_sems.at[part, step],
                device_id={"grp": peer},
                device_id_type=MESH,
            )
            copy.start()
            copies.append(copy)
        local = pltpu.make_async_copy(source, out_ref.at[me, window], local_sems.at[part])
        local.start()
        copies.append(local)

    spread(0, own_ref, pl.ds(0, rows))
    to_partner.wait()
    spread(1, partner_rows, pl.ds(rows, partner_rows.shape[0]))
    for copy in copies:
        copy.wait()


def weights_gather(own, for_partner, count, collective_id):
    rows = own.shape[0] + for_partner.shape[0]
    return pl.pallas_call(
        functools.partial(weights_gather_kernel, count),
        out_shape=jax.ShapeDtypeStruct((count, rows) + own.shape[1:], own.dtype),
        in_specs=[pl.BlockSpec(memory_space=pltpu.VMEM)] * 2,
        out_specs=pl.BlockSpec(memory_space=pl.ANY),
        scratch_shapes=[
            pltpu.VMEM(for_partner.shape, for_partner.dtype),
            pltpu.SemaphoreType.DMA((2, count)),
            pltpu.SemaphoreType.DMA((2, count)),
            pltpu.SemaphoreType.DMA((2,)),
            pltpu.SemaphoreType.DMA((2,)),
        ],
        compiler_params=pltpu.CompilerParams(collective_id=collective_id, has_side_effects=True),
    )(own, for_partner)


def exchange_kernel(axis, count, scatter, send_ref, out_ref, landed, send_sems, recv_sems):
    me = lax.axis_index(axis)
    barrier = pltpu.get_barrier_semaphore()
    for step in range(1, count):
        peer = lax.rem(me + step, count)
        pl.semaphore_signal(barrier, inc=1, device_id={axis: peer}, device_id_type=MESH)
    pl.semaphore_wait(barrier, count - 1)
    copies = []
    for step in range(1, count):
        peer = lax.rem(me + step, count)
        source = send_ref.at[peer] if scatter else send_ref
        copy = pltpu.make_async_remote_copy(
            src_ref=source,
            dst_ref=landed.at[me],
            send_sem=send_sems.at[step],
            recv_sem=recv_sems.at[step],
            device_id={axis: peer},
            device_id_type=MESH,
        )
        copy.start()
        copies.append(copy)
    landed[me] = send_ref[me] if scatter else send_ref[...]
    for copy in copies:
        copy.wait()
    if scatter:
        width = landed.shape[-1]
        for source in range(count):
            out_ref[:, source * width:(source + 1) * width] = landed[source]
    else:
        out_ref[...] = landed[...]


def exchange(x, axis, count, scatter, collective_id):
    piece = x.shape[1:] if scatter else x.shape
    result = (piece[0], count * piece[1]) if scatter else (count,) + piece
    return pl.pallas_call(
        functools.partial(exchange_kernel, axis, count, scatter),
        out_shape=jax.ShapeDtypeStruct(result, x.dtype),
        in_specs=[pl.BlockSpec(memory_space=pltpu.VMEM)],
        out_specs=pl.BlockSpec(memory_space=pltpu.VMEM),
        scratch_shapes=[
            pltpu.VMEM((count,) + piece, x.dtype),
            pltpu.SemaphoreType.DMA((count,)),
            pltpu.SemaphoreType.DMA((count,)),
        ],
        compiler_params=pltpu.CompilerParams(collective_id=collective_id, has_side_effects=True),
    )(x)


def on_device(tokens, trainer_panels, panel_home, lengths):
    tp_count = lax.axis_size("tp")
    grp_count = lax.axis_size("grp")
    member_id = lax.axis_index("tp")
    kv_count = (panel_home.shape[0] - tp_count) // 2
    group_size = tp_count // kv_count
    head_dim = trainer_panels.shape[2]
    block_rows = trainer_panels.shape[1]
    half_rows = block_rows // 2
    seq_total = tokens.shape[0]

    core = member_id % 2
    partner_perm = [(i, i ^ 1) for i in range(tp_count)]
    all_halves = chip_ring_gather(trainer_panels, tp_count // 2, 2)
    all_halves = all_halves.reshape((-1,) + all_halves.shape[2:])
    kv_id = member_id // group_size
    quarter = member_id % group_size
    kv_panel = tp_count + kv_id + kv_count * (quarter // 2)
    half = core
    partner_id = member_id ^ 1
    q_mine = all_halves[panel_home[member_id]]
    kv_half = all_halves[panel_home[kv_panel]]
    for_partner = all_halves[panel_home[partner_id]]
    gathered = weights_gather(jnp.concatenate([q_mine, kv_half], axis=0), for_partner, grp_count, 0)
    q_here = gathered[:, :half_rows]
    kv_weights = gathered[:, half_rows:block_rows]
    q_there = gathered[:, block_rows:]
    q_weights = jnp.where(
        core == 0,
        jnp.concatenate([q_here, q_there], axis=1),
        jnp.concatenate([q_there, q_here], axis=1),
    ).reshape(grp_count * block_rows, head_dim)

    use_half = lax.broadcasted_iota(jnp.int32, (1, 2, 1, 1), 1) == half
    kv_rows = jnp.where(use_half, kv_weights[:, None], jnp.zeros_like(kv_weights[:, None]))
    both_weights = jnp.concatenate(
        [q_weights, kv_rows.reshape(grp_count * block_rows, head_dim)], axis=1
    )
    projected = jnp.dot(tokens, both_weights, preferred_element_type=jnp.float32)
    return tail(projected, lengths, tp_count, 1)


def solution(mesh):
    placed = (P("grp", None), P("tp", "grp", None), P(), P("grp", None))
    return jax.shard_map(
        on_device, mesh=mesh, in_specs=placed, out_specs=P(("grp", "tp"), None), check_vma=False
    )
```

```python
import functools

import jax
import jax.numpy as jnp
from jax import lax
from jax.experimental import pallas as pl
from jax.experimental.pallas import tpu as pltpu
from jax.sharding import PartitionSpec as P

MESH = pl.DeviceIdType.MESH


def ring_kernel(count, stride, chunks, send_ref, out_ref, landed, send_sems, recv_sems):
    me = lax.axis_index("tp")
    total = count * stride
    right, left = lax.rem(me + stride, total), lax.rem(me + total - stride, total)
    spot = me // stride
    barrier = pltpu.get_barrier_semaphore()
    for neighbour in (left, right):
        pl.semaphore_signal(barrier, inc=1, device_id={"tp": neighbour}, device_id_type=MESH)
    pl.semaphore_wait(barrier, 2)

    def incoming(origin, chunk):
        return pltpu.make_async_remote_copy(
            src_ref=send_ref.at[chunk],
            dst_ref=landed.at[origin, chunk],
            send_sem=send_sems.at[0, 0, 0],
            recv_sem=recv_sems.at[origin, chunk],
            device_id={"tp": right},
            device_id_type=MESH,
        )

    landed[spot] = send_ref[...]
    sends = []
    far_right, far_left = count // 2, (count - 1) // 2
    for step in range(1, far_right + 1):
        for chunk in range(chunks):
            streams = [(0, right, lax.rem(spot + count - (step - 1), count))]
            if step <= far_left:
                streams.append((1, left, lax.rem(spot + step - 1, count)))
            for way, target, origin in streams:
                if step > 1:
                    incoming(origin, chunk).wait_recv()
                source = send_ref.at[chunk] if step == 1 else landed.at[origin, chunk]
                copy = pltpu.make_async_remote_copy(
                    src_ref=source,
                    dst_ref=landed.at[origin, chunk],
                    send_sem=send_sems.at[way, step, chunk],
                    recv_sem=recv_sems.at[origin, chunk],
                    device_id={"tp": target},
                    device_id_type=MESH,
                )
                copy.start()
                sends.append(copy)
    for chunk in range(chunks):
        incoming(lax.rem(spot + count - far_right, count), chunk).wait_recv()
        incoming(lax.rem(spot + far_left, count), chunk).wait_recv()
    for copy in sends:
        copy.wait_send()
    out_ref[...] = landed[...]


def ring_gather(x, count, stride, chunks, collective_id):
    x = x.reshape((chunks, x.shape[0] // chunks) + x.shape[1:])
    gathered = pl.pallas_call(
        functools.partial(ring_kernel, count, stride, chunks),
        out_shape=jax.ShapeDtypeStruct((count,) + x.shape, x.dtype),
        in_specs=[pl.BlockSpec(memory_space=pltpu.VMEM)],
        out_specs=pl.BlockSpec(memory_space=pltpu.VMEM),
        scratch_shapes=[
            pltpu.VMEM((count,) + x.shape, x.dtype),
            pltpu.SemaphoreType.DMA((2, count // 2 + 1, chunks)),
            pltpu.SemaphoreType.DMA((count, chunks)),
        ],
        compiler_params=pltpu.CompilerParams(collective_id=collective_id, has_side_effects=True),
    )(x)
    return gathered.reshape((count * x.shape[0] * x.shape[1],) + x.shape[2:])


def chip_ring_kernel(count, panels_ref, out_ref, landed, send_sems, recv_sems):
    me = lax.axis_index("tp")
    total = 2 * count
    core = me % 2
    partner = me + 1 - 2 * core
    right, left = lax.rem(me + 2, total), lax.rem(me + total - 2, total)
    spot = me // 2
    half = panels_ref.shape[1] // 2
    barrier = pltpu.get_barrier_semaphore()
    for neighbour in (left, right, partner):
        pl.semaphore_signal(barrier, inc=1, device_id={"tp": neighbour}, device_id_type=MESH)
    pl.semaphore_wait(barrier, 3)

    def rows_of(slot, which):
        return panels_ref.at[slot, pl.ds(pl.multiple_of(which * half, 16), half)]

    def incoming(origin, chunk):
        return pltpu.make_async_remote_copy(
            src_ref=rows_of(0, 0),
            dst_ref=landed.at[origin, chunk],
            send_sem=send_sems.at[0, 0, 0],
            recv_sem=recv_sems.at[origin, chunk],
            device_id={"tp": right},
            device_id_type=MESH,
        )

    sends = []

    def send(source, origin, chunk, sem, target):
        copy = pltpu.make_async_remote_copy(
            src_ref=source,
            dst_ref=landed.at[origin, chunk],
            send_sem=sem,
            recv_sem=recv_sems.at[origin, chunk],
            device_id={"tp": target},
            device_id_type=MESH,
        )
        copy.start()
        sends.append(copy)

    own = [2 * core + j for j in range(2)]
    theirs = [2 * (1 - core) + j for j in range(2)]
    for j in range(2):
        send(rows_of(j, 1 - core), spot, own[j], send_sems.at[0, 0, 1 + j], partner)
        landed[spot, own[j]] = rows_of(j, core)[...]
    far_right, far_left = count // 2, (count - 1) // 2
    first = [(rows_of(j, core), own[j]) for j in range(2)] + [(None, theirs[j]) for j in range(2)]
    for position, (source, chunk) in enumerate(first):
        if source is None:
            incoming(spot, chunk).wait_recv()
            source = landed.at[spot, chunk]
        send(source, spot, chunk, send_sems.at[0, 1, position], right)
        if far_left >= 1:
            send(source, spot, chunk, send_sems.at[1, 1, position], left)
    for step in range(2, far_right + 1):
        for chunk in range(4):
            streams = [(0, right, lax.rem(spot + count - (step - 1), count))]
            if step <= far_left:
                streams.append((1, left, lax.rem(spot + step - 1, count)))
            for way, target, origin in streams:
                incoming(origin, chunk).wait_recv()
                send(landed.at[origin, chunk], origin, chunk, send_sems.at[way, step, chunk], target)
    for chunk in range(4):
        incoming(lax.rem(spot + count - far_right, count), chunk).wait_recv()
        incoming(lax.rem(spot + far_left, count), chunk).wait_recv()
    for copy in sends:
        copy.wait_send()
    out_ref[...] = landed[...]


def chip_ring_gather(panels, count, collective_id):
    slots, rows, width = panels.shape
    return pl.pallas_call(
        functools.partial(chip_ring_kernel, count),
        out_shape=jax.ShapeDtypeStruct((count, 2 * slots, rows // 2, width), panels.dtype),
        in_specs=[pl.BlockSpec(memory_space=pltpu.VMEM)],
        out_specs=pl.BlockSpec(memory_space=pltpu.VMEM),
        scratch_shapes=[
            pltpu.VMEM((count, 2 * slots, rows // 2, width), panels.dtype),
            pltpu.SemaphoreType.DMA((2, count // 2 + 1, 2 * slots)),
            pltpu.SemaphoreType.DMA((count, 2 * slots)),
        ],
        compiler_params=pltpu.CompilerParams(collective_id=collective_id, has_side_effects=True),
    )(panels)


def kv_share_kernel(part_ref, out_ref, partner_part, mine, theirs, send_sems, recv_sems):
    me = lax.axis_index("tp")
    partner = me + 1 - 2 * (me % 2)
    across = me + 2 - 4 * ((me // 2) % 2)
    barrier = pltpu.get_barrier_semaphore()
    for neighbour in (partner, across):
        pl.semaphore_signal(barrier, inc=1, device_id={"tp": neighbour}, device_id_type=MESH)
    pl.semaphore_wait(barrier, 2)
    first = pltpu.make_async_remote_copy(
        src_ref=part_ref, dst_ref=partner_part, send_sem=send_sems.at[0], recv_sem=recv_sems.at[0],
        device_id={"tp": partner}, device_id_type=MESH,
    )
    first.start()
    first.wait()
    mine[...] = (part_ref[...] + partner_part[...]).astype(mine.dtype)
    second = pltpu.make_async_remote_copy(
        src_ref=mine, dst_ref=theirs, send_sem=send_sems.at[1], recv_sem=recv_sems.at[1],
        device_id={"tp": across}, device_id_type=MESH,
    )
    second.start()
    second.wait()
    holds_k = (me % 4) < 2
    out_ref[0] = jnp.where(holds_k, mine[...], theirs[...])
    out_ref[1] = jnp.where(holds_k, theirs[...], mine[...])


def kv_share(part, collective_id):
    return pl.pallas_call(
        kv_share_kernel,
        out_shape=jax.ShapeDtypeStruct((2,) + part.shape, jnp.bfloat16),
        in_specs=[pl.BlockSpec(memory_space=pltpu.VMEM)],
        out_specs=pl.BlockSpec(memory_space=pltpu.VMEM),
        scratch_shapes=[
            pltpu.VMEM(part.shape, part.dtype),
            pltpu.VMEM(part.shape, jnp.bfloat16),
            pltpu.VMEM(part.shape, jnp.bfloat16),
            pltpu.SemaphoreType.DMA((2,)),
            pltpu.SemaphoreType.DMA((2,)),
        ],
        compiler_params=pltpu.CompilerParams(collective_id=collective_id, has_side_effects=True),
    )(part)


def tail_kernel(count, scale, tokens_ref, weights_ref, lengths_ref, out_ref,
                part_ref, partner_part, mine, theirs, staged, landed, send_sems, recv_sems):
    width = landed.shape[-1]
    me = lax.axis_index("tp")
    partner = me + 1 - 2 * (me % 2)
    across = me + 2 - 4 * ((me // 2) % 2)
    barrier = pltpu.get_barrier_semaphore()
    for step in range(1, count):
        peer = lax.rem(me + step, count)
        pl.semaphore_signal(barrier, inc=1, device_id={"tp": peer}, device_id_type=MESH)
    projected = jnp.dot(tokens_ref[...], weights_ref[...], preferred_element_type=jnp.float32)
    part_ref[...] = projected[:, width:]
    query = projected[:, :width].astype(jnp.bfloat16)
    pl.semaphore_wait(barrier, count - 1)
    first = pltpu.make_async_remote_copy(
        src_ref=part_ref, dst_ref=partner_part, send_sem=send_sems.at[0], recv_sem=recv_sems.at[0],
        device_id={"tp": partner}, device_id_type=MESH,
    )
    first.start()
    first.wait()
    mine[...] = (part_ref[...] + partner_part[...]).astype(mine.dtype)
    second = pltpu.make_async_remote_copy(
        src_ref=mine, dst_ref=theirs, send_sem=send_sems.at[1], recv_sem=recv_sems.at[1],
        device_id={"tp": across}, device_id_type=MESH,
    )
    second.start()
    second.wait()
    holds_k = (me % 4) < 2
    keys = jnp.where(holds_k, mine[...], theirs[...])
    values = jnp.where(holds_k, theirs[...], mine[...])

    scores = lax.dot_general(
        query, keys, (((1,), (1,)), ((), ())), preferred_element_type=jnp.float32
    ) * scale
    seq = scores.shape[0]
    row = lax.broadcasted_iota(jnp.int32, (seq, seq), 0)
    col = lax.broadcasted_iota(jnp.int32, (seq, seq), 1)
    row_segment = jnp.zeros((seq, seq), jnp.int32)
    col_segment = jnp.zeros((seq, seq), jnp.int32)
    bound = lengths_ref[0, 0] * 0
    for response in range(lengths_ref.shape[1]):
        bound = bound + lengths_ref[0, response]
        row_segment = row_segment + (row >= bound).astype(jnp.int32)
        col_segment = col_segment + (col >= bound).astype(jnp.int32)
    allowed = (row_segment == col_segment) & (col <= row)
    masked = jnp.where(allowed, scores, -jnp.inf)
    peak = jnp.max(masked, axis=1, keepdims=True)
    weights = jnp.exp(masked - peak)
    probs = (weights / jnp.sum(weights, axis=1, keepdims=True)).astype(jnp.bfloat16)
    context = jnp.dot(probs, values, preferred_element_type=jnp.float32)
    rows = seq // count
    for target in range(count):
        staged[target] = context[target * rows:(target + 1) * rows]

    copies = []
    for step in range(1, count):
        peer = lax.rem(me + step, count)
        copy = pltpu.make_async_remote_copy(
            src_ref=staged.at[peer],
            dst_ref=landed.at[me],
            send_sem=send_sems.at[1 + step],
            recv_sem=recv_sems.at[1 + step],
            device_id={"tp": peer},
            device_id_type=MESH,
        )
        copy.start()
        copies.append(copy)
    landed[me] = staged[me]
    for copy in copies:
        copy.wait()
    for source in range(count):
        out_ref[:, source * width:(source + 1) * width] = landed[source]


def tail(tokens, weights, lengths, count, collective_id):
    seq, width = tokens.shape[0], weights.shape[1] // 2
    part = jax.ShapeDtypeStruct((seq, width), jnp.float32)
    rows = seq // count
    vmem = pl.BlockSpec(memory_space=pltpu.VMEM)
    return pl.pallas_call(
        functools.partial(tail_kernel, count, width ** (-0.5)),
        out_shape=jax.ShapeDtypeStruct((rows, count * width), jnp.float32),
        in_specs=[vmem, vmem, pl.BlockSpec(memory_space=pltpu.SMEM)],
        out_specs=vmem,
        scratch_shapes=[
            pltpu.VMEM(part.shape, part.dtype),
            pltpu.VMEM(part.shape, part.dtype),
            pltpu.VMEM(part.shape, jnp.bfloat16),
            pltpu.VMEM(part.shape, jnp.bfloat16),
            pltpu.VMEM((count, rows, width), jnp.float32),
            pltpu.VMEM((count, rows, width), jnp.float32),
            pltpu.SemaphoreType.DMA((count + 1,)),
            pltpu.SemaphoreType.DMA((count + 1,)),
        ],
        compiler_params=pltpu.CompilerParams(collective_id=collective_id, has_side_effects=True),
    )(tokens, weights, lengths)


def grid_kernel(width, send_ref, out_ref, landed, send_sems, recv_sems):
    me = lax.axis_index("grp")
    core = lax.axis_index("tp") % 2
    col, row = me % width, me // width

    def node(c, r):
        return lax.rem(r + width, width) * width + lax.rem(c + width, width)

    def along(dim, c, r, k):
        return node(c + k, r) if dim == 0 else node(c, r + k)

    barrier = pltpu.get_barrier_semaphore()
    neighbours = [node(col + 1, row), node(col - 1, row), node(col, row + 1), node(col, row - 1)]
    for neighbour in neighbours:
        pl.semaphore_signal(barrier, inc=1, device_id={"grp": neighbour}, device_id_type=MESH)
    pl.semaphore_wait(barrier, 4)

    landed[me] = send_ref[...]
    sends = []

    def send(source, origin, half, target):
        copy = pltpu.make_async_remote_copy(
            src_ref=source,
            dst_ref=landed.at[origin, half],
            send_sem=send_sems.at[len(sends)],
            recv_sem=recv_sems.at[origin, half],
            device_id={"grp": target},
            device_id_type=MESH,
        )
        copy.start()
        sends.append(copy)

    def arrive(origin, half):
        pltpu.make_async_remote_copy(
            src_ref=send_ref.at[half],
            dst_ref=landed.at[origin, half],
            send_sem=send_sems.at[0],
            recv_sem=recv_sems.at[origin, half],
            device_id={"grp": neighbours[0]},
            device_id_type=MESH,
        ).wait_recv()

    ahead = 1 - 2 * core

    def phase(lines, half, dim):
        for k in (1, -1):
            for line in lines:
                origin = along(1 - dim, col, row, line)
                source = send_ref.at[half] if line == 0 else landed.at[origin, half]
                send(source, origin, half, along(dim, col, row, k))
        for line in lines:
            for k in (1, -1):
                arrive(along(dim, along(1 - dim, col, row, line) % width, along(1 - dim, col, row, line) // width, k), half)
        for line in lines:
            base = along(1 - dim, col, row, line)
            bc, br = base % width, base // width
            send(landed.at[along(dim, bc, br, -ahead), half], along(dim, bc, br, -ahead), half,
                 along(dim, col, row, ahead))
        for line in lines:
            base = along(1 - dim, col, row, line)
            arrive(along(dim, base % width, base // width, 2), half)

    phase([0], 0, 0)
    phase([0], 1, 1)
    phase([0, 1, -1, 2], 0, 1)
    phase([0, 1, -1, 2], 1, 0)
    for copy in sends:
        copy.wait_send()
    out_ref[...] = landed[...]


def grid_gather(x, width, collective_id):
    count = width * width
    x = x.reshape((2, x.shape[0] // 2) + x.shape[1:])
    gathered = pl.pallas_call(
        functools.partial(grid_kernel, width),
        out_shape=jax.ShapeDtypeStruct((count,) + x.shape, x.dtype),
        in_specs=[pl.BlockSpec(memory_space=pltpu.VMEM)],
        out_specs=pl.BlockSpec(memory_space=pltpu.VMEM),
        scratch_shapes=[
            pltpu.VMEM((count,) + x.shape, x.dtype),
            pltpu.SemaphoreType.DMA((2 * (count - 1),)),
            pltpu.SemaphoreType.DMA((count, 2)),
        ],
        compiler_params=pltpu.CompilerParams(collective_id=collective_id, has_side_effects=True),
    )(x)
    return gathered.reshape((count, x.shape[0] * x.shape[1]) + x.shape[2:])


def gather_hbm_kernel(axis, count, send_ref, out_ref, send_sems, recv_sems, local_sem):
    me = lax.axis_index(axis)
    barrier = pltpu.get_barrier_semaphore()
    for step in range(1, count):
        peer = lax.rem(me + step, count)
        pl.semaphore_signal(barrier, inc=1, device_id={axis: peer}, device_id_type=MESH)
    pl.semaphore_wait(barrier, count - 1)
    copies = []
    for step in range(1, count):
        peer = lax.rem(me + step, count)
        copy = pltpu.make_async_remote_copy(
            src_ref=send_ref,
            dst_ref=out_ref.at[me],
            send_sem=send_sems.at[step],
            recv_sem=recv_sems.at[step],
            device_id={axis: peer},
            device_id_type=MESH,
        )
        copy.start()
        copies.append(copy)
    local = pltpu.make_async_copy(send_ref, out_ref.at[me], local_sem)
    local.start()
    for copy in copies:
        copy.wait()
    local.wait()


def gather_hbm(x, axis, count, collective_id):
    return pl.pallas_call(
        functools.partial(gather_hbm_kernel, axis, count),
        out_shape=jax.ShapeDtypeStruct((count,) + x.shape, x.dtype),
        in_specs=[pl.BlockSpec(memory_space=pltpu.VMEM)],
        out_specs=pl.BlockSpec(memory_space=pl.ANY),
        scratch_shapes=[
            pltpu.SemaphoreType.DMA((count,)),
            pltpu.SemaphoreType.DMA((count,)),
            pltpu.SemaphoreType.DMA(()),
        ],
        compiler_params=pltpu.CompilerParams(collective_id=collective_id, has_side_effects=True),
    )(x)


def weights_gather_kernel(count, own_ref, for_partner_ref, out_ref, partner_rows,
                          send_sems, recv_sems, partner_sems, local_sems):
    me = lax.axis_index("grp")
    member = lax.axis_index("tp")
    partner = member + 1 - 2 * (member % 2)
    rows = own_ref.shape[0]
    barrier = pltpu.get_barrier_semaphore()
    pl.semaphore_signal(barrier, inc=1, device_id={"tp": partner}, device_id_type=MESH)
    for step in range(1, count):
        peer = lax.rem(me + step, count)
        pl.semaphore_signal(barrier, inc=1, device_id={"grp": peer}, device_id_type=MESH)
    pl.semaphore_wait(barrier, count)
    to_partner = pltpu.make_async_remote_copy(
        src_ref=for_partner_ref, dst_ref=partner_rows, send_sem=partner_sems.at[0],
        recv_sem=partner_sems.at[1], device_id={"tp": partner}, device_id_type=MESH,
    )
    to_partner.start()
    copies = []

    def spread(part, source, window):
        for step in range(1, count):
            peer = lax.rem(me + step, count)
            copy = pltpu.make_async_remote_copy(
                src_ref=source,
                dst_ref=out_ref.at[me, window],
                send_sem=send_sems.at[part, step],
                recv_sem=recv_sems.at[part, step],
                device_id={"grp": peer},
                device_id_type=MESH,
            )
            copy.start()
            copies.append(copy)
        local = pltpu.make_async_copy(source, out_ref.at[me, window], local_sems.at[part])
        local.start()
        copies.append(local)

    spread(0, own_ref, pl.ds(0, rows))
    to_partner.wait()
    spread(1, partner_rows, pl.ds(rows, partner_rows.shape[0]))
    for copy in copies:
        copy.wait()


def weights_gather(own, for_partner, count, collective_id):
    rows = own.shape[0] + for_partner.shape[0]
    return pl.pallas_call(
        functools.partial(weights_gather_kernel, count),
        out_shape=jax.ShapeDtypeStruct((count, rows) + own.shape[1:], own.dtype),
        in_specs=[pl.BlockSpec(memory_space=pltpu.VMEM)] * 2,
        out_specs=pl.BlockSpec(memory_space=pl.ANY),
        scratch_shapes=[
            pltpu.VMEM(for_partner.shape, for_partner.dtype),
            pltpu.SemaphoreType.DMA((2, count)),
            pltpu.SemaphoreType.DMA((2, count)),
            pltpu.SemaphoreType.DMA((2,)),
            pltpu.SemaphoreType.DMA((2,)),
        ],
        compiler_params=pltpu.CompilerParams(collective_id=collective_id, has_side_effects=True),
    )(own, for_partner)


def exchange_kernel(axis, count, scatter, send_ref, out_ref, landed, send_sems, recv_sems):
    me = lax.axis_index(axis)
    barrier = pltpu.get_barrier_semaphore()
    for step in range(1, count):
        peer = lax.rem(me + step, count)
        pl.semaphore_signal(barrier, inc=1, device_id={axis: peer}, device_id_type=MESH)
    pl.semaphore_wait(barrier, count - 1)
    copies = []
    for step in range(1, count):
        peer = lax.rem(me + step, count)
        source = send_ref.at[peer] if scatter else send_ref
        copy = pltpu.make_async_remote_copy(
            src_ref=source,
            dst_ref=landed.at[me],
            send_sem=send_sems.at[step],
            recv_sem=recv_sems.at[step],
            device_id={axis: peer},
            device_id_type=MESH,
        )
        copy.start()
        copies.append(copy)
    landed[me] = send_ref[me] if scatter else send_ref[...]
    for copy in copies:
        copy.wait()
    if scatter:
        width = landed.shape[-1]
        for source in range(count):
            out_ref[:, source * width:(source + 1) * width] = landed[source]
    else:
        out_ref[...] = landed[...]


def exchange(x, axis, count, scatter, collective_id):
    piece = x.shape[1:] if scatter else x.shape
    result = (piece[0], count * piece[1]) if scatter else (count,) + piece
    return pl.pallas_call(
        functools.partial(exchange_kernel, axis, count, scatter),
        out_shape=jax.ShapeDtypeStruct(result, x.dtype),
        in_specs=[pl.BlockSpec(memory_space=pltpu.VMEM)],
        out_specs=pl.BlockSpec(memory_space=pltpu.VMEM),
        scratch_shapes=[
            pltpu.VMEM((count,) + piece, x.dtype),
            pltpu.SemaphoreType.DMA((count,)),
            pltpu.SemaphoreType.DMA((count,)),
        ],
        compiler_params=pltpu.CompilerParams(collective_id=collective_id, has_side_effects=True),
    )(x)


def on_device(tokens, trainer_panels, panel_home, lengths):
    tp_count = lax.axis_size("tp")
    grp_count = lax.axis_size("grp")
    member_id = lax.axis_index("tp")
    kv_count = (panel_home.shape[0] - tp_count) // 2
    group_size = tp_count // kv_count
    head_dim = trainer_panels.shape[2]
    block_rows = trainer_panels.shape[1]
    half_rows = block_rows // 2
    seq_total = tokens.shape[0]

    core = member_id % 2
    partner_perm = [(i, i ^ 1) for i in range(tp_count)]
    all_halves = chip_ring_gather(trainer_panels, tp_count // 2, 2)
    all_halves = all_halves.reshape((-1,) + all_halves.shape[2:])
    kv_id = member_id // group_size
    quarter = member_id % group_size
    kv_panel = tp_count + kv_id + kv_count * (quarter // 2)
    half = core
    partner_id = member_id ^ 1
    q_mine = all_halves[panel_home[member_id]]
    kv_half = all_halves[panel_home[kv_panel]]
    for_partner = all_halves[panel_home[partner_id]]
    gathered = weights_gather(jnp.concatenate([q_mine, kv_half], axis=0), for_partner, grp_count, 0)
    q_here = gathered[:, :half_rows]
    kv_weights = gathered[:, half_rows:block_rows]
    q_there = gathered[:, block_rows:]
    q_weights = jnp.where(
        core == 0,
        jnp.concatenate([q_here, q_there], axis=1),
        jnp.concatenate([q_there, q_here], axis=1),
    ).reshape(grp_count * block_rows, head_dim)

    use_half = lax.broadcasted_iota(jnp.int32, (1, 2, 1, 1), 1) == half
    kv_rows = jnp.where(use_half, kv_weights[:, None], jnp.zeros_like(kv_weights[:, None]))
    both_weights = jnp.concatenate(
        [q_weights, kv_rows.reshape(grp_count * block_rows, head_dim)], axis=1
    )
    return tail(tokens, both_weights, lengths, tp_count, 1)


def solution(mesh):
    placed = (P("grp", None), P("tp", "grp", None), P(), P("grp", None))
    return jax.shard_map(
        on_device, mesh=mesh, in_specs=placed, out_specs=P(("grp", "tp"), None), check_vma=False
    )
```

```python
import functools

import jax
import jax.numpy as jnp
from jax import lax
from jax.experimental import pallas as pl
from jax.experimental.pallas import tpu as pltpu
from jax.sharding import PartitionSpec as P

MESH = pl.DeviceIdType.MESH


def ring_kernel(count, stride, chunks, send_ref, out_ref, landed, send_sems, recv_sems):
    me = lax.axis_index("tp")
    total = count * stride
    right, left = lax.rem(me + stride, total), lax.rem(me + total - stride, total)
    spot = me // stride
    barrier = pltpu.get_barrier_semaphore()
    for neighbour in (left, right):
        pl.semaphore_signal(barrier, inc=1, device_id={"tp": neighbour}, device_id_type=MESH)
    pl.semaphore_wait(barrier, 2)

    def incoming(origin, chunk):
        return pltpu.make_async_remote_copy(
            src_ref=send_ref.at[chunk],
            dst_ref=landed.at[origin, chunk],
            send_sem=send_sems.at[0, 0, 0],
            recv_sem=recv_sems.at[origin, chunk],
            device_id={"tp": right},
            device_id_type=MESH,
        )

    landed[spot] = send_ref[...]
    sends = []
    far_right, far_left = count // 2, (count - 1) // 2
    for step in range(1, far_right + 1):
        for chunk in range(chunks):
            streams = [(0, right, lax.rem(spot + count - (step - 1), count))]
            if step <= far_left:
                streams.append((1, left, lax.rem(spot + step - 1, count)))
            for way, target, origin in streams:
                if step > 1:
                    incoming(origin, chunk).wait_recv()
                source = send_ref.at[chunk] if step == 1 else landed.at[origin, chunk]
                copy = pltpu.make_async_remote_copy(
                    src_ref=source,
                    dst_ref=landed.at[origin, chunk],
                    send_sem=send_sems.at[way, step, chunk],
                    recv_sem=recv_sems.at[origin, chunk],
                    device_id={"tp": target},
                    device_id_type=MESH,
                )
                copy.start()
                sends.append(copy)
    for chunk in range(chunks):
        incoming(lax.rem(spot + count - far_right, count), chunk).wait_recv()
        incoming(lax.rem(spot + far_left, count), chunk).wait_recv()
    for copy in sends:
        copy.wait_send()
    out_ref[...] = landed[...]


def ring_gather(x, count, stride, chunks, collective_id):
    x = x.reshape((chunks, x.shape[0] // chunks) + x.shape[1:])
    gathered = pl.pallas_call(
        functools.partial(ring_kernel, count, stride, chunks),
        out_shape=jax.ShapeDtypeStruct((count,) + x.shape, x.dtype),
        in_specs=[pl.BlockSpec(memory_space=pltpu.VMEM)],
        out_specs=pl.BlockSpec(memory_space=pltpu.VMEM),
        scratch_shapes=[
            pltpu.VMEM((count,) + x.shape, x.dtype),
            pltpu.SemaphoreType.DMA((2, count // 2 + 1, chunks)),
            pltpu.SemaphoreType.DMA((count, chunks)),
        ],
        compiler_params=pltpu.CompilerParams(collective_id=collective_id, has_side_effects=True),
    )(x)
    return gathered.reshape((count * x.shape[0] * x.shape[1],) + x.shape[2:])


def chip_ring_kernel(count, panels_ref, out_ref, landed, send_sems, recv_sems):
    me = lax.axis_index("tp")
    total = 2 * count
    core = me % 2
    partner = me + 1 - 2 * core
    right, left = lax.rem(me + 2, total), lax.rem(me + total - 2, total)
    spot = me // 2
    half = panels_ref.shape[1] // 2
    barrier = pltpu.get_barrier_semaphore()
    for neighbour in (left, right, partner):
        pl.semaphore_signal(barrier, inc=1, device_id={"tp": neighbour}, device_id_type=MESH)
    pl.semaphore_wait(barrier, 3)

    def rows_of(slot, which):
        return panels_ref.at[slot, pl.ds(pl.multiple_of(which * half, 16), half)]

    def incoming(origin, chunk):
        return pltpu.make_async_remote_copy(
            src_ref=rows_of(0, 0),
            dst_ref=landed.at[origin, chunk],
            send_sem=send_sems.at[0, 0, 0],
            recv_sem=recv_sems.at[origin, chunk],
            device_id={"tp": right},
            device_id_type=MESH,
        )

    sends = []

    def send(source, origin, chunk, sem, target):
        copy = pltpu.make_async_remote_copy(
            src_ref=source,
            dst_ref=landed.at[origin, chunk],
            send_sem=sem,
            recv_sem=recv_sems.at[origin, chunk],
            device_id={"tp": target},
            device_id_type=MESH,
        )
        copy.start()
        sends.append(copy)

    own = [2 * core + j for j in range(2)]
    theirs = [2 * (1 - core) + j for j in range(2)]
    for j in range(2):
        send(rows_of(j, 1 - core), spot, own[j], send_sems.at[0, 0, 1 + j], partner)
        landed[spot, own[j]] = rows_of(j, core)[...]
    far_right, far_left = count // 2, (count - 1) // 2
    first = [(rows_of(j, core), own[j]) for j in range(2)] + [(None, theirs[j]) for j in range(2)]
    for position, (source, chunk) in enumerate(first):
        if source is None:
            incoming(spot, chunk).wait_recv()
            source = landed.at[spot, chunk]
        send(source, spot, chunk, send_sems.at[0, 1, position], right)
        if far_left >= 1:
            send(source, spot, chunk, send_sems.at[1, 1, position], left)
    for step in range(2, far_right + 1):
        for chunk in range(4):
            streams = [(0, right, lax.rem(spot + count - (step - 1), count))]
            if step <= far_left:
                streams.append((1, left, lax.rem(spot + step - 1, count)))
            for way, target, origin in streams:
                incoming(origin, chunk).wait_recv()
                send(landed.at[origin, chunk], origin, chunk, send_sems.at[way, step, chunk], target)
    for chunk in range(4):
        incoming(lax.rem(spot + count - far_right, count), chunk).wait_recv()
        incoming(lax.rem(spot + far_left, count), chunk).wait_recv()
    for copy in sends:
        copy.wait_send()
    out_ref[...] = landed[...]


def chip_ring_gather(panels, count, collective_id):
    slots, rows, width = panels.shape
    return pl.pallas_call(
        functools.partial(chip_ring_kernel, count),
        out_shape=jax.ShapeDtypeStruct((count, 2 * slots, rows // 2, width), panels.dtype),
        in_specs=[pl.BlockSpec(memory_space=pltpu.VMEM)],
        out_specs=pl.BlockSpec(memory_space=pltpu.VMEM),
        scratch_shapes=[
            pltpu.VMEM((count, 2 * slots, rows // 2, width), panels.dtype),
            pltpu.SemaphoreType.DMA((2, count // 2 + 1, 2 * slots)),
            pltpu.SemaphoreType.DMA((count, 2 * slots)),
        ],
        compiler_params=pltpu.CompilerParams(collective_id=collective_id, has_side_effects=True),
    )(panels)


def kv_share_kernel(part_ref, out_ref, partner_part, mine, theirs, send_sems, recv_sems):
    me = lax.axis_index("tp")
    partner = me + 1 - 2 * (me % 2)
    across = me + 2 - 4 * ((me // 2) % 2)
    barrier = pltpu.get_barrier_semaphore()
    for neighbour in (partner, across):
        pl.semaphore_signal(barrier, inc=1, device_id={"tp": neighbour}, device_id_type=MESH)
    pl.semaphore_wait(barrier, 2)
    first = pltpu.make_async_remote_copy(
        src_ref=part_ref, dst_ref=partner_part, send_sem=send_sems.at[0], recv_sem=recv_sems.at[0],
        device_id={"tp": partner}, device_id_type=MESH,
    )
    first.start()
    first.wait()
    mine[...] = (part_ref[...] + partner_part[...]).astype(mine.dtype)
    second = pltpu.make_async_remote_copy(
        src_ref=mine, dst_ref=theirs, send_sem=send_sems.at[1], recv_sem=recv_sems.at[1],
        device_id={"tp": across}, device_id_type=MESH,
    )
    second.start()
    second.wait()
    holds_k = (me % 4) < 2
    out_ref[0] = jnp.where(holds_k, mine[...], theirs[...])
    out_ref[1] = jnp.where(holds_k, theirs[...], mine[...])


def kv_share(part, collective_id):
    return pl.pallas_call(
        kv_share_kernel,
        out_shape=jax.ShapeDtypeStruct((2,) + part.shape, jnp.bfloat16),
        in_specs=[pl.BlockSpec(memory_space=pltpu.VMEM)],
        out_specs=pl.BlockSpec(memory_space=pltpu.VMEM),
        scratch_shapes=[
            pltpu.VMEM(part.shape, part.dtype),
            pltpu.VMEM(part.shape, jnp.bfloat16),
            pltpu.VMEM(part.shape, jnp.bfloat16),
            pltpu.SemaphoreType.DMA((2,)),
            pltpu.SemaphoreType.DMA((2,)),
        ],
        compiler_params=pltpu.CompilerParams(collective_id=collective_id, has_side_effects=True),
    )(part)


def tail_kernel(count, scale, tokens_ref, gathered_hbm, lengths_ref, out_ref,
                gathered, load_sem, part_ref, partner_part, mine, theirs, staged, landed, send_sems, recv_sems):
    width = landed.shape[-1]
    me = lax.axis_index("tp")
    partner = me + 1 - 2 * (me % 2)
    across = me + 2 - 4 * ((me // 2) % 2)
    load = pltpu.make_async_copy(gathered_hbm, gathered, load_sem)
    load.start()
    barrier = pltpu.get_barrier_semaphore()
    for step in range(1, count):
        peer = lax.rem(me + step, count)
        pl.semaphore_signal(barrier, inc=1, device_id={"tp": peer}, device_id_type=MESH)
    load.wait()
    core = me % 2
    half = gathered.shape[1] // 3
    sources = gathered.shape[0]
    first_half = core == 0
    projected = jnp.zeros((tokens_ref.shape[0], 2 * width), jnp.float32)
    for pair in range(sources // 2):
        q_parts, kv_parts = [], []
        for source in (2 * pair, 2 * pair + 1):
            here = gathered[source, 0:half]
            kv = gathered[source, half:2 * half]
            there = gathered[source, 2 * half:3 * half]
            zero = jnp.zeros_like(kv)
            q_parts.append(jnp.where(first_half, jnp.concatenate([here, there], axis=0),
                                     jnp.concatenate([there, here], axis=0)))
            kv_parts.append(jnp.where(first_half, jnp.concatenate([kv, zero], axis=0),
                                      jnp.concatenate([zero, kv], axis=0)))
        slab = jnp.concatenate(
            [jnp.concatenate(q_parts, axis=0), jnp.concatenate(kv_parts, axis=0)], axis=1
        )
        columns = slab.shape[0]
        projected = projected + jnp.dot(
            tokens_ref[:, pair * columns:(pair + 1) * columns], slab, preferred_element_type=jnp.float32
        )
    part_ref[...] = projected[:, width:]
    query = projected[:, :width].astype(jnp.bfloat16)
    pl.semaphore_wait(barrier, count - 1)
    first = pltpu.make_async_remote_copy(
        src_ref=part_ref, dst_ref=partner_part, send_sem=send_sems.at[0], recv_sem=recv_sems.at[0],
        device_id={"tp": partner}, device_id_type=MESH,
    )
    first.start()
    first.wait()
    mine[...] = (part_ref[...] + partner_part[...]).astype(mine.dtype)
    second = pltpu.make_async_remote_copy(
        src_ref=mine, dst_ref=theirs, send_sem=send_sems.at[1], recv_sem=recv_sems.at[1],
        device_id={"tp": across}, device_id_type=MESH,
    )
    second.start()
    second.wait()
    holds_k = (me % 4) < 2
    keys = jnp.where(holds_k, mine[...], theirs[...])
    values = jnp.where(holds_k, theirs[...], mine[...])

    scores = lax.dot_general(
        query, keys, (((1,), (1,)), ((), ())), preferred_element_type=jnp.float32
    ) * scale
    seq = scores.shape[0]
    row = lax.broadcasted_iota(jnp.int32, (seq, seq), 0)
    col = lax.broadcasted_iota(jnp.int32, (seq, seq), 1)
    row_segment = jnp.zeros((seq, seq), jnp.int32)
    col_segment = jnp.zeros((seq, seq), jnp.int32)
    bound = lengths_ref[0, 0] * 0
    for response in range(lengths_ref.shape[1]):
        bound = bound + lengths_ref[0, response]
        row_segment = row_segment + (row >= bound).astype(jnp.int32)
        col_segment = col_segment + (col >= bound).astype(jnp.int32)
    allowed = (row_segment == col_segment) & (col <= row)
    masked = jnp.where(allowed, scores, -jnp.inf)
    peak = jnp.max(masked, axis=1, keepdims=True)
    weights = jnp.exp(masked - peak)
    probs = (weights / jnp.sum(weights, axis=1, keepdims=True)).astype(jnp.bfloat16)
    context = jnp.dot(probs, values, preferred_element_type=jnp.float32)
    rows = seq // count
    for target in range(count):
        staged[target] = context[target * rows:(target + 1) * rows]

    copies = []
    for step in range(1, count):
        peer = lax.rem(me + step, count)
        copy = pltpu.make_async_remote_copy(
            src_ref=staged.at[peer],
            dst_ref=landed.at[me],
            send_sem=send_sems.at[1 + step],
            recv_sem=recv_sems.at[1 + step],
            device_id={"tp": peer},
            device_id_type=MESH,
        )
        copy.start()
        copies.append(copy)
    landed[me] = staged[me]
    for copy in copies:
        copy.wait()
    for source in range(count):
        out_ref[:, source * width:(source + 1) * width] = landed[source]


def tail(tokens, gathered, lengths, count, collective_id):
    seq, width = tokens.shape[0], gathered.shape[2]
    part = jax.ShapeDtypeStruct((seq, width), jnp.float32)
    rows = seq // count
    vmem = pl.BlockSpec(memory_space=pltpu.VMEM)
    return pl.pallas_call(
        functools.partial(tail_kernel, count, width ** (-0.5)),
        out_shape=jax.ShapeDtypeStruct((rows, count * width), jnp.float32),
        in_specs=[vmem, pl.BlockSpec(memory_space=pl.ANY), pl.BlockSpec(memory_space=pltpu.SMEM)],
        out_specs=vmem,
        scratch_shapes=[
            pltpu.VMEM(gathered.shape, gathered.dtype),
            pltpu.SemaphoreType.DMA(()),
            pltpu.VMEM(part.shape, part.dtype),
            pltpu.VMEM(part.shape, part.dtype),
            pltpu.VMEM(part.shape, jnp.bfloat16),
            pltpu.VMEM(part.shape, jnp.bfloat16),
            pltpu.VMEM((count, rows, width), jnp.float32),
            pltpu.VMEM((count, rows, width), jnp.float32),
            pltpu.SemaphoreType.DMA((count + 1,)),
            pltpu.SemaphoreType.DMA((count + 1,)),
        ],
        compiler_params=pltpu.CompilerParams(collective_id=collective_id, has_side_effects=True),
    )(tokens, gathered, lengths)


def grid_kernel(width, send_ref, out_ref, landed, send_sems, recv_sems):
    me = lax.axis_index("grp")
    core = lax.axis_index("tp") % 2
    col, row = me % width, me // width

    def node(c, r):
        return lax.rem(r + width, width) * width + lax.rem(c + width, width)

    def along(dim, c, r, k):
        return node(c + k, r) if dim == 0 else node(c, r + k)

    barrier = pltpu.get_barrier_semaphore()
    neighbours = [node(col + 1, row), node(col - 1, row), node(col, row + 1), node(col, row - 1)]
    for neighbour in neighbours:
        pl.semaphore_signal(barrier, inc=1, device_id={"grp": neighbour}, device_id_type=MESH)
    pl.semaphore_wait(barrier, 4)

    landed[me] = send_ref[...]
    sends = []

    def send(source, origin, half, target):
        copy = pltpu.make_async_remote_copy(
            src_ref=source,
            dst_ref=landed.at[origin, half],
            send_sem=send_sems.at[len(sends)],
            recv_sem=recv_sems.at[origin, half],
            device_id={"grp": target},
            device_id_type=MESH,
        )
        copy.start()
        sends.append(copy)

    def arrive(origin, half):
        pltpu.make_async_remote_copy(
            src_ref=send_ref.at[half],
            dst_ref=landed.at[origin, half],
            send_sem=send_sems.at[0],
            recv_sem=recv_sems.at[origin, half],
            device_id={"grp": neighbours[0]},
            device_id_type=MESH,
        ).wait_recv()

    ahead = 1 - 2 * core

    def phase(lines, half, dim):
        for k in (1, -1):
            for line in lines:
                origin = along(1 - dim, col, row, line)
                source = send_ref.at[half] if line == 0 else landed.at[origin, half]
                send(source, origin, half, along(dim, col, row, k))
        for line in lines:
            for k in (1, -1):
                arrive(along(dim, along(1 - dim, col, row, line) % width, along(1 - dim, col, row, line) // width, k), half)
        for line in lines:
            base = along(1 - dim, col, row, line)
            bc, br = base % width, base // width
            send(landed.at[along(dim, bc, br, -ahead), half], along(dim, bc, br, -ahead), half,
                 along(dim, col, row, ahead))
        for line in lines:
            base = along(1 - dim, col, row, line)
            arrive(along(dim, base % width, base // width, 2), half)

    phase([0], 0, 0)
    phase([0], 1, 1)
    phase([0, 1, -1, 2], 0, 1)
    phase([0, 1, -1, 2], 1, 0)
    for copy in sends:
        copy.wait_send()
    out_ref[...] = landed[...]


def grid_gather(x, width, collective_id):
    count = width * width
    x = x.reshape((2, x.shape[0] // 2) + x.shape[1:])
    gathered = pl.pallas_call(
        functools.partial(grid_kernel, width),
        out_shape=jax.ShapeDtypeStruct((count,) + x.shape, x.dtype),
        in_specs=[pl.BlockSpec(memory_space=pltpu.VMEM)],
        out_specs=pl.BlockSpec(memory_space=pltpu.VMEM),
        scratch_shapes=[
            pltpu.VMEM((count,) + x.shape, x.dtype),
            pltpu.SemaphoreType.DMA((2 * (count - 1),)),
            pltpu.SemaphoreType.DMA((count, 2)),
        ],
        compiler_params=pltpu.CompilerParams(collective_id=collective_id, has_side_effects=True),
    )(x)
    return gathered.reshape((count, x.shape[0] * x.shape[1]) + x.shape[2:])


def gather_hbm_kernel(axis, count, send_ref, out_ref, send_sems, recv_sems, local_sem):
    me = lax.axis_index(axis)
    barrier = pltpu.get_barrier_semaphore()
    for step in range(1, count):
        peer = lax.rem(me + step, count)
        pl.semaphore_signal(barrier, inc=1, device_id={axis: peer}, device_id_type=MESH)
    pl.semaphore_wait(barrier, count - 1)
    copies = []
    for step in range(1, count):
        peer = lax.rem(me + step, count)
        copy = pltpu.make_async_remote_copy(
            src_ref=send_ref,
            dst_ref=out_ref.at[me],
            send_sem=send_sems.at[step],
            recv_sem=recv_sems.at[step],
            device_id={axis: peer},
            device_id_type=MESH,
        )
        copy.start()
        copies.append(copy)
    local = pltpu.make_async_copy(send_ref, out_ref.at[me], local_sem)
    local.start()
    for copy in copies:
        copy.wait()
    local.wait()


def gather_hbm(x, axis, count, collective_id):
    return pl.pallas_call(
        functools.partial(gather_hbm_kernel, axis, count),
        out_shape=jax.ShapeDtypeStruct((count,) + x.shape, x.dtype),
        in_specs=[pl.BlockSpec(memory_space=pltpu.VMEM)],
        out_specs=pl.BlockSpec(memory_space=pl.ANY),
        scratch_shapes=[
            pltpu.SemaphoreType.DMA((count,)),
            pltpu.SemaphoreType.DMA((count,)),
            pltpu.SemaphoreType.DMA(()),
        ],
        compiler_params=pltpu.CompilerParams(collective_id=collective_id, has_side_effects=True),
    )(x)


def weights_gather_kernel(count, own_ref, for_partner_ref, out_ref, partner_rows,
                          send_sems, recv_sems, partner_sems, local_sems):
    me = lax.axis_index("grp")
    member = lax.axis_index("tp")
    partner = member + 1 - 2 * (member % 2)
    rows = own_ref.shape[0]
    barrier = pltpu.get_barrier_semaphore()
    pl.semaphore_signal(barrier, inc=1, device_id={"tp": partner}, device_id_type=MESH)
    for step in range(1, count):
        peer = lax.rem(me + step, count)
        pl.semaphore_signal(barrier, inc=1, device_id={"grp": peer}, device_id_type=MESH)
    pl.semaphore_wait(barrier, count)
    to_partner = pltpu.make_async_remote_copy(
        src_ref=for_partner_ref, dst_ref=partner_rows, send_sem=partner_sems.at[0],
        recv_sem=partner_sems.at[1], device_id={"tp": partner}, device_id_type=MESH,
    )
    to_partner.start()
    copies = []

    def spread(part, source, window):
        for step in range(1, count):
            peer = lax.rem(me + step, count)
            copy = pltpu.make_async_remote_copy(
                src_ref=source,
                dst_ref=out_ref.at[me, window],
                send_sem=send_sems.at[part, step],
                recv_sem=recv_sems.at[part, step],
                device_id={"grp": peer},
                device_id_type=MESH,
            )
            copy.start()
            copies.append(copy)
        local = pltpu.make_async_copy(source, out_ref.at[me, window], local_sems.at[part])
        local.start()
        copies.append(local)

    spread(0, own_ref, pl.ds(0, rows))
    to_partner.wait()
    spread(1, partner_rows, pl.ds(rows, partner_rows.shape[0]))
    for copy in copies:
        copy.wait()


def weights_gather(own, for_partner, count, collective_id):
    rows = own.shape[0] + for_partner.shape[0]
    return pl.pallas_call(
        functools.partial(weights_gather_kernel, count),
        out_shape=jax.ShapeDtypeStruct((count, rows) + own.shape[1:], own.dtype),
        in_specs=[pl.BlockSpec(memory_space=pltpu.VMEM)] * 2,
        out_specs=pl.BlockSpec(memory_space=pl.ANY),
        scratch_shapes=[
            pltpu.VMEM(for_partner.shape, for_partner.dtype),
            pltpu.SemaphoreType.DMA((2, count)),
            pltpu.SemaphoreType.DMA((2, count)),
            pltpu.SemaphoreType.DMA((2,)),
            pltpu.SemaphoreType.DMA((2,)),
        ],
        compiler_params=pltpu.CompilerParams(collective_id=collective_id, has_side_effects=True),
    )(own, for_partner)


def exchange_kernel(axis, count, scatter, send_ref, out_ref, landed, send_sems, recv_sems):
    me = lax.axis_index(axis)
    barrier = pltpu.get_barrier_semaphore()
    for step in range(1, count):
        peer = lax.rem(me + step, count)
        pl.semaphore_signal(barrier, inc=1, device_id={axis: peer}, device_id_type=MESH)
    pl.semaphore_wait(barrier, count - 1)
    copies = []
    for step in range(1, count):
        peer = lax.rem(me + step, count)
        source = send_ref.at[peer] if scatter else send_ref
        copy = pltpu.make_async_remote_copy(
            src_ref=source,
            dst_ref=landed.at[me],
            send_sem=send_sems.at[step],
            recv_sem=recv_sems.at[step],
            device_id={axis: peer},
            device_id_type=MESH,
        )
        copy.start()
        copies.append(copy)
    landed[me] = send_ref[me] if scatter else send_ref[...]
    for copy in copies:
        copy.wait()
    if scatter:
        width = landed.shape[-1]
        for source in range(count):
            out_ref[:, source * width:(source + 1) * width] = landed[source]
    else:
        out_ref[...] = landed[...]


def exchange(x, axis, count, scatter, collective_id):
    piece = x.shape[1:] if scatter else x.shape
    result = (piece[0], count * piece[1]) if scatter else (count,) + piece
    return pl.pallas_call(
        functools.partial(exchange_kernel, axis, count, scatter),
        out_shape=jax.ShapeDtypeStruct(result, x.dtype),
        in_specs=[pl.BlockSpec(memory_space=pltpu.VMEM)],
        out_specs=pl.BlockSpec(memory_space=pltpu.VMEM),
        scratch_shapes=[
            pltpu.VMEM((count,) + piece, x.dtype),
            pltpu.SemaphoreType.DMA((count,)),
            pltpu.SemaphoreType.DMA((count,)),
        ],
        compiler_params=pltpu.CompilerParams(collective_id=collective_id, has_side_effects=True),
    )(x)


def on_device(tokens, trainer_panels, panel_home, lengths):
    tp_count = lax.axis_size("tp")
    grp_count = lax.axis_size("grp")
    member_id = lax.axis_index("tp")
    kv_count = (panel_home.shape[0] - tp_count) // 2
    group_size = tp_count // kv_count
    head_dim = trainer_panels.shape[2]
    block_rows = trainer_panels.shape[1]
    half_rows = block_rows // 2
    seq_total = tokens.shape[0]

    core = member_id % 2
    partner_perm = [(i, i ^ 1) for i in range(tp_count)]
    all_halves = chip_ring_gather(trainer_panels, tp_count // 2, 2)
    all_halves = all_halves.reshape((-1,) + all_halves.shape[2:])
    kv_id = member_id // group_size
    quarter = member_id % group_size
    kv_panel = tp_count + kv_id + kv_count * (quarter // 2)
    half = core
    partner_id = member_id ^ 1
    q_mine = all_halves[panel_home[member_id]]
    kv_half = all_halves[panel_home[kv_panel]]
    for_partner = all_halves[panel_home[partner_id]]
    gathered = weights_gather(jnp.concatenate([q_mine, kv_half], axis=0), for_partner, grp_count, 0)
    return tail(tokens, gathered, lengths, tp_count, 1)


def solution(mesh):
    placed = (P("grp", None), P("tp", "grp", None), P(), P("grp", None))
    return jax.shard_map(
        on_device, mesh=mesh, in_specs=placed, out_specs=P(("grp", "tp"), None), check_vma=False
    )
```

```python
import functools

import jax
import jax.numpy as jnp
from jax import lax
from jax.experimental import pallas as pl
from jax.experimental.pallas import tpu as pltpu
from jax.sharding import PartitionSpec as P

MESH = pl.DeviceIdType.MESH


def ring_kernel(count, stride, chunks, send_ref, out_ref, landed, send_sems, recv_sems):
    me = lax.axis_index("tp")
    total = count * stride
    right, left = lax.rem(me + stride, total), lax.rem(me + total - stride, total)
    spot = me // stride
    barrier = pltpu.get_barrier_semaphore()
    for neighbour in (left, right):
        pl.semaphore_signal(barrier, inc=1, device_id={"tp": neighbour}, device_id_type=MESH)
    pl.semaphore_wait(barrier, 2)

    def incoming(origin, chunk):
        return pltpu.make_async_remote_copy(
            src_ref=send_ref.at[chunk],
            dst_ref=landed.at[origin, chunk],
            send_sem=send_sems.at[0, 0, 0],
            recv_sem=recv_sems.at[origin, chunk],
            device_id={"tp": right},
            device_id_type=MESH,
        )

    landed[spot] = send_ref[...]
    sends = []
    far_right, far_left = count // 2, (count - 1) // 2
    for step in range(1, far_right + 1):
        for chunk in range(chunks):
            streams = [(0, right, lax.rem(spot + count - (step - 1), count))]
            if step <= far_left:
                streams.append((1, left, lax.rem(spot + step - 1, count)))
            for way, target, origin in streams:
                if step > 1:
                    incoming(origin, chunk).wait_recv()
                source = send_ref.at[chunk] if step == 1 else landed.at[origin, chunk]
                copy = pltpu.make_async_remote_copy(
                    src_ref=source,
                    dst_ref=landed.at[origin, chunk],
                    send_sem=send_sems.at[way, step, chunk],
                    recv_sem=recv_sems.at[origin, chunk],
                    device_id={"tp": target},
                    device_id_type=MESH,
                )
                copy.start()
                sends.append(copy)
    for chunk in range(chunks):
        incoming(lax.rem(spot + count - far_right, count), chunk).wait_recv()
        incoming(lax.rem(spot + far_left, count), chunk).wait_recv()
    for copy in sends:
        copy.wait_send()
    out_ref[...] = landed[...]


def ring_gather(x, count, stride, chunks, collective_id):
    x = x.reshape((chunks, x.shape[0] // chunks) + x.shape[1:])
    gathered = pl.pallas_call(
        functools.partial(ring_kernel, count, stride, chunks),
        out_shape=jax.ShapeDtypeStruct((count,) + x.shape, x.dtype),
        in_specs=[pl.BlockSpec(memory_space=pltpu.VMEM)],
        out_specs=pl.BlockSpec(memory_space=pltpu.VMEM),
        scratch_shapes=[
            pltpu.VMEM((count,) + x.shape, x.dtype),
            pltpu.SemaphoreType.DMA((2, count // 2 + 1, chunks)),
            pltpu.SemaphoreType.DMA((count, chunks)),
        ],
        compiler_params=pltpu.CompilerParams(collective_id=collective_id, has_side_effects=True),
    )(x)
    return gathered.reshape((count * x.shape[0] * x.shape[1],) + x.shape[2:])


def chip_ring_kernel(count, panels_ref, home_ref, own_ref, partner_ref, landed, send_sems, recv_sems):
    me = lax.axis_index("tp")
    total = 2 * count
    core = me % 2
    partner = me + 1 - 2 * core
    right, left = lax.rem(me + 2, total), lax.rem(me + total - 2, total)
    spot = me // 2
    half = panels_ref.shape[1] // 2
    barrier = pltpu.get_barrier_semaphore()
    for neighbour in (left, right, partner):
        pl.semaphore_signal(barrier, inc=1, device_id={"tp": neighbour}, device_id_type=MESH)
    pl.semaphore_wait(barrier, 3)

    def rows_of(slot, which):
        return panels_ref.at[slot, pl.ds(pl.multiple_of(which * half, 16), half)]

    def incoming(origin, chunk):
        return pltpu.make_async_remote_copy(
            src_ref=rows_of(0, 0),
            dst_ref=landed.at[origin, chunk],
            send_sem=send_sems.at[0, 0, 0],
            recv_sem=recv_sems.at[origin, chunk],
            device_id={"tp": right},
            device_id_type=MESH,
        )

    sends = []

    def send(source, origin, chunk, sem, target):
        copy = pltpu.make_async_remote_copy(
            src_ref=source,
            dst_ref=landed.at[origin, chunk],
            send_sem=sem,
            recv_sem=recv_sems.at[origin, chunk],
            device_id={"tp": target},
            device_id_type=MESH,
        )
        copy.start()
        sends.append(copy)

    own = [2 * core + j for j in range(2)]
    theirs = [2 * (1 - core) + j for j in range(2)]
    for j in range(2):
        send(rows_of(j, 1 - core), spot, own[j], send_sems.at[0, 0, 1 + j], partner)
        landed[spot, own[j]] = rows_of(j, core)[...]
    far_right, far_left = count // 2, (count - 1) // 2
    first = [(rows_of(j, core), own[j]) for j in range(2)] + [(None, theirs[j]) for j in range(2)]
    for position, (source, chunk) in enumerate(first):
        if source is None:
            incoming(spot, chunk).wait_recv()
            source = landed.at[spot, chunk]
        send(source, spot, chunk, send_sems.at[0, 1, position], right)
        if far_left >= 1:
            send(source, spot, chunk, send_sems.at[1, 1, position], left)
    for step in range(2, far_right + 1):
        for chunk in range(4):
            streams = [(0, right, lax.rem(spot + count - (step - 1), count))]
            if step <= far_left:
                streams.append((1, left, lax.rem(spot + step - 1, count)))
            for way, target, origin in streams:
                incoming(origin, chunk).wait_recv()
                send(landed.at[origin, chunk], origin, chunk, send_sems.at[way, step, chunk], target)
    for chunk in range(4):
        incoming(lax.rem(spot + count - far_right, count), chunk).wait_recv()
        incoming(lax.rem(spot + far_left, count), chunk).wait_recv()
    for copy in sends:
        copy.wait_send()
    heads = total
    kv_heads = (home_ref.shape[0] - heads) // 2
    group = heads // kv_heads
    quarter = me % group
    kv_panel = heads + me // group + kv_heads * (quarter // 2)
    chip_slots = landed.shape[1]

    def block(panel):
        slot = home_ref[panel]
        return landed[slot // chip_slots, slot % chip_slots]

    own_ref[0:half] = block(me)
    own_ref[half:2 * half] = block(kv_panel)
    partner_ref[...] = block(partner)


def chip_ring_gather(panels, home, count, collective_id):
    slots, rows, width = panels.shape
    return pl.pallas_call(
        functools.partial(chip_ring_kernel, count),
        out_shape=(
            jax.ShapeDtypeStruct((rows, width), panels.dtype),
            jax.ShapeDtypeStruct((rows // 2, width), panels.dtype),
        ),
        in_specs=[pl.BlockSpec(memory_space=pltpu.VMEM), pl.BlockSpec(memory_space=pltpu.SMEM)],
        out_specs=(pl.BlockSpec(memory_space=pltpu.VMEM), pl.BlockSpec(memory_space=pltpu.VMEM)),
        scratch_shapes=[
            pltpu.VMEM((count, 2 * slots, rows // 2, width), panels.dtype),
            pltpu.SemaphoreType.DMA((2, count // 2 + 1, 2 * slots)),
            pltpu.SemaphoreType.DMA((count, 2 * slots)),
        ],
        compiler_params=pltpu.CompilerParams(collective_id=collective_id, has_side_effects=True),
    )(panels, home)


def kv_share_kernel(part_ref, out_ref, partner_part, mine, theirs, send_sems, recv_sems):
    me = lax.axis_index("tp")
    partner = me + 1 - 2 * (me % 2)
    across = me + 2 - 4 * ((me // 2) % 2)
    barrier = pltpu.get_barrier_semaphore()
    for neighbour in (partner, across):
        pl.semaphore_signal(barrier, inc=1, device_id={"tp": neighbour}, device_id_type=MESH)
    pl.semaphore_wait(barrier, 2)
    first = pltpu.make_async_remote_copy(
        src_ref=part_ref, dst_ref=partner_part, send_sem=send_sems.at[0], recv_sem=recv_sems.at[0],
        device_id={"tp": partner}, device_id_type=MESH,
    )
    first.start()
    first.wait()
    mine[...] = (part_ref[...] + partner_part[...]).astype(mine.dtype)
    second = pltpu.make_async_remote_copy(
        src_ref=mine, dst_ref=theirs, send_sem=send_sems.at[1], recv_sem=recv_sems.at[1],
        device_id={"tp": across}, device_id_type=MESH,
    )
    second.start()
    second.wait()
    holds_k = (me % 4) < 2
    out_ref[0] = jnp.where(holds_k, mine[...], theirs[...])
    out_ref[1] = jnp.where(holds_k, theirs[...], mine[...])


def kv_share(part, collective_id):
    return pl.pallas_call(
        kv_share_kernel,
        out_shape=jax.ShapeDtypeStruct((2,) + part.shape, jnp.bfloat16),
        in_specs=[pl.BlockSpec(memory_space=pltpu.VMEM)],
        out_specs=pl.BlockSpec(memory_space=pltpu.VMEM),
        scratch_shapes=[
            pltpu.VMEM(part.shape, part.dtype),
            pltpu.VMEM(part.shape, jnp.bfloat16),
            pltpu.VMEM(part.shape, jnp.bfloat16),
            pltpu.SemaphoreType.DMA((2,)),
            pltpu.SemaphoreType.DMA((2,)),
        ],
        compiler_params=pltpu.CompilerParams(collective_id=collective_id, has_side_effects=True),
    )(part)


def tail_kernel(count, scale, tokens_ref, gathered_hbm, lengths_ref, out_ref,
                gathered, load_sem, part_ref, partner_part, mine, theirs, staged, landed, send_sems, recv_sems):
    width = landed.shape[-1]
    me = lax.axis_index("tp")
    partner = me + 1 - 2 * (me % 2)
    across = me + 2 - 4 * ((me // 2) % 2)
    load = pltpu.make_async_copy(gathered_hbm, gathered, load_sem)
    load.start()
    barrier = pltpu.get_barrier_semaphore()
    for step in range(1, count):
        peer = lax.rem(me + step, count)
        pl.semaphore_signal(barrier, inc=1, device_id={"tp": peer}, device_id_type=MESH)
    load.wait()
    core = me % 2
    half = gathered.shape[1] // 3
    sources = gathered.shape[0]
    first_half = core == 0
    projected = jnp.zeros((tokens_ref.shape[0], 2 * width), jnp.float32)
    for pair in range(sources // 2):
        q_parts, kv_parts = [], []
        for source in (2 * pair, 2 * pair + 1):
            here = gathered[source, 0:half]
            kv = gathered[source, half:2 * half]
            there = gathered[source, 2 * half:3 * half]
            zero = jnp.zeros_like(kv)
            q_parts.append(jnp.where(first_half, jnp.concatenate([here, there], axis=0),
                                     jnp.concatenate([there, here], axis=0)))
            kv_parts.append(jnp.where(first_half, jnp.concatenate([kv, zero], axis=0),
                                      jnp.concatenate([zero, kv], axis=0)))
        slab = jnp.concatenate(
            [jnp.concatenate(q_parts, axis=0), jnp.concatenate(kv_parts, axis=0)], axis=1
        )
        columns = slab.shape[0]
        projected = projected + jnp.dot(
            tokens_ref[:, pair * columns:(pair + 1) * columns], slab, preferred_element_type=jnp.float32
        )
    part_ref[...] = projected[:, width:]
    query = projected[:, :width].astype(jnp.bfloat16)
    pl.semaphore_wait(barrier, count - 1)
    first = pltpu.make_async_remote_copy(
        src_ref=part_ref, dst_ref=partner_part, send_sem=send_sems.at[0], recv_sem=recv_sems.at[0],
        device_id={"tp": partner}, device_id_type=MESH,
    )
    first.start()
    first.wait()
    mine[...] = (part_ref[...] + partner_part[...]).astype(mine.dtype)
    second = pltpu.make_async_remote_copy(
        src_ref=mine, dst_ref=theirs, send_sem=send_sems.at[1], recv_sem=recv_sems.at[1],
        device_id={"tp": across}, device_id_type=MESH,
    )
    second.start()
    second.wait()
    holds_k = (me % 4) < 2
    keys = jnp.where(holds_k, mine[...], theirs[...])
    values = jnp.where(holds_k, theirs[...], mine[...])

    scores = lax.dot_general(
        query, keys, (((1,), (1,)), ((), ())), preferred_element_type=jnp.float32
    ) * scale
    seq = scores.shape[0]
    row = lax.broadcasted_iota(jnp.int32, (seq, seq), 0)
    col = lax.broadcasted_iota(jnp.int32, (seq, seq), 1)
    row_segment = jnp.zeros((seq, seq), jnp.int32)
    col_segment = jnp.zeros((seq, seq), jnp.int32)
    bound = lengths_ref[0, 0] * 0
    for response in range(lengths_ref.shape[1]):
        bound = bound + lengths_ref[0, response]
        row_segment = row_segment + (row >= bound).astype(jnp.int32)
        col_segment = col_segment + (col >= bound).astype(jnp.int32)
    allowed = (row_segment == col_segment) & (col <= row)
    masked = jnp.where(allowed, scores, -jnp.inf)
    peak = jnp.max(masked, axis=1, keepdims=True)
    weights = jnp.exp(masked - peak)
    probs = (weights / jnp.sum(weights, axis=1, keepdims=True)).astype(jnp.bfloat16)
    context = jnp.dot(probs, values, preferred_element_type=jnp.float32)
    rows = seq // count
    for target in range(count):
        staged[target] = context[target * rows:(target + 1) * rows]

    copies = []
    for step in range(1, count):
        peer = lax.rem(me + step, count)
        copy = pltpu.make_async_remote_copy(
            src_ref=staged.at[peer],
            dst_ref=landed.at[me],
            send_sem=send_sems.at[1 + step],
            recv_sem=recv_sems.at[1 + step],
            device_id={"tp": peer},
            device_id_type=MESH,
        )
        copy.start()
        copies.append(copy)
    landed[me] = staged[me]
    for copy in copies:
        copy.wait()
    for source in range(count):
        out_ref[:, source * width:(source + 1) * width] = landed[source]


def tail(tokens, gathered, lengths, count, collective_id):
    seq, width = tokens.shape[0], gathered.shape[2]
    part = jax.ShapeDtypeStruct((seq, width), jnp.float32)
    rows = seq // count
    vmem = pl.BlockSpec(memory_space=pltpu.VMEM)
    return pl.pallas_call(
        functools.partial(tail_kernel, count, width ** (-0.5)),
        out_shape=jax.ShapeDtypeStruct((rows, count * width), jnp.float32),
        in_specs=[vmem, pl.BlockSpec(memory_space=pl.ANY), pl.BlockSpec(memory_space=pltpu.SMEM)],
        out_specs=vmem,
        scratch_shapes=[
            pltpu.VMEM(gathered.shape, gathered.dtype),
            pltpu.SemaphoreType.DMA(()),
            pltpu.VMEM(part.shape, part.dtype),
            pltpu.VMEM(part.shape, part.dtype),
            pltpu.VMEM(part.shape, jnp.bfloat16),
            pltpu.VMEM(part.shape, jnp.bfloat16),
            pltpu.VMEM((count, rows, width), jnp.float32),
            pltpu.VMEM((count, rows, width), jnp.float32),
            pltpu.SemaphoreType.DMA((count + 1,)),
            pltpu.SemaphoreType.DMA((count + 1,)),
        ],
        compiler_params=pltpu.CompilerParams(collective_id=collective_id, has_side_effects=True),
    )(tokens, gathered, lengths)


def grid_kernel(width, send_ref, out_ref, landed, send_sems, recv_sems):
    me = lax.axis_index("grp")
    core = lax.axis_index("tp") % 2
    col, row = me % width, me // width

    def node(c, r):
        return lax.rem(r + width, width) * width + lax.rem(c + width, width)

    def along(dim, c, r, k):
        return node(c + k, r) if dim == 0 else node(c, r + k)

    barrier = pltpu.get_barrier_semaphore()
    neighbours = [node(col + 1, row), node(col - 1, row), node(col, row + 1), node(col, row - 1)]
    for neighbour in neighbours:
        pl.semaphore_signal(barrier, inc=1, device_id={"grp": neighbour}, device_id_type=MESH)
    pl.semaphore_wait(barrier, 4)

    landed[me] = send_ref[...]
    sends = []

    def send(source, origin, half, target):
        copy = pltpu.make_async_remote_copy(
            src_ref=source,
            dst_ref=landed.at[origin, half],
            send_sem=send_sems.at[len(sends)],
            recv_sem=recv_sems.at[origin, half],
            device_id={"grp": target},
            device_id_type=MESH,
        )
        copy.start()
        sends.append(copy)

    def arrive(origin, half):
        pltpu.make_async_remote_copy(
            src_ref=send_ref.at[half],
            dst_ref=landed.at[origin, half],
            send_sem=send_sems.at[0],
            recv_sem=recv_sems.at[origin, half],
            device_id={"grp": neighbours[0]},
            device_id_type=MESH,
        ).wait_recv()

    ahead = 1 - 2 * core

    def phase(lines, half, dim):
        for k in (1, -1):
            for line in lines:
                origin = along(1 - dim, col, row, line)
                source = send_ref.at[half] if line == 0 else landed.at[origin, half]
                send(source, origin, half, along(dim, col, row, k))
        for line in lines:
            for k in (1, -1):
                arrive(along(dim, along(1 - dim, col, row, line) % width, along(1 - dim, col, row, line) // width, k), half)
        for line in lines:
            base = along(1 - dim, col, row, line)
            bc, br = base % width, base // width
            send(landed.at[along(dim, bc, br, -ahead), half], along(dim, bc, br, -ahead), half,
                 along(dim, col, row, ahead))
        for line in lines:
            base = along(1 - dim, col, row, line)
            arrive(along(dim, base % width, base // width, 2), half)

    phase([0], 0, 0)
    phase([0], 1, 1)
    phase([0, 1, -1, 2], 0, 1)
    phase([0, 1, -1, 2], 1, 0)
    for copy in sends:
        copy.wait_send()
    out_ref[...] = landed[...]


def grid_gather(x, width, collective_id):
    count = width * width
    x = x.reshape((2, x.shape[0] // 2) + x.shape[1:])
    gathered = pl.pallas_call(
        functools.partial(grid_kernel, width),
        out_shape=jax.ShapeDtypeStruct((count,) + x.shape, x.dtype),
        in_specs=[pl.BlockSpec(memory_space=pltpu.VMEM)],
        out_specs=pl.BlockSpec(memory_space=pltpu.VMEM),
        scratch_shapes=[
            pltpu.VMEM((count,) + x.shape, x.dtype),
            pltpu.SemaphoreType.DMA((2 * (count - 1),)),
            pltpu.SemaphoreType.DMA((count, 2)),
        ],
        compiler_params=pltpu.CompilerParams(collective_id=collective_id, has_side_effects=True),
    )(x)
    return gathered.reshape((count, x.shape[0] * x.shape[1]) + x.shape[2:])


def gather_hbm_kernel(axis, count, send_ref, out_ref, send_sems, recv_sems, local_sem):
    me = lax.axis_index(axis)
    barrier = pltpu.get_barrier_semaphore()
    for step in range(1, count):
        peer = lax.rem(me + step, count)
        pl.semaphore_signal(barrier, inc=1, device_id={axis: peer}, device_id_type=MESH)
    pl.semaphore_wait(barrier, count - 1)
    copies = []
    for step in range(1, count):
        peer = lax.rem(me + step, count)
        copy = pltpu.make_async_remote_copy(
            src_ref=send_ref,
            dst_ref=out_ref.at[me],
            send_sem=send_sems.at[step],
            recv_sem=recv_sems.at[step],
            device_id={axis: peer},
            device_id_type=MESH,
        )
        copy.start()
        copies.append(copy)
    local = pltpu.make_async_copy(send_ref, out_ref.at[me], local_sem)
    local.start()
    for copy in copies:
        copy.wait()
    local.wait()


def gather_hbm(x, axis, count, collective_id):
    return pl.pallas_call(
        functools.partial(gather_hbm_kernel, axis, count),
        out_shape=jax.ShapeDtypeStruct((count,) + x.shape, x.dtype),
        in_specs=[pl.BlockSpec(memory_space=pltpu.VMEM)],
        out_specs=pl.BlockSpec(memory_space=pl.ANY),
        scratch_shapes=[
            pltpu.SemaphoreType.DMA((count,)),
            pltpu.SemaphoreType.DMA((count,)),
            pltpu.SemaphoreType.DMA(()),
        ],
        compiler_params=pltpu.CompilerParams(collective_id=collective_id, has_side_effects=True),
    )(x)


def weights_gather_kernel(count, own_ref, for_partner_ref, out_ref, partner_rows,
                          send_sems, recv_sems, partner_sems, local_sems):
    me = lax.axis_index("grp")
    member = lax.axis_index("tp")
    partner = member + 1 - 2 * (member % 2)
    rows = own_ref.shape[0]
    barrier = pltpu.get_barrier_semaphore()
    pl.semaphore_signal(barrier, inc=1, device_id={"tp": partner}, device_id_type=MESH)
    for step in range(1, count):
        peer = lax.rem(me + step, count)
        pl.semaphore_signal(barrier, inc=1, device_id={"grp": peer}, device_id_type=MESH)
    pl.semaphore_wait(barrier, count)
    to_partner = pltpu.make_async_remote_copy(
        src_ref=for_partner_ref, dst_ref=partner_rows, send_sem=partner_sems.at[0],
        recv_sem=partner_sems.at[1], device_id={"tp": partner}, device_id_type=MESH,
    )
    to_partner.start()
    copies = []

    def spread(part, source, window):
        for step in range(1, count):
            peer = lax.rem(me + step, count)
            copy = pltpu.make_async_remote_copy(
                src_ref=source,
                dst_ref=out_ref.at[me, window],
                send_sem=send_sems.at[part, step],
                recv_sem=recv_sems.at[part, step],
                device_id={"grp": peer},
                device_id_type=MESH,
            )
            copy.start()
            copies.append(copy)
        local = pltpu.make_async_copy(source, out_ref.at[me, window], local_sems.at[part])
        local.start()
        copies.append(local)

    spread(0, own_ref, pl.ds(0, rows))
    to_partner.wait()
    spread(1, partner_rows, pl.ds(rows, partner_rows.shape[0]))
    for copy in copies:
        copy.wait()


def weights_gather(own, for_partner, count, collective_id):
    rows = own.shape[0] + for_partner.shape[0]
    return pl.pallas_call(
        functools.partial(weights_gather_kernel, count),
        out_shape=jax.ShapeDtypeStruct((count, rows) + own.shape[1:], own.dtype),
        in_specs=[pl.BlockSpec(memory_space=pltpu.VMEM)] * 2,
        out_specs=pl.BlockSpec(memory_space=pl.ANY),
        scratch_shapes=[
            pltpu.VMEM(for_partner.shape, for_partner.dtype),
            pltpu.SemaphoreType.DMA((2, count)),
            pltpu.SemaphoreType.DMA((2, count)),
            pltpu.SemaphoreType.DMA((2,)),
            pltpu.SemaphoreType.DMA((2,)),
        ],
        compiler_params=pltpu.CompilerParams(collective_id=collective_id, has_side_effects=True),
    )(own, for_partner)


def exchange_kernel(axis, count, scatter, send_ref, out_ref, landed, send_sems, recv_sems):
    me = lax.axis_index(axis)
    barrier = pltpu.get_barrier_semaphore()
    for step in range(1, count):
        peer = lax.rem(me + step, count)
        pl.semaphore_signal(barrier, inc=1, device_id={axis: peer}, device_id_type=MESH)
    pl.semaphore_wait(barrier, count - 1)
    copies = []
    for step in range(1, count):
        peer = lax.rem(me + step, count)
        source = send_ref.at[peer] if scatter else send_ref
        copy = pltpu.make_async_remote_copy(
            src_ref=source,
            dst_ref=landed.at[me],
            send_sem=send_sems.at[step],
            recv_sem=recv_sems.at[step],
            device_id={axis: peer},
            device_id_type=MESH,
        )
        copy.start()
        copies.append(copy)
    landed[me] = send_ref[me] if scatter else send_ref[...]
    for copy in copies:
        copy.wait()
    if scatter:
        width = landed.shape[-1]
        for source in range(count):
            out_ref[:, source * width:(source + 1) * width] = landed[source]
    else:
        out_ref[...] = landed[...]


def exchange(x, axis, count, scatter, collective_id):
    piece = x.shape[1:] if scatter else x.shape
    result = (piece[0], count * piece[1]) if scatter else (count,) + piece
    return pl.pallas_call(
        functools.partial(exchange_kernel, axis, count, scatter),
        out_shape=jax.ShapeDtypeStruct(result, x.dtype),
        in_specs=[pl.BlockSpec(memory_space=pltpu.VMEM)],
        out_specs=pl.BlockSpec(memory_space=pltpu.VMEM),
        scratch_shapes=[
            pltpu.VMEM((count,) + piece, x.dtype),
            pltpu.SemaphoreType.DMA((count,)),
            pltpu.SemaphoreType.DMA((count,)),
        ],
        compiler_params=pltpu.CompilerParams(collective_id=collective_id, has_side_effects=True),
    )(x)


def on_device(tokens, trainer_panels, panel_home, lengths):
    tp_count = lax.axis_size("tp")
    grp_count = lax.axis_size("grp")
    member_id = lax.axis_index("tp")
    kv_count = (panel_home.shape[0] - tp_count) // 2
    group_size = tp_count // kv_count
    head_dim = trainer_panels.shape[2]
    block_rows = trainer_panels.shape[1]
    half_rows = block_rows // 2
    seq_total = tokens.shape[0]

    own, for_partner = chip_ring_gather(trainer_panels, panel_home, tp_count // 2, 2)
    gathered = weights_gather(own, for_partner, grp_count, 0)
    return tail(tokens, gathered, lengths, tp_count, 1)


def solution(mesh):
    placed = (P("grp", None), P("tp", "grp", None), P(), P("grp", None))
    return jax.shard_map(
        on_device, mesh=mesh, in_specs=placed, out_specs=P(("grp", "tp"), None), check_vma=False
    )
```

```python
import functools

import jax
import jax.numpy as jnp
from jax import lax
from jax.experimental import pallas as pl
from jax.experimental.pallas import tpu as pltpu
from jax.sharding import PartitionSpec as P

MESH = pl.DeviceIdType.MESH


def ring_kernel(count, stride, chunks, send_ref, out_ref, landed, send_sems, recv_sems):
    me = lax.axis_index("tp")
    total = count * stride
    right, left = lax.rem(me + stride, total), lax.rem(me + total - stride, total)
    spot = me // stride
    barrier = pltpu.get_barrier_semaphore()
    for neighbour in (left, right):
        pl.semaphore_signal(barrier, inc=1, device_id={"tp": neighbour}, device_id_type=MESH)
    pl.semaphore_wait(barrier, 2)

    def incoming(origin, chunk):
        return pltpu.make_async_remote_copy(
            src_ref=send_ref.at[chunk],
            dst_ref=landed.at[origin, chunk],
            send_sem=send_sems.at[0, 0, 0],
            recv_sem=recv_sems.at[origin, chunk],
            device_id={"tp": right},
            device_id_type=MESH,
        )

    landed[spot] = send_ref[...]
    sends = []
    far_right, far_left = count // 2, (count - 1) // 2
    for step in range(1, far_right + 1):
        for chunk in range(chunks):
            streams = [(0, right, lax.rem(spot + count - (step - 1), count))]
            if step <= far_left:
                streams.append((1, left, lax.rem(spot + step - 1, count)))
            for way, target, origin in streams:
                if step > 1:
                    incoming(origin, chunk).wait_recv()
                source = send_ref.at[chunk] if step == 1 else landed.at[origin, chunk]
                copy = pltpu.make_async_remote_copy(
                    src_ref=source,
                    dst_ref=landed.at[origin, chunk],
                    send_sem=send_sems.at[way, step, chunk],
                    recv_sem=recv_sems.at[origin, chunk],
                    device_id={"tp": target},
                    device_id_type=MESH,
                )
                copy.start()
                sends.append(copy)
    for chunk in range(chunks):
        incoming(lax.rem(spot + count - far_right, count), chunk).wait_recv()
        incoming(lax.rem(spot + far_left, count), chunk).wait_recv()
    for copy in sends:
        copy.wait_send()
    out_ref[...] = landed[...]


def ring_gather(x, count, stride, chunks, collective_id):
    x = x.reshape((chunks, x.shape[0] // chunks) + x.shape[1:])
    gathered = pl.pallas_call(
        functools.partial(ring_kernel, count, stride, chunks),
        out_shape=jax.ShapeDtypeStruct((count,) + x.shape, x.dtype),
        in_specs=[pl.BlockSpec(memory_space=pltpu.VMEM)],
        out_specs=pl.BlockSpec(memory_space=pltpu.VMEM),
        scratch_shapes=[
            pltpu.VMEM((count,) + x.shape, x.dtype),
            pltpu.SemaphoreType.DMA((2, count // 2 + 1, chunks)),
            pltpu.SemaphoreType.DMA((count, chunks)),
        ],
        compiler_params=pltpu.CompilerParams(collective_id=collective_id, has_side_effects=True),
    )(x)
    return gathered.reshape((count * x.shape[0] * x.shape[1],) + x.shape[2:])


def chip_ring_kernel(count, panels_ref, home_ref, own_ref, partner_ref, landed, send_sems, recv_sems):
    me = lax.axis_index("tp")
    total = 2 * count
    core = me % 2
    partner = me + 1 - 2 * core
    right, left = lax.rem(me + 2, total), lax.rem(me + total - 2, total)
    spot = me // 2
    half = panels_ref.shape[1] // 2
    barrier = pltpu.get_barrier_semaphore()
    for neighbour in (left, right, partner):
        pl.semaphore_signal(barrier, inc=1, device_id={"tp": neighbour}, device_id_type=MESH)
    pl.semaphore_wait(barrier, 3)

    def rows_of(slot, which):
        return panels_ref.at[slot, pl.ds(pl.multiple_of(which * half, 16), half)]

    def incoming(origin, chunk):
        return pltpu.make_async_remote_copy(
            src_ref=rows_of(0, 0),
            dst_ref=landed.at[origin, chunk],
            send_sem=send_sems.at[0, 0, 0],
            recv_sem=recv_sems.at[origin, chunk],
            device_id={"tp": right},
            device_id_type=MESH,
        )

    sends = []

    def send(source, origin, chunk, sem, target):
        copy = pltpu.make_async_remote_copy(
            src_ref=source,
            dst_ref=landed.at[origin, chunk],
            send_sem=sem,
            recv_sem=recv_sems.at[origin, chunk],
            device_id={"tp": target},
            device_id_type=MESH,
        )
        copy.start()
        sends.append(copy)

    own = [2 * core + j for j in range(2)]
    theirs = [2 * (1 - core) + j for j in range(2)]
    for j in range(2):
        send(rows_of(j, 1 - core), spot, own[j], send_sems.at[0, 0, 1 + j], partner)
        landed[spot, own[j]] = rows_of(j, core)[...]
    far_right, far_left = count // 2, (count - 1) // 2
    first = [(rows_of(j, core), own[j]) for j in range(2)] + [(None, theirs[j]) for j in range(2)]
    for position, (source, chunk) in enumerate(first):
        if source is None:
            incoming(spot, chunk).wait_recv()
            source = landed.at[spot, chunk]
        send(source, spot, chunk, send_sems.at[0, 1, position], right)
        if far_left >= 1:
            send(source, spot, chunk, send_sems.at[1, 1, position], left)
    for step in range(2, far_right + 1):
        for chunk in range(4):
            streams = [(0, right, lax.rem(spot + count - (step - 1), count))]
            if step <= far_left:
                streams.append((1, left, lax.rem(spot + step - 1, count)))
            for way, target, origin in streams:
                incoming(origin, chunk).wait_recv()
                send(landed.at[origin, chunk], origin, chunk, send_sems.at[way, step, chunk], target)
    for chunk in range(4):
        incoming(lax.rem(spot + count - far_right, count), chunk).wait_recv()
        incoming(lax.rem(spot + far_left, count), chunk).wait_recv()
    for copy in sends:
        copy.wait_send()
    heads = total
    kv_heads = (home_ref.shape[0] - heads) // 2
    group = heads // kv_heads
    quarter = me % group
    kv_panel = heads + me // group + kv_heads * (quarter // 2)
    chip_slots = landed.shape[1]

    def block(panel):
        slot = home_ref[panel]
        return landed[slot // chip_slots, slot % chip_slots]

    own_ref[0:half] = block(me)
    own_ref[half:2 * half] = block(kv_panel)
    partner_ref[...] = block(partner)


def chip_ring_gather(panels, home, count, collective_id):
    slots, rows, width = panels.shape
    return pl.pallas_call(
        functools.partial(chip_ring_kernel, count),
        out_shape=(
            jax.ShapeDtypeStruct((rows, width), panels.dtype),
            jax.ShapeDtypeStruct((rows // 2, width), panels.dtype),
        ),
        in_specs=[pl.BlockSpec(memory_space=pltpu.VMEM), pl.BlockSpec(memory_space=pltpu.SMEM)],
        out_specs=(pl.BlockSpec(memory_space=pltpu.VMEM), pl.BlockSpec(memory_space=pltpu.VMEM)),
        scratch_shapes=[
            pltpu.VMEM((count, 2 * slots, rows // 2, width), panels.dtype),
            pltpu.SemaphoreType.DMA((2, count // 2 + 1, 2 * slots)),
            pltpu.SemaphoreType.DMA((count, 2 * slots)),
        ],
        compiler_params=pltpu.CompilerParams(collective_id=collective_id, has_side_effects=True),
    )(panels, home)


def kv_share_kernel(part_ref, out_ref, partner_part, mine, theirs, send_sems, recv_sems):
    me = lax.axis_index("tp")
    partner = me + 1 - 2 * (me % 2)
    across = me + 2 - 4 * ((me // 2) % 2)
    barrier = pltpu.get_barrier_semaphore()
    for neighbour in (partner, across):
        pl.semaphore_signal(barrier, inc=1, device_id={"tp": neighbour}, device_id_type=MESH)
    pl.semaphore_wait(barrier, 2)
    first = pltpu.make_async_remote_copy(
        src_ref=part_ref, dst_ref=partner_part, send_sem=send_sems.at[0], recv_sem=recv_sems.at[0],
        device_id={"tp": partner}, device_id_type=MESH,
    )
    first.start()
    first.wait()
    mine[...] = (part_ref[...] + partner_part[...]).astype(mine.dtype)
    second = pltpu.make_async_remote_copy(
        src_ref=mine, dst_ref=theirs, send_sem=send_sems.at[1], recv_sem=recv_sems.at[1],
        device_id={"tp": across}, device_id_type=MESH,
    )
    second.start()
    second.wait()
    holds_k = (me % 4) < 2
    out_ref[0] = jnp.where(holds_k, mine[...], theirs[...])
    out_ref[1] = jnp.where(holds_k, theirs[...], mine[...])


def kv_share(part, collective_id):
    return pl.pallas_call(
        kv_share_kernel,
        out_shape=jax.ShapeDtypeStruct((2,) + part.shape, jnp.bfloat16),
        in_specs=[pl.BlockSpec(memory_space=pltpu.VMEM)],
        out_specs=pl.BlockSpec(memory_space=pltpu.VMEM),
        scratch_shapes=[
            pltpu.VMEM(part.shape, part.dtype),
            pltpu.VMEM(part.shape, jnp.bfloat16),
            pltpu.VMEM(part.shape, jnp.bfloat16),
            pltpu.SemaphoreType.DMA((2,)),
            pltpu.SemaphoreType.DMA((2,)),
        ],
        compiler_params=pltpu.CompilerParams(collective_id=collective_id, has_side_effects=True),
    )(part)


def tail_kernel(count, scale, tokens_ref, gathered_hbm, lengths_ref, out_ref,
                gathered, load_sem, part_ref, partner_part, mine, theirs, staged, landed, send_sems, recv_sems):
    width = landed.shape[-1]
    me = lax.axis_index("tp")
    partner = me + 1 - 2 * (me % 2)
    across = me + 2 - 4 * ((me // 2) % 2)
    load = pltpu.make_async_copy(gathered_hbm, gathered, load_sem)
    load.start()
    barrier = pltpu.get_barrier_semaphore()
    for step in range(1, count):
        peer = lax.rem(me + step, count)
        pl.semaphore_signal(barrier, inc=1, device_id={"tp": peer}, device_id_type=MESH)
    load.wait()
    core = me % 2
    half = gathered.shape[1] // 3
    sources = gathered.shape[0]
    first_half = core == 0
    def project(which):
        total = jnp.zeros((tokens_ref.shape[0], width), jnp.float32)
        for pair in range(sources // 2):
            parts = []
            for source in (2 * pair, 2 * pair + 1):
                here = gathered[source, 0:half]
                kv = gathered[source, half:2 * half]
                there = gathered[source, 2 * half:3 * half]
                if which == "q":
                    parts.append(jnp.where(first_half, jnp.concatenate([here, there], axis=0),
                                           jnp.concatenate([there, here], axis=0)))
                else:
                    zero = jnp.zeros_like(kv)
                    parts.append(jnp.where(first_half, jnp.concatenate([kv, zero], axis=0),
                                           jnp.concatenate([zero, kv], axis=0)))
            slab = jnp.concatenate(parts, axis=0)
            columns = slab.shape[0]
            total = total + jnp.dot(
                tokens_ref[:, pair * columns:(pair + 1) * columns], slab, preferred_element_type=jnp.float32
            )
        return total

    part_ref[...] = project("kv")
    pl.semaphore_wait(barrier, count - 1)
    first = pltpu.make_async_remote_copy(
        src_ref=part_ref, dst_ref=partner_part, send_sem=send_sems.at[0], recv_sem=recv_sems.at[0],
        device_id={"tp": partner}, device_id_type=MESH,
    )
    first.start()
    query = project("q").astype(jnp.bfloat16)
    first.wait()
    mine[...] = (part_ref[...] + partner_part[...]).astype(mine.dtype)
    second = pltpu.make_async_remote_copy(
        src_ref=mine, dst_ref=theirs, send_sem=send_sems.at[1], recv_sem=recv_sems.at[1],
        device_id={"tp": across}, device_id_type=MESH,
    )
    second.start()
    second.wait()
    holds_k = (me % 4) < 2
    keys = jnp.where(holds_k, mine[...], theirs[...])
    values = jnp.where(holds_k, theirs[...], mine[...])

    scores = lax.dot_general(
        query, keys, (((1,), (1,)), ((), ())), preferred_element_type=jnp.float32
    ) * scale
    seq = scores.shape[0]
    row = lax.broadcasted_iota(jnp.int32, (seq, seq), 0)
    col = lax.broadcasted_iota(jnp.int32, (seq, seq), 1)
    row_segment = jnp.zeros((seq, seq), jnp.int32)
    col_segment = jnp.zeros((seq, seq), jnp.int32)
    bound = lengths_ref[0, 0] * 0
    for response in range(lengths_ref.shape[1]):
        bound = bound + lengths_ref[0, response]
        row_segment = row_segment + (row >= bound).astype(jnp.int32)
        col_segment = col_segment + (col >= bound).astype(jnp.int32)
    allowed = (row_segment == col_segment) & (col <= row)
    masked = jnp.where(allowed, scores, -jnp.inf)
    peak = jnp.max(masked, axis=1, keepdims=True)
    weights = jnp.exp(masked - peak)
    probs = (weights / jnp.sum(weights, axis=1, keepdims=True)).astype(jnp.bfloat16)
    context = jnp.dot(probs, values, preferred_element_type=jnp.float32)
    rows = seq // count
    for target in range(count):
        staged[target] = context[target * rows:(target + 1) * rows]

    copies = []
    for step in range(1, count):
        peer = lax.rem(me + step, count)
        copy = pltpu.make_async_remote_copy(
            src_ref=staged.at[peer],
            dst_ref=landed.at[me],
            send_sem=send_sems.at[1 + step],
            recv_sem=recv_sems.at[1 + step],
            device_id={"tp": peer},
            device_id_type=MESH,
        )
        copy.start()
        copies.append(copy)
    landed[me] = staged[me]
    for copy in copies:
        copy.wait()
    for source in range(count):
        out_ref[:, source * width:(source + 1) * width] = landed[source]


def tail(tokens, gathered, lengths, count, collective_id):
    seq, width = tokens.shape[0], gathered.shape[2]
    part = jax.ShapeDtypeStruct((seq, width), jnp.float32)
    rows = seq // count
    vmem = pl.BlockSpec(memory_space=pltpu.VMEM)
    return pl.pallas_call(
        functools.partial(tail_kernel, count, width ** (-0.5)),
        out_shape=jax.ShapeDtypeStruct((rows, count * width), jnp.float32),
        in_specs=[vmem, pl.BlockSpec(memory_space=pl.ANY), pl.BlockSpec(memory_space=pltpu.SMEM)],
        out_specs=vmem,
        scratch_shapes=[
            pltpu.VMEM(gathered.shape, gathered.dtype),
            pltpu.SemaphoreType.DMA(()),
            pltpu.VMEM(part.shape, part.dtype),
            pltpu.VMEM(part.shape, part.dtype),
            pltpu.VMEM(part.shape, jnp.bfloat16),
            pltpu.VMEM(part.shape, jnp.bfloat16),
            pltpu.VMEM((count, rows, width), jnp.float32),
            pltpu.VMEM((count, rows, width), jnp.float32),
            pltpu.SemaphoreType.DMA((count + 1,)),
            pltpu.SemaphoreType.DMA((count + 1,)),
        ],
        compiler_params=pltpu.CompilerParams(collective_id=collective_id, has_side_effects=True),
    )(tokens, gathered, lengths)


def grid_kernel(width, send_ref, out_ref, landed, send_sems, recv_sems):
    me = lax.axis_index("grp")
    core = lax.axis_index("tp") % 2
    col, row = me % width, me // width

    def node(c, r):
        return lax.rem(r + width, width) * width + lax.rem(c + width, width)

    def along(dim, c, r, k):
        return node(c + k, r) if dim == 0 else node(c, r + k)

    barrier = pltpu.get_barrier_semaphore()
    neighbours = [node(col + 1, row), node(col - 1, row), node(col, row + 1), node(col, row - 1)]
    for neighbour in neighbours:
        pl.semaphore_signal(barrier, inc=1, device_id={"grp": neighbour}, device_id_type=MESH)
    pl.semaphore_wait(barrier, 4)

    landed[me] = send_ref[...]
    sends = []

    def send(source, origin, half, target):
        copy = pltpu.make_async_remote_copy(
            src_ref=source,
            dst_ref=landed.at[origin, half],
            send_sem=send_sems.at[len(sends)],
            recv_sem=recv_sems.at[origin, half],
            device_id={"grp": target},
            device_id_type=MESH,
        )
        copy.start()
        sends.append(copy)

    def arrive(origin, half):
        pltpu.make_async_remote_copy(
            src_ref=send_ref.at[half],
            dst_ref=landed.at[origin, half],
            send_sem=send_sems.at[0],
            recv_sem=recv_sems.at[origin, half],
            device_id={"grp": neighbours[0]},
            device_id_type=MESH,
        ).wait_recv()

    ahead = 1 - 2 * core

    def phase(lines, half, dim):
        for k in (1, -1):
            for line in lines:
                origin = along(1 - dim, col, row, line)
                source = send_ref.at[half] if line == 0 else landed.at[origin, half]
                send(source, origin, half, along(dim, col, row, k))
        for line in lines:
            for k in (1, -1):
                arrive(along(dim, along(1 - dim, col, row, line) % width, along(1 - dim, col, row, line) // width, k), half)
        for line in lines:
            base = along(1 - dim, col, row, line)
            bc, br = base % width, base // width
            send(landed.at[along(dim, bc, br, -ahead), half], along(dim, bc, br, -ahead), half,
                 along(dim, col, row, ahead))
        for line in lines:
            base = along(1 - dim, col, row, line)
            arrive(along(dim, base % width, base // width, 2), half)

    phase([0], 0, 0)
    phase([0], 1, 1)
    phase([0, 1, -1, 2], 0, 1)
    phase([0, 1, -1, 2], 1, 0)
    for copy in sends:
        copy.wait_send()
    out_ref[...] = landed[...]


def grid_gather(x, width, collective_id):
    count = width * width
    x = x.reshape((2, x.shape[0] // 2) + x.shape[1:])
    gathered = pl.pallas_call(
        functools.partial(grid_kernel, width),
        out_shape=jax.ShapeDtypeStruct((count,) + x.shape, x.dtype),
        in_specs=[pl.BlockSpec(memory_space=pltpu.VMEM)],
        out_specs=pl.BlockSpec(memory_space=pltpu.VMEM),
        scratch_shapes=[
            pltpu.VMEM((count,) + x.shape, x.dtype),
            pltpu.SemaphoreType.DMA((2 * (count - 1),)),
            pltpu.SemaphoreType.DMA((count, 2)),
        ],
        compiler_params=pltpu.CompilerParams(collective_id=collective_id, has_side_effects=True),
    )(x)
    return gathered.reshape((count, x.shape[0] * x.shape[1]) + x.shape[2:])


def gather_hbm_kernel(axis, count, send_ref, out_ref, send_sems, recv_sems, local_sem):
    me = lax.axis_index(axis)
    barrier = pltpu.get_barrier_semaphore()
    for step in range(1, count):
        peer = lax.rem(me + step, count)
        pl.semaphore_signal(barrier, inc=1, device_id={axis: peer}, device_id_type=MESH)
    pl.semaphore_wait(barrier, count - 1)
    copies = []
    for step in range(1, count):
        peer = lax.rem(me + step, count)
        copy = pltpu.make_async_remote_copy(
            src_ref=send_ref,
            dst_ref=out_ref.at[me],
            send_sem=send_sems.at[step],
            recv_sem=recv_sems.at[step],
            device_id={axis: peer},
            device_id_type=MESH,
        )
        copy.start()
        copies.append(copy)
    local = pltpu.make_async_copy(send_ref, out_ref.at[me], local_sem)
    local.start()
    for copy in copies:
        copy.wait()
    local.wait()


def gather_hbm(x, axis, count, collective_id):
    return pl.pallas_call(
        functools.partial(gather_hbm_kernel, axis, count),
        out_shape=jax.ShapeDtypeStruct((count,) + x.shape, x.dtype),
        in_specs=[pl.BlockSpec(memory_space=pltpu.VMEM)],
        out_specs=pl.BlockSpec(memory_space=pl.ANY),
        scratch_shapes=[
            pltpu.SemaphoreType.DMA((count,)),
            pltpu.SemaphoreType.DMA((count,)),
            pltpu.SemaphoreType.DMA(()),
        ],
        compiler_params=pltpu.CompilerParams(collective_id=collective_id, has_side_effects=True),
    )(x)


def weights_gather_kernel(count, own_ref, for_partner_ref, out_ref, partner_rows,
                          send_sems, recv_sems, partner_sems, local_sems):
    me = lax.axis_index("grp")
    member = lax.axis_index("tp")
    partner = member + 1 - 2 * (member % 2)
    rows = own_ref.shape[0]
    barrier = pltpu.get_barrier_semaphore()
    pl.semaphore_signal(barrier, inc=1, device_id={"tp": partner}, device_id_type=MESH)
    for step in range(1, count):
        peer = lax.rem(me + step, count)
        pl.semaphore_signal(barrier, inc=1, device_id={"grp": peer}, device_id_type=MESH)
    pl.semaphore_wait(barrier, count)
    to_partner = pltpu.make_async_remote_copy(
        src_ref=for_partner_ref, dst_ref=partner_rows, send_sem=partner_sems.at[0],
        recv_sem=partner_sems.at[1], device_id={"tp": partner}, device_id_type=MESH,
    )
    to_partner.start()
    copies = []

    def spread(part, source, window):
        for step in range(1, count):
            peer = lax.rem(me + step, count)
            copy = pltpu.make_async_remote_copy(
                src_ref=source,
                dst_ref=out_ref.at[me, window],
                send_sem=send_sems.at[part, step],
                recv_sem=recv_sems.at[part, step],
                device_id={"grp": peer},
                device_id_type=MESH,
            )
            copy.start()
            copies.append(copy)
        local = pltpu.make_async_copy(source, out_ref.at[me, window], local_sems.at[part])
        local.start()
        copies.append(local)

    spread(0, own_ref, pl.ds(0, rows))
    to_partner.wait()
    spread(1, partner_rows, pl.ds(rows, partner_rows.shape[0]))
    for copy in copies:
        copy.wait()


def weights_gather(own, for_partner, count, collective_id):
    rows = own.shape[0] + for_partner.shape[0]
    return pl.pallas_call(
        functools.partial(weights_gather_kernel, count),
        out_shape=jax.ShapeDtypeStruct((count, rows) + own.shape[1:], own.dtype),
        in_specs=[pl.BlockSpec(memory_space=pltpu.VMEM)] * 2,
        out_specs=pl.BlockSpec(memory_space=pl.ANY),
        scratch_shapes=[
            pltpu.VMEM(for_partner.shape, for_partner.dtype),
            pltpu.SemaphoreType.DMA((2, count)),
            pltpu.SemaphoreType.DMA((2, count)),
            pltpu.SemaphoreType.DMA((2,)),
            pltpu.SemaphoreType.DMA((2,)),
        ],
        compiler_params=pltpu.CompilerParams(collective_id=collective_id, has_side_effects=True),
    )(own, for_partner)


def exchange_kernel(axis, count, scatter, send_ref, out_ref, landed, send_sems, recv_sems):
    me = lax.axis_index(axis)
    barrier = pltpu.get_barrier_semaphore()
    for step in range(1, count):
        peer = lax.rem(me + step, count)
        pl.semaphore_signal(barrier, inc=1, device_id={axis: peer}, device_id_type=MESH)
    pl.semaphore_wait(barrier, count - 1)
    copies = []
    for step in range(1, count):
        peer = lax.rem(me + step, count)
        source = send_ref.at[peer] if scatter else send_ref
        copy = pltpu.make_async_remote_copy(
            src_ref=source,
            dst_ref=landed.at[me],
            send_sem=send_sems.at[step],
            recv_sem=recv_sems.at[step],
            device_id={axis: peer},
            device_id_type=MESH,
        )
        copy.start()
        copies.append(copy)
    landed[me] = send_ref[me] if scatter else send_ref[...]
    for copy in copies:
        copy.wait()
    if scatter:
        width = landed.shape[-1]
        for source in range(count):
            out_ref[:, source * width:(source + 1) * width] = landed[source]
    else:
        out_ref[...] = landed[...]


def exchange(x, axis, count, scatter, collective_id):
    piece = x.shape[1:] if scatter else x.shape
    result = (piece[0], count * piece[1]) if scatter else (count,) + piece
    return pl.pallas_call(
        functools.partial(exchange_kernel, axis, count, scatter),
        out_shape=jax.ShapeDtypeStruct(result, x.dtype),
        in_specs=[pl.BlockSpec(memory_space=pltpu.VMEM)],
        out_specs=pl.BlockSpec(memory_space=pltpu.VMEM),
        scratch_shapes=[
            pltpu.VMEM((count,) + piece, x.dtype),
            pltpu.SemaphoreType.DMA((count,)),
            pltpu.SemaphoreType.DMA((count,)),
        ],
        compiler_params=pltpu.CompilerParams(collective_id=collective_id, has_side_effects=True),
    )(x)


def on_device(tokens, trainer_panels, panel_home, lengths):
    tp_count = lax.axis_size("tp")
    grp_count = lax.axis_size("grp")
    member_id = lax.axis_index("tp")
    kv_count = (panel_home.shape[0] - tp_count) // 2
    group_size = tp_count // kv_count
    head_dim = trainer_panels.shape[2]
    block_rows = trainer_panels.shape[1]
    half_rows = block_rows // 2
    seq_total = tokens.shape[0]

    own, for_partner = chip_ring_gather(trainer_panels, panel_home, tp_count // 2, 2)
    gathered = weights_gather(own, for_partner, grp_count, 0)
    return tail(tokens, gathered, lengths, tp_count, 1)


def solution(mesh):
    placed = (P("grp", None), P("tp", "grp", None), P(), P("grp", None))
    return jax.shard_map(
        on_device, mesh=mesh, in_specs=placed, out_specs=P(("grp", "tp"), None), check_vma=False
    )
```

```python
import functools

import jax
import jax.numpy as jnp
from jax import lax
from jax.experimental import pallas as pl
from jax.experimental.pallas import tpu as pltpu
from jax.sharding import PartitionSpec as P

MESH = pl.DeviceIdType.MESH


def ring_kernel(count, stride, chunks, send_ref, out_ref, landed, send_sems, recv_sems):
    me = lax.axis_index("tp")
    total = count * stride
    right, left = lax.rem(me + stride, total), lax.rem(me + total - stride, total)
    spot = me // stride
    barrier = pltpu.get_barrier_semaphore()
    for neighbour in (left, right):
        pl.semaphore_signal(barrier, inc=1, device_id={"tp": neighbour}, device_id_type=MESH)
    pl.semaphore_wait(barrier, 2)

    def incoming(origin, chunk):
        return pltpu.make_async_remote_copy(
            src_ref=send_ref.at[chunk],
            dst_ref=landed.at[origin, chunk],
            send_sem=send_sems.at[0, 0, 0],
            recv_sem=recv_sems.at[origin, chunk],
            device_id={"tp": right},
            device_id_type=MESH,
        )

    landed[spot] = send_ref[...]
    sends = []
    far_right, far_left = count // 2, (count - 1) // 2
    for step in range(1, far_right + 1):
        for chunk in range(chunks):
            streams = [(0, right, lax.rem(spot + count - (step - 1), count))]
            if step <= far_left:
                streams.append((1, left, lax.rem(spot + step - 1, count)))
            for way, target, origin in streams:
                if step > 1:
                    incoming(origin, chunk).wait_recv()
                source = send_ref.at[chunk] if step == 1 else landed.at[origin, chunk]
                copy = pltpu.make_async_remote_copy(
                    src_ref=source,
                    dst_ref=landed.at[origin, chunk],
                    send_sem=send_sems.at[way, step, chunk],
                    recv_sem=recv_sems.at[origin, chunk],
                    device_id={"tp": target},
                    device_id_type=MESH,
                )
                copy.start()
                sends.append(copy)
    for chunk in range(chunks):
        incoming(lax.rem(spot + count - far_right, count), chunk).wait_recv()
        incoming(lax.rem(spot + far_left, count), chunk).wait_recv()
    for copy in sends:
        copy.wait_send()
    out_ref[...] = landed[...]


def ring_gather(x, count, stride, chunks, collective_id):
    x = x.reshape((chunks, x.shape[0] // chunks) + x.shape[1:])
    gathered = pl.pallas_call(
        functools.partial(ring_kernel, count, stride, chunks),
        out_shape=jax.ShapeDtypeStruct((count,) + x.shape, x.dtype),
        in_specs=[pl.BlockSpec(memory_space=pltpu.VMEM)],
        out_specs=pl.BlockSpec(memory_space=pltpu.VMEM),
        scratch_shapes=[
            pltpu.VMEM((count,) + x.shape, x.dtype),
            pltpu.SemaphoreType.DMA((2, count // 2 + 1, chunks)),
            pltpu.SemaphoreType.DMA((count, chunks)),
        ],
        compiler_params=pltpu.CompilerParams(collective_id=collective_id, has_side_effects=True),
    )(x)
    return gathered.reshape((count * x.shape[0] * x.shape[1],) + x.shape[2:])


def chip_ring_kernel(count, panels_ref, home_ref, own_ref, partner_ref, landed, send_sems, recv_sems):
    me = lax.axis_index("tp")
    total = 2 * count
    core = me % 2
    partner = me + 1 - 2 * core
    right, left = lax.rem(me + 2, total), lax.rem(me + total - 2, total)
    spot = me // 2
    half = panels_ref.shape[1] // 2
    barrier = pltpu.get_barrier_semaphore()
    for neighbour in (left, right, partner):
        pl.semaphore_signal(barrier, inc=1, device_id={"tp": neighbour}, device_id_type=MESH)
    pl.semaphore_wait(barrier, 3)

    def rows_of(slot, which):
        return panels_ref.at[slot, pl.ds(pl.multiple_of(which * half, 16), half)]

    def incoming(origin, chunk):
        return pltpu.make_async_remote_copy(
            src_ref=rows_of(0, 0),
            dst_ref=landed.at[origin, chunk],
            send_sem=send_sems.at[0, 0, 0],
            recv_sem=recv_sems.at[origin, chunk],
            device_id={"tp": right},
            device_id_type=MESH,
        )

    sends = []

    def send(source, origin, chunk, sem, target):
        copy = pltpu.make_async_remote_copy(
            src_ref=source,
            dst_ref=landed.at[origin, chunk],
            send_sem=sem,
            recv_sem=recv_sems.at[origin, chunk],
            device_id={"tp": target},
            device_id_type=MESH,
        )
        copy.start()
        sends.append(copy)

    own = [2 * core + j for j in range(2)]
    theirs = [2 * (1 - core) + j for j in range(2)]
    for j in range(2):
        send(rows_of(j, 1 - core), spot, own[j], send_sems.at[0, 0, 1 + j], partner)
        landed[spot, own[j]] = rows_of(j, core)[...]
    far_right, far_left = count // 2, (count - 1) // 2
    first = [(rows_of(j, core), own[j]) for j in range(2)] + [(None, theirs[j]) for j in range(2)]
    for position, (source, chunk) in enumerate(first):
        if source is None:
            incoming(spot, chunk).wait_recv()
            source = landed.at[spot, chunk]
        send(source, spot, chunk, send_sems.at[0, 1, position], right)
        if far_left >= 1:
            send(source, spot, chunk, send_sems.at[1, 1, position], left)
    for step in range(2, far_right + 1):
        for chunk in range(4):
            streams = [(0, right, lax.rem(spot + count - (step - 1), count))]
            if step <= far_left:
                streams.append((1, left, lax.rem(spot + step - 1, count)))
            for way, target, origin in streams:
                incoming(origin, chunk).wait_recv()
                send(landed.at[origin, chunk], origin, chunk, send_sems.at[way, step, chunk], target)
    for chunk in range(4):
        incoming(lax.rem(spot + count - far_right, count), chunk).wait_recv()
        incoming(lax.rem(spot + far_left, count), chunk).wait_recv()
    for copy in sends:
        copy.wait_send()
    heads = total
    kv_heads = (home_ref.shape[0] - heads) // 2
    group = heads // kv_heads
    quarter = me % group
    kv_panel = heads + me // group + kv_heads * (quarter // 2)
    chip_slots = landed.shape[1]

    def block(panel):
        slot = home_ref[panel]
        return landed[slot // chip_slots, slot % chip_slots]

    own_ref[0:half] = block(me)
    own_ref[half:2 * half] = block(kv_panel)
    partner_ref[...] = block(partner)


def chip_ring_gather(panels, home, count, collective_id):
    slots, rows, width = panels.shape
    return pl.pallas_call(
        functools.partial(chip_ring_kernel, count),
        out_shape=(
            jax.ShapeDtypeStruct((rows, width), panels.dtype),
            jax.ShapeDtypeStruct((rows // 2, width), panels.dtype),
        ),
        in_specs=[pl.BlockSpec(memory_space=pltpu.VMEM), pl.BlockSpec(memory_space=pltpu.SMEM)],
        out_specs=(pl.BlockSpec(memory_space=pltpu.VMEM), pl.BlockSpec(memory_space=pltpu.VMEM)),
        scratch_shapes=[
            pltpu.VMEM((count, 2 * slots, rows // 2, width), panels.dtype),
            pltpu.SemaphoreType.DMA((2, count // 2 + 1, 2 * slots)),
            pltpu.SemaphoreType.DMA((count, 2 * slots)),
        ],
        compiler_params=pltpu.CompilerParams(collective_id=collective_id, has_side_effects=True),
    )(panels, home)


def kv_share_kernel(part_ref, out_ref, partner_part, mine, theirs, send_sems, recv_sems):
    me = lax.axis_index("tp")
    partner = me + 1 - 2 * (me % 2)
    across = me + 2 - 4 * ((me // 2) % 2)
    barrier = pltpu.get_barrier_semaphore()
    for neighbour in (partner, across):
        pl.semaphore_signal(barrier, inc=1, device_id={"tp": neighbour}, device_id_type=MESH)
    pl.semaphore_wait(barrier, 2)
    first = pltpu.make_async_remote_copy(
        src_ref=part_ref, dst_ref=partner_part, send_sem=send_sems.at[0], recv_sem=recv_sems.at[0],
        device_id={"tp": partner}, device_id_type=MESH,
    )
    first.start()
    first.wait()
    mine[...] = (part_ref[...] + partner_part[...]).astype(mine.dtype)
    second = pltpu.make_async_remote_copy(
        src_ref=mine, dst_ref=theirs, send_sem=send_sems.at[1], recv_sem=recv_sems.at[1],
        device_id={"tp": across}, device_id_type=MESH,
    )
    second.start()
    second.wait()
    holds_k = (me % 4) < 2
    out_ref[0] = jnp.where(holds_k, mine[...], theirs[...])
    out_ref[1] = jnp.where(holds_k, theirs[...], mine[...])


def kv_share(part, collective_id):
    return pl.pallas_call(
        kv_share_kernel,
        out_shape=jax.ShapeDtypeStruct((2,) + part.shape, jnp.bfloat16),
        in_specs=[pl.BlockSpec(memory_space=pltpu.VMEM)],
        out_specs=pl.BlockSpec(memory_space=pltpu.VMEM),
        scratch_shapes=[
            pltpu.VMEM(part.shape, part.dtype),
            pltpu.VMEM(part.shape, jnp.bfloat16),
            pltpu.VMEM(part.shape, jnp.bfloat16),
            pltpu.SemaphoreType.DMA((2,)),
            pltpu.SemaphoreType.DMA((2,)),
        ],
        compiler_params=pltpu.CompilerParams(collective_id=collective_id, has_side_effects=True),
    )(part)


def tail_kernel(count, scale, tokens_ref, gathered_hbm, lengths_ref, out_ref,
                gathered, load_sem, part_ref, partner_part, mine, theirs, staged, landed, send_sems, recv_sems):
    width = landed.shape[-1]
    me = lax.axis_index("tp")
    partner = me + 1 - 2 * (me % 2)
    across = me + 2 - 4 * ((me // 2) % 2)
    load = pltpu.make_async_copy(gathered_hbm, gathered, load_sem)
    load.start()
    barrier = pltpu.get_barrier_semaphore()
    for step in range(1, count):
        peer = lax.rem(me + step, count)
        pl.semaphore_signal(barrier, inc=1, device_id={"tp": peer}, device_id_type=MESH)
    load.wait()
    core = me % 2
    half = gathered.shape[1] // 3
    sources = gathered.shape[0]
    first_half = core == 0
    projected = jnp.zeros((tokens_ref.shape[0], 2 * width), jnp.float32)
    for pair in range(sources // 2):
        q_parts, kv_parts = [], []
        for source in (2 * pair, 2 * pair + 1):
            here = gathered[source, 0:half]
            kv = gathered[source, half:2 * half]
            there = gathered[source, 2 * half:3 * half]
            zero = jnp.zeros_like(kv)
            q_parts.append(jnp.where(first_half, jnp.concatenate([here, there], axis=0),
                                     jnp.concatenate([there, here], axis=0)))
            kv_parts.append(jnp.where(first_half, jnp.concatenate([kv, zero], axis=0),
                                      jnp.concatenate([zero, kv], axis=0)))
        slab = jnp.concatenate(
            [jnp.concatenate(q_parts, axis=0), jnp.concatenate(kv_parts, axis=0)], axis=1
        )
        columns = slab.shape[0]
        projected = projected + jnp.dot(
            tokens_ref[:, pair * columns:(pair + 1) * columns], slab, preferred_element_type=jnp.float32
        )
    part_ref[...] = projected[:, width:]
    query = projected[:, :width].astype(jnp.bfloat16)
    pl.semaphore_wait(barrier, count - 1)
    first = pltpu.make_async_remote_copy(
        src_ref=part_ref, dst_ref=partner_part, send_sem=send_sems.at[0], recv_sem=recv_sems.at[0],
        device_id={"tp": partner}, device_id_type=MESH,
    )
    first.start()
    first.wait()
    mine[...] = (part_ref[...] + partner_part[...]).astype(mine.dtype)
    second = pltpu.make_async_remote_copy(
        src_ref=mine, dst_ref=theirs, send_sem=send_sems.at[1], recv_sem=recv_sems.at[1],
        device_id={"tp": across}, device_id_type=MESH,
    )
    second.start()
    second.wait()
    holds_k = (me % 4) < 2
    keys = jnp.where(holds_k, mine[...], theirs[...])
    values = jnp.where(holds_k, theirs[...], mine[...])

    scores = lax.dot_general(
        query, keys, (((1,), (1,)), ((), ())), preferred_element_type=jnp.float32
    ) * scale
    seq = scores.shape[0]
    row = lax.broadcasted_iota(jnp.int32, (seq, seq), 0)
    col = lax.broadcasted_iota(jnp.int32, (seq, seq), 1)
    row_segment = jnp.zeros((seq, seq), jnp.int32)
    col_segment = jnp.zeros((seq, seq), jnp.int32)
    bound = lengths_ref[0, 0] * 0
    for response in range(lengths_ref.shape[1]):
        bound = bound + lengths_ref[0, response]
        row_segment = row_segment + (row >= bound).astype(jnp.int32)
        col_segment = col_segment + (col >= bound).astype(jnp.int32)
    allowed = (row_segment == col_segment) & (col <= row)
    masked = jnp.where(allowed, scores, -jnp.inf)
    peak = jnp.max(masked, axis=1, keepdims=True)
    weights = jnp.exp(masked - peak)
    probs = (weights / jnp.sum(weights, axis=1, keepdims=True)).astype(jnp.bfloat16)
    context = jnp.dot(probs, values, preferred_element_type=jnp.float32)
    rows = seq // count
    for target in range(count):
        staged[target] = context[target * rows:(target + 1) * rows]

    copies = []
    for step in range(1, count):
        peer = lax.rem(me + step, count)
        copy = pltpu.make_async_remote_copy(
            src_ref=staged.at[peer],
            dst_ref=landed.at[me],
            send_sem=send_sems.at[1 + step],
            recv_sem=recv_sems.at[1 + step],
            device_id={"tp": peer},
            device_id_type=MESH,
        )
        copy.start()
        copies.append(copy)
    landed[me] = staged[me]
    for copy in copies:
        copy.wait()
    out_ref[...] = landed[...]


def tail(tokens, gathered, lengths, count, collective_id):
    seq, width = tokens.shape[0], gathered.shape[2]
    part = jax.ShapeDtypeStruct((seq, width), jnp.float32)
    rows = seq // count
    vmem = pl.BlockSpec(memory_space=pltpu.VMEM)
    return pl.pallas_call(
        functools.partial(tail_kernel, count, width ** (-0.5)),
        out_shape=jax.ShapeDtypeStruct((count, rows, width), jnp.float32),
        in_specs=[vmem, pl.BlockSpec(memory_space=pl.ANY), pl.BlockSpec(memory_space=pltpu.SMEM)],
        out_specs=vmem,
        scratch_shapes=[
            pltpu.VMEM(gathered.shape, gathered.dtype),
            pltpu.SemaphoreType.DMA(()),
            pltpu.VMEM(part.shape, part.dtype),
            pltpu.VMEM(part.shape, part.dtype),
            pltpu.VMEM(part.shape, jnp.bfloat16),
            pltpu.VMEM(part.shape, jnp.bfloat16),
            pltpu.VMEM((count, rows, width), jnp.float32),
            pltpu.VMEM((count, rows, width), jnp.float32),
            pltpu.SemaphoreType.DMA((count + 1,)),
            pltpu.SemaphoreType.DMA((count + 1,)),
        ],
        compiler_params=pltpu.CompilerParams(collective_id=collective_id, has_side_effects=True),
    )(tokens, gathered, lengths)


def grid_kernel(width, send_ref, out_ref, landed, send_sems, recv_sems):
    me = lax.axis_index("grp")
    core = lax.axis_index("tp") % 2
    col, row = me % width, me // width

    def node(c, r):
        return lax.rem(r + width, width) * width + lax.rem(c + width, width)

    def along(dim, c, r, k):
        return node(c + k, r) if dim == 0 else node(c, r + k)

    barrier = pltpu.get_barrier_semaphore()
    neighbours = [node(col + 1, row), node(col - 1, row), node(col, row + 1), node(col, row - 1)]
    for neighbour in neighbours:
        pl.semaphore_signal(barrier, inc=1, device_id={"grp": neighbour}, device_id_type=MESH)
    pl.semaphore_wait(barrier, 4)

    landed[me] = send_ref[...]
    sends = []

    def send(source, origin, half, target):
        copy = pltpu.make_async_remote_copy(
            src_ref=source,
            dst_ref=landed.at[origin, half],
            send_sem=send_sems.at[len(sends)],
            recv_sem=recv_sems.at[origin, half],
            device_id={"grp": target},
            device_id_type=MESH,
        )
        copy.start()
        sends.append(copy)

    def arrive(origin, half):
        pltpu.make_async_remote_copy(
            src_ref=send_ref.at[half],
            dst_ref=landed.at[origin, half],
            send_sem=send_sems.at[0],
            recv_sem=recv_sems.at[origin, half],
            device_id={"grp": neighbours[0]},
            device_id_type=MESH,
        ).wait_recv()

    ahead = 1 - 2 * core

    def phase(lines, half, dim):
        for k in (1, -1):
            for line in lines:
                origin = along(1 - dim, col, row, line)
                source = send_ref.at[half] if line == 0 else landed.at[origin, half]
                send(source, origin, half, along(dim, col, row, k))
        for line in lines:
            for k in (1, -1):
                arrive(along(dim, along(1 - dim, col, row, line) % width, along(1 - dim, col, row, line) // width, k), half)
        for line in lines:
            base = along(1 - dim, col, row, line)
            bc, br = base % width, base // width
            send(landed.at[along(dim, bc, br, -ahead), half], along(dim, bc, br, -ahead), half,
                 along(dim, col, row, ahead))
        for line in lines:
            base = along(1 - dim, col, row, line)
            arrive(along(dim, base % width, base // width, 2), half)

    phase([0], 0, 0)
    phase([0], 1, 1)
    phase([0, 1, -1, 2], 0, 1)
    phase([0, 1, -1, 2], 1, 0)
    for copy in sends:
        copy.wait_send()
    out_ref[...] = landed[...]


def grid_gather(x, width, collective_id):
    count = width * width
    x = x.reshape((2, x.shape[0] // 2) + x.shape[1:])
    gathered = pl.pallas_call(
        functools.partial(grid_kernel, width),
        out_shape=jax.ShapeDtypeStruct((count,) + x.shape, x.dtype),
        in_specs=[pl.BlockSpec(memory_space=pltpu.VMEM)],
        out_specs=pl.BlockSpec(memory_space=pltpu.VMEM),
        scratch_shapes=[
            pltpu.VMEM((count,) + x.shape, x.dtype),
            pltpu.SemaphoreType.DMA((2 * (count - 1),)),
            pltpu.SemaphoreType.DMA((count, 2)),
        ],
        compiler_params=pltpu.CompilerParams(collective_id=collective_id, has_side_effects=True),
    )(x)
    return gathered.reshape((count, x.shape[0] * x.shape[1]) + x.shape[2:])


def gather_hbm_kernel(axis, count, send_ref, out_ref, send_sems, recv_sems, local_sem):
    me = lax.axis_index(axis)
    barrier = pltpu.get_barrier_semaphore()
    for step in range(1, count):
        peer = lax.rem(me + step, count)
        pl.semaphore_signal(barrier, inc=1, device_id={axis: peer}, device_id_type=MESH)
    pl.semaphore_wait(barrier, count - 1)
    copies = []
    for step in range(1, count):
        peer = lax.rem(me + step, count)
        copy = pltpu.make_async_remote_copy(
            src_ref=send_ref,
            dst_ref=out_ref.at[me],
            send_sem=send_sems.at[step],
            recv_sem=recv_sems.at[step],
            device_id={axis: peer},
            device_id_type=MESH,
        )
        copy.start()
        copies.append(copy)
    local = pltpu.make_async_copy(send_ref, out_ref.at[me], local_sem)
    local.start()
    for copy in copies:
        copy.wait()
    local.wait()


def gather_hbm(x, axis, count, collective_id):
    return pl.pallas_call(
        functools.partial(gather_hbm_kernel, axis, count),
        out_shape=jax.ShapeDtypeStruct((count,) + x.shape, x.dtype),
        in_specs=[pl.BlockSpec(memory_space=pltpu.VMEM)],
        out_specs=pl.BlockSpec(memory_space=pl.ANY),
        scratch_shapes=[
            pltpu.SemaphoreType.DMA((count,)),
            pltpu.SemaphoreType.DMA((count,)),
            pltpu.SemaphoreType.DMA(()),
        ],
        compiler_params=pltpu.CompilerParams(collective_id=collective_id, has_side_effects=True),
    )(x)


def weights_gather_kernel(count, own_ref, for_partner_ref, out_ref, partner_rows,
                          send_sems, recv_sems, partner_sems, local_sems):
    me = lax.axis_index("grp")
    member = lax.axis_index("tp")
    partner = member + 1 - 2 * (member % 2)
    rows = own_ref.shape[0]
    barrier = pltpu.get_barrier_semaphore()
    pl.semaphore_signal(barrier, inc=1, device_id={"tp": partner}, device_id_type=MESH)
    for step in range(1, count):
        peer = lax.rem(me + step, count)
        pl.semaphore_signal(barrier, inc=1, device_id={"grp": peer}, device_id_type=MESH)
    pl.semaphore_wait(barrier, count)
    to_partner = pltpu.make_async_remote_copy(
        src_ref=for_partner_ref, dst_ref=partner_rows, send_sem=partner_sems.at[0],
        recv_sem=partner_sems.at[1], device_id={"tp": partner}, device_id_type=MESH,
    )
    to_partner.start()
    copies = []

    def spread(part, source, window):
        for step in range(1, count):
            peer = lax.rem(me + step, count)
            copy = pltpu.make_async_remote_copy(
                src_ref=source,
                dst_ref=out_ref.at[me, window],
                send_sem=send_sems.at[part, step],
                recv_sem=recv_sems.at[part, step],
                device_id={"grp": peer},
                device_id_type=MESH,
            )
            copy.start()
            copies.append(copy)
        local = pltpu.make_async_copy(source, out_ref.at[me, window], local_sems.at[part])
        local.start()
        copies.append(local)

    spread(0, own_ref, pl.ds(0, rows))
    to_partner.wait()
    spread(1, partner_rows, pl.ds(rows, partner_rows.shape[0]))
    for copy in copies:
        copy.wait()


def weights_gather(own, for_partner, count, collective_id):
    rows = own.shape[0] + for_partner.shape[0]
    return pl.pallas_call(
        functools.partial(weights_gather_kernel, count),
        out_shape=jax.ShapeDtypeStruct((count, rows) + own.shape[1:], own.dtype),
        in_specs=[pl.BlockSpec(memory_space=pltpu.VMEM)] * 2,
        out_specs=pl.BlockSpec(memory_space=pl.ANY),
        scratch_shapes=[
            pltpu.VMEM(for_partner.shape, for_partner.dtype),
            pltpu.SemaphoreType.DMA((2, count)),
            pltpu.SemaphoreType.DMA((2, count)),
            pltpu.SemaphoreType.DMA((2,)),
            pltpu.SemaphoreType.DMA((2,)),
        ],
        compiler_params=pltpu.CompilerParams(collective_id=collective_id, has_side_effects=True),
    )(own, for_partner)


def exchange_kernel(axis, count, scatter, send_ref, out_ref, landed, send_sems, recv_sems):
    me = lax.axis_index(axis)
    barrier = pltpu.get_barrier_semaphore()
    for step in range(1, count):
        peer = lax.rem(me + step, count)
        pl.semaphore_signal(barrier, inc=1, device_id={axis: peer}, device_id_type=MESH)
    pl.semaphore_wait(barrier, count - 1)
    copies = []
    for step in range(1, count):
        peer = lax.rem(me + step, count)
        source = send_ref.at[peer] if scatter else send_ref
        copy = pltpu.make_async_remote_copy(
            src_ref=source,
            dst_ref=landed.at[me],
            send_sem=send_sems.at[step],
            recv_sem=recv_sems.at[step],
            device_id={axis: peer},
            device_id_type=MESH,
        )
        copy.start()
        copies.append(copy)
    landed[me] = send_ref[me] if scatter else send_ref[...]
    for copy in copies:
        copy.wait()
    if scatter:
        width = landed.shape[-1]
        for source in range(count):
            out_ref[:, source * width:(source + 1) * width] = landed[source]
    else:
        out_ref[...] = landed[...]


def exchange(x, axis, count, scatter, collective_id):
    piece = x.shape[1:] if scatter else x.shape
    result = (piece[0], count * piece[1]) if scatter else (count,) + piece
    return pl.pallas_call(
        functools.partial(exchange_kernel, axis, count, scatter),
        out_shape=jax.ShapeDtypeStruct(result, x.dtype),
        in_specs=[pl.BlockSpec(memory_space=pltpu.VMEM)],
        out_specs=pl.BlockSpec(memory_space=pltpu.VMEM),
        scratch_shapes=[
            pltpu.VMEM((count,) + piece, x.dtype),
            pltpu.SemaphoreType.DMA((count,)),
            pltpu.SemaphoreType.DMA((count,)),
        ],
        compiler_params=pltpu.CompilerParams(collective_id=collective_id, has_side_effects=True),
    )(x)


def on_device(tokens, trainer_panels, panel_home, lengths):
    tp_count = lax.axis_size("tp")
    grp_count = lax.axis_size("grp")
    member_id = lax.axis_index("tp")
    kv_count = (panel_home.shape[0] - tp_count) // 2
    group_size = tp_count // kv_count
    head_dim = trainer_panels.shape[2]
    block_rows = trainer_panels.shape[1]
    half_rows = block_rows // 2
    seq_total = tokens.shape[0]

    own, for_partner = chip_ring_gather(trainer_panels, panel_home, tp_count // 2, 2)
    gathered = weights_gather(own, for_partner, grp_count, 0)
    arrived = tail(tokens, gathered, lengths, tp_count, 1)
    return jnp.transpose(arrived, (1, 0, 2)).reshape(arrived.shape[1], tp_count * head_dim)


def solution(mesh):
    placed = (P("grp", None), P("tp", "grp", None), P(), P("grp", None))
    return jax.shard_map(
        on_device, mesh=mesh, in_specs=placed, out_specs=P(("grp", "tp"), None), check_vma=False
    )
```

```python
import functools

import jax
import jax.numpy as jnp
from jax import lax
from jax.experimental import pallas as pl
from jax.experimental.pallas import tpu as pltpu
from jax.sharding import PartitionSpec as P

MESH = pl.DeviceIdType.MESH


def ring_kernel(count, stride, chunks, send_ref, out_ref, landed, send_sems, recv_sems):
    me = lax.axis_index("tp")
    total = count * stride
    right, left = lax.rem(me + stride, total), lax.rem(me + total - stride, total)
    spot = me // stride
    barrier = pltpu.get_barrier_semaphore()
    for neighbour in (left, right):
        pl.semaphore_signal(barrier, inc=1, device_id={"tp": neighbour}, device_id_type=MESH)
    pl.semaphore_wait(barrier, 2)

    def incoming(origin, chunk):
        return pltpu.make_async_remote_copy(
            src_ref=send_ref.at[chunk],
            dst_ref=landed.at[origin, chunk],
            send_sem=send_sems.at[0, 0, 0],
            recv_sem=recv_sems.at[origin, chunk],
            device_id={"tp": right},
            device_id_type=MESH,
        )

    landed[spot] = send_ref[...]
    sends = []
    far_right, far_left = count // 2, (count - 1) // 2
    for step in range(1, far_right + 1):
        for chunk in range(chunks):
            streams = [(0, right, lax.rem(spot + count - (step - 1), count))]
            if step <= far_left:
                streams.append((1, left, lax.rem(spot + step - 1, count)))
            for way, target, origin in streams:
                if step > 1:
                    incoming(origin, chunk).wait_recv()
                source = send_ref.at[chunk] if step == 1 else landed.at[origin, chunk]
                copy = pltpu.make_async_remote_copy(
                    src_ref=source,
                    dst_ref=landed.at[origin, chunk],
                    send_sem=send_sems.at[way, step, chunk],
                    recv_sem=recv_sems.at[origin, chunk],
                    device_id={"tp": target},
                    device_id_type=MESH,
                )
                copy.start()
                sends.append(copy)
    for chunk in range(chunks):
        incoming(lax.rem(spot + count - far_right, count), chunk).wait_recv()
        incoming(lax.rem(spot + far_left, count), chunk).wait_recv()
    for copy in sends:
        copy.wait_send()
    out_ref[...] = landed[...]


def ring_gather(x, count, stride, chunks, collective_id):
    x = x.reshape((chunks, x.shape[0] // chunks) + x.shape[1:])
    gathered = pl.pallas_call(
        functools.partial(ring_kernel, count, stride, chunks),
        out_shape=jax.ShapeDtypeStruct((count,) + x.shape, x.dtype),
        in_specs=[pl.BlockSpec(memory_space=pltpu.VMEM)],
        out_specs=pl.BlockSpec(memory_space=pltpu.VMEM),
        scratch_shapes=[
            pltpu.VMEM((count,) + x.shape, x.dtype),
            pltpu.SemaphoreType.DMA((2, count // 2 + 1, chunks)),
            pltpu.SemaphoreType.DMA((count, chunks)),
        ],
        compiler_params=pltpu.CompilerParams(collective_id=collective_id, has_side_effects=True),
    )(x)
    return gathered.reshape((count * x.shape[0] * x.shape[1],) + x.shape[2:])


def chip_ring_kernel(count, groups, panels_ref, home_ref, out_ref, landed, send_sems, recv_sems,
                     own_ref, partner_ref, partner_rows, grp_send_sems, grp_recv_sems, partner_sems, local_sems):
    me = lax.axis_index("tp")
    here = lax.axis_index("grp")
    total = 2 * count
    core = me % 2
    partner = me + 1 - 2 * core
    right, left = lax.rem(me + 2, total), lax.rem(me + total - 2, total)
    spot = me // 2
    half = panels_ref.shape[1] // 2
    barrier = pltpu.get_barrier_semaphore()
    for neighbour in (left, right, partner):
        pl.semaphore_signal(barrier, inc=1, device_id={"tp": neighbour}, device_id_type=MESH)
    for step in range(1, groups):
        peer = lax.rem(here + step, groups)
        pl.semaphore_signal(barrier, inc=1, device_id={"grp": peer}, device_id_type=MESH)
    pl.semaphore_wait(barrier, 2 + groups)

    def rows_of(slot, which):
        return panels_ref.at[slot, pl.ds(pl.multiple_of(which * half, 16), half)]

    def incoming(origin, chunk):
        return pltpu.make_async_remote_copy(
            src_ref=rows_of(0, 0),
            dst_ref=landed.at[origin, chunk],
            send_sem=send_sems.at[0, 0, 0],
            recv_sem=recv_sems.at[origin, chunk],
            device_id={"tp": right},
            device_id_type=MESH,
        )

    sends = []

    def send(source, origin, chunk, sem, target):
        copy = pltpu.make_async_remote_copy(
            src_ref=source,
            dst_ref=landed.at[origin, chunk],
            send_sem=sem,
            recv_sem=recv_sems.at[origin, chunk],
            device_id={"tp": target},
            device_id_type=MESH,
        )
        copy.start()
        sends.append(copy)

    own = [2 * core + j for j in range(2)]
    theirs = [2 * (1 - core) + j for j in range(2)]
    for j in range(2):
        send(rows_of(j, 1 - core), spot, own[j], send_sems.at[0, 0, 1 + j], partner)
        landed[spot, own[j]] = rows_of(j, core)[...]
    far_right, far_left = count // 2, (count - 1) // 2
    first = [(rows_of(j, core), own[j]) for j in range(2)] + [(None, theirs[j]) for j in range(2)]
    for position, (source, chunk) in enumerate(first):
        if source is None:
            incoming(spot, chunk).wait_recv()
            source = landed.at[spot, chunk]
        send(source, spot, chunk, send_sems.at[0, 1, position], right)
        if far_left >= 1:
            send(source, spot, chunk, send_sems.at[1, 1, position], left)
    for step in range(2, far_right + 1):
        for chunk in range(4):
            streams = [(0, right, lax.rem(spot + count - (step - 1), count))]
            if step <= far_left:
                streams.append((1, left, lax.rem(spot + step - 1, count)))
            for way, target, origin in streams:
                incoming(origin, chunk).wait_recv()
                send(landed.at[origin, chunk], origin, chunk, send_sems.at[way, step, chunk], target)
    for chunk in range(4):
        incoming(lax.rem(spot + count - far_right, count), chunk).wait_recv()
        incoming(lax.rem(spot + far_left, count), chunk).wait_recv()
    for copy in sends:
        copy.wait_send()
    heads = total
    kv_heads = (home_ref.shape[0] - heads) // 2
    group = heads // kv_heads
    quarter = me % group
    kv_panel = heads + me // group + kv_heads * (quarter // 2)
    chip_slots = landed.shape[1]

    def block(panel):
        slot = home_ref[panel]
        return landed[slot // chip_slots, slot % chip_slots]

    own_ref[0:half] = block(me)
    own_ref[half:2 * half] = block(kv_panel)
    partner_ref[...] = block(partner)

    to_partner = pltpu.make_async_remote_copy(
        src_ref=partner_ref, dst_ref=partner_rows, send_sem=partner_sems.at[0],
        recv_sem=partner_sems.at[1], device_id={"tp": partner}, device_id_type=MESH,
    )
    to_partner.start()
    copies = []

    def spread(part, source, window):
        for step in range(1, groups):
            peer = lax.rem(here + step, groups)
            copy = pltpu.make_async_remote_copy(
                src_ref=source,
                dst_ref=out_ref.at[here, window],
                send_sem=grp_send_sems.at[part, step],
                recv_sem=grp_recv_sems.at[part, step],
                device_id={"grp": peer},
                device_id_type=MESH,
            )
            copy.start()
            copies.append(copy)
        local = pltpu.make_async_copy(source, out_ref.at[here, window], local_sems.at[part])
        local.start()
        copies.append(local)

    spread(0, own_ref, pl.ds(0, 2 * half))
    to_partner.wait()
    spread(1, partner_rows, pl.ds(2 * half, half))
    for copy in copies:
        copy.wait()


def chip_ring_gather(panels, home, count, groups, collective_id):
    slots, rows, width = panels.shape
    return pl.pallas_call(
        functools.partial(chip_ring_kernel, count, groups),
        out_shape=jax.ShapeDtypeStruct((groups, rows + rows // 2, width), panels.dtype),
        in_specs=[pl.BlockSpec(memory_space=pltpu.VMEM), pl.BlockSpec(memory_space=pltpu.SMEM)],
        out_specs=pl.BlockSpec(memory_space=pl.ANY),
        scratch_shapes=[
            pltpu.VMEM((count, 2 * slots, rows // 2, width), panels.dtype),
            pltpu.SemaphoreType.DMA((2, count // 2 + 1, 2 * slots)),
            pltpu.SemaphoreType.DMA((count, 2 * slots)),
            pltpu.VMEM((rows, width), panels.dtype),
            pltpu.VMEM((rows // 2, width), panels.dtype),
            pltpu.VMEM((rows // 2, width), panels.dtype),
            pltpu.SemaphoreType.DMA((2, groups)),
            pltpu.SemaphoreType.DMA((2, groups)),
            pltpu.SemaphoreType.DMA((2,)),
            pltpu.SemaphoreType.DMA((2,)),
        ],
        compiler_params=pltpu.CompilerParams(collective_id=collective_id, has_side_effects=True),
    )(panels, home)


def kv_share_kernel(part_ref, out_ref, partner_part, mine, theirs, send_sems, recv_sems):
    me = lax.axis_index("tp")
    partner = me + 1 - 2 * (me % 2)
    across = me + 2 - 4 * ((me // 2) % 2)
    barrier = pltpu.get_barrier_semaphore()
    for neighbour in (partner, across):
        pl.semaphore_signal(barrier, inc=1, device_id={"tp": neighbour}, device_id_type=MESH)
    pl.semaphore_wait(barrier, 2)
    first = pltpu.make_async_remote_copy(
        src_ref=part_ref, dst_ref=partner_part, send_sem=send_sems.at[0], recv_sem=recv_sems.at[0],
        device_id={"tp": partner}, device_id_type=MESH,
    )
    first.start()
    first.wait()
    mine[...] = (part_ref[...] + partner_part[...]).astype(mine.dtype)
    second = pltpu.make_async_remote_copy(
        src_ref=mine, dst_ref=theirs, send_sem=send_sems.at[1], recv_sem=recv_sems.at[1],
        device_id={"tp": across}, device_id_type=MESH,
    )
    second.start()
    second.wait()
    holds_k = (me % 4) < 2
    out_ref[0] = jnp.where(holds_k, mine[...], theirs[...])
    out_ref[1] = jnp.where(holds_k, theirs[...], mine[...])


def kv_share(part, collective_id):
    return pl.pallas_call(
        kv_share_kernel,
        out_shape=jax.ShapeDtypeStruct((2,) + part.shape, jnp.bfloat16),
        in_specs=[pl.BlockSpec(memory_space=pltpu.VMEM)],
        out_specs=pl.BlockSpec(memory_space=pltpu.VMEM),
        scratch_shapes=[
            pltpu.VMEM(part.shape, part.dtype),
            pltpu.VMEM(part.shape, jnp.bfloat16),
            pltpu.VMEM(part.shape, jnp.bfloat16),
            pltpu.SemaphoreType.DMA((2,)),
            pltpu.SemaphoreType.DMA((2,)),
        ],
        compiler_params=pltpu.CompilerParams(collective_id=collective_id, has_side_effects=True),
    )(part)


def tail_kernel(count, scale, tokens_ref, gathered_hbm, lengths_ref, out_ref,
                gathered, load_sem, part_ref, partner_part, mine, theirs, staged, landed, send_sems, recv_sems):
    width = landed.shape[-1]
    me = lax.axis_index("tp")
    partner = me + 1 - 2 * (me % 2)
    across = me + 2 - 4 * ((me // 2) % 2)
    load = pltpu.make_async_copy(gathered_hbm, gathered, load_sem)
    load.start()
    barrier = pltpu.get_barrier_semaphore()
    for step in range(1, count):
        peer = lax.rem(me + step, count)
        pl.semaphore_signal(barrier, inc=1, device_id={"tp": peer}, device_id_type=MESH)
    load.wait()
    core = me % 2
    half = gathered.shape[1] // 3
    sources = gathered.shape[0]
    first_half = core == 0
    projected = jnp.zeros((tokens_ref.shape[0], 2 * width), jnp.float32)
    for pair in range(sources // 2):
        q_parts, kv_parts = [], []
        for source in (2 * pair, 2 * pair + 1):
            here = gathered[source, 0:half]
            kv = gathered[source, half:2 * half]
            there = gathered[source, 2 * half:3 * half]
            zero = jnp.zeros_like(kv)
            q_parts.append(jnp.where(first_half, jnp.concatenate([here, there], axis=0),
                                     jnp.concatenate([there, here], axis=0)))
            kv_parts.append(jnp.where(first_half, jnp.concatenate([kv, zero], axis=0),
                                      jnp.concatenate([zero, kv], axis=0)))
        slab = jnp.concatenate(
            [jnp.concatenate(q_parts, axis=0), jnp.concatenate(kv_parts, axis=0)], axis=1
        )
        columns = slab.shape[0]
        projected = projected + jnp.dot(
            tokens_ref[:, pair * columns:(pair + 1) * columns], slab, preferred_element_type=jnp.float32
        )
    part_ref[...] = projected[:, width:]
    query = projected[:, :width].astype(jnp.bfloat16)
    pl.semaphore_wait(barrier, count - 1)
    first = pltpu.make_async_remote_copy(
        src_ref=part_ref, dst_ref=partner_part, send_sem=send_sems.at[0], recv_sem=recv_sems.at[0],
        device_id={"tp": partner}, device_id_type=MESH,
    )
    first.start()
    first.wait()
    mine[...] = (part_ref[...] + partner_part[...]).astype(mine.dtype)
    second = pltpu.make_async_remote_copy(
        src_ref=mine, dst_ref=theirs, send_sem=send_sems.at[1], recv_sem=recv_sems.at[1],
        device_id={"tp": across}, device_id_type=MESH,
    )
    second.start()
    second.wait()
    holds_k = (me % 4) < 2
    keys = jnp.where(holds_k, mine[...], theirs[...])
    values = jnp.where(holds_k, theirs[...], mine[...])

    scores = lax.dot_general(
        query, keys, (((1,), (1,)), ((), ())), preferred_element_type=jnp.float32
    ) * scale
    seq = scores.shape[0]
    row = lax.broadcasted_iota(jnp.int32, (seq, seq), 0)
    col = lax.broadcasted_iota(jnp.int32, (seq, seq), 1)
    row_segment = jnp.zeros((seq, seq), jnp.int32)
    col_segment = jnp.zeros((seq, seq), jnp.int32)
    bound = lengths_ref[0, 0] * 0
    for response in range(lengths_ref.shape[1]):
        bound = bound + lengths_ref[0, response]
        row_segment = row_segment + (row >= bound).astype(jnp.int32)
        col_segment = col_segment + (col >= bound).astype(jnp.int32)
    allowed = (row_segment == col_segment) & (col <= row)
    masked = jnp.where(allowed, scores, -jnp.inf)
    peak = jnp.max(masked, axis=1, keepdims=True)
    weights = jnp.exp(masked - peak)
    probs = (weights / jnp.sum(weights, axis=1, keepdims=True)).astype(jnp.bfloat16)
    context = jnp.dot(probs, values, preferred_element_type=jnp.float32)
    rows = seq // count
    for target in range(count):
        staged[target] = context[target * rows:(target + 1) * rows]

    copies = []
    for step in range(1, count):
        peer = lax.rem(me + step, count)
        copy = pltpu.make_async_remote_copy(
            src_ref=staged.at[peer],
            dst_ref=landed.at[me],
            send_sem=send_sems.at[1 + step],
            recv_sem=recv_sems.at[1 + step],
            device_id={"tp": peer},
            device_id_type=MESH,
        )
        copy.start()
        copies.append(copy)
    landed[me] = staged[me]
    for copy in copies:
        copy.wait()
    for source in range(count):
        out_ref[:, source * width:(source + 1) * width] = landed[source]


def tail(tokens, gathered, lengths, count, collective_id):
    seq, width = tokens.shape[0], gathered.shape[2]
    part = jax.ShapeDtypeStruct((seq, width), jnp.float32)
    rows = seq // count
    vmem = pl.BlockSpec(memory_space=pltpu.VMEM)
    return pl.pallas_call(
        functools.partial(tail_kernel, count, width ** (-0.5)),
        out_shape=jax.ShapeDtypeStruct((rows, count * width), jnp.float32),
        in_specs=[vmem, pl.BlockSpec(memory_space=pl.ANY), pl.BlockSpec(memory_space=pltpu.SMEM)],
        out_specs=vmem,
        scratch_shapes=[
            pltpu.VMEM(gathered.shape, gathered.dtype),
            pltpu.SemaphoreType.DMA(()),
            pltpu.VMEM(part.shape, part.dtype),
            pltpu.VMEM(part.shape, part.dtype),
            pltpu.VMEM(part.shape, jnp.bfloat16),
            pltpu.VMEM(part.shape, jnp.bfloat16),
            pltpu.VMEM((count, rows, width), jnp.float32),
            pltpu.VMEM((count, rows, width), jnp.float32),
            pltpu.SemaphoreType.DMA((count + 1,)),
            pltpu.SemaphoreType.DMA((count + 1,)),
        ],
        compiler_params=pltpu.CompilerParams(collective_id=collective_id, has_side_effects=True),
    )(tokens, gathered, lengths)


def grid_kernel(width, send_ref, out_ref, landed, send_sems, recv_sems):
    me = lax.axis_index("grp")
    core = lax.axis_index("tp") % 2
    col, row = me % width, me // width

    def node(c, r):
        return lax.rem(r + width, width) * width + lax.rem(c + width, width)

    def along(dim, c, r, k):
        return node(c + k, r) if dim == 0 else node(c, r + k)

    barrier = pltpu.get_barrier_semaphore()
    neighbours = [node(col + 1, row), node(col - 1, row), node(col, row + 1), node(col, row - 1)]
    for neighbour in neighbours:
        pl.semaphore_signal(barrier, inc=1, device_id={"grp": neighbour}, device_id_type=MESH)
    pl.semaphore_wait(barrier, 4)

    landed[me] = send_ref[...]
    sends = []

    def send(source, origin, half, target):
        copy = pltpu.make_async_remote_copy(
            src_ref=source,
            dst_ref=landed.at[origin, half],
            send_sem=send_sems.at[len(sends)],
            recv_sem=recv_sems.at[origin, half],
            device_id={"grp": target},
            device_id_type=MESH,
        )
        copy.start()
        sends.append(copy)

    def arrive(origin, half):
        pltpu.make_async_remote_copy(
            src_ref=send_ref.at[half],
            dst_ref=landed.at[origin, half],
            send_sem=send_sems.at[0],
            recv_sem=recv_sems.at[origin, half],
            device_id={"grp": neighbours[0]},
            device_id_type=MESH,
        ).wait_recv()

    ahead = 1 - 2 * core

    def phase(lines, half, dim):
        for k in (1, -1):
            for line in lines:
                origin = along(1 - dim, col, row, line)
                source = send_ref.at[half] if line == 0 else landed.at[origin, half]
                send(source, origin, half, along(dim, col, row, k))
        for line in lines:
            for k in (1, -1):
                arrive(along(dim, along(1 - dim, col, row, line) % width, along(1 - dim, col, row, line) // width, k), half)
        for line in lines:
            base = along(1 - dim, col, row, line)
            bc, br = base % width, base // width
            send(landed.at[along(dim, bc, br, -ahead), half], along(dim, bc, br, -ahead), half,
                 along(dim, col, row, ahead))
        for line in lines:
            base = along(1 - dim, col, row, line)
            arrive(along(dim, base % width, base // width, 2), half)

    phase([0], 0, 0)
    phase([0], 1, 1)
    phase([0, 1, -1, 2], 0, 1)
    phase([0, 1, -1, 2], 1, 0)
    for copy in sends:
        copy.wait_send()
    out_ref[...] = landed[...]


def grid_gather(x, width, collective_id):
    count = width * width
    x = x.reshape((2, x.shape[0] // 2) + x.shape[1:])
    gathered = pl.pallas_call(
        functools.partial(grid_kernel, width),
        out_shape=jax.ShapeDtypeStruct((count,) + x.shape, x.dtype),
        in_specs=[pl.BlockSpec(memory_space=pltpu.VMEM)],
        out_specs=pl.BlockSpec(memory_space=pltpu.VMEM),
        scratch_shapes=[
            pltpu.VMEM((count,) + x.shape, x.dtype),
            pltpu.SemaphoreType.DMA((2 * (count - 1),)),
            pltpu.SemaphoreType.DMA((count, 2)),
        ],
        compiler_params=pltpu.CompilerParams(collective_id=collective_id, has_side_effects=True),
    )(x)
    return gathered.reshape((count, x.shape[0] * x.shape[1]) + x.shape[2:])


def gather_hbm_kernel(axis, count, send_ref, out_ref, send_sems, recv_sems, local_sem):
    me = lax.axis_index(axis)
    barrier = pltpu.get_barrier_semaphore()
    for step in range(1, count):
        peer = lax.rem(me + step, count)
        pl.semaphore_signal(barrier, inc=1, device_id={axis: peer}, device_id_type=MESH)
    pl.semaphore_wait(barrier, count - 1)
    copies = []
    for step in range(1, count):
        peer = lax.rem(me + step, count)
        copy = pltpu.make_async_remote_copy(
            src_ref=send_ref,
            dst_ref=out_ref.at[me],
            send_sem=send_sems.at[step],
            recv_sem=recv_sems.at[step],
            device_id={axis: peer},
            device_id_type=MESH,
        )
        copy.start()
        copies.append(copy)
    local = pltpu.make_async_copy(send_ref, out_ref.at[me], local_sem)
    local.start()
    for copy in copies:
        copy.wait()
    local.wait()


def gather_hbm(x, axis, count, collective_id):
    return pl.pallas_call(
        functools.partial(gather_hbm_kernel, axis, count),
        out_shape=jax.ShapeDtypeStruct((count,) + x.shape, x.dtype),
        in_specs=[pl.BlockSpec(memory_space=pltpu.VMEM)],
        out_specs=pl.BlockSpec(memory_space=pl.ANY),
        scratch_shapes=[
            pltpu.SemaphoreType.DMA((count,)),
            pltpu.SemaphoreType.DMA((count,)),
            pltpu.SemaphoreType.DMA(()),
        ],
        compiler_params=pltpu.CompilerParams(collective_id=collective_id, has_side_effects=True),
    )(x)


def weights_gather_kernel(count, own_ref, for_partner_ref, out_ref, partner_rows,
                          send_sems, recv_sems, partner_sems, local_sems):
    me = lax.axis_index("grp")
    member = lax.axis_index("tp")
    partner = member + 1 - 2 * (member % 2)
    rows = own_ref.shape[0]
    barrier = pltpu.get_barrier_semaphore()
    pl.semaphore_signal(barrier, inc=1, device_id={"tp": partner}, device_id_type=MESH)
    for step in range(1, count):
        peer = lax.rem(me + step, count)
        pl.semaphore_signal(barrier, inc=1, device_id={"grp": peer}, device_id_type=MESH)
    pl.semaphore_wait(barrier, count)
    to_partner = pltpu.make_async_remote_copy(
        src_ref=for_partner_ref, dst_ref=partner_rows, send_sem=partner_sems.at[0],
        recv_sem=partner_sems.at[1], device_id={"tp": partner}, device_id_type=MESH,
    )
    to_partner.start()
    copies = []

    def spread(part, source, window):
        for step in range(1, count):
            peer = lax.rem(me + step, count)
            copy = pltpu.make_async_remote_copy(
                src_ref=source,
                dst_ref=out_ref.at[me, window],
                send_sem=send_sems.at[part, step],
                recv_sem=recv_sems.at[part, step],
                device_id={"grp": peer},
                device_id_type=MESH,
            )
            copy.start()
            copies.append(copy)
        local = pltpu.make_async_copy(source, out_ref.at[me, window], local_sems.at[part])
        local.start()
        copies.append(local)

    spread(0, own_ref, pl.ds(0, rows))
    to_partner.wait()
    spread(1, partner_rows, pl.ds(rows, partner_rows.shape[0]))
    for copy in copies:
        copy.wait()


def weights_gather(own, for_partner, count, collective_id):
    rows = own.shape[0] + for_partner.shape[0]
    return pl.pallas_call(
        functools.partial(weights_gather_kernel, count),
        out_shape=jax.ShapeDtypeStruct((count, rows) + own.shape[1:], own.dtype),
        in_specs=[pl.BlockSpec(memory_space=pltpu.VMEM)] * 2,
        out_specs=pl.BlockSpec(memory_space=pl.ANY),
        scratch_shapes=[
            pltpu.VMEM(for_partner.shape, for_partner.dtype),
            pltpu.SemaphoreType.DMA((2, count)),
            pltpu.SemaphoreType.DMA((2, count)),
            pltpu.SemaphoreType.DMA((2,)),
            pltpu.SemaphoreType.DMA((2,)),
        ],
        compiler_params=pltpu.CompilerParams(collective_id=collective_id, has_side_effects=True),
    )(own, for_partner)


def exchange_kernel(axis, count, scatter, send_ref, out_ref, landed, send_sems, recv_sems):
    me = lax.axis_index(axis)
    barrier = pltpu.get_barrier_semaphore()
    for step in range(1, count):
        peer = lax.rem(me + step, count)
        pl.semaphore_signal(barrier, inc=1, device_id={axis: peer}, device_id_type=MESH)
    pl.semaphore_wait(barrier, count - 1)
    copies = []
    for step in range(1, count):
        peer = lax.rem(me + step, count)
        source = send_ref.at[peer] if scatter else send_ref
        copy = pltpu.make_async_remote_copy(
            src_ref=source,
            dst_ref=landed.at[me],
            send_sem=send_sems.at[step],
            recv_sem=recv_sems.at[step],
            device_id={axis: peer},
            device_id_type=MESH,
        )
        copy.start()
        copies.append(copy)
    landed[me] = send_ref[me] if scatter else send_ref[...]
    for copy in copies:
        copy.wait()
    if scatter:
        width = landed.shape[-1]
        for source in range(count):
            out_ref[:, source * width:(source + 1) * width] = landed[source]
    else:
        out_ref[...] = landed[...]


def exchange(x, axis, count, scatter, collective_id):
    piece = x.shape[1:] if scatter else x.shape
    result = (piece[0], count * piece[1]) if scatter else (count,) + piece
    return pl.pallas_call(
        functools.partial(exchange_kernel, axis, count, scatter),
        out_shape=jax.ShapeDtypeStruct(result, x.dtype),
        in_specs=[pl.BlockSpec(memory_space=pltpu.VMEM)],
        out_specs=pl.BlockSpec(memory_space=pltpu.VMEM),
        scratch_shapes=[
            pltpu.VMEM((count,) + piece, x.dtype),
            pltpu.SemaphoreType.DMA((count,)),
            pltpu.SemaphoreType.DMA((count,)),
        ],
        compiler_params=pltpu.CompilerParams(collective_id=collective_id, has_side_effects=True),
    )(x)


def on_device(tokens, trainer_panels, panel_home, lengths):
    tp_count = lax.axis_size("tp")
    grp_count = lax.axis_size("grp")
    member_id = lax.axis_index("tp")
    kv_count = (panel_home.shape[0] - tp_count) // 2
    group_size = tp_count // kv_count
    head_dim = trainer_panels.shape[2]
    block_rows = trainer_panels.shape[1]
    half_rows = block_rows // 2
    seq_total = tokens.shape[0]

    gathered = chip_ring_gather(trainer_panels, panel_home, tp_count // 2, grp_count, 2)
    return tail(tokens, gathered, lengths, tp_count, 1)


def solution(mesh):
    placed = (P("grp", None), P("tp", "grp", None), P(), P("grp", None))
    return jax.shard_map(
        on_device, mesh=mesh, in_specs=placed, out_specs=P(("grp", "tp"), None), check_vma=False
    )
```

```python
import functools

import jax
import jax.numpy as jnp
from jax import lax
from jax.experimental import pallas as pl
from jax.experimental.pallas import tpu as pltpu
from jax.sharding import PartitionSpec as P

MESH = pl.DeviceIdType.MESH


def ring_kernel(count, stride, chunks, send_ref, out_ref, landed, send_sems, recv_sems):
    me = lax.axis_index("tp")
    total = count * stride
    right, left = lax.rem(me + stride, total), lax.rem(me + total - stride, total)
    spot = me // stride
    barrier = pltpu.get_barrier_semaphore()
    for neighbour in (left, right):
        pl.semaphore_signal(barrier, inc=1, device_id={"tp": neighbour}, device_id_type=MESH)
    pl.semaphore_wait(barrier, 2)

    def incoming(origin, chunk):
        return pltpu.make_async_remote_copy(
            src_ref=send_ref.at[chunk],
            dst_ref=landed.at[origin, chunk],
            send_sem=send_sems.at[0, 0, 0],
            recv_sem=recv_sems.at[origin, chunk],
            device_id={"tp": right},
            device_id_type=MESH,
        )

    landed[spot] = send_ref[...]
    sends = []
    far_right, far_left = count // 2, (count - 1) // 2
    for step in range(1, far_right + 1):
        for chunk in range(chunks):
            streams = [(0, right, lax.rem(spot + count - (step - 1), count))]
            if step <= far_left:
                streams.append((1, left, lax.rem(spot + step - 1, count)))
            for way, target, origin in streams:
                if step > 1:
                    incoming(origin, chunk).wait_recv()
                source = send_ref.at[chunk] if step == 1 else landed.at[origin, chunk]
                copy = pltpu.make_async_remote_copy(
                    src_ref=source,
                    dst_ref=landed.at[origin, chunk],
                    send_sem=send_sems.at[way, step, chunk],
                    recv_sem=recv_sems.at[origin, chunk],
                    device_id={"tp": target},
                    device_id_type=MESH,
                )
                copy.start()
                sends.append(copy)
    for chunk in range(chunks):
        incoming(lax.rem(spot + count - far_right, count), chunk).wait_recv()
        incoming(lax.rem(spot + far_left, count), chunk).wait_recv()
    for copy in sends:
        copy.wait_send()
    out_ref[...] = landed[...]


def ring_gather(x, count, stride, chunks, collective_id):
    x = x.reshape((chunks, x.shape[0] // chunks) + x.shape[1:])
    gathered = pl.pallas_call(
        functools.partial(ring_kernel, count, stride, chunks),
        out_shape=jax.ShapeDtypeStruct((count,) + x.shape, x.dtype),
        in_specs=[pl.BlockSpec(memory_space=pltpu.VMEM)],
        out_specs=pl.BlockSpec(memory_space=pltpu.VMEM),
        scratch_shapes=[
            pltpu.VMEM((count,) + x.shape, x.dtype),
            pltpu.SemaphoreType.DMA((2, count // 2 + 1, chunks)),
            pltpu.SemaphoreType.DMA((count, chunks)),
        ],
        compiler_params=pltpu.CompilerParams(collective_id=collective_id, has_side_effects=True),
    )(x)
    return gathered.reshape((count * x.shape[0] * x.shape[1],) + x.shape[2:])


def chip_ring_kernel(count, groups, panels_ref, home_ref, out_ref, landed, send_sems, recv_sems,
                     own_ref, partner_ref, partner_rows, grp_send_sems, grp_recv_sems, partner_sems, local_sems,
                     greet=True):
    me = lax.axis_index("tp")
    here = lax.axis_index("grp")
    total = 2 * count
    core = me % 2
    partner = me + 1 - 2 * core
    right, left = lax.rem(me + 2, total), lax.rem(me + total - 2, total)
    spot = me // 2
    half = panels_ref.shape[1] // 2
    if greet:
        barrier = pltpu.get_barrier_semaphore()
        for neighbour in (left, right, partner):
            pl.semaphore_signal(barrier, inc=1, device_id={"tp": neighbour}, device_id_type=MESH)
        for step in range(1, groups):
            peer = lax.rem(here + step, groups)
            pl.semaphore_signal(barrier, inc=1, device_id={"grp": peer}, device_id_type=MESH)
        pl.semaphore_wait(barrier, 2 + groups)

    def rows_of(slot, which):
        return panels_ref.at[slot, pl.ds(pl.multiple_of(which * half, 16), half)]

    def incoming(origin, chunk):
        return pltpu.make_async_remote_copy(
            src_ref=rows_of(0, 0),
            dst_ref=landed.at[origin, chunk],
            send_sem=send_sems.at[0, 0, 0],
            recv_sem=recv_sems.at[origin, chunk],
            device_id={"tp": right},
            device_id_type=MESH,
        )

    sends = []

    def send(source, origin, chunk, sem, target):
        copy = pltpu.make_async_remote_copy(
            src_ref=source,
            dst_ref=landed.at[origin, chunk],
            send_sem=sem,
            recv_sem=recv_sems.at[origin, chunk],
            device_id={"tp": target},
            device_id_type=MESH,
        )
        copy.start()
        sends.append(copy)

    own = [2 * core + j for j in range(2)]
    theirs = [2 * (1 - core) + j for j in range(2)]
    for j in range(2):
        send(rows_of(j, 1 - core), spot, own[j], send_sems.at[0, 0, 1 + j], partner)
        landed[spot, own[j]] = rows_of(j, core)[...]
    far_right, far_left = count // 2, (count - 1) // 2
    first = [(rows_of(j, core), own[j]) for j in range(2)] + [(None, theirs[j]) for j in range(2)]
    for position, (source, chunk) in enumerate(first):
        if source is None:
            incoming(spot, chunk).wait_recv()
            source = landed.at[spot, chunk]
        send(source, spot, chunk, send_sems.at[0, 1, position], right)
        if far_left >= 1:
            send(source, spot, chunk, send_sems.at[1, 1, position], left)
    for step in range(2, far_right + 1):
        for chunk in range(4):
            streams = [(0, right, lax.rem(spot + count - (step - 1), count))]
            if step <= far_left:
                streams.append((1, left, lax.rem(spot + step - 1, count)))
            for way, target, origin in streams:
                incoming(origin, chunk).wait_recv()
                send(landed.at[origin, chunk], origin, chunk, send_sems.at[way, step, chunk], target)
    for chunk in range(4):
        incoming(lax.rem(spot + count - far_right, count), chunk).wait_recv()
        incoming(lax.rem(spot + far_left, count), chunk).wait_recv()
    for copy in sends:
        copy.wait_send()
    heads = total
    kv_heads = (home_ref.shape[0] - heads) // 2
    group = heads // kv_heads
    quarter = me % group
    kv_panel = heads + me // group + kv_heads * (quarter // 2)
    chip_slots = landed.shape[1]

    def block(panel):
        slot = home_ref[panel]
        return landed[slot // chip_slots, slot % chip_slots]

    own_ref[0:half] = block(me)
    own_ref[half:2 * half] = block(kv_panel)
    partner_ref[...] = block(partner)

    to_partner = pltpu.make_async_remote_copy(
        src_ref=partner_ref, dst_ref=partner_rows, send_sem=partner_sems.at[0],
        recv_sem=partner_sems.at[1], device_id={"tp": partner}, device_id_type=MESH,
    )
    to_partner.start()
    copies = []

    def spread(part, source, window):
        for step in range(1, groups):
            peer = lax.rem(here + step, groups)
            copy = pltpu.make_async_remote_copy(
                src_ref=source,
                dst_ref=out_ref.at[here, window],
                send_sem=grp_send_sems.at[part, step],
                recv_sem=grp_recv_sems.at[part, step],
                device_id={"grp": peer},
                device_id_type=MESH,
            )
            copy.start()
            copies.append(copy)
        local = pltpu.make_async_copy(source, out_ref.at[here, window], local_sems.at[part])
        local.start()
        copies.append(local)

    spread(0, own_ref, pl.ds(0, 2 * half))
    to_partner.wait()
    spread(1, partner_rows, pl.ds(2 * half, half))
    for copy in copies:
        copy.wait()


def chip_ring_gather(panels, home, count, groups, collective_id):
    slots, rows, width = panels.shape
    return pl.pallas_call(
        functools.partial(chip_ring_kernel, count, groups),
        out_shape=jax.ShapeDtypeStruct((groups, rows + rows // 2, width), panels.dtype),
        in_specs=[pl.BlockSpec(memory_space=pltpu.VMEM), pl.BlockSpec(memory_space=pltpu.SMEM)],
        out_specs=pl.BlockSpec(memory_space=pl.ANY),
        scratch_shapes=[
            pltpu.VMEM((count, 2 * slots, rows // 2, width), panels.dtype),
            pltpu.SemaphoreType.DMA((2, count // 2 + 1, 2 * slots)),
            pltpu.SemaphoreType.DMA((count, 2 * slots)),
            pltpu.VMEM((rows, width), panels.dtype),
            pltpu.VMEM((rows // 2, width), panels.dtype),
            pltpu.VMEM((rows // 2, width), panels.dtype),
            pltpu.SemaphoreType.DMA((2, groups)),
            pltpu.SemaphoreType.DMA((2, groups)),
            pltpu.SemaphoreType.DMA((2,)),
            pltpu.SemaphoreType.DMA((2,)),
        ],
        compiler_params=pltpu.CompilerParams(collective_id=collective_id, has_side_effects=True),
    )(panels, home)


def kv_share_kernel(part_ref, out_ref, partner_part, mine, theirs, send_sems, recv_sems):
    me = lax.axis_index("tp")
    partner = me + 1 - 2 * (me % 2)
    across = me + 2 - 4 * ((me // 2) % 2)
    barrier = pltpu.get_barrier_semaphore()
    for neighbour in (partner, across):
        pl.semaphore_signal(barrier, inc=1, device_id={"tp": neighbour}, device_id_type=MESH)
    pl.semaphore_wait(barrier, 2)
    first = pltpu.make_async_remote_copy(
        src_ref=part_ref, dst_ref=partner_part, send_sem=send_sems.at[0], recv_sem=recv_sems.at[0],
        device_id={"tp": partner}, device_id_type=MESH,
    )
    first.start()
    first.wait()
    mine[...] = (part_ref[...] + partner_part[...]).astype(mine.dtype)
    second = pltpu.make_async_remote_copy(
        src_ref=mine, dst_ref=theirs, send_sem=send_sems.at[1], recv_sem=recv_sems.at[1],
        device_id={"tp": across}, device_id_type=MESH,
    )
    second.start()
    second.wait()
    holds_k = (me % 4) < 2
    out_ref[0] = jnp.where(holds_k, mine[...], theirs[...])
    out_ref[1] = jnp.where(holds_k, theirs[...], mine[...])


def kv_share(part, collective_id):
    return pl.pallas_call(
        kv_share_kernel,
        out_shape=jax.ShapeDtypeStruct((2,) + part.shape, jnp.bfloat16),
        in_specs=[pl.BlockSpec(memory_space=pltpu.VMEM)],
        out_specs=pl.BlockSpec(memory_space=pltpu.VMEM),
        scratch_shapes=[
            pltpu.VMEM(part.shape, part.dtype),
            pltpu.VMEM(part.shape, jnp.bfloat16),
            pltpu.VMEM(part.shape, jnp.bfloat16),
            pltpu.SemaphoreType.DMA((2,)),
            pltpu.SemaphoreType.DMA((2,)),
        ],
        compiler_params=pltpu.CompilerParams(collective_id=collective_id, has_side_effects=True),
    )(part)


def tail_kernel(count, scale, tokens_ref, gathered_hbm, lengths_ref, out_ref,
                gathered, load_sem, part_ref, partner_part, mine, theirs, staged, landed, send_sems, recv_sems,
                greet=True):
    width = landed.shape[-1]
    me = lax.axis_index("tp")
    partner = me + 1 - 2 * (me % 2)
    across = me + 2 - 4 * ((me // 2) % 2)
    if greet:
        load = pltpu.make_async_copy(gathered_hbm, gathered, load_sem)
        load.start()
        barrier = pltpu.get_barrier_semaphore()
        for step in range(1, count):
            peer = lax.rem(me + step, count)
            pl.semaphore_signal(barrier, inc=1, device_id={"tp": peer}, device_id_type=MESH)
        load.wait()
    core = me % 2
    half = gathered.shape[1] // 3
    sources = gathered.shape[0]
    first_half = core == 0
    projected = jnp.zeros((tokens_ref.shape[0], 2 * width), jnp.float32)
    for pair in range(sources // 2):
        q_parts, kv_parts = [], []
        for source in (2 * pair, 2 * pair + 1):
            here = gathered[source, 0:half]
            kv = gathered[source, half:2 * half]
            there = gathered[source, 2 * half:3 * half]
            zero = jnp.zeros_like(kv)
            q_parts.append(jnp.where(first_half, jnp.concatenate([here, there], axis=0),
                                     jnp.concatenate([there, here], axis=0)))
            kv_parts.append(jnp.where(first_half, jnp.concatenate([kv, zero], axis=0),
                                      jnp.concatenate([zero, kv], axis=0)))
        slab = jnp.concatenate(
            [jnp.concatenate(q_parts, axis=0), jnp.concatenate(kv_parts, axis=0)], axis=1
        )
        columns = slab.shape[0]
        projected = projected + jnp.dot(
            tokens_ref[:, pair * columns:(pair + 1) * columns], slab, preferred_element_type=jnp.float32
        )
    part_ref[...] = projected[:, width:]
    query = projected[:, :width].astype(jnp.bfloat16)
    if greet:
        pl.semaphore_wait(barrier, count - 1)
    first = pltpu.make_async_remote_copy(
        src_ref=part_ref, dst_ref=partner_part, send_sem=send_sems.at[0], recv_sem=recv_sems.at[0],
        device_id={"tp": partner}, device_id_type=MESH,
    )
    first.start()
    first.wait()
    mine[...] = (part_ref[...] + partner_part[...]).astype(mine.dtype)
    second = pltpu.make_async_remote_copy(
        src_ref=mine, dst_ref=theirs, send_sem=send_sems.at[1], recv_sem=recv_sems.at[1],
        device_id={"tp": across}, device_id_type=MESH,
    )
    second.start()
    second.wait()
    holds_k = (me % 4) < 2
    keys = jnp.where(holds_k, mine[...], theirs[...])
    values = jnp.where(holds_k, theirs[...], mine[...])

    scores = lax.dot_general(
        query, keys, (((1,), (1,)), ((), ())), preferred_element_type=jnp.float32
    ) * scale
    seq = scores.shape[0]
    row = lax.broadcasted_iota(jnp.int32, (seq, seq), 0)
    col = lax.broadcasted_iota(jnp.int32, (seq, seq), 1)
    row_segment = jnp.zeros((seq, seq), jnp.int32)
    col_segment = jnp.zeros((seq, seq), jnp.int32)
    bound = lengths_ref[0, 0] * 0
    for response in range(lengths_ref.shape[1]):
        bound = bound + lengths_ref[0, response]
        row_segment = row_segment + (row >= bound).astype(jnp.int32)
        col_segment = col_segment + (col >= bound).astype(jnp.int32)
    allowed = (row_segment == col_segment) & (col <= row)
    masked = jnp.where(allowed, scores, -jnp.inf)
    peak = jnp.max(masked, axis=1, keepdims=True)
    weights = jnp.exp(masked - peak)
    probs = (weights / jnp.sum(weights, axis=1, keepdims=True)).astype(jnp.bfloat16)
    context = jnp.dot(probs, values, preferred_element_type=jnp.float32)
    rows = seq // count
    for target in range(count):
        staged[target] = context[target * rows:(target + 1) * rows]

    copies = []
    for step in range(1, count):
        peer = lax.rem(me + step, count)
        copy = pltpu.make_async_remote_copy(
            src_ref=staged.at[peer],
            dst_ref=landed.at[me],
            send_sem=send_sems.at[1 + step],
            recv_sem=recv_sems.at[1 + step],
            device_id={"tp": peer},
            device_id_type=MESH,
        )
        copy.start()
        copies.append(copy)
    landed[me] = staged[me]
    for copy in copies:
        copy.wait()
    for source in range(count):
        out_ref[:, source * width:(source + 1) * width] = landed[source]


def tail(tokens, gathered, lengths, count, collective_id):
    seq, width = tokens.shape[0], gathered.shape[2]
    part = jax.ShapeDtypeStruct((seq, width), jnp.float32)
    rows = seq // count
    vmem = pl.BlockSpec(memory_space=pltpu.VMEM)
    return pl.pallas_call(
        functools.partial(tail_kernel, count, width ** (-0.5)),
        out_shape=jax.ShapeDtypeStruct((rows, count * width), jnp.float32),
        in_specs=[vmem, pl.BlockSpec(memory_space=pl.ANY), pl.BlockSpec(memory_space=pltpu.SMEM)],
        out_specs=vmem,
        scratch_shapes=[
            pltpu.VMEM(gathered.shape, gathered.dtype),
            pltpu.SemaphoreType.DMA(()),
            pltpu.VMEM(part.shape, part.dtype),
            pltpu.VMEM(part.shape, part.dtype),
            pltpu.VMEM(part.shape, jnp.bfloat16),
            pltpu.VMEM(part.shape, jnp.bfloat16),
            pltpu.VMEM((count, rows, width), jnp.float32),
            pltpu.VMEM((count, rows, width), jnp.float32),
            pltpu.SemaphoreType.DMA((count + 1,)),
            pltpu.SemaphoreType.DMA((count + 1,)),
        ],
        compiler_params=pltpu.CompilerParams(collective_id=collective_id, has_side_effects=True),
    )(tokens, gathered, lengths)


def whole_kernel(count, groups, scale, panels_ref, home_ref, tokens_ref, lengths_ref, out_ref, *scratch):
    ring_scratch, gathered, tail_scratch = scratch[:10], scratch[10], scratch[11:]
    me = lax.axis_index("tp")
    here = lax.axis_index("grp")
    total = 2 * count
    barrier = pltpu.get_barrier_semaphore()
    for step in range(1, total):
        peer = lax.rem(me + step, total)
        pl.semaphore_signal(barrier, inc=1, device_id={"tp": peer}, device_id_type=MESH)
    for step in range(1, groups):
        peer = lax.rem(here + step, groups)
        pl.semaphore_signal(barrier, inc=1, device_id={"grp": peer}, device_id_type=MESH)
    pl.semaphore_wait(barrier, total + groups - 2)
    chip_ring_kernel(count, groups, panels_ref, home_ref, gathered, *ring_scratch, greet=False)
    tail_kernel(total, scale, tokens_ref, None, lengths_ref, out_ref, gathered, None, *tail_scratch, greet=False)


def whole(panels, home, tokens, lengths, count, groups, collective_id):
    slots, rows, width = panels.shape
    seq = tokens.shape[0]
    total = 2 * count
    out_rows = seq // total
    part = (seq, width)
    vmem = pl.BlockSpec(memory_space=pltpu.VMEM)
    smem = pl.BlockSpec(memory_space=pltpu.SMEM)
    return pl.pallas_call(
        functools.partial(whole_kernel, count, groups, width ** (-0.5)),
        out_shape=jax.ShapeDtypeStruct((out_rows, total * width), jnp.float32),
        in_specs=[vmem, smem, vmem, smem],
        out_specs=vmem,
        scratch_shapes=[
            pltpu.VMEM((count, 2 * slots, rows // 2, width), panels.dtype),
            pltpu.SemaphoreType.DMA((2, count // 2 + 1, 2 * slots)),
            pltpu.SemaphoreType.DMA((count, 2 * slots)),
            pltpu.VMEM((rows, width), panels.dtype),
            pltpu.VMEM((rows // 2, width), panels.dtype),
            pltpu.VMEM((rows // 2, width), panels.dtype),
            pltpu.SemaphoreType.DMA((2, groups)),
            pltpu.SemaphoreType.DMA((2, groups)),
            pltpu.SemaphoreType.DMA((2,)),
            pltpu.SemaphoreType.DMA((2,)),
            pltpu.VMEM((groups, rows + rows // 2, width), panels.dtype),
            pltpu.VMEM(part, jnp.float32),
            pltpu.VMEM(part, jnp.float32),
            pltpu.VMEM(part, jnp.bfloat16),
            pltpu.VMEM(part, jnp.bfloat16),
            pltpu.VMEM((total, out_rows, width), jnp.float32),
            pltpu.VMEM((total, out_rows, width), jnp.float32),
            pltpu.SemaphoreType.DMA((total + 1,)),
            pltpu.SemaphoreType.DMA((total + 1,)),
        ],
        compiler_params=pltpu.CompilerParams(collective_id=collective_id, has_side_effects=True),
    )(panels, home, tokens, lengths)


def grid_kernel(width, send_ref, out_ref, landed, send_sems, recv_sems):
    me = lax.axis_index("grp")
    core = lax.axis_index("tp") % 2
    col, row = me % width, me // width

    def node(c, r):
        return lax.rem(r + width, width) * width + lax.rem(c + width, width)

    def along(dim, c, r, k):
        return node(c + k, r) if dim == 0 else node(c, r + k)

    barrier = pltpu.get_barrier_semaphore()
    neighbours = [node(col + 1, row), node(col - 1, row), node(col, row + 1), node(col, row - 1)]
    for neighbour in neighbours:
        pl.semaphore_signal(barrier, inc=1, device_id={"grp": neighbour}, device_id_type=MESH)
    pl.semaphore_wait(barrier, 4)

    landed[me] = send_ref[...]
    sends = []

    def send(source, origin, half, target):
        copy = pltpu.make_async_remote_copy(
            src_ref=source,
            dst_ref=landed.at[origin, half],
            send_sem=send_sems.at[len(sends)],
            recv_sem=recv_sems.at[origin, half],
            device_id={"grp": target},
            device_id_type=MESH,
        )
        copy.start()
        sends.append(copy)

    def arrive(origin, half):
        pltpu.make_async_remote_copy(
            src_ref=send_ref.at[half],
            dst_ref=landed.at[origin, half],
            send_sem=send_sems.at[0],
            recv_sem=recv_sems.at[origin, half],
            device_id={"grp": neighbours[0]},
            device_id_type=MESH,
        ).wait_recv()

    ahead = 1 - 2 * core

    def phase(lines, half, dim):
        for k in (1, -1):
            for line in lines:
                origin = along(1 - dim, col, row, line)
                source = send_ref.at[half] if line == 0 else landed.at[origin, half]
                send(source, origin, half, along(dim, col, row, k))
        for line in lines:
            for k in (1, -1):
                arrive(along(dim, along(1 - dim, col, row, line) % width, along(1 - dim, col, row, line) // width, k), half)
        for line in lines:
            base = along(1 - dim, col, row, line)
            bc, br = base % width, base // width
            send(landed.at[along(dim, bc, br, -ahead), half], along(dim, bc, br, -ahead), half,
                 along(dim, col, row, ahead))
        for line in lines:
            base = along(1 - dim, col, row, line)
            arrive(along(dim, base % width, base // width, 2), half)

    phase([0], 0, 0)
    phase([0], 1, 1)
    phase([0, 1, -1, 2], 0, 1)
    phase([0, 1, -1, 2], 1, 0)
    for copy in sends:
        copy.wait_send()
    out_ref[...] = landed[...]


def grid_gather(x, width, collective_id):
    count = width * width
    x = x.reshape((2, x.shape[0] // 2) + x.shape[1:])
    gathered = pl.pallas_call(
        functools.partial(grid_kernel, width),
        out_shape=jax.ShapeDtypeStruct((count,) + x.shape, x.dtype),
        in_specs=[pl.BlockSpec(memory_space=pltpu.VMEM)],
        out_specs=pl.BlockSpec(memory_space=pltpu.VMEM),
        scratch_shapes=[
            pltpu.VMEM((count,) + x.shape, x.dtype),
            pltpu.SemaphoreType.DMA((2 * (count - 1),)),
            pltpu.SemaphoreType.DMA((count, 2)),
        ],
        compiler_params=pltpu.CompilerParams(collective_id=collective_id, has_side_effects=True),
    )(x)
    return gathered.reshape((count, x.shape[0] * x.shape[1]) + x.shape[2:])


def gather_hbm_kernel(axis, count, send_ref, out_ref, send_sems, recv_sems, local_sem):
    me = lax.axis_index(axis)
    barrier = pltpu.get_barrier_semaphore()
    for step in range(1, count):
        peer = lax.rem(me + step, count)
        pl.semaphore_signal(barrier, inc=1, device_id={axis: peer}, device_id_type=MESH)
    pl.semaphore_wait(barrier, count - 1)
    copies = []
    for step in range(1, count):
        peer = lax.rem(me + step, count)
        copy = pltpu.make_async_remote_copy(
            src_ref=send_ref,
            dst_ref=out_ref.at[me],
            send_sem=send_sems.at[step],
            recv_sem=recv_sems.at[step],
            device_id={axis: peer},
            device_id_type=MESH,
        )
        copy.start()
        copies.append(copy)
    local = pltpu.make_async_copy(send_ref, out_ref.at[me], local_sem)
    local.start()
    for copy in copies:
        copy.wait()
    local.wait()


def gather_hbm(x, axis, count, collective_id):
    return pl.pallas_call(
        functools.partial(gather_hbm_kernel, axis, count),
        out_shape=jax.ShapeDtypeStruct((count,) + x.shape, x.dtype),
        in_specs=[pl.BlockSpec(memory_space=pltpu.VMEM)],
        out_specs=pl.BlockSpec(memory_space=pl.ANY),
        scratch_shapes=[
            pltpu.SemaphoreType.DMA((count,)),
            pltpu.SemaphoreType.DMA((count,)),
            pltpu.SemaphoreType.DMA(()),
        ],
        compiler_params=pltpu.CompilerParams(collective_id=collective_id, has_side_effects=True),
    )(x)


def weights_gather_kernel(count, own_ref, for_partner_ref, out_ref, partner_rows,
                          send_sems, recv_sems, partner_sems, local_sems):
    me = lax.axis_index("grp")
    member = lax.axis_index("tp")
    partner = member + 1 - 2 * (member % 2)
    rows = own_ref.shape[0]
    barrier = pltpu.get_barrier_semaphore()
    pl.semaphore_signal(barrier, inc=1, device_id={"tp": partner}, device_id_type=MESH)
    for step in range(1, count):
        peer = lax.rem(me + step, count)
        pl.semaphore_signal(barrier, inc=1, device_id={"grp": peer}, device_id_type=MESH)
    pl.semaphore_wait(barrier, count)
    to_partner = pltpu.make_async_remote_copy(
        src_ref=for_partner_ref, dst_ref=partner_rows, send_sem=partner_sems.at[0],
        recv_sem=partner_sems.at[1], device_id={"tp": partner}, device_id_type=MESH,
    )
    to_partner.start()
    copies = []

    def spread(part, source, window):
        for step in range(1, count):
            peer = lax.rem(me + step, count)
            copy = pltpu.make_async_remote_copy(
                src_ref=source,
                dst_ref=out_ref.at[me, window],
                send_sem=send_sems.at[part, step],
                recv_sem=recv_sems.at[part, step],
                device_id={"grp": peer},
                device_id_type=MESH,
            )
            copy.start()
            copies.append(copy)
        local = pltpu.make_async_copy(source, out_ref.at[me, window], local_sems.at[part])
        local.start()
        copies.append(local)

    spread(0, own_ref, pl.ds(0, rows))
    to_partner.wait()
    spread(1, partner_rows, pl.ds(rows, partner_rows.shape[0]))
    for copy in copies:
        copy.wait()


def weights_gather(own, for_partner, count, collective_id):
    rows = own.shape[0] + for_partner.shape[0]
    return pl.pallas_call(
        functools.partial(weights_gather_kernel, count),
        out_shape=jax.ShapeDtypeStruct((count, rows) + own.shape[1:], own.dtype),
        in_specs=[pl.BlockSpec(memory_space=pltpu.VMEM)] * 2,
        out_specs=pl.BlockSpec(memory_space=pl.ANY),
        scratch_shapes=[
            pltpu.VMEM(for_partner.shape, for_partner.dtype),
            pltpu.SemaphoreType.DMA((2, count)),
            pltpu.SemaphoreType.DMA((2, count)),
            pltpu.SemaphoreType.DMA((2,)),
            pltpu.SemaphoreType.DMA((2,)),
        ],
        compiler_params=pltpu.CompilerParams(collective_id=collective_id, has_side_effects=True),
    )(own, for_partner)


def exchange_kernel(axis, count, scatter, send_ref, out_ref, landed, send_sems, recv_sems):
    me = lax.axis_index(axis)
    barrier = pltpu.get_barrier_semaphore()
    for step in range(1, count):
        peer = lax.rem(me + step, count)
        pl.semaphore_signal(barrier, inc=1, device_id={axis: peer}, device_id_type=MESH)
    pl.semaphore_wait(barrier, count - 1)
    copies = []
    for step in range(1, count):
        peer = lax.rem(me + step, count)
        source = send_ref.at[peer] if scatter else send_ref
        copy = pltpu.make_async_remote_copy(
            src_ref=source,
            dst_ref=landed.at[me],
            send_sem=send_sems.at[step],
            recv_sem=recv_sems.at[step],
            device_id={axis: peer},
            device_id_type=MESH,
        )
        copy.start()
        copies.append(copy)
    landed[me] = send_ref[me] if scatter else send_ref[...]
    for copy in copies:
        copy.wait()
    if scatter:
        width = landed.shape[-1]
        for source in range(count):
            out_ref[:, source * width:(source + 1) * width] = landed[source]
    else:
        out_ref[...] = landed[...]


def exchange(x, axis, count, scatter, collective_id):
    piece = x.shape[1:] if scatter else x.shape
    result = (piece[0], count * piece[1]) if scatter else (count,) + piece
    return pl.pallas_call(
        functools.partial(exchange_kernel, axis, count, scatter),
        out_shape=jax.ShapeDtypeStruct(result, x.dtype),
        in_specs=[pl.BlockSpec(memory_space=pltpu.VMEM)],
        out_specs=pl.BlockSpec(memory_space=pltpu.VMEM),
        scratch_shapes=[
            pltpu.VMEM((count,) + piece, x.dtype),
            pltpu.SemaphoreType.DMA((count,)),
            pltpu.SemaphoreType.DMA((count,)),
        ],
        compiler_params=pltpu.CompilerParams(collective_id=collective_id, has_side_effects=True),
    )(x)


def on_device(tokens, trainer_panels, panel_home, lengths):
    tp_count = lax.axis_size("tp")
    grp_count = lax.axis_size("grp")
    member_id = lax.axis_index("tp")
    kv_count = (panel_home.shape[0] - tp_count) // 2
    group_size = tp_count // kv_count
    head_dim = trainer_panels.shape[2]
    block_rows = trainer_panels.shape[1]
    half_rows = block_rows // 2
    seq_total = tokens.shape[0]

    return whole(trainer_panels, panel_home, tokens, lengths, tp_count // 2, grp_count, 4)


def solution(mesh):
    placed = (P("grp", None), P("tp", "grp", None), P(), P("grp", None))
    return jax.shard_map(
        on_device, mesh=mesh, in_specs=placed, out_specs=P(("grp", "tp"), None), check_vma=False
    )
```

```python
import functools

import jax
import jax.numpy as jnp
from jax import lax
from jax.experimental import pallas as pl
from jax.experimental.pallas import tpu as pltpu
from jax.sharding import PartitionSpec as P

MESH = pl.DeviceIdType.MESH


def ring_kernel(count, stride, chunks, send_ref, out_ref, landed, send_sems, recv_sems):
    me = lax.axis_index("tp")
    total = count * stride
    right, left = lax.rem(me + stride, total), lax.rem(me + total - stride, total)
    spot = me // stride
    barrier = pltpu.get_barrier_semaphore()
    for neighbour in (left, right):
        pl.semaphore_signal(barrier, inc=1, device_id={"tp": neighbour}, device_id_type=MESH)
    pl.semaphore_wait(barrier, 2)

    def incoming(origin, chunk):
        return pltpu.make_async_remote_copy(
            src_ref=send_ref.at[chunk],
            dst_ref=landed.at[origin, chunk],
            send_sem=send_sems.at[0, 0, 0],
            recv_sem=recv_sems.at[origin, chunk],
            device_id={"tp": right},
            device_id_type=MESH,
        )

    landed[spot] = send_ref[...]
    sends = []
    far_right, far_left = count // 2, (count - 1) // 2
    for step in range(1, far_right + 1):
        for chunk in range(chunks):
            streams = [(0, right, lax.rem(spot + count - (step - 1), count))]
            if step <= far_left:
                streams.append((1, left, lax.rem(spot + step - 1, count)))
            for way, target, origin in streams:
                if step > 1:
                    incoming(origin, chunk).wait_recv()
                source = send_ref.at[chunk] if step == 1 else landed.at[origin, chunk]
                copy = pltpu.make_async_remote_copy(
                    src_ref=source,
                    dst_ref=landed.at[origin, chunk],
                    send_sem=send_sems.at[way, step, chunk],
                    recv_sem=recv_sems.at[origin, chunk],
                    device_id={"tp": target},
                    device_id_type=MESH,
                )
                copy.start()
                sends.append(copy)
    for chunk in range(chunks):
        incoming(lax.rem(spot + count - far_right, count), chunk).wait_recv()
        incoming(lax.rem(spot + far_left, count), chunk).wait_recv()
    for copy in sends:
        copy.wait_send()
    out_ref[...] = landed[...]


def ring_gather(x, count, stride, chunks, collective_id):
    x = x.reshape((chunks, x.shape[0] // chunks) + x.shape[1:])
    gathered = pl.pallas_call(
        functools.partial(ring_kernel, count, stride, chunks),
        out_shape=jax.ShapeDtypeStruct((count,) + x.shape, x.dtype),
        in_specs=[pl.BlockSpec(memory_space=pltpu.VMEM)],
        out_specs=pl.BlockSpec(memory_space=pltpu.VMEM),
        scratch_shapes=[
            pltpu.VMEM((count,) + x.shape, x.dtype),
            pltpu.SemaphoreType.DMA((2, count // 2 + 1, chunks)),
            pltpu.SemaphoreType.DMA((count, chunks)),
        ],
        compiler_params=pltpu.CompilerParams(collective_id=collective_id, has_side_effects=True),
    )(x)
    return gathered.reshape((count * x.shape[0] * x.shape[1],) + x.shape[2:])


def chip_ring_kernel(count, groups, panels_ref, home_ref, out_ref, landed, send_sems, recv_sems,
                     own_ref, partner_ref, partner_rows, grp_send_sems, grp_recv_sems, partner_sems, local_sems,
                     greet=True):
    me = lax.axis_index("tp")
    here = lax.axis_index("grp")
    total = 2 * count
    core = me % 2
    partner = me + 1 - 2 * core
    right, left = lax.rem(me + 2, total), lax.rem(me + total - 2, total)
    spot = me // 2
    half = panels_ref.shape[1] // 2
    if greet:
        barrier = pltpu.get_barrier_semaphore()
        for neighbour in (left, right, partner):
            pl.semaphore_signal(barrier, inc=1, device_id={"tp": neighbour}, device_id_type=MESH)
        for step in range(1, groups):
            peer = lax.rem(here + step, groups)
            pl.semaphore_signal(barrier, inc=1, device_id={"grp": peer}, device_id_type=MESH)
        pl.semaphore_wait(barrier, 2 + groups)

    def rows_of(slot, which):
        return panels_ref.at[slot, pl.ds(pl.multiple_of(which * half, 16), half)]

    def incoming(origin, chunk):
        return pltpu.make_async_remote_copy(
            src_ref=rows_of(0, 0),
            dst_ref=landed.at[origin, chunk],
            send_sem=send_sems.at[0, 0, 0],
            recv_sem=recv_sems.at[origin, chunk],
            device_id={"tp": right},
            device_id_type=MESH,
        )

    sends = []

    def send(source, origin, chunk, sem, target):
        copy = pltpu.make_async_remote_copy(
            src_ref=source,
            dst_ref=landed.at[origin, chunk],
            send_sem=sem,
            recv_sem=recv_sems.at[origin, chunk],
            device_id={"tp": target},
            device_id_type=MESH,
        )
        copy.start()
        sends.append(copy)

    own = [2 * core + j for j in range(2)]
    theirs = [2 * (1 - core) + j for j in range(2)]
    for j in range(2):
        send(rows_of(j, 1 - core), spot, own[j], send_sems.at[0, 0, 1 + j], partner)
        landed[spot, own[j]] = rows_of(j, core)[...]
    far_right, far_left = count // 2, (count - 1) // 2
    first = [(rows_of(j, core), own[j]) for j in range(2)] + [(None, theirs[j]) for j in range(2)]
    for position, (source, chunk) in enumerate(first):
        if source is None:
            incoming(spot, chunk).wait_recv()
            source = landed.at[spot, chunk]
        send(source, spot, chunk, send_sems.at[0, 1, position], right)
        if far_left >= 1:
            send(source, spot, chunk, send_sems.at[1, 1, position], left)
    for step in range(2, far_right + 1):
        for chunk in range(4):
            streams = [(0, right, lax.rem(spot + count - (step - 1), count))]
            if step <= far_left:
                streams.append((1, left, lax.rem(spot + step - 1, count)))
            for way, target, origin in streams:
                incoming(origin, chunk).wait_recv()
                send(landed.at[origin, chunk], origin, chunk, send_sems.at[way, step, chunk], target)
    for chunk in range(4):
        incoming(lax.rem(spot + count - far_right, count), chunk).wait_recv()
        incoming(lax.rem(spot + far_left, count), chunk).wait_recv()
    for copy in sends:
        copy.wait_send()
    heads = total
    kv_heads = (home_ref.shape[0] - heads) // 2
    group = heads // kv_heads
    quarter = me % group
    kv_panel = heads + me // group + kv_heads * (quarter // 2)
    chip_slots = landed.shape[1]

    def block(panel):
        slot = home_ref[panel]
        return landed[slot // chip_slots, slot % chip_slots]

    own_ref[0:half] = block(me)
    own_ref[half:2 * half] = block(kv_panel)
    partner_ref[...] = block(partner)

    to_partner = pltpu.make_async_remote_copy(
        src_ref=partner_ref, dst_ref=partner_rows, send_sem=partner_sems.at[0],
        recv_sem=partner_sems.at[1], device_id={"tp": partner}, device_id_type=MESH,
    )
    to_partner.start()
    copies, local_copies = [], []

    def spread(part, source, window):
        for step in range(1, groups):
            peer = lax.rem(here + step, groups)
            copy = pltpu.make_async_remote_copy(
                src_ref=source,
                dst_ref=out_ref.at[here, window],
                send_sem=grp_send_sems.at[part, step],
                recv_sem=grp_recv_sems.at[part, step],
                device_id={"grp": peer},
                device_id_type=MESH,
            )
            copy.start()
            copies.append(copy)
        local = pltpu.make_async_copy(source, out_ref.at[here, window], local_sems.at[part])
        local.start()
        local_copies.append(local)

    spread(0, own_ref, pl.ds(0, 2 * half))
    to_partner.wait()
    spread(1, partner_rows, pl.ds(2 * half, half))
    for copy in local_copies:
        copy.wait()
    if greet:
        for copy in copies:
            copy.wait()
        return None
    windows = [(own_ref, pl.ds(0, 2 * half)), (partner_rows, pl.ds(2 * half, half))]

    def arrive(source):
        step = lax.rem(here + groups - source, groups)

        @pl.when(step != 0)
        def _():
            for part, (shape_ref, window) in enumerate(windows):
                pltpu.make_async_remote_copy(
                    src_ref=shape_ref,
                    dst_ref=out_ref.at[here, window],
                    send_sem=grp_send_sems.at[part, 0],
                    recv_sem=grp_recv_sems.at[part, step],
                    device_id={"grp": lax.rem(here + 1, groups)},
                    device_id_type=MESH,
                ).wait_recv()

    def finish():
        for copy in copies:
            copy.wait_send()

    return arrive, finish


def chip_ring_gather(panels, home, count, groups, collective_id):
    slots, rows, width = panels.shape
    return pl.pallas_call(
        functools.partial(chip_ring_kernel, count, groups),
        out_shape=jax.ShapeDtypeStruct((groups, rows + rows // 2, width), panels.dtype),
        in_specs=[pl.BlockSpec(memory_space=pltpu.VMEM), pl.BlockSpec(memory_space=pltpu.SMEM)],
        out_specs=pl.BlockSpec(memory_space=pl.ANY),
        scratch_shapes=[
            pltpu.VMEM((count, 2 * slots, rows // 2, width), panels.dtype),
            pltpu.SemaphoreType.DMA((2, count // 2 + 1, 2 * slots)),
            pltpu.SemaphoreType.DMA((count, 2 * slots)),
            pltpu.VMEM((rows, width), panels.dtype),
            pltpu.VMEM((rows // 2, width), panels.dtype),
            pltpu.VMEM((rows // 2, width), panels.dtype),
            pltpu.SemaphoreType.DMA((2, groups)),
            pltpu.SemaphoreType.DMA((2, groups)),
            pltpu.SemaphoreType.DMA((2,)),
            pltpu.SemaphoreType.DMA((2,)),
        ],
        compiler_params=pltpu.CompilerParams(collective_id=collective_id, has_side_effects=True),
    )(panels, home)


def kv_share_kernel(part_ref, out_ref, partner_part, mine, theirs, send_sems, recv_sems):
    me = lax.axis_index("tp")
    partner = me + 1 - 2 * (me % 2)
    across = me + 2 - 4 * ((me // 2) % 2)
    barrier = pltpu.get_barrier_semaphore()
    for neighbour in (partner, across):
        pl.semaphore_signal(barrier, inc=1, device_id={"tp": neighbour}, device_id_type=MESH)
    pl.semaphore_wait(barrier, 2)
    first = pltpu.make_async_remote_copy(
        src_ref=part_ref, dst_ref=partner_part, send_sem=send_sems.at[0], recv_sem=recv_sems.at[0],
        device_id={"tp": partner}, device_id_type=MESH,
    )
    first.start()
    first.wait()
    mine[...] = (part_ref[...] + partner_part[...]).astype(mine.dtype)
    second = pltpu.make_async_remote_copy(
        src_ref=mine, dst_ref=theirs, send_sem=send_sems.at[1], recv_sem=recv_sems.at[1],
        device_id={"tp": across}, device_id_type=MESH,
    )
    second.start()
    second.wait()
    holds_k = (me % 4) < 2
    out_ref[0] = jnp.where(holds_k, mine[...], theirs[...])
    out_ref[1] = jnp.where(holds_k, theirs[...], mine[...])


def kv_share(part, collective_id):
    return pl.pallas_call(
        kv_share_kernel,
        out_shape=jax.ShapeDtypeStruct((2,) + part.shape, jnp.bfloat16),
        in_specs=[pl.BlockSpec(memory_space=pltpu.VMEM)],
        out_specs=pl.BlockSpec(memory_space=pltpu.VMEM),
        scratch_shapes=[
            pltpu.VMEM(part.shape, part.dtype),
            pltpu.VMEM(part.shape, jnp.bfloat16),
            pltpu.VMEM(part.shape, jnp.bfloat16),
            pltpu.SemaphoreType.DMA((2,)),
            pltpu.SemaphoreType.DMA((2,)),
        ],
        compiler_params=pltpu.CompilerParams(collective_id=collective_id, has_side_effects=True),
    )(part)


def tail_kernel(count, scale, tokens_ref, gathered_hbm, lengths_ref, out_ref,
                gathered, load_sem, part_ref, partner_part, mine, theirs, staged, landed, send_sems, recv_sems,
                greet=True, arrive=None):
    width = landed.shape[-1]
    me = lax.axis_index("tp")
    partner = me + 1 - 2 * (me % 2)
    across = me + 2 - 4 * ((me // 2) % 2)
    if greet:
        load = pltpu.make_async_copy(gathered_hbm, gathered, load_sem)
        load.start()
        barrier = pltpu.get_barrier_semaphore()
        for step in range(1, count):
            peer = lax.rem(me + step, count)
            pl.semaphore_signal(barrier, inc=1, device_id={"tp": peer}, device_id_type=MESH)
        load.wait()
    core = me % 2
    half = gathered.shape[1] // 3
    sources = gathered.shape[0]
    first_half = core == 0
    projected = jnp.zeros((tokens_ref.shape[0], 2 * width), jnp.float32)
    for pair in range(sources // 2):
        if arrive is not None:
            arrive(2 * pair)
            arrive(2 * pair + 1)
        q_parts, kv_parts = [], []
        for source in (2 * pair, 2 * pair + 1):
            here = gathered[source, 0:half]
            kv = gathered[source, half:2 * half]
            there = gathered[source, 2 * half:3 * half]
            zero = jnp.zeros_like(kv)
            q_parts.append(jnp.where(first_half, jnp.concatenate([here, there], axis=0),
                                     jnp.concatenate([there, here], axis=0)))
            kv_parts.append(jnp.where(first_half, jnp.concatenate([kv, zero], axis=0),
                                      jnp.concatenate([zero, kv], axis=0)))
        slab = jnp.concatenate(
            [jnp.concatenate(q_parts, axis=0), jnp.concatenate(kv_parts, axis=0)], axis=1
        )
        columns = slab.shape[0]
        projected = projected + jnp.dot(
            tokens_ref[:, pair * columns:(pair + 1) * columns], slab, preferred_element_type=jnp.float32
        )
    part_ref[...] = projected[:, width:]
    query = projected[:, :width].astype(jnp.bfloat16)
    if greet:
        pl.semaphore_wait(barrier, count - 1)
    first = pltpu.make_async_remote_copy(
        src_ref=part_ref, dst_ref=partner_part, send_sem=send_sems.at[0], recv_sem=recv_sems.at[0],
        device_id={"tp": partner}, device_id_type=MESH,
    )
    first.start()
    first.wait()
    mine[...] = (part_ref[...] + partner_part[...]).astype(mine.dtype)
    second = pltpu.make_async_remote_copy(
        src_ref=mine, dst_ref=theirs, send_sem=send_sems.at[1], recv_sem=recv_sems.at[1],
        device_id={"tp": across}, device_id_type=MESH,
    )
    second.start()
    second.wait()
    holds_k = (me % 4) < 2
    keys = jnp.where(holds_k, mine[...], theirs[...])
    values = jnp.where(holds_k, theirs[...], mine[...])

    scores = lax.dot_general(
        query, keys, (((1,), (1,)), ((), ())), preferred_element_type=jnp.float32
    ) * scale
    seq = scores.shape[0]
    row = lax.broadcasted_iota(jnp.int32, (seq, seq), 0)
    col = lax.broadcasted_iota(jnp.int32, (seq, seq), 1)
    row_segment = jnp.zeros((seq, seq), jnp.int32)
    col_segment = jnp.zeros((seq, seq), jnp.int32)
    bound = lengths_ref[0, 0] * 0
    for response in range(lengths_ref.shape[1]):
        bound = bound + lengths_ref[0, response]
        row_segment = row_segment + (row >= bound).astype(jnp.int32)
        col_segment = col_segment + (col >= bound).astype(jnp.int32)
    allowed = (row_segment == col_segment) & (col <= row)
    masked = jnp.where(allowed, scores, -jnp.inf)
    peak = jnp.max(masked, axis=1, keepdims=True)
    weights = jnp.exp(masked - peak)
    probs = (weights / jnp.sum(weights, axis=1, keepdims=True)).astype(jnp.bfloat16)
    context = jnp.dot(probs, values, preferred_element_type=jnp.float32)
    rows = seq // count
    for target in range(count):
        staged[target] = context[target * rows:(target + 1) * rows]

    copies = []
    for step in range(1, count):
        peer = lax.rem(me + step, count)
        copy = pltpu.make_async_remote_copy(
            src_ref=staged.at[peer],
            dst_ref=landed.at[me],
            send_sem=send_sems.at[1 + step],
            recv_sem=recv_sems.at[1 + step],
            device_id={"tp": peer},
            device_id_type=MESH,
        )
        copy.start()
        copies.append(copy)
    landed[me] = staged[me]
    for copy in copies:
        copy.wait()
    for source in range(count):
        out_ref[:, source * width:(source + 1) * width] = landed[source]


def tail(tokens, gathered, lengths, count, collective_id):
    seq, width = tokens.shape[0], gathered.shape[2]
    part = jax.ShapeDtypeStruct((seq, width), jnp.float32)
    rows = seq // count
    vmem = pl.BlockSpec(memory_space=pltpu.VMEM)
    return pl.pallas_call(
        functools.partial(tail_kernel, count, width ** (-0.5)),
        out_shape=jax.ShapeDtypeStruct((rows, count * width), jnp.float32),
        in_specs=[vmem, pl.BlockSpec(memory_space=pl.ANY), pl.BlockSpec(memory_space=pltpu.SMEM)],
        out_specs=vmem,
        scratch_shapes=[
            pltpu.VMEM(gathered.shape, gathered.dtype),
            pltpu.SemaphoreType.DMA(()),
            pltpu.VMEM(part.shape, part.dtype),
            pltpu.VMEM(part.shape, part.dtype),
            pltpu.VMEM(part.shape, jnp.bfloat16),
            pltpu.VMEM(part.shape, jnp.bfloat16),
            pltpu.VMEM((count, rows, width), jnp.float32),
            pltpu.VMEM((count, rows, width), jnp.float32),
            pltpu.SemaphoreType.DMA((count + 1,)),
            pltpu.SemaphoreType.DMA((count + 1,)),
        ],
        compiler_params=pltpu.CompilerParams(collective_id=collective_id, has_side_effects=True),
    )(tokens, gathered, lengths)


def whole_kernel(count, groups, scale, panels_ref, home_ref, tokens_ref, lengths_ref, out_ref, *scratch):
    ring_scratch, gathered, tail_scratch = scratch[:10], scratch[10], scratch[11:]
    me = lax.axis_index("tp")
    here = lax.axis_index("grp")
    total = 2 * count
    barrier = pltpu.get_barrier_semaphore()
    for step in range(1, total):
        peer = lax.rem(me + step, total)
        pl.semaphore_signal(barrier, inc=1, device_id={"tp": peer}, device_id_type=MESH)
    for step in range(1, groups):
        peer = lax.rem(here + step, groups)
        pl.semaphore_signal(barrier, inc=1, device_id={"grp": peer}, device_id_type=MESH)
    pl.semaphore_wait(barrier, total + groups - 2)
    arrive, finish = chip_ring_kernel(count, groups, panels_ref, home_ref, gathered, *ring_scratch, greet=False)
    tail_kernel(total, scale, tokens_ref, None, lengths_ref, out_ref, gathered, None, *tail_scratch, greet=False,
                arrive=arrive)
    finish()


def whole(panels, home, tokens, lengths, count, groups, collective_id):
    slots, rows, width = panels.shape
    seq = tokens.shape[0]
    total = 2 * count
    out_rows = seq // total
    part = (seq, width)
    vmem = pl.BlockSpec(memory_space=pltpu.VMEM)
    smem = pl.BlockSpec(memory_space=pltpu.SMEM)
    return pl.pallas_call(
        functools.partial(whole_kernel, count, groups, width ** (-0.5)),
        out_shape=jax.ShapeDtypeStruct((out_rows, total * width), jnp.float32),
        in_specs=[vmem, smem, vmem, smem],
        out_specs=vmem,
        scratch_shapes=[
            pltpu.VMEM((count, 2 * slots, rows // 2, width), panels.dtype),
            pltpu.SemaphoreType.DMA((2, count // 2 + 1, 2 * slots)),
            pltpu.SemaphoreType.DMA((count, 2 * slots)),
            pltpu.VMEM((rows, width), panels.dtype),
            pltpu.VMEM((rows // 2, width), panels.dtype),
            pltpu.VMEM((rows // 2, width), panels.dtype),
            pltpu.SemaphoreType.DMA((2, groups)),
            pltpu.SemaphoreType.DMA((2, groups)),
            pltpu.SemaphoreType.DMA((2,)),
            pltpu.SemaphoreType.DMA((2,)),
            pltpu.VMEM((groups, rows + rows // 2, width), panels.dtype),
            pltpu.VMEM(part, jnp.float32),
            pltpu.VMEM(part, jnp.float32),
            pltpu.VMEM(part, jnp.bfloat16),
            pltpu.VMEM(part, jnp.bfloat16),
            pltpu.VMEM((total, out_rows, width), jnp.float32),
            pltpu.VMEM((total, out_rows, width), jnp.float32),
            pltpu.SemaphoreType.DMA((total + 1,)),
            pltpu.SemaphoreType.DMA((total + 1,)),
        ],
        compiler_params=pltpu.CompilerParams(collective_id=collective_id, has_side_effects=True),
    )(panels, home, tokens, lengths)


def grid_kernel(width, send_ref, out_ref, landed, send_sems, recv_sems):
    me = lax.axis_index("grp")
    core = lax.axis_index("tp") % 2
    col, row = me % width, me // width

    def node(c, r):
        return lax.rem(r + width, width) * width + lax.rem(c + width, width)

    def along(dim, c, r, k):
        return node(c + k, r) if dim == 0 else node(c, r + k)

    barrier = pltpu.get_barrier_semaphore()
    neighbours = [node(col + 1, row), node(col - 1, row), node(col, row + 1), node(col, row - 1)]
    for neighbour in neighbours:
        pl.semaphore_signal(barrier, inc=1, device_id={"grp": neighbour}, device_id_type=MESH)
    pl.semaphore_wait(barrier, 4)

    landed[me] = send_ref[...]
    sends = []

    def send(source, origin, half, target):
        copy = pltpu.make_async_remote_copy(
            src_ref=source,
            dst_ref=landed.at[origin, half],
            send_sem=send_sems.at[len(sends)],
            recv_sem=recv_sems.at[origin, half],
            device_id={"grp": target},
            device_id_type=MESH,
        )
        copy.start()
        sends.append(copy)

    def arrive(origin, half):
        pltpu.make_async_remote_copy(
            src_ref=send_ref.at[half],
            dst_ref=landed.at[origin, half],
            send_sem=send_sems.at[0],
            recv_sem=recv_sems.at[origin, half],
            device_id={"grp": neighbours[0]},
            device_id_type=MESH,
        ).wait_recv()

    ahead = 1 - 2 * core

    def phase(lines, half, dim):
        for k in (1, -1):
            for line in lines:
                origin = along(1 - dim, col, row, line)
                source = send_ref.at[half] if line == 0 else landed.at[origin, half]
                send(source, origin, half, along(dim, col, row, k))
        for line in lines:
            for k in (1, -1):
                arrive(along(dim, along(1 - dim, col, row, line) % width, along(1 - dim, col, row, line) // width, k), half)
        for line in lines:
            base = along(1 - dim, col, row, line)
            bc, br = base % width, base // width
            send(landed.at[along(dim, bc, br, -ahead), half], along(dim, bc, br, -ahead), half,
                 along(dim, col, row, ahead))
        for line in lines:
            base = along(1 - dim, col, row, line)
            arrive(along(dim, base % width, base // width, 2), half)

    phase([0], 0, 0)
    phase([0], 1, 1)
    phase([0, 1, -1, 2], 0, 1)
    phase([0, 1, -1, 2], 1, 0)
    for copy in sends:
        copy.wait_send()
    out_ref[...] = landed[...]


def grid_gather(x, width, collective_id):
    count = width * width
    x = x.reshape((2, x.shape[0] // 2) + x.shape[1:])
    gathered = pl.pallas_call(
        functools.partial(grid_kernel, width),
        out_shape=jax.ShapeDtypeStruct((count,) + x.shape, x.dtype),
        in_specs=[pl.BlockSpec(memory_space=pltpu.VMEM)],
        out_specs=pl.BlockSpec(memory_space=pltpu.VMEM),
        scratch_shapes=[
            pltpu.VMEM((count,) + x.shape, x.dtype),
            pltpu.SemaphoreType.DMA((2 * (count - 1),)),
            pltpu.SemaphoreType.DMA((count, 2)),
        ],
        compiler_params=pltpu.CompilerParams(collective_id=collective_id, has_side_effects=True),
    )(x)
    return gathered.reshape((count, x.shape[0] * x.shape[1]) + x.shape[2:])


def gather_hbm_kernel(axis, count, send_ref, out_ref, send_sems, recv_sems, local_sem):
    me = lax.axis_index(axis)
    barrier = pltpu.get_barrier_semaphore()
    for step in range(1, count):
        peer = lax.rem(me + step, count)
        pl.semaphore_signal(barrier, inc=1, device_id={axis: peer}, device_id_type=MESH)
    pl.semaphore_wait(barrier, count - 1)
    copies = []
    for step in range(1, count):
        peer = lax.rem(me + step, count)
        copy = pltpu.make_async_remote_copy(
            src_ref=send_ref,
            dst_ref=out_ref.at[me],
            send_sem=send_sems.at[step],
            recv_sem=recv_sems.at[step],
            device_id={axis: peer},
            device_id_type=MESH,
        )
        copy.start()
        copies.append(copy)
    local = pltpu.make_async_copy(send_ref, out_ref.at[me], local_sem)
    local.start()
    for copy in copies:
        copy.wait()
    local.wait()


def gather_hbm(x, axis, count, collective_id):
    return pl.pallas_call(
        functools.partial(gather_hbm_kernel, axis, count),
        out_shape=jax.ShapeDtypeStruct((count,) + x.shape, x.dtype),
        in_specs=[pl.BlockSpec(memory_space=pltpu.VMEM)],
        out_specs=pl.BlockSpec(memory_space=pl.ANY),
        scratch_shapes=[
            pltpu.SemaphoreType.DMA((count,)),
            pltpu.SemaphoreType.DMA((count,)),
            pltpu.SemaphoreType.DMA(()),
        ],
        compiler_params=pltpu.CompilerParams(collective_id=collective_id, has_side_effects=True),
    )(x)


def weights_gather_kernel(count, own_ref, for_partner_ref, out_ref, partner_rows,
                          send_sems, recv_sems, partner_sems, local_sems):
    me = lax.axis_index("grp")
    member = lax.axis_index("tp")
    partner = member + 1 - 2 * (member % 2)
    rows = own_ref.shape[0]
    barrier = pltpu.get_barrier_semaphore()
    pl.semaphore_signal(barrier, inc=1, device_id={"tp": partner}, device_id_type=MESH)
    for step in range(1, count):
        peer = lax.rem(me + step, count)
        pl.semaphore_signal(barrier, inc=1, device_id={"grp": peer}, device_id_type=MESH)
    pl.semaphore_wait(barrier, count)
    to_partner = pltpu.make_async_remote_copy(
        src_ref=for_partner_ref, dst_ref=partner_rows, send_sem=partner_sems.at[0],
        recv_sem=partner_sems.at[1], device_id={"tp": partner}, device_id_type=MESH,
    )
    to_partner.start()
    copies = []

    def spread(part, source, window):
        for step in range(1, count):
            peer = lax.rem(me + step, count)
            copy = pltpu.make_async_remote_copy(
                src_ref=source,
                dst_ref=out_ref.at[me, window],
                send_sem=send_sems.at[part, step],
                recv_sem=recv_sems.at[part, step],
                device_id={"grp": peer},
                device_id_type=MESH,
            )
            copy.start()
            copies.append(copy)
        local = pltpu.make_async_copy(source, out_ref.at[me, window], local_sems.at[part])
        local.start()
        copies.append(local)

    spread(0, own_ref, pl.ds(0, rows))
    to_partner.wait()
    spread(1, partner_rows, pl.ds(rows, partner_rows.shape[0]))
    for copy in copies:
        copy.wait()


def weights_gather(own, for_partner, count, collective_id):
    rows = own.shape[0] + for_partner.shape[0]
    return pl.pallas_call(
        functools.partial(weights_gather_kernel, count),
        out_shape=jax.ShapeDtypeStruct((count, rows) + own.shape[1:], own.dtype),
        in_specs=[pl.BlockSpec(memory_space=pltpu.VMEM)] * 2,
        out_specs=pl.BlockSpec(memory_space=pl.ANY),
        scratch_shapes=[
            pltpu.VMEM(for_partner.shape, for_partner.dtype),
            pltpu.SemaphoreType.DMA((2, count)),
            pltpu.SemaphoreType.DMA((2, count)),
            pltpu.SemaphoreType.DMA((2,)),
            pltpu.SemaphoreType.DMA((2,)),
        ],
        compiler_params=pltpu.CompilerParams(collective_id=collective_id, has_side_effects=True),
    )(own, for_partner)


def exchange_kernel(axis, count, scatter, send_ref, out_ref, landed, send_sems, recv_sems):
    me = lax.axis_index(axis)
    barrier = pltpu.get_barrier_semaphore()
    for step in range(1, count):
        peer = lax.rem(me + step, count)
        pl.semaphore_signal(barrier, inc=1, device_id={axis: peer}, device_id_type=MESH)
    pl.semaphore_wait(barrier, count - 1)
    copies = []
    for step in range(1, count):
        peer = lax.rem(me + step, count)
        source = send_ref.at[peer] if scatter else send_ref
        copy = pltpu.make_async_remote_copy(
            src_ref=source,
            dst_ref=landed.at[me],
            send_sem=send_sems.at[step],
            recv_sem=recv_sems.at[step],
            device_id={axis: peer},
            device_id_type=MESH,
        )
        copy.start()
        copies.append(copy)
    landed[me] = send_ref[me] if scatter else send_ref[...]
    for copy in copies:
        copy.wait()
    if scatter:
        width = landed.shape[-1]
        for source in range(count):
            out_ref[:, source * width:(source + 1) * width] = landed[source]
    else:
        out_ref[...] = landed[...]


def exchange(x, axis, count, scatter, collective_id):
    piece = x.shape[1:] if scatter else x.shape
    result = (piece[0], count * piece[1]) if scatter else (count,) + piece
    return pl.pallas_call(
        functools.partial(exchange_kernel, axis, count, scatter),
        out_shape=jax.ShapeDtypeStruct(result, x.dtype),
        in_specs=[pl.BlockSpec(memory_space=pltpu.VMEM)],
        out_specs=pl.BlockSpec(memory_space=pltpu.VMEM),
        scratch_shapes=[
            pltpu.VMEM((count,) + piece, x.dtype),
            pltpu.SemaphoreType.DMA((count,)),
            pltpu.SemaphoreType.DMA((count,)),
        ],
        compiler_params=pltpu.CompilerParams(collective_id=collective_id, has_side_effects=True),
    )(x)


def on_device(tokens, trainer_panels, panel_home, lengths):
    tp_count = lax.axis_size("tp")
    grp_count = lax.axis_size("grp")
    member_id = lax.axis_index("tp")
    kv_count = (panel_home.shape[0] - tp_count) // 2
    group_size = tp_count // kv_count
    head_dim = trainer_panels.shape[2]
    block_rows = trainer_panels.shape[1]
    half_rows = block_rows // 2
    seq_total = tokens.shape[0]

    return whole(trainer_panels, panel_home, tokens, lengths, tp_count // 2, grp_count, 4)


def solution(mesh):
    placed = (P("grp", None), P("tp", "grp", None), P(), P("grp", None))
    return jax.shard_map(
        on_device, mesh=mesh, in_specs=placed, out_specs=P(("grp", "tp"), None), check_vma=False
    )
```

```python
import functools

import jax
import jax.numpy as jnp
from jax import lax
from jax.experimental import pallas as pl
from jax.experimental.pallas import tpu as pltpu
from jax.sharding import PartitionSpec as P

MESH = pl.DeviceIdType.MESH


def ring_kernel(count, stride, chunks, send_ref, out_ref, landed, send_sems, recv_sems):
    me = lax.axis_index("tp")
    total = count * stride
    right, left = lax.rem(me + stride, total), lax.rem(me + total - stride, total)
    spot = me // stride
    barrier = pltpu.get_barrier_semaphore()
    for neighbour in (left, right):
        pl.semaphore_signal(barrier, inc=1, device_id={"tp": neighbour}, device_id_type=MESH)
    pl.semaphore_wait(barrier, 2)

    def incoming(origin, chunk):
        return pltpu.make_async_remote_copy(
            src_ref=send_ref.at[chunk],
            dst_ref=landed.at[origin, chunk],
            send_sem=send_sems.at[0, 0, 0],
            recv_sem=recv_sems.at[origin, chunk],
            device_id={"tp": right},
            device_id_type=MESH,
        )

    landed[spot] = send_ref[...]
    sends = []
    far_right, far_left = count // 2, (count - 1) // 2
    for step in range(1, far_right + 1):
        for chunk in range(chunks):
            streams = [(0, right, lax.rem(spot + count - (step - 1), count))]
            if step <= far_left:
                streams.append((1, left, lax.rem(spot + step - 1, count)))
            for way, target, origin in streams:
                if step > 1:
                    incoming(origin, chunk).wait_recv()
                source = send_ref.at[chunk] if step == 1 else landed.at[origin, chunk]
                copy = pltpu.make_async_remote_copy(
                    src_ref=source,
                    dst_ref=landed.at[origin, chunk],
                    send_sem=send_sems.at[way, step, chunk],
                    recv_sem=recv_sems.at[origin, chunk],
                    device_id={"tp": target},
                    device_id_type=MESH,
                )
                copy.start()
                sends.append(copy)
    for chunk in range(chunks):
        incoming(lax.rem(spot + count - far_right, count), chunk).wait_recv()
        incoming(lax.rem(spot + far_left, count), chunk).wait_recv()
    for copy in sends:
        copy.wait_send()
    out_ref[...] = landed[...]


def ring_gather(x, count, stride, chunks, collective_id):
    x = x.reshape((chunks, x.shape[0] // chunks) + x.shape[1:])
    gathered = pl.pallas_call(
        functools.partial(ring_kernel, count, stride, chunks),
        out_shape=jax.ShapeDtypeStruct((count,) + x.shape, x.dtype),
        in_specs=[pl.BlockSpec(memory_space=pltpu.VMEM)],
        out_specs=pl.BlockSpec(memory_space=pltpu.VMEM),
        scratch_shapes=[
            pltpu.VMEM((count,) + x.shape, x.dtype),
            pltpu.SemaphoreType.DMA((2, count // 2 + 1, chunks)),
            pltpu.SemaphoreType.DMA((count, chunks)),
        ],
        compiler_params=pltpu.CompilerParams(collective_id=collective_id, has_side_effects=True),
    )(x)
    return gathered.reshape((count * x.shape[0] * x.shape[1],) + x.shape[2:])


def chip_ring_kernel(count, groups, panels_ref, home_ref, out_ref, landed, send_sems, recv_sems,
                     own_ref, partner_ref, partner_rows, grp_send_sems, grp_recv_sems, partner_sems, local_sems,
                     greet=True):
    me = lax.axis_index("tp")
    here = lax.axis_index("grp")
    total = 2 * count
    core = me % 2
    partner = me + 1 - 2 * core
    right, left = lax.rem(me + 2, total), lax.rem(me + total - 2, total)
    spot = me // 2
    half = panels_ref.shape[1] // 2
    if greet:
        barrier = pltpu.get_barrier_semaphore()
        for neighbour in (left, right, partner):
            pl.semaphore_signal(barrier, inc=1, device_id={"tp": neighbour}, device_id_type=MESH)
        for step in range(1, groups):
            peer = lax.rem(here + step, groups)
            pl.semaphore_signal(barrier, inc=1, device_id={"grp": peer}, device_id_type=MESH)
        pl.semaphore_wait(barrier, 2 + groups)

    def rows_of(slot, which):
        return panels_ref.at[slot, pl.ds(pl.multiple_of(which * half, 16), half)]

    def incoming(origin, chunk):
        return pltpu.make_async_remote_copy(
            src_ref=rows_of(0, 0),
            dst_ref=landed.at[origin, chunk],
            send_sem=send_sems.at[0, 0, 0],
            recv_sem=recv_sems.at[origin, chunk],
            device_id={"tp": right},
            device_id_type=MESH,
        )

    sends = []

    def send(source, origin, chunk, sem, target):
        copy = pltpu.make_async_remote_copy(
            src_ref=source,
            dst_ref=landed.at[origin, chunk],
            send_sem=sem,
            recv_sem=recv_sems.at[origin, chunk],
            device_id={"tp": target},
            device_id_type=MESH,
        )
        copy.start()
        sends.append(copy)

    own = [2 * core + j for j in range(2)]
    theirs = [2 * (1 - core) + j for j in range(2)]
    for j in range(2):
        send(rows_of(j, 1 - core), spot, own[j], send_sems.at[0, 0, 1 + j], partner)
        landed[spot, own[j]] = rows_of(j, core)[...]
    far_right, far_left = count // 2, (count - 1) // 2
    first = [(rows_of(j, core), own[j]) for j in range(2)] + [(None, theirs[j]) for j in range(2)]
    for position, (source, chunk) in enumerate(first):
        if source is None:
            incoming(spot, chunk).wait_recv()
            source = landed.at[spot, chunk]
        send(source, spot, chunk, send_sems.at[0, 1, position], right)
        if far_left >= 1:
            send(source, spot, chunk, send_sems.at[1, 1, position], left)
    for step in range(2, far_right + 1):
        for chunk in range(4):
            streams = [(0, right, lax.rem(spot + count - (step - 1), count))]
            if step <= far_left:
                streams.append((1, left, lax.rem(spot + step - 1, count)))
            for way, target, origin in streams:
                incoming(origin, chunk).wait_recv()
                send(landed.at[origin, chunk], origin, chunk, send_sems.at[way, step, chunk], target)
    for chunk in range(4):
        incoming(lax.rem(spot + count - far_right, count), chunk).wait_recv()
        incoming(lax.rem(spot + far_left, count), chunk).wait_recv()
    for copy in sends:
        copy.wait_send()
    heads = total
    kv_heads = (home_ref.shape[0] - heads) // 2
    group = heads // kv_heads
    quarter = me % group
    kv_panel = heads + me // group + kv_heads * (quarter // 2)
    chip_slots = landed.shape[1]

    def block(panel):
        slot = home_ref[panel]
        return landed[slot // chip_slots, slot % chip_slots]

    own_ref[0:half] = block(me)
    own_ref[half:2 * half] = block(kv_panel)
    partner_ref[...] = block(partner)

    to_partner = pltpu.make_async_remote_copy(
        src_ref=partner_ref, dst_ref=partner_rows, send_sem=partner_sems.at[0],
        recv_sem=partner_sems.at[1], device_id={"tp": partner}, device_id_type=MESH,
    )
    to_partner.start()
    copies, local_copies = [], []

    def spread(part, source, window):
        for step in range(1, groups):
            peer = lax.rem(here + step, groups)
            copy = pltpu.make_async_remote_copy(
                src_ref=source,
                dst_ref=out_ref.at[here, window],
                send_sem=grp_send_sems.at[part, step],
                recv_sem=grp_recv_sems.at[part, step],
                device_id={"grp": peer},
                device_id_type=MESH,
            )
            copy.start()
            copies.append(copy)
        local = pltpu.make_async_copy(source, out_ref.at[here, window], local_sems.at[part])
        local.start()
        local_copies.append(local)

    spread(0, own_ref, pl.ds(0, 2 * half))
    to_partner.wait()
    spread(1, partner_rows, pl.ds(2 * half, half))
    for copy in local_copies:
        copy.wait()
    if greet:
        for copy in copies:
            copy.wait()
        return None
    windows = [(own_ref, pl.ds(0, 2 * half)), (partner_rows, pl.ds(2 * half, half))]

    def arrive(source):
        step = lax.rem(here + groups - source, groups)

        @pl.when(step != 0)
        def _():
            for part, (shape_ref, window) in enumerate(windows):
                pltpu.make_async_remote_copy(
                    src_ref=shape_ref,
                    dst_ref=out_ref.at[here, window],
                    send_sem=grp_send_sems.at[part, 0],
                    recv_sem=grp_recv_sems.at[part, step],
                    device_id={"grp": lax.rem(here + 1, groups)},
                    device_id_type=MESH,
                ).wait_recv()

    def finish():
        for copy in copies:
            copy.wait_send()

    return arrive, finish


def chip_ring_gather(panels, home, count, groups, collective_id):
    slots, rows, width = panels.shape
    return pl.pallas_call(
        functools.partial(chip_ring_kernel, count, groups),
        out_shape=jax.ShapeDtypeStruct((groups, rows + rows // 2, width), panels.dtype),
        in_specs=[pl.BlockSpec(memory_space=pltpu.VMEM), pl.BlockSpec(memory_space=pltpu.SMEM)],
        out_specs=pl.BlockSpec(memory_space=pl.ANY),
        scratch_shapes=[
            pltpu.VMEM((count, 2 * slots, rows // 2, width), panels.dtype),
            pltpu.SemaphoreType.DMA((2, count // 2 + 1, 2 * slots)),
            pltpu.SemaphoreType.DMA((count, 2 * slots)),
            pltpu.VMEM((rows, width), panels.dtype),
            pltpu.VMEM((rows // 2, width), panels.dtype),
            pltpu.VMEM((rows // 2, width), panels.dtype),
            pltpu.SemaphoreType.DMA((2, groups)),
            pltpu.SemaphoreType.DMA((2, groups)),
            pltpu.SemaphoreType.DMA((2,)),
            pltpu.SemaphoreType.DMA((2,)),
        ],
        compiler_params=pltpu.CompilerParams(collective_id=collective_id, has_side_effects=True),
    )(panels, home)


def kv_share_kernel(part_ref, out_ref, partner_part, mine, theirs, send_sems, recv_sems):
    me = lax.axis_index("tp")
    partner = me + 1 - 2 * (me % 2)
    across = me + 2 - 4 * ((me // 2) % 2)
    barrier = pltpu.get_barrier_semaphore()
    for neighbour in (partner, across):
        pl.semaphore_signal(barrier, inc=1, device_id={"tp": neighbour}, device_id_type=MESH)
    pl.semaphore_wait(barrier, 2)
    first = pltpu.make_async_remote_copy(
        src_ref=part_ref, dst_ref=partner_part, send_sem=send_sems.at[0], recv_sem=recv_sems.at[0],
        device_id={"tp": partner}, device_id_type=MESH,
    )
    first.start()
    first.wait()
    mine[...] = (part_ref[...] + partner_part[...]).astype(mine.dtype)
    second = pltpu.make_async_remote_copy(
        src_ref=mine, dst_ref=theirs, send_sem=send_sems.at[1], recv_sem=recv_sems.at[1],
        device_id={"tp": across}, device_id_type=MESH,
    )
    second.start()
    second.wait()
    holds_k = (me % 4) < 2
    out_ref[0] = jnp.where(holds_k, mine[...], theirs[...])
    out_ref[1] = jnp.where(holds_k, theirs[...], mine[...])


def kv_share(part, collective_id):
    return pl.pallas_call(
        kv_share_kernel,
        out_shape=jax.ShapeDtypeStruct((2,) + part.shape, jnp.bfloat16),
        in_specs=[pl.BlockSpec(memory_space=pltpu.VMEM)],
        out_specs=pl.BlockSpec(memory_space=pltpu.VMEM),
        scratch_shapes=[
            pltpu.VMEM(part.shape, part.dtype),
            pltpu.VMEM(part.shape, jnp.bfloat16),
            pltpu.VMEM(part.shape, jnp.bfloat16),
            pltpu.SemaphoreType.DMA((2,)),
            pltpu.SemaphoreType.DMA((2,)),
        ],
        compiler_params=pltpu.CompilerParams(collective_id=collective_id, has_side_effects=True),
    )(part)


def tail_kernel(count, scale, tokens_ref, gathered_hbm, lengths_ref, out_ref,
                gathered, load_sem, part_ref, partner_part, mine, theirs, staged, landed, send_sems, recv_sems,
                greet=True, arrive=None):
    width = landed.shape[-1]
    me = lax.axis_index("tp")
    partner = me + 1 - 2 * (me % 2)
    across = me + 2 - 4 * ((me // 2) % 2)
    if greet:
        load = pltpu.make_async_copy(gathered_hbm, gathered, load_sem)
        load.start()
        barrier = pltpu.get_barrier_semaphore()
        for step in range(1, count):
            peer = lax.rem(me + step, count)
            pl.semaphore_signal(barrier, inc=1, device_id={"tp": peer}, device_id_type=MESH)
        load.wait()
    core = me % 2
    half = gathered.shape[1] // 3
    sources = gathered.shape[0]
    first_half = core == 0
    projected = jnp.zeros((tokens_ref.shape[0], 2 * width), jnp.float32)
    for pair in range(sources // 2):
        if arrive is not None:
            arrive(2 * pair)
            arrive(2 * pair + 1)
        q_parts, kv_parts = [], []
        for source in (2 * pair, 2 * pair + 1):
            here = gathered[source, 0:half]
            kv = gathered[source, half:2 * half]
            there = gathered[source, 2 * half:3 * half]
            zero = jnp.zeros_like(kv)
            q_parts.append(jnp.where(first_half, jnp.concatenate([here, there], axis=0),
                                     jnp.concatenate([there, here], axis=0)))
            kv_parts.append(jnp.where(first_half, jnp.concatenate([kv, zero], axis=0),
                                      jnp.concatenate([zero, kv], axis=0)))
        slab = jnp.concatenate(
            [jnp.concatenate(q_parts, axis=0), jnp.concatenate(kv_parts, axis=0)], axis=1
        )
        columns = slab.shape[0]
        projected = projected + jnp.dot(
            tokens_ref[:, pair * columns:(pair + 1) * columns], slab, preferred_element_type=jnp.float32
        )
    part_ref[...] = projected[:, width:]
    query = projected[:, :width].astype(jnp.bfloat16)
    if greet:
        pl.semaphore_wait(barrier, count - 1)
    first = pltpu.make_async_remote_copy(
        src_ref=part_ref, dst_ref=partner_part, send_sem=send_sems.at[0], recv_sem=recv_sems.at[0],
        device_id={"tp": partner}, device_id_type=MESH,
    )
    first.start()
    first.wait()
    mine[...] = (part_ref[...] + partner_part[...]).astype(mine.dtype)
    second = pltpu.make_async_remote_copy(
        src_ref=mine, dst_ref=theirs, send_sem=send_sems.at[1], recv_sem=recv_sems.at[1],
        device_id={"tp": across}, device_id_type=MESH,
    )
    second.start()
    second.wait()
    holds_k = (me % 4) < 2
    keys = jnp.where(holds_k, mine[...], theirs[...])
    values = jnp.where(holds_k, theirs[...], mine[...])

    seq = query.shape[0]
    rows = seq // count
    blocks = 4
    block_rows = seq // blocks
    col = lax.broadcasted_iota(jnp.int32, (block_rows, seq), 1)
    col_segment = jnp.zeros((block_rows, seq), jnp.int32)
    bounds = []
    bound = lengths_ref[0, 0] * 0
    for response in range(lengths_ref.shape[1]):
        bound = bound + lengths_ref[0, response]
        bounds.append(bound)
        col_segment = col_segment + (col >= bound).astype(jnp.int32)
    copies = []
    for block in range(blocks):
        first_row = block * block_rows
        scores = lax.dot_general(
            query[first_row:first_row + block_rows], keys, (((1,), (1,)), ((), ())),
            preferred_element_type=jnp.float32,
        ) * scale
        row = lax.broadcasted_iota(jnp.int32, (block_rows, seq), 0) + first_row
        row_segment = jnp.zeros((block_rows, seq), jnp.int32)
        for bound in bounds:
            row_segment = row_segment + (row >= bound).astype(jnp.int32)
        allowed = (row_segment == col_segment) & (col <= row)
        masked = jnp.where(allowed, scores, -jnp.inf)
        peak = jnp.max(masked, axis=1, keepdims=True)
        weights = jnp.exp(masked - peak)
        probs = (weights / jnp.sum(weights, axis=1, keepdims=True)).astype(jnp.bfloat16)
        context = jnp.dot(probs, values, preferred_element_type=jnp.float32)
        per_block = block_rows // rows
        for i in range(per_block):
            target = block * per_block + i
            staged[target] = context[i * rows:(i + 1) * rows]
        for i in range(per_block):
            target = block * per_block + i
            copy = pltpu.make_async_remote_copy(
                src_ref=staged.at[target],
                dst_ref=landed.at[me],
                send_sem=send_sems.at[2 + target],
                recv_sem=recv_sems.at[2 + me],
                device_id={"tp": target},
                device_id_type=MESH,
            )

            @pl.when(target != me)
            def _():
                copy.start()

            copies.append((target, copy))
    landed[me] = staged[me]
    for target, copy in copies:
        @pl.when(target != me)
        def _():
            copy.wait_send()
    for source in range(count):
        incoming = pltpu.make_async_remote_copy(
            src_ref=staged.at[source],
            dst_ref=landed.at[source],
            send_sem=send_sems.at[0],
            recv_sem=recv_sems.at[2 + source],
            device_id={"tp": partner},
            device_id_type=MESH,
        )

        @pl.when(source != me)
        def _():
            incoming.wait_recv()
    for source in range(count):
        out_ref[:, source * width:(source + 1) * width] = landed[source]


def tail(tokens, gathered, lengths, count, collective_id):
    seq, width = tokens.shape[0], gathered.shape[2]
    part = jax.ShapeDtypeStruct((seq, width), jnp.float32)
    rows = seq // count
    vmem = pl.BlockSpec(memory_space=pltpu.VMEM)
    return pl.pallas_call(
        functools.partial(tail_kernel, count, width ** (-0.5)),
        out_shape=jax.ShapeDtypeStruct((rows, count * width), jnp.float32),
        in_specs=[vmem, pl.BlockSpec(memory_space=pl.ANY), pl.BlockSpec(memory_space=pltpu.SMEM)],
        out_specs=vmem,
        scratch_shapes=[
            pltpu.VMEM(gathered.shape, gathered.dtype),
            pltpu.SemaphoreType.DMA(()),
            pltpu.VMEM(part.shape, part.dtype),
            pltpu.VMEM(part.shape, part.dtype),
            pltpu.VMEM(part.shape, jnp.bfloat16),
            pltpu.VMEM(part.shape, jnp.bfloat16),
            pltpu.VMEM((count, rows, width), jnp.float32),
            pltpu.VMEM((count, rows, width), jnp.float32),
            pltpu.SemaphoreType.DMA((count + 1,)),
            pltpu.SemaphoreType.DMA((count + 1,)),
        ],
        compiler_params=pltpu.CompilerParams(collective_id=collective_id, has_side_effects=True),
    )(tokens, gathered, lengths)


def whole_kernel(count, groups, scale, panels_ref, home_ref, tokens_ref, lengths_ref, out_ref, *scratch):
    ring_scratch, gathered, tail_scratch = scratch[:10], scratch[10], scratch[11:]
    me = lax.axis_index("tp")
    here = lax.axis_index("grp")
    total = 2 * count
    barrier = pltpu.get_barrier_semaphore()
    for step in range(1, total):
        peer = lax.rem(me + step, total)
        pl.semaphore_signal(barrier, inc=1, device_id={"tp": peer}, device_id_type=MESH)
    for step in range(1, groups):
        peer = lax.rem(here + step, groups)
        pl.semaphore_signal(barrier, inc=1, device_id={"grp": peer}, device_id_type=MESH)
    pl.semaphore_wait(barrier, total + groups - 2)
    arrive, finish = chip_ring_kernel(count, groups, panels_ref, home_ref, gathered, *ring_scratch, greet=False)
    tail_kernel(total, scale, tokens_ref, None, lengths_ref, out_ref, gathered, None, *tail_scratch, greet=False,
                arrive=arrive)
    finish()


def whole(panels, home, tokens, lengths, count, groups, collective_id):
    slots, rows, width = panels.shape
    seq = tokens.shape[0]
    total = 2 * count
    out_rows = seq // total
    part = (seq, width)
    vmem = pl.BlockSpec(memory_space=pltpu.VMEM)
    smem = pl.BlockSpec(memory_space=pltpu.SMEM)
    return pl.pallas_call(
        functools.partial(whole_kernel, count, groups, width ** (-0.5)),
        out_shape=jax.ShapeDtypeStruct((out_rows, total * width), jnp.float32),
        in_specs=[vmem, smem, vmem, smem],
        out_specs=vmem,
        scratch_shapes=[
            pltpu.VMEM((count, 2 * slots, rows // 2, width), panels.dtype),
            pltpu.SemaphoreType.DMA((2, count // 2 + 1, 2 * slots)),
            pltpu.SemaphoreType.DMA((count, 2 * slots)),
            pltpu.VMEM((rows, width), panels.dtype),
            pltpu.VMEM((rows // 2, width), panels.dtype),
            pltpu.VMEM((rows // 2, width), panels.dtype),
            pltpu.SemaphoreType.DMA((2, groups)),
            pltpu.SemaphoreType.DMA((2, groups)),
            pltpu.SemaphoreType.DMA((2,)),
            pltpu.SemaphoreType.DMA((2,)),
            pltpu.VMEM((groups, rows + rows // 2, width), panels.dtype),
            pltpu.VMEM(part, jnp.float32),
            pltpu.VMEM(part, jnp.float32),
            pltpu.VMEM(part, jnp.bfloat16),
            pltpu.VMEM(part, jnp.bfloat16),
            pltpu.VMEM((total, out_rows, width), jnp.float32),
            pltpu.VMEM((total, out_rows, width), jnp.float32),
            pltpu.SemaphoreType.DMA((total + 2,)),
            pltpu.SemaphoreType.DMA((total + 2,)),
        ],
        compiler_params=pltpu.CompilerParams(collective_id=collective_id, has_side_effects=True),
    )(panels, home, tokens, lengths)


def grid_kernel(width, send_ref, out_ref, landed, send_sems, recv_sems):
    me = lax.axis_index("grp")
    core = lax.axis_index("tp") % 2
    col, row = me % width, me // width

    def node(c, r):
        return lax.rem(r + width, width) * width + lax.rem(c + width, width)

    def along(dim, c, r, k):
        return node(c + k, r) if dim == 0 else node(c, r + k)

    barrier = pltpu.get_barrier_semaphore()
    neighbours = [node(col + 1, row), node(col - 1, row), node(col, row + 1), node(col, row - 1)]
    for neighbour in neighbours:
        pl.semaphore_signal(barrier, inc=1, device_id={"grp": neighbour}, device_id_type=MESH)
    pl.semaphore_wait(barrier, 4)

    landed[me] = send_ref[...]
    sends = []

    def send(source, origin, half, target):
        copy = pltpu.make_async_remote_copy(
            src_ref=source,
            dst_ref=landed.at[origin, half],
            send_sem=send_sems.at[len(sends)],
            recv_sem=recv_sems.at[origin, half],
            device_id={"grp": target},
            device_id_type=MESH,
        )
        copy.start()
        sends.append(copy)

    def arrive(origin, half):
        pltpu.make_async_remote_copy(
            src_ref=send_ref.at[half],
            dst_ref=landed.at[origin, half],
            send_sem=send_sems.at[0],
            recv_sem=recv_sems.at[origin, half],
            device_id={"grp": neighbours[0]},
            device_id_type=MESH,
        ).wait_recv()

    ahead = 1 - 2 * core

    def phase(lines, half, dim):
        for k in (1, -1):
            for line in lines:
                origin = along(1 - dim, col, row, line)
                source = send_ref.at[half] if line == 0 else landed.at[origin, half]
                send(source, origin, half, along(dim, col, row, k))
        for line in lines:
            for k in (1, -1):
                arrive(along(dim, along(1 - dim, col, row, line) % width, along(1 - dim, col, row, line) // width, k), half)
        for line in lines:
            base = along(1 - dim, col, row, line)
            bc, br = base % width, base // width
            send(landed.at[along(dim, bc, br, -ahead), half], along(dim, bc, br, -ahead), half,
                 along(dim, col, row, ahead))
        for line in lines:
            base = along(1 - dim, col, row, line)
            arrive(along(dim, base % width, base // width, 2), half)

    phase([0], 0, 0)
    phase([0], 1, 1)
    phase([0, 1, -1, 2], 0, 1)
    phase([0, 1, -1, 2], 1, 0)
    for copy in sends:
        copy.wait_send()
    out_ref[...] = landed[...]


def grid_gather(x, width, collective_id):
    count = width * width
    x = x.reshape((2, x.shape[0] // 2) + x.shape[1:])
    gathered = pl.pallas_call(
        functools.partial(grid_kernel, width),
        out_shape=jax.ShapeDtypeStruct((count,) + x.shape, x.dtype),
        in_specs=[pl.BlockSpec(memory_space=pltpu.VMEM)],
        out_specs=pl.BlockSpec(memory_space=pltpu.VMEM),
        scratch_shapes=[
            pltpu.VMEM((count,) + x.shape, x.dtype),
            pltpu.SemaphoreType.DMA((2 * (count - 1),)),
            pltpu.SemaphoreType.DMA((count, 2)),
        ],
        compiler_params=pltpu.CompilerParams(collective_id=collective_id, has_side_effects=True),
    )(x)
    return gathered.reshape((count, x.shape[0] * x.shape[1]) + x.shape[2:])


def gather_hbm_kernel(axis, count, send_ref, out_ref, send_sems, recv_sems, local_sem):
    me = lax.axis_index(axis)
    barrier = pltpu.get_barrier_semaphore()
    for step in range(1, count):
        peer = lax.rem(me + step, count)
        pl.semaphore_signal(barrier, inc=1, device_id={axis: peer}, device_id_type=MESH)
    pl.semaphore_wait(barrier, count - 1)
    copies = []
    for step in range(1, count):
        peer = lax.rem(me + step, count)
        copy = pltpu.make_async_remote_copy(
            src_ref=send_ref,
            dst_ref=out_ref.at[me],
            send_sem=send_sems.at[step],
            recv_sem=recv_sems.at[step],
            device_id={axis: peer},
            device_id_type=MESH,
        )
        copy.start()
        copies.append(copy)
    local = pltpu.make_async_copy(send_ref, out_ref.at[me], local_sem)
    local.start()
    for copy in copies:
        copy.wait()
    local.wait()


def gather_hbm(x, axis, count, collective_id):
    return pl.pallas_call(
        functools.partial(gather_hbm_kernel, axis, count),
        out_shape=jax.ShapeDtypeStruct((count,) + x.shape, x.dtype),
        in_specs=[pl.BlockSpec(memory_space=pltpu.VMEM)],
        out_specs=pl.BlockSpec(memory_space=pl.ANY),
        scratch_shapes=[
            pltpu.SemaphoreType.DMA((count,)),
            pltpu.SemaphoreType.DMA((count,)),
            pltpu.SemaphoreType.DMA(()),
        ],
        compiler_params=pltpu.CompilerParams(collective_id=collective_id, has_side_effects=True),
    )(x)


def weights_gather_kernel(count, own_ref, for_partner_ref, out_ref, partner_rows,
                          send_sems, recv_sems, partner_sems, local_sems):
    me = lax.axis_index("grp")
    member = lax.axis_index("tp")
    partner = member + 1 - 2 * (member % 2)
    rows = own_ref.shape[0]
    barrier = pltpu.get_barrier_semaphore()
    pl.semaphore_signal(barrier, inc=1, device_id={"tp": partner}, device_id_type=MESH)
    for step in range(1, count):
        peer = lax.rem(me + step, count)
        pl.semaphore_signal(barrier, inc=1, device_id={"grp": peer}, device_id_type=MESH)
    pl.semaphore_wait(barrier, count)
    to_partner = pltpu.make_async_remote_copy(
        src_ref=for_partner_ref, dst_ref=partner_rows, send_sem=partner_sems.at[0],
        recv_sem=partner_sems.at[1], device_id={"tp": partner}, device_id_type=MESH,
    )
    to_partner.start()
    copies = []

    def spread(part, source, window):
        for step in range(1, count):
            peer = lax.rem(me + step, count)
            copy = pltpu.make_async_remote_copy(
                src_ref=source,
                dst_ref=out_ref.at[me, window],
                send_sem=send_sems.at[part, step],
                recv_sem=recv_sems.at[part, step],
                device_id={"grp": peer},
                device_id_type=MESH,
            )
            copy.start()
            copies.append(copy)
        local = pltpu.make_async_copy(source, out_ref.at[me, window], local_sems.at[part])
        local.start()
        copies.append(local)

    spread(0, own_ref, pl.ds(0, rows))
    to_partner.wait()
    spread(1, partner_rows, pl.ds(rows, partner_rows.shape[0]))
    for copy in copies:
        copy.wait()


def weights_gather(own, for_partner, count, collective_id):
    rows = own.shape[0] + for_partner.shape[0]
    return pl.pallas_call(
        functools.partial(weights_gather_kernel, count),
        out_shape=jax.ShapeDtypeStruct((count, rows) + own.shape[1:], own.dtype),
        in_specs=[pl.BlockSpec(memory_space=pltpu.VMEM)] * 2,
        out_specs=pl.BlockSpec(memory_space=pl.ANY),
        scratch_shapes=[
            pltpu.VMEM(for_partner.shape, for_partner.dtype),
            pltpu.SemaphoreType.DMA((2, count)),
            pltpu.SemaphoreType.DMA((2, count)),
            pltpu.SemaphoreType.DMA((2,)),
            pltpu.SemaphoreType.DMA((2,)),
        ],
        compiler_params=pltpu.CompilerParams(collective_id=collective_id, has_side_effects=True),
    )(own, for_partner)


def exchange_kernel(axis, count, scatter, send_ref, out_ref, landed, send_sems, recv_sems):
    me = lax.axis_index(axis)
    barrier = pltpu.get_barrier_semaphore()
    for step in range(1, count):
        peer = lax.rem(me + step, count)
        pl.semaphore_signal(barrier, inc=1, device_id={axis: peer}, device_id_type=MESH)
    pl.semaphore_wait(barrier, count - 1)
    copies = []
    for step in range(1, count):
        peer = lax.rem(me + step, count)
        source = send_ref.at[peer] if scatter else send_ref
        copy = pltpu.make_async_remote_copy(
            src_ref=source,
            dst_ref=landed.at[me],
            send_sem=send_sems.at[step],
            recv_sem=recv_sems.at[step],
            device_id={axis: peer},
            device_id_type=MESH,
        )
        copy.start()
        copies.append(copy)
    landed[me] = send_ref[me] if scatter else send_ref[...]
    for copy in copies:
        copy.wait()
    if scatter:
        width = landed.shape[-1]
        for source in range(count):
            out_ref[:, source * width:(source + 1) * width] = landed[source]
    else:
        out_ref[...] = landed[...]


def exchange(x, axis, count, scatter, collective_id):
    piece = x.shape[1:] if scatter else x.shape
    result = (piece[0], count * piece[1]) if scatter else (count,) + piece
    return pl.pallas_call(
        functools.partial(exchange_kernel, axis, count, scatter),
        out_shape=jax.ShapeDtypeStruct(result, x.dtype),
        in_specs=[pl.BlockSpec(memory_space=pltpu.VMEM)],
        out_specs=pl.BlockSpec(memory_space=pltpu.VMEM),
        scratch_shapes=[
            pltpu.VMEM((count,) + piece, x.dtype),
            pltpu.SemaphoreType.DMA((count,)),
            pltpu.SemaphoreType.DMA((count,)),
        ],
        compiler_params=pltpu.CompilerParams(collective_id=collective_id, has_side_effects=True),
    )(x)


def on_device(tokens, trainer_panels, panel_home, lengths):
    tp_count = lax.axis_size("tp")
    grp_count = lax.axis_size("grp")
    member_id = lax.axis_index("tp")
    kv_count = (panel_home.shape[0] - tp_count) // 2
    group_size = tp_count // kv_count
    head_dim = trainer_panels.shape[2]
    block_rows = trainer_panels.shape[1]
    half_rows = block_rows // 2
    seq_total = tokens.shape[0]

    return whole(trainer_panels, panel_home, tokens, lengths, tp_count // 2, grp_count, 4)


def solution(mesh):
    placed = (P("grp", None), P("tp", "grp", None), P(), P("grp", None))
    return jax.shard_map(
        on_device, mesh=mesh, in_specs=placed, out_specs=P(("grp", "tp"), None), check_vma=False
    )
```

```python
import functools

import jax
import jax.numpy as jnp
from jax import lax
from jax.experimental import pallas as pl
from jax.experimental.pallas import tpu as pltpu
from jax.sharding import PartitionSpec as P

MESH = pl.DeviceIdType.MESH


def ring_kernel(count, stride, chunks, send_ref, out_ref, landed, send_sems, recv_sems):
    me = lax.axis_index("tp")
    total = count * stride
    right, left = lax.rem(me + stride, total), lax.rem(me + total - stride, total)
    spot = me // stride
    barrier = pltpu.get_barrier_semaphore()
    for neighbour in (left, right):
        pl.semaphore_signal(barrier, inc=1, device_id={"tp": neighbour}, device_id_type=MESH)
    pl.semaphore_wait(barrier, 2)

    def incoming(origin, chunk):
        return pltpu.make_async_remote_copy(
            src_ref=send_ref.at[chunk],
            dst_ref=landed.at[origin, chunk],
            send_sem=send_sems.at[0, 0, 0],
            recv_sem=recv_sems.at[origin, chunk],
            device_id={"tp": right},
            device_id_type=MESH,
        )

    landed[spot] = send_ref[...]
    sends = []
    far_right, far_left = count // 2, (count - 1) // 2
    for step in range(1, far_right + 1):
        for chunk in range(chunks):
            streams = [(0, right, lax.rem(spot + count - (step - 1), count))]
            if step <= far_left:
                streams.append((1, left, lax.rem(spot + step - 1, count)))
            for way, target, origin in streams:
                if step > 1:
                    incoming(origin, chunk).wait_recv()
                source = send_ref.at[chunk] if step == 1 else landed.at[origin, chunk]
                copy = pltpu.make_async_remote_copy(
                    src_ref=source,
                    dst_ref=landed.at[origin, chunk],
                    send_sem=send_sems.at[way, step, chunk],
                    recv_sem=recv_sems.at[origin, chunk],
                    device_id={"tp": target},
                    device_id_type=MESH,
                )
                copy.start()
                sends.append(copy)
    for chunk in range(chunks):
        incoming(lax.rem(spot + count - far_right, count), chunk).wait_recv()
        incoming(lax.rem(spot + far_left, count), chunk).wait_recv()
    for copy in sends:
        copy.wait_send()
    out_ref[...] = landed[...]


def ring_gather(x, count, stride, chunks, collective_id):
    x = x.reshape((chunks, x.shape[0] // chunks) + x.shape[1:])
    gathered = pl.pallas_call(
        functools.partial(ring_kernel, count, stride, chunks),
        out_shape=jax.ShapeDtypeStruct((count,) + x.shape, x.dtype),
        in_specs=[pl.BlockSpec(memory_space=pltpu.VMEM)],
        out_specs=pl.BlockSpec(memory_space=pltpu.VMEM),
        scratch_shapes=[
            pltpu.VMEM((count,) + x.shape, x.dtype),
            pltpu.SemaphoreType.DMA((2, count // 2 + 1, chunks)),
            pltpu.SemaphoreType.DMA((count, chunks)),
        ],
        compiler_params=pltpu.CompilerParams(collective_id=collective_id, has_side_effects=True),
    )(x)
    return gathered.reshape((count * x.shape[0] * x.shape[1],) + x.shape[2:])


def chip_ring_kernel(count, groups, panels_ref, home_ref, out_ref, landed, send_sems, recv_sems,
                     own_ref, partner_ref, partner_rows, grp_send_sems, grp_recv_sems, partner_sems, local_sems,
                     greet=True):
    me = lax.axis_index("tp")
    here = lax.axis_index("grp")
    total = 2 * count
    core = me % 2
    partner = me + 1 - 2 * core
    right, left = lax.rem(me + 2, total), lax.rem(me + total - 2, total)
    spot = me // 2
    half = panels_ref.shape[1] // 2
    if greet:
        barrier = pltpu.get_barrier_semaphore()
        for neighbour in (left, right, partner):
            pl.semaphore_signal(barrier, inc=1, device_id={"tp": neighbour}, device_id_type=MESH)
        for step in range(1, groups):
            peer = lax.rem(here + step, groups)
            pl.semaphore_signal(barrier, inc=1, device_id={"grp": peer}, device_id_type=MESH)
        pl.semaphore_wait(barrier, 2 + groups)

    def rows_of(slot, which):
        return panels_ref.at[slot, pl.ds(pl.multiple_of(which * half, 16), half)]

    def incoming(origin, chunk):
        return pltpu.make_async_remote_copy(
            src_ref=rows_of(0, 0),
            dst_ref=landed.at[origin, chunk],
            send_sem=send_sems.at[0, 0, 0],
            recv_sem=recv_sems.at[origin, chunk],
            device_id={"tp": right},
            device_id_type=MESH,
        )

    sends = []

    def send(source, origin, chunk, sem, target):
        copy = pltpu.make_async_remote_copy(
            src_ref=source,
            dst_ref=landed.at[origin, chunk],
            send_sem=sem,
            recv_sem=recv_sems.at[origin, chunk],
            device_id={"tp": target},
            device_id_type=MESH,
        )
        copy.start()
        sends.append(copy)

    own = [2 * core + j for j in range(2)]
    theirs = [2 * (1 - core) + j for j in range(2)]
    for j in range(2):
        send(rows_of(j, 1 - core), spot, own[j], send_sems.at[0, 0, 1 + j], partner)
        landed[spot, own[j]] = rows_of(j, core)[...]
    far_right, far_left = count // 2, (count - 1) // 2
    first = [(rows_of(j, core), own[j]) for j in range(2)] + [(None, theirs[j]) for j in range(2)]
    for position, (source, chunk) in enumerate(first):
        if source is None:
            incoming(spot, chunk).wait_recv()
            source = landed.at[spot, chunk]
        send(source, spot, chunk, send_sems.at[0, 1, position], right)
        if far_left >= 1:
            send(source, spot, chunk, send_sems.at[1, 1, position], left)
    for step in range(2, far_right + 1):
        for chunk in range(4):
            streams = [(0, right, lax.rem(spot + count - (step - 1), count))]
            if step <= far_left:
                streams.append((1, left, lax.rem(spot + step - 1, count)))
            for way, target, origin in streams:
                incoming(origin, chunk).wait_recv()
                send(landed.at[origin, chunk], origin, chunk, send_sems.at[way, step, chunk], target)
    for chunk in range(4):
        incoming(lax.rem(spot + count - far_right, count), chunk).wait_recv()
        incoming(lax.rem(spot + far_left, count), chunk).wait_recv()
    for copy in sends:
        copy.wait_send()
    heads = total
    kv_heads = (home_ref.shape[0] - heads) // 2
    group = heads // kv_heads
    quarter = me % group
    kv_panel = heads + me // group + kv_heads * (quarter // 2)
    chip_slots = landed.shape[1]

    def block(panel):
        slot = home_ref[panel]
        return landed[slot // chip_slots, slot % chip_slots]

    own_ref[0:half] = block(me)
    own_ref[half:2 * half] = block(kv_panel)
    partner_ref[...] = block(partner)

    to_partner = pltpu.make_async_remote_copy(
        src_ref=partner_ref, dst_ref=partner_rows, send_sem=partner_sems.at[0],
        recv_sem=partner_sems.at[1], device_id={"tp": partner}, device_id_type=MESH,
    )
    to_partner.start()
    copies, local_copies = [], []

    def spread(part, source, window):
        for step in range(1, groups):
            peer = lax.rem(here + step, groups)
            copy = pltpu.make_async_remote_copy(
                src_ref=source,
                dst_ref=out_ref.at[here, window],
                send_sem=grp_send_sems.at[part, step],
                recv_sem=grp_recv_sems.at[part, step],
                device_id={"grp": peer},
                device_id_type=MESH,
            )
            copy.start()
            copies.append(copy)
        local = pltpu.make_async_copy(source, out_ref.at[here, window], local_sems.at[part])
        local.start()
        local_copies.append(local)

    spread(0, own_ref, pl.ds(0, 2 * half))
    to_partner.wait()
    spread(1, partner_rows, pl.ds(2 * half, half))
    for copy in local_copies:
        copy.wait()
    if greet:
        for copy in copies:
            copy.wait()
        return None
    windows = [(own_ref, pl.ds(0, 2 * half)), (partner_rows, pl.ds(2 * half, half))]

    def arrive(source):
        step = lax.rem(here + groups - source, groups)

        @pl.when(step != 0)
        def _():
            for part, (shape_ref, window) in enumerate(windows):
                pltpu.make_async_remote_copy(
                    src_ref=shape_ref,
                    dst_ref=out_ref.at[here, window],
                    send_sem=grp_send_sems.at[part, 0],
                    recv_sem=grp_recv_sems.at[part, step],
                    device_id={"grp": lax.rem(here + 1, groups)},
                    device_id_type=MESH,
                ).wait_recv()

    def finish():
        for copy in copies:
            copy.wait_send()

    return arrive, finish


def chip_ring_gather(panels, home, count, groups, collective_id):
    slots, rows, width = panels.shape
    return pl.pallas_call(
        functools.partial(chip_ring_kernel, count, groups),
        out_shape=jax.ShapeDtypeStruct((groups, rows + rows // 2, width), panels.dtype),
        in_specs=[pl.BlockSpec(memory_space=pltpu.VMEM), pl.BlockSpec(memory_space=pltpu.SMEM)],
        out_specs=pl.BlockSpec(memory_space=pl.ANY),
        scratch_shapes=[
            pltpu.VMEM((count, 2 * slots, rows // 2, width), panels.dtype),
            pltpu.SemaphoreType.DMA((2, count // 2 + 1, 2 * slots)),
            pltpu.SemaphoreType.DMA((count, 2 * slots)),
            pltpu.VMEM((rows, width), panels.dtype),
            pltpu.VMEM((rows // 2, width), panels.dtype),
            pltpu.VMEM((rows // 2, width), panels.dtype),
            pltpu.SemaphoreType.DMA((2, groups)),
            pltpu.SemaphoreType.DMA((2, groups)),
            pltpu.SemaphoreType.DMA((2,)),
            pltpu.SemaphoreType.DMA((2,)),
        ],
        compiler_params=pltpu.CompilerParams(collective_id=collective_id, has_side_effects=True),
    )(panels, home)


def kv_share_kernel(part_ref, out_ref, partner_part, mine, theirs, send_sems, recv_sems):
    me = lax.axis_index("tp")
    partner = me + 1 - 2 * (me % 2)
    across = me + 2 - 4 * ((me // 2) % 2)
    barrier = pltpu.get_barrier_semaphore()
    for neighbour in (partner, across):
        pl.semaphore_signal(barrier, inc=1, device_id={"tp": neighbour}, device_id_type=MESH)
    pl.semaphore_wait(barrier, 2)
    first = pltpu.make_async_remote_copy(
        src_ref=part_ref, dst_ref=partner_part, send_sem=send_sems.at[0], recv_sem=recv_sems.at[0],
        device_id={"tp": partner}, device_id_type=MESH,
    )
    first.start()
    first.wait()
    mine[...] = (part_ref[...] + partner_part[...]).astype(mine.dtype)
    second = pltpu.make_async_remote_copy(
        src_ref=mine, dst_ref=theirs, send_sem=send_sems.at[1], recv_sem=recv_sems.at[1],
        device_id={"tp": across}, device_id_type=MESH,
    )
    second.start()
    second.wait()
    holds_k = (me % 4) < 2
    out_ref[0] = jnp.where(holds_k, mine[...], theirs[...])
    out_ref[1] = jnp.where(holds_k, theirs[...], mine[...])


def kv_share(part, collective_id):
    return pl.pallas_call(
        kv_share_kernel,
        out_shape=jax.ShapeDtypeStruct((2,) + part.shape, jnp.bfloat16),
        in_specs=[pl.BlockSpec(memory_space=pltpu.VMEM)],
        out_specs=pl.BlockSpec(memory_space=pltpu.VMEM),
        scratch_shapes=[
            pltpu.VMEM(part.shape, part.dtype),
            pltpu.VMEM(part.shape, jnp.bfloat16),
            pltpu.VMEM(part.shape, jnp.bfloat16),
            pltpu.SemaphoreType.DMA((2,)),
            pltpu.SemaphoreType.DMA((2,)),
        ],
        compiler_params=pltpu.CompilerParams(collective_id=collective_id, has_side_effects=True),
    )(part)


def tail_kernel(count, scale, tokens_ref, gathered_hbm, lengths_ref, out_ref,
                gathered, load_sem, part_ref, partner_part, mine, theirs, staged, landed, send_sems, recv_sems,
                greet=True, arrive=None):
    width = landed.shape[-1]
    me = lax.axis_index("tp")
    partner = me + 1 - 2 * (me % 2)
    across = me + 2 - 4 * ((me // 2) % 2)
    if greet:
        load = pltpu.make_async_copy(gathered_hbm, gathered, load_sem)
        load.start()
        barrier = pltpu.get_barrier_semaphore()
        for step in range(1, count):
            peer = lax.rem(me + step, count)
            pl.semaphore_signal(barrier, inc=1, device_id={"tp": peer}, device_id_type=MESH)
        load.wait()
    core = me % 2
    half = gathered.shape[1] // 3
    sources = gathered.shape[0]
    first_half = core == 0
    projected = jnp.zeros((tokens_ref.shape[0], 2 * width), jnp.float32)
    for pair in range(sources // 2):
        if arrive is not None:
            arrive(2 * pair)
            arrive(2 * pair + 1)
        q_parts, kv_parts = [], []
        for source in (2 * pair, 2 * pair + 1):
            here = gathered[source, 0:half]
            kv = gathered[source, half:2 * half]
            there = gathered[source, 2 * half:3 * half]
            zero = jnp.zeros_like(kv)
            q_parts.append(jnp.where(first_half, jnp.concatenate([here, there], axis=0),
                                     jnp.concatenate([there, here], axis=0)))
            kv_parts.append(jnp.where(first_half, jnp.concatenate([kv, zero], axis=0),
                                      jnp.concatenate([zero, kv], axis=0)))
        slab = jnp.concatenate(
            [jnp.concatenate(q_parts, axis=0), jnp.concatenate(kv_parts, axis=0)], axis=1
        )
        columns = slab.shape[0]
        projected = projected + jnp.dot(
            tokens_ref[:, pair * columns:(pair + 1) * columns], slab, preferred_element_type=jnp.float32
        )
    part_ref[...] = projected[:, width:]
    query = projected[:, :width].astype(jnp.bfloat16)
    if greet:
        pl.semaphore_wait(barrier, count - 1)
    first = pltpu.make_async_remote_copy(
        src_ref=part_ref, dst_ref=partner_part, send_sem=send_sems.at[0], recv_sem=recv_sems.at[0],
        device_id={"tp": partner}, device_id_type=MESH,
    )
    first.start()
    first.wait()
    mine[...] = (part_ref[...] + partner_part[...]).astype(mine.dtype)
    second = pltpu.make_async_remote_copy(
        src_ref=mine, dst_ref=theirs, send_sem=send_sems.at[1], recv_sem=recv_sems.at[1],
        device_id={"tp": across}, device_id_type=MESH,
    )
    second.start()
    second.wait()
    holds_k = (me % 4) < 2
    keys = jnp.where(holds_k, mine[...], theirs[...])
    values = jnp.where(holds_k, theirs[...], mine[...])

    seq = query.shape[0]
    rows = seq // count
    blocks = 8
    block_rows = seq // blocks
    col = lax.broadcasted_iota(jnp.int32, (block_rows, seq), 1)
    col_segment = jnp.zeros((block_rows, seq), jnp.int32)
    bounds = []
    bound = lengths_ref[0, 0] * 0
    for response in range(lengths_ref.shape[1]):
        bound = bound + lengths_ref[0, response]
        bounds.append(bound)
        col_segment = col_segment + (col >= bound).astype(jnp.int32)
    copies = []
    for block in range(blocks):
        first_row = block * block_rows
        scores = lax.dot_general(
            query[first_row:first_row + block_rows], keys, (((1,), (1,)), ((), ())),
            preferred_element_type=jnp.float32,
        ) * scale
        row = lax.broadcasted_iota(jnp.int32, (block_rows, seq), 0) + first_row
        row_segment = jnp.zeros((block_rows, seq), jnp.int32)
        for bound in bounds:
            row_segment = row_segment + (row >= bound).astype(jnp.int32)
        allowed = (row_segment == col_segment) & (col <= row)
        masked = jnp.where(allowed, scores, -jnp.inf)
        peak = jnp.max(masked, axis=1, keepdims=True)
        weights = jnp.exp(masked - peak)
        probs = (weights / jnp.sum(weights, axis=1, keepdims=True)).astype(jnp.bfloat16)
        context = jnp.dot(probs, values, preferred_element_type=jnp.float32)
        per_block = block_rows // rows
        for i in range(per_block):
            target = block * per_block + i
            staged[target] = context[i * rows:(i + 1) * rows]
        for i in range(per_block):
            target = block * per_block + i
            copy = pltpu.make_async_remote_copy(
                src_ref=staged.at[target],
                dst_ref=landed.at[me],
                send_sem=send_sems.at[2 + target],
                recv_sem=recv_sems.at[2 + me],
                device_id={"tp": target},
                device_id_type=MESH,
            )

            @pl.when(target != me)
            def _():
                copy.start()

            copies.append((target, copy))
    landed[me] = staged[me]
    for target, copy in copies:
        @pl.when(target != me)
        def _():
            copy.wait_send()
    for source in range(count):
        incoming = pltpu.make_async_remote_copy(
            src_ref=staged.at[source],
            dst_ref=landed.at[source],
            send_sem=send_sems.at[0],
            recv_sem=recv_sems.at[2 + source],
            device_id={"tp": partner},
            device_id_type=MESH,
        )

        @pl.when(source != me)
        def _():
            incoming.wait_recv()
    for source in range(count):
        out_ref[:, source * width:(source + 1) * width] = landed[source]


def tail(tokens, gathered, lengths, count, collective_id):
    seq, width = tokens.shape[0], gathered.shape[2]
    part = jax.ShapeDtypeStruct((seq, width), jnp.float32)
    rows = seq // count
    vmem = pl.BlockSpec(memory_space=pltpu.VMEM)
    return pl.pallas_call(
        functools.partial(tail_kernel, count, width ** (-0.5)),
        out_shape=jax.ShapeDtypeStruct((rows, count * width), jnp.float32),
        in_specs=[vmem, pl.BlockSpec(memory_space=pl.ANY), pl.BlockSpec(memory_space=pltpu.SMEM)],
        out_specs=vmem,
        scratch_shapes=[
            pltpu.VMEM(gathered.shape, gathered.dtype),
            pltpu.SemaphoreType.DMA(()),
            pltpu.VMEM(part.shape, part.dtype),
            pltpu.VMEM(part.shape, part.dtype),
            pltpu.VMEM(part.shape, jnp.bfloat16),
            pltpu.VMEM(part.shape, jnp.bfloat16),
            pltpu.VMEM((count, rows, width), jnp.float32),
            pltpu.VMEM((count, rows, width), jnp.float32),
            pltpu.SemaphoreType.DMA((count + 1,)),
            pltpu.SemaphoreType.DMA((count + 1,)),
        ],
        compiler_params=pltpu.CompilerParams(collective_id=collective_id, has_side_effects=True),
    )(tokens, gathered, lengths)


def whole_kernel(count, groups, scale, panels_ref, home_ref, tokens_ref, lengths_ref, out_ref, *scratch):
    ring_scratch, gathered, tail_scratch = scratch[:10], scratch[10], scratch[11:]
    me = lax.axis_index("tp")
    here = lax.axis_index("grp")
    total = 2 * count
    barrier = pltpu.get_barrier_semaphore()
    for step in range(1, total):
        peer = lax.rem(me + step, total)
        pl.semaphore_signal(barrier, inc=1, device_id={"tp": peer}, device_id_type=MESH)
    for step in range(1, groups):
        peer = lax.rem(here + step, groups)
        pl.semaphore_signal(barrier, inc=1, device_id={"grp": peer}, device_id_type=MESH)
    pl.semaphore_wait(barrier, total + groups - 2)
    arrive, finish = chip_ring_kernel(count, groups, panels_ref, home_ref, gathered, *ring_scratch, greet=False)
    tail_kernel(total, scale, tokens_ref, None, lengths_ref, out_ref, gathered, None, *tail_scratch, greet=False,
                arrive=arrive)
    finish()


def whole(panels, home, tokens, lengths, count, groups, collective_id):
    slots, rows, width = panels.shape
    seq = tokens.shape[0]
    total = 2 * count
    out_rows = seq // total
    part = (seq, width)
    vmem = pl.BlockSpec(memory_space=pltpu.VMEM)
    smem = pl.BlockSpec(memory_space=pltpu.SMEM)
    return pl.pallas_call(
        functools.partial(whole_kernel, count, groups, width ** (-0.5)),
        out_shape=jax.ShapeDtypeStruct((out_rows, total * width), jnp.float32),
        in_specs=[vmem, smem, vmem, smem],
        out_specs=vmem,
        scratch_shapes=[
            pltpu.VMEM((count, 2 * slots, rows // 2, width), panels.dtype),
            pltpu.SemaphoreType.DMA((2, count // 2 + 1, 2 * slots)),
            pltpu.SemaphoreType.DMA((count, 2 * slots)),
            pltpu.VMEM((rows, width), panels.dtype),
            pltpu.VMEM((rows // 2, width), panels.dtype),
            pltpu.VMEM((rows // 2, width), panels.dtype),
            pltpu.SemaphoreType.DMA((2, groups)),
            pltpu.SemaphoreType.DMA((2, groups)),
            pltpu.SemaphoreType.DMA((2,)),
            pltpu.SemaphoreType.DMA((2,)),
            pltpu.VMEM((groups, rows + rows // 2, width), panels.dtype),
            pltpu.VMEM(part, jnp.float32),
            pltpu.VMEM(part, jnp.float32),
            pltpu.VMEM(part, jnp.bfloat16),
            pltpu.VMEM(part, jnp.bfloat16),
            pltpu.VMEM((total, out_rows, width), jnp.float32),
            pltpu.VMEM((total, out_rows, width), jnp.float32),
            pltpu.SemaphoreType.DMA((total + 2,)),
            pltpu.SemaphoreType.DMA((total + 2,)),
        ],
        compiler_params=pltpu.CompilerParams(collective_id=collective_id, has_side_effects=True),
    )(panels, home, tokens, lengths)


def grid_kernel(width, send_ref, out_ref, landed, send_sems, recv_sems):
    me = lax.axis_index("grp")
    core = lax.axis_index("tp") % 2
    col, row = me % width, me // width

    def node(c, r):
        return lax.rem(r + width, width) * width + lax.rem(c + width, width)

    def along(dim, c, r, k):
        return node(c + k, r) if dim == 0 else node(c, r + k)

    barrier = pltpu.get_barrier_semaphore()
    neighbours = [node(col + 1, row), node(col - 1, row), node(col, row + 1), node(col, row - 1)]
    for neighbour in neighbours:
        pl.semaphore_signal(barrier, inc=1, device_id={"grp": neighbour}, device_id_type=MESH)
    pl.semaphore_wait(barrier, 4)

    landed[me] = send_ref[...]
    sends = []

    def send(source, origin, half, target):
        copy = pltpu.make_async_remote_copy(
            src_ref=source,
            dst_ref=landed.at[origin, half],
            send_sem=send_sems.at[len(sends)],
            recv_sem=recv_sems.at[origin, half],
            device_id={"grp": target},
            device_id_type=MESH,
        )
        copy.start()
        sends.append(copy)

    def arrive(origin, half):
        pltpu.make_async_remote_copy(
            src_ref=send_ref.at[half],
            dst_ref=landed.at[origin, half],
            send_sem=send_sems.at[0],
            recv_sem=recv_sems.at[origin, half],
            device_id={"grp": neighbours[0]},
            device_id_type=MESH,
        ).wait_recv()

    ahead = 1 - 2 * core

    def phase(lines, half, dim):
        for k in (1, -1):
            for line in lines:
                origin = along(1 - dim, col, row, line)
                source = send_ref.at[half] if line == 0 else landed.at[origin, half]
                send(source, origin, half, along(dim, col, row, k))
        for line in lines:
            for k in (1, -1):
                arrive(along(dim, along(1 - dim, col, row, line) % width, along(1 - dim, col, row, line) // width, k), half)
        for line in lines:
            base = along(1 - dim, col, row, line)
            bc, br = base % width, base // width
            send(landed.at[along(dim, bc, br, -ahead), half], along(dim, bc, br, -ahead), half,
                 along(dim, col, row, ahead))
        for line in lines:
            base = along(1 - dim, col, row, line)
            arrive(along(dim, base % width, base // width, 2), half)

    phase([0], 0, 0)
    phase([0], 1, 1)
    phase([0, 1, -1, 2], 0, 1)
    phase([0, 1, -1, 2], 1, 0)
    for copy in sends:
        copy.wait_send()
    out_ref[...] = landed[...]


def grid_gather(x, width, collective_id):
    count = width * width
    x = x.reshape((2, x.shape[0] // 2) + x.shape[1:])
    gathered = pl.pallas_call(
        functools.partial(grid_kernel, width),
        out_shape=jax.ShapeDtypeStruct((count,) + x.shape, x.dtype),
        in_specs=[pl.BlockSpec(memory_space=pltpu.VMEM)],
        out_specs=pl.BlockSpec(memory_space=pltpu.VMEM),
        scratch_shapes=[
            pltpu.VMEM((count,) + x.shape, x.dtype),
            pltpu.SemaphoreType.DMA((2 * (count - 1),)),
            pltpu.SemaphoreType.DMA((count, 2)),
        ],
        compiler_params=pltpu.CompilerParams(collective_id=collective_id, has_side_effects=True),
    )(x)
    return gathered.reshape((count, x.shape[0] * x.shape[1]) + x.shape[2:])


def gather_hbm_kernel(axis, count, send_ref, out_ref, send_sems, recv_sems, local_sem):
    me = lax.axis_index(axis)
    barrier = pltpu.get_barrier_semaphore()
    for step in range(1, count):
        peer = lax.rem(me + step, count)
        pl.semaphore_signal(barrier, inc=1, device_id={axis: peer}, device_id_type=MESH)
    pl.semaphore_wait(barrier, count - 1)
    copies = []
    for step in range(1, count):
        peer = lax.rem(me + step, count)
        copy = pltpu.make_async_remote_copy(
            src_ref=send_ref,
            dst_ref=out_ref.at[me],
            send_sem=send_sems.at[step],
            recv_sem=recv_sems.at[step],
            device_id={axis: peer},
            device_id_type=MESH,
        )
        copy.start()
        copies.append(copy)
    local = pltpu.make_async_copy(send_ref, out_ref.at[me], local_sem)
    local.start()
    for copy in copies:
        copy.wait()
    local.wait()


def gather_hbm(x, axis, count, collective_id):
    return pl.pallas_call(
        functools.partial(gather_hbm_kernel, axis, count),
        out_shape=jax.ShapeDtypeStruct((count,) + x.shape, x.dtype),
        in_specs=[pl.BlockSpec(memory_space=pltpu.VMEM)],
        out_specs=pl.BlockSpec(memory_space=pl.ANY),
        scratch_shapes=[
            pltpu.SemaphoreType.DMA((count,)),
            pltpu.SemaphoreType.DMA((count,)),
            pltpu.SemaphoreType.DMA(()),
        ],
        compiler_params=pltpu.CompilerParams(collective_id=collective_id, has_side_effects=True),
    )(x)


def weights_gather_kernel(count, own_ref, for_partner_ref, out_ref, partner_rows,
                          send_sems, recv_sems, partner_sems, local_sems):
    me = lax.axis_index("grp")
    member = lax.axis_index("tp")
    partner = member + 1 - 2 * (member % 2)
    rows = own_ref.shape[0]
    barrier = pltpu.get_barrier_semaphore()
    pl.semaphore_signal(barrier, inc=1, device_id={"tp": partner}, device_id_type=MESH)
    for step in range(1, count):
        peer = lax.rem(me + step, count)
        pl.semaphore_signal(barrier, inc=1, device_id={"grp": peer}, device_id_type=MESH)
    pl.semaphore_wait(barrier, count)
    to_partner = pltpu.make_async_remote_copy(
        src_ref=for_partner_ref, dst_ref=partner_rows, send_sem=partner_sems.at[0],
        recv_sem=partner_sems.at[1], device_id={"tp": partner}, device_id_type=MESH,
    )
    to_partner.start()
    copies = []

    def spread(part, source, window):
        for step in range(1, count):
            peer = lax.rem(me + step, count)
            copy = pltpu.make_async_remote_copy(
                src_ref=source,
                dst_ref=out_ref.at[me, window],
                send_sem=send_sems.at[part, step],
                recv_sem=recv_sems.at[part, step],
                device_id={"grp": peer},
                device_id_type=MESH,
            )
            copy.start()
            copies.append(copy)
        local = pltpu.make_async_copy(source, out_ref.at[me, window], local_sems.at[part])
        local.start()
        copies.append(local)

    spread(0, own_ref, pl.ds(0, rows))
    to_partner.wait()
    spread(1, partner_rows, pl.ds(rows, partner_rows.shape[0]))
    for copy in copies:
        copy.wait()


def weights_gather(own, for_partner, count, collective_id):
    rows = own.shape[0] + for_partner.shape[0]
    return pl.pallas_call(
        functools.partial(weights_gather_kernel, count),
        out_shape=jax.ShapeDtypeStruct((count, rows) + own.shape[1:], own.dtype),
        in_specs=[pl.BlockSpec(memory_space=pltpu.VMEM)] * 2,
        out_specs=pl.BlockSpec(memory_space=pl.ANY),
        scratch_shapes=[
            pltpu.VMEM(for_partner.shape, for_partner.dtype),
            pltpu.SemaphoreType.DMA((2, count)),
            pltpu.SemaphoreType.DMA((2, count)),
            pltpu.SemaphoreType.DMA((2,)),
            pltpu.SemaphoreType.DMA((2,)),
        ],
        compiler_params=pltpu.CompilerParams(collective_id=collective_id, has_side_effects=True),
    )(own, for_partner)


def exchange_kernel(axis, count, scatter, send_ref, out_ref, landed, send_sems, recv_sems):
    me = lax.axis_index(axis)
    barrier = pltpu.get_barrier_semaphore()
    for step in range(1, count):
        peer = lax.rem(me + step, count)
        pl.semaphore_signal(barrier, inc=1, device_id={axis: peer}, device_id_type=MESH)
    pl.semaphore_wait(barrier, count - 1)
    copies = []
    for step in range(1, count):
        peer = lax.rem(me + step, count)
        source = send_ref.at[peer] if scatter else send_ref
        copy = pltpu.make_async_remote_copy(
            src_ref=source,
            dst_ref=landed.at[me],
            send_sem=send_sems.at[step],
            recv_sem=recv_sems.at[step],
            device_id={axis: peer},
            device_id_type=MESH,
        )
        copy.start()
        copies.append(copy)
    landed[me] = send_ref[me] if scatter else send_ref[...]
    for copy in copies:
        copy.wait()
    if scatter:
        width = landed.shape[-1]
        for source in range(count):
            out_ref[:, source * width:(source + 1) * width] = landed[source]
    else:
        out_ref[...] = landed[...]


def exchange(x, axis, count, scatter, collective_id):
    piece = x.shape[1:] if scatter else x.shape
    result = (piece[0], count * piece[1]) if scatter else (count,) + piece
    return pl.pallas_call(
        functools.partial(exchange_kernel, axis, count, scatter),
        out_shape=jax.ShapeDtypeStruct(result, x.dtype),
        in_specs=[pl.BlockSpec(memory_space=pltpu.VMEM)],
        out_specs=pl.BlockSpec(memory_space=pltpu.VMEM),
        scratch_shapes=[
            pltpu.VMEM((count,) + piece, x.dtype),
            pltpu.SemaphoreType.DMA((count,)),
            pltpu.SemaphoreType.DMA((count,)),
        ],
        compiler_params=pltpu.CompilerParams(collective_id=collective_id, has_side_effects=True),
    )(x)


def on_device(tokens, trainer_panels, panel_home, lengths):
    tp_count = lax.axis_size("tp")
    grp_count = lax.axis_size("grp")
    member_id = lax.axis_index("tp")
    kv_count = (panel_home.shape[0] - tp_count) // 2
    group_size = tp_count // kv_count
    head_dim = trainer_panels.shape[2]
    block_rows = trainer_panels.shape[1]
    half_rows = block_rows // 2
    seq_total = tokens.shape[0]

    return whole(trainer_panels, panel_home, tokens, lengths, tp_count // 2, grp_count, 4)


def solution(mesh):
    placed = (P("grp", None), P("tp", "grp", None), P(), P("grp", None))
    return jax.shard_map(
        on_device, mesh=mesh, in_specs=placed, out_specs=P(("grp", "tp"), None), check_vma=False
    )
```

```python
import functools

import jax
import jax.numpy as jnp
from jax import lax
from jax.experimental import pallas as pl
from jax.experimental.pallas import tpu as pltpu
from jax.sharding import PartitionSpec as P

MESH = pl.DeviceIdType.MESH


def ring_kernel(count, stride, chunks, send_ref, out_ref, landed, send_sems, recv_sems):
    me = lax.axis_index("tp")
    total = count * stride
    right, left = lax.rem(me + stride, total), lax.rem(me + total - stride, total)
    spot = me // stride
    barrier = pltpu.get_barrier_semaphore()
    for neighbour in (left, right):
        pl.semaphore_signal(barrier, inc=1, device_id={"tp": neighbour}, device_id_type=MESH)
    pl.semaphore_wait(barrier, 2)

    def incoming(origin, chunk):
        return pltpu.make_async_remote_copy(
            src_ref=send_ref.at[chunk],
            dst_ref=landed.at[origin, chunk],
            send_sem=send_sems.at[0, 0, 0],
            recv_sem=recv_sems.at[origin, chunk],
            device_id={"tp": right},
            device_id_type=MESH,
        )

    landed[spot] = send_ref[...]
    sends = []
    far_right, far_left = count // 2, (count - 1) // 2
    for step in range(1, far_right + 1):
        for chunk in range(chunks):
            streams = [(0, right, lax.rem(spot + count - (step - 1), count))]
            if step <= far_left:
                streams.append((1, left, lax.rem(spot + step - 1, count)))
            for way, target, origin in streams:
                if step > 1:
                    incoming(origin, chunk).wait_recv()
                source = send_ref.at[chunk] if step == 1 else landed.at[origin, chunk]
                copy = pltpu.make_async_remote_copy(
                    src_ref=source,
                    dst_ref=landed.at[origin, chunk],
                    send_sem=send_sems.at[way, step, chunk],
                    recv_sem=recv_sems.at[origin, chunk],
                    device_id={"tp": target},
                    device_id_type=MESH,
                )
                copy.start()
                sends.append(copy)
    for chunk in range(chunks):
        incoming(lax.rem(spot + count - far_right, count), chunk).wait_recv()
        incoming(lax.rem(spot + far_left, count), chunk).wait_recv()
    for copy in sends:
        copy.wait_send()
    out_ref[...] = landed[...]


def ring_gather(x, count, stride, chunks, collective_id):
    x = x.reshape((chunks, x.shape[0] // chunks) + x.shape[1:])
    gathered = pl.pallas_call(
        functools.partial(ring_kernel, count, stride, chunks),
        out_shape=jax.ShapeDtypeStruct((count,) + x.shape, x.dtype),
        in_specs=[pl.BlockSpec(memory_space=pltpu.VMEM)],
        out_specs=pl.BlockSpec(memory_space=pltpu.VMEM),
        scratch_shapes=[
            pltpu.VMEM((count,) + x.shape, x.dtype),
            pltpu.SemaphoreType.DMA((2, count // 2 + 1, chunks)),
            pltpu.SemaphoreType.DMA((count, chunks)),
        ],
        compiler_params=pltpu.CompilerParams(collective_id=collective_id, has_side_effects=True),
    )(x)
    return gathered.reshape((count * x.shape[0] * x.shape[1],) + x.shape[2:])


def chip_ring_kernel(count, groups, panels_ref, home_ref, out_ref, landed, send_sems, recv_sems,
                     own_ref, partner_ref, partner_rows, grp_send_sems, grp_recv_sems, partner_sems, local_sems,
                     greet=True):
    me = lax.axis_index("tp")
    here = lax.axis_index("grp")
    total = 2 * count
    core = me % 2
    partner = me + 1 - 2 * core
    right, left = lax.rem(me + 2, total), lax.rem(me + total - 2, total)
    spot = me // 2
    half = panels_ref.shape[1] // 2
    if greet:
        barrier = pltpu.get_barrier_semaphore()
        for neighbour in (left, right, partner):
            pl.semaphore_signal(barrier, inc=1, device_id={"tp": neighbour}, device_id_type=MESH)
        for step in range(1, groups):
            peer = lax.rem(here + step, groups)
            pl.semaphore_signal(barrier, inc=1, device_id={"grp": peer}, device_id_type=MESH)
        pl.semaphore_wait(barrier, 2 + groups)

    def rows_of(slot, which):
        return panels_ref.at[slot, pl.ds(pl.multiple_of(which * half, 16), half)]

    def incoming(origin, chunk):
        return pltpu.make_async_remote_copy(
            src_ref=rows_of(0, 0),
            dst_ref=landed.at[origin, chunk],
            send_sem=send_sems.at[0, 0, 0],
            recv_sem=recv_sems.at[origin, chunk],
            device_id={"tp": right},
            device_id_type=MESH,
        )

    sends = []

    def send(source, origin, chunk, sem, target):
        copy = pltpu.make_async_remote_copy(
            src_ref=source,
            dst_ref=landed.at[origin, chunk],
            send_sem=sem,
            recv_sem=recv_sems.at[origin, chunk],
            device_id={"tp": target},
            device_id_type=MESH,
        )
        copy.start()
        sends.append(copy)

    own = [2 * core + j for j in range(2)]
    theirs = [2 * (1 - core) + j for j in range(2)]
    for j in range(2):
        send(rows_of(j, 1 - core), spot, own[j], send_sems.at[0, 0, 1 + j], partner)
        landed[spot, own[j]] = rows_of(j, core)[...]
    far_right, far_left = count // 2, (count - 1) // 2
    first = [(rows_of(j, core), own[j]) for j in range(2)] + [(None, theirs[j]) for j in range(2)]
    for position, (source, chunk) in enumerate(first):
        if source is None:
            incoming(spot, chunk).wait_recv()
            source = landed.at[spot, chunk]
        send(source, spot, chunk, send_sems.at[0, 1, position], right)
        if far_left >= 1:
            send(source, spot, chunk, send_sems.at[1, 1, position], left)
    for step in range(2, far_right + 1):
        for chunk in range(4):
            streams = [(0, right, lax.rem(spot + count - (step - 1), count))]
            if step <= far_left:
                streams.append((1, left, lax.rem(spot + step - 1, count)))
            for way, target, origin in streams:
                incoming(origin, chunk).wait_recv()
                send(landed.at[origin, chunk], origin, chunk, send_sems.at[way, step, chunk], target)
    for chunk in range(4):
        incoming(lax.rem(spot + count - far_right, count), chunk).wait_recv()
        incoming(lax.rem(spot + far_left, count), chunk).wait_recv()
    for copy in sends:
        copy.wait_send()
    heads = total
    kv_heads = (home_ref.shape[0] - heads) // 2
    group = heads // kv_heads
    quarter = me % group
    kv_panel = heads + me // group + kv_heads * (quarter // 2)
    chip_slots = landed.shape[1]

    def block(panel):
        slot = home_ref[panel]
        return landed[slot // chip_slots, slot % chip_slots]

    own_ref[0:half] = block(me)
    own_ref[half:2 * half] = block(kv_panel)
    partner_ref[...] = block(partner)

    to_partner = pltpu.make_async_remote_copy(
        src_ref=partner_ref, dst_ref=partner_rows, send_sem=partner_sems.at[0],
        recv_sem=partner_sems.at[1], device_id={"tp": partner}, device_id_type=MESH,
    )
    to_partner.start()
    copies, local_copies = [], []

    def spread(part, source, window):
        for step in range(1, groups):
            peer = lax.rem(here + step, groups)
            copy = pltpu.make_async_remote_copy(
                src_ref=source,
                dst_ref=out_ref.at[here, window],
                send_sem=grp_send_sems.at[part, step],
                recv_sem=grp_recv_sems.at[part, step],
                device_id={"grp": peer},
                device_id_type=MESH,
            )
            copy.start()
            copies.append(copy)
        local = pltpu.make_async_copy(source, out_ref.at[here, window], local_sems.at[part])
        local.start()
        local_copies.append(local)

    spread(0, own_ref, pl.ds(0, 2 * half))
    to_partner.wait()
    spread(1, partner_rows, pl.ds(2 * half, half))
    for copy in local_copies:
        copy.wait()
    if greet:
        for copy in copies:
            copy.wait()
        return None
    windows = [(own_ref, pl.ds(0, 2 * half)), (partner_rows, pl.ds(2 * half, half))]

    def arrive(source):
        step = lax.rem(here + groups - source, groups)

        @pl.when(step != 0)
        def _():
            for part, (shape_ref, window) in enumerate(windows):
                pltpu.make_async_remote_copy(
                    src_ref=shape_ref,
                    dst_ref=out_ref.at[here, window],
                    send_sem=grp_send_sems.at[part, 0],
                    recv_sem=grp_recv_sems.at[part, step],
                    device_id={"grp": lax.rem(here + 1, groups)},
                    device_id_type=MESH,
                ).wait_recv()

    def finish():
        for copy in copies:
            copy.wait_send()

    return arrive, finish


def chip_ring_gather(panels, home, count, groups, collective_id):
    slots, rows, width = panels.shape
    return pl.pallas_call(
        functools.partial(chip_ring_kernel, count, groups),
        out_shape=jax.ShapeDtypeStruct((groups, rows + rows // 2, width), panels.dtype),
        in_specs=[pl.BlockSpec(memory_space=pltpu.VMEM), pl.BlockSpec(memory_space=pltpu.SMEM)],
        out_specs=pl.BlockSpec(memory_space=pl.ANY),
        scratch_shapes=[
            pltpu.VMEM((count, 2 * slots, rows // 2, width), panels.dtype),
            pltpu.SemaphoreType.DMA((2, count // 2 + 1, 2 * slots)),
            pltpu.SemaphoreType.DMA((count, 2 * slots)),
            pltpu.VMEM((rows, width), panels.dtype),
            pltpu.VMEM((rows // 2, width), panels.dtype),
            pltpu.VMEM((rows // 2, width), panels.dtype),
            pltpu.SemaphoreType.DMA((2, groups)),
            pltpu.SemaphoreType.DMA((2, groups)),
            pltpu.SemaphoreType.DMA((2,)),
            pltpu.SemaphoreType.DMA((2,)),
        ],
        compiler_params=pltpu.CompilerParams(collective_id=collective_id, has_side_effects=True),
    )(panels, home)


def kv_share_kernel(part_ref, out_ref, partner_part, mine, theirs, send_sems, recv_sems):
    me = lax.axis_index("tp")
    partner = me + 1 - 2 * (me % 2)
    across = me + 2 - 4 * ((me // 2) % 2)
    barrier = pltpu.get_barrier_semaphore()
    for neighbour in (partner, across):
        pl.semaphore_signal(barrier, inc=1, device_id={"tp": neighbour}, device_id_type=MESH)
    pl.semaphore_wait(barrier, 2)
    first = pltpu.make_async_remote_copy(
        src_ref=part_ref, dst_ref=partner_part, send_sem=send_sems.at[0], recv_sem=recv_sems.at[0],
        device_id={"tp": partner}, device_id_type=MESH,
    )
    first.start()
    first.wait()
    mine[...] = (part_ref[...] + partner_part[...]).astype(mine.dtype)
    second = pltpu.make_async_remote_copy(
        src_ref=mine, dst_ref=theirs, send_sem=send_sems.at[1], recv_sem=recv_sems.at[1],
        device_id={"tp": across}, device_id_type=MESH,
    )
    second.start()
    second.wait()
    holds_k = (me % 4) < 2
    out_ref[0] = jnp.where(holds_k, mine[...], theirs[...])
    out_ref[1] = jnp.where(holds_k, theirs[...], mine[...])


def kv_share(part, collective_id):
    return pl.pallas_call(
        kv_share_kernel,
        out_shape=jax.ShapeDtypeStruct((2,) + part.shape, jnp.bfloat16),
        in_specs=[pl.BlockSpec(memory_space=pltpu.VMEM)],
        out_specs=pl.BlockSpec(memory_space=pltpu.VMEM),
        scratch_shapes=[
            pltpu.VMEM(part.shape, part.dtype),
            pltpu.VMEM(part.shape, jnp.bfloat16),
            pltpu.VMEM(part.shape, jnp.bfloat16),
            pltpu.SemaphoreType.DMA((2,)),
            pltpu.SemaphoreType.DMA((2,)),
        ],
        compiler_params=pltpu.CompilerParams(collective_id=collective_id, has_side_effects=True),
    )(part)


def tail_kernel(count, scale, tokens_ref, gathered_hbm, lengths_ref, out_ref,
                gathered, load_sem, part_ref, partner_part, mine, theirs, staged, landed, send_sems, recv_sems,
                greet=True, arrive=None):
    width = landed.shape[-1]
    me = lax.axis_index("tp")
    partner = me + 1 - 2 * (me % 2)
    across = me + 2 - 4 * ((me // 2) % 2)
    if greet:
        load = pltpu.make_async_copy(gathered_hbm, gathered, load_sem)
        load.start()
        barrier = pltpu.get_barrier_semaphore()
        for step in range(1, count):
            peer = lax.rem(me + step, count)
            pl.semaphore_signal(barrier, inc=1, device_id={"tp": peer}, device_id_type=MESH)
        load.wait()
    core = me % 2
    half = gathered.shape[1] // 3
    sources = gathered.shape[0]
    first_half = core == 0
    projected = jnp.zeros((tokens_ref.shape[0], 2 * width), jnp.float32)
    for pair in range(sources // 2):
        if arrive is not None:
            arrive(2 * pair)
            arrive(2 * pair + 1)
        q_parts, kv_parts = [], []
        for source in (2 * pair, 2 * pair + 1):
            here = gathered[source, 0:half]
            kv = gathered[source, half:2 * half]
            there = gathered[source, 2 * half:3 * half]
            zero = jnp.zeros_like(kv)
            q_parts.append(jnp.where(first_half, jnp.concatenate([here, there], axis=0),
                                     jnp.concatenate([there, here], axis=0)))
            kv_parts.append(jnp.where(first_half, jnp.concatenate([kv, zero], axis=0),
                                      jnp.concatenate([zero, kv], axis=0)))
        slab = jnp.concatenate(
            [jnp.concatenate(q_parts, axis=0), jnp.concatenate(kv_parts, axis=0)], axis=1
        )
        columns = slab.shape[0]
        projected = projected + jnp.dot(
            tokens_ref[:, pair * columns:(pair + 1) * columns], slab, preferred_element_type=jnp.float32
        )
    part_ref[...] = projected[:, width:]
    query = projected[:, :width].astype(jnp.bfloat16)
    if greet:
        pl.semaphore_wait(barrier, count - 1)
    first = pltpu.make_async_remote_copy(
        src_ref=part_ref, dst_ref=partner_part, send_sem=send_sems.at[0], recv_sem=recv_sems.at[0],
        device_id={"tp": partner}, device_id_type=MESH,
    )
    first.start()
    first.wait()
    mine[...] = (part_ref[...] + partner_part[...]).astype(mine.dtype)
    second = pltpu.make_async_remote_copy(
        src_ref=mine, dst_ref=theirs, send_sem=send_sems.at[1], recv_sem=recv_sems.at[1],
        device_id={"tp": across}, device_id_type=MESH,
    )
    second.start()
    second.wait()
    holds_k = (me % 4) < 2
    keys = jnp.where(holds_k, mine[...], theirs[...])
    values = jnp.where(holds_k, theirs[...], mine[...])

    seq = query.shape[0]
    rows = seq // count
    blocks = 4
    block_rows = seq // blocks
    bounds = []
    bound = lengths_ref[0, 0] * 0
    for response in range(lengths_ref.shape[1]):
        bound = bound + lengths_ref[0, response]
        bounds.append(bound)
    copies = []
    for block in range(blocks):
        first_row = block * block_rows
        seen = first_row + block_rows
        scores = lax.dot_general(
            query[first_row:seen], keys[0:seen], (((1,), (1,)), ((), ())),
            preferred_element_type=jnp.float32,
        ) * scale
        row = lax.broadcasted_iota(jnp.int32, (block_rows, seen), 0) + first_row
        col = lax.broadcasted_iota(jnp.int32, (block_rows, seen), 1)
        row_segment = jnp.zeros((block_rows, seen), jnp.int32)
        col_segment = jnp.zeros((block_rows, seen), jnp.int32)
        for bound in bounds:
            row_segment = row_segment + (row >= bound).astype(jnp.int32)
            col_segment = col_segment + (col >= bound).astype(jnp.int32)
        allowed = (row_segment == col_segment) & (col <= row)
        masked = jnp.where(allowed, scores, -jnp.inf)
        peak = jnp.max(masked, axis=1, keepdims=True)
        weights = jnp.exp(masked - peak)
        probs = (weights / jnp.sum(weights, axis=1, keepdims=True)).astype(jnp.bfloat16)
        context = jnp.dot(probs, values[0:seen], preferred_element_type=jnp.float32)
        per_block = block_rows // rows
        for i in range(per_block):
            target = block * per_block + i
            staged[target] = context[i * rows:(i + 1) * rows]
        for i in range(per_block):
            target = block * per_block + i
            copy = pltpu.make_async_remote_copy(
                src_ref=staged.at[target],
                dst_ref=landed.at[me],
                send_sem=send_sems.at[2 + target],
                recv_sem=recv_sems.at[2 + me],
                device_id={"tp": target},
                device_id_type=MESH,
            )

            @pl.when(target != me)
            def _():
                copy.start()

            copies.append((target, copy))
    landed[me] = staged[me]
    for target, copy in copies:
        @pl.when(target != me)
        def _():
            copy.wait_send()
    for source in range(count):
        incoming = pltpu.make_async_remote_copy(
            src_ref=staged.at[source],
            dst_ref=landed.at[source],
            send_sem=send_sems.at[0],
            recv_sem=recv_sems.at[2 + source],
            device_id={"tp": partner},
            device_id_type=MESH,
        )

        @pl.when(source != me)
        def _():
            incoming.wait_recv()
    for source in range(count):
        out_ref[:, source * width:(source + 1) * width] = landed[source]


def tail(tokens, gathered, lengths, count, collective_id):
    seq, width = tokens.shape[0], gathered.shape[2]
    part = jax.ShapeDtypeStruct((seq, width), jnp.float32)
    rows = seq // count
    vmem = pl.BlockSpec(memory_space=pltpu.VMEM)
    return pl.pallas_call(
        functools.partial(tail_kernel, count, width ** (-0.5)),
        out_shape=jax.ShapeDtypeStruct((rows, count * width), jnp.float32),
        in_specs=[vmem, pl.BlockSpec(memory_space=pl.ANY), pl.BlockSpec(memory_space=pltpu.SMEM)],
        out_specs=vmem,
        scratch_shapes=[
            pltpu.VMEM(gathered.shape, gathered.dtype),
            pltpu.SemaphoreType.DMA(()),
            pltpu.VMEM(part.shape, part.dtype),
            pltpu.VMEM(part.shape, part.dtype),
            pltpu.VMEM(part.shape, jnp.bfloat16),
            pltpu.VMEM(part.shape, jnp.bfloat16),
            pltpu.VMEM((count, rows, width), jnp.float32),
            pltpu.VMEM((count, rows, width), jnp.float32),
            pltpu.SemaphoreType.DMA((count + 1,)),
            pltpu.SemaphoreType.DMA((count + 1,)),
        ],
        compiler_params=pltpu.CompilerParams(collective_id=collective_id, has_side_effects=True),
    )(tokens, gathered, lengths)


def whole_kernel(count, groups, scale, panels_ref, home_ref, tokens_ref, lengths_ref, out_ref, *scratch):
    ring_scratch, gathered, tail_scratch = scratch[:10], scratch[10], scratch[11:]
    me = lax.axis_index("tp")
    here = lax.axis_index("grp")
    total = 2 * count
    barrier = pltpu.get_barrier_semaphore()
    for step in range(1, total):
        peer = lax.rem(me + step, total)
        pl.semaphore_signal(barrier, inc=1, device_id={"tp": peer}, device_id_type=MESH)
    for step in range(1, groups):
        peer = lax.rem(here + step, groups)
        pl.semaphore_signal(barrier, inc=1, device_id={"grp": peer}, device_id_type=MESH)
    pl.semaphore_wait(barrier, total + groups - 2)
    arrive, finish = chip_ring_kernel(count, groups, panels_ref, home_ref, gathered, *ring_scratch, greet=False)
    tail_kernel(total, scale, tokens_ref, None, lengths_ref, out_ref, gathered, None, *tail_scratch, greet=False,
                arrive=arrive)
    finish()


def whole(panels, home, tokens, lengths, count, groups, collective_id):
    slots, rows, width = panels.shape
    seq = tokens.shape[0]
    total = 2 * count
    out_rows = seq // total
    part = (seq, width)
    vmem = pl.BlockSpec(memory_space=pltpu.VMEM)
    smem = pl.BlockSpec(memory_space=pltpu.SMEM)
    return pl.pallas_call(
        functools.partial(whole_kernel, count, groups, width ** (-0.5)),
        out_shape=jax.ShapeDtypeStruct((out_rows, total * width), jnp.float32),
        in_specs=[vmem, smem, vmem, smem],
        out_specs=vmem,
        scratch_shapes=[
            pltpu.VMEM((count, 2 * slots, rows // 2, width), panels.dtype),
            pltpu.SemaphoreType.DMA((2, count // 2 + 1, 2 * slots)),
            pltpu.SemaphoreType.DMA((count, 2 * slots)),
            pltpu.VMEM((rows, width), panels.dtype),
            pltpu.VMEM((rows // 2, width), panels.dtype),
            pltpu.VMEM((rows // 2, width), panels.dtype),
            pltpu.SemaphoreType.DMA((2, groups)),
            pltpu.SemaphoreType.DMA((2, groups)),
            pltpu.SemaphoreType.DMA((2,)),
            pltpu.SemaphoreType.DMA((2,)),
            pltpu.VMEM((groups, rows + rows // 2, width), panels.dtype),
            pltpu.VMEM(part, jnp.float32),
            pltpu.VMEM(part, jnp.float32),
            pltpu.VMEM(part, jnp.bfloat16),
            pltpu.VMEM(part, jnp.bfloat16),
            pltpu.VMEM((total, out_rows, width), jnp.float32),
            pltpu.VMEM((total, out_rows, width), jnp.float32),
            pltpu.SemaphoreType.DMA((total + 2,)),
            pltpu.SemaphoreType.DMA((total + 2,)),
        ],
        compiler_params=pltpu.CompilerParams(collective_id=collective_id, has_side_effects=True),
    )(panels, home, tokens, lengths)


def grid_kernel(width, send_ref, out_ref, landed, send_sems, recv_sems):
    me = lax.axis_index("grp")
    core = lax.axis_index("tp") % 2
    col, row = me % width, me // width

    def node(c, r):
        return lax.rem(r + width, width) * width + lax.rem(c + width, width)

    def along(dim, c, r, k):
        return node(c + k, r) if dim == 0 else node(c, r + k)

    barrier = pltpu.get_barrier_semaphore()
    neighbours = [node(col + 1, row), node(col - 1, row), node(col, row + 1), node(col, row - 1)]
    for neighbour in neighbours:
        pl.semaphore_signal(barrier, inc=1, device_id={"grp": neighbour}, device_id_type=MESH)
    pl.semaphore_wait(barrier, 4)

    landed[me] = send_ref[...]
    sends = []

    def send(source, origin, half, target):
        copy = pltpu.make_async_remote_copy(
            src_ref=source,
            dst_ref=landed.at[origin, half],
            send_sem=send_sems.at[len(sends)],
            recv_sem=recv_sems.at[origin, half],
            device_id={"grp": target},
            device_id_type=MESH,
        )
        copy.start()
        sends.append(copy)

    def arrive(origin, half):
        pltpu.make_async_remote_copy(
            src_ref=send_ref.at[half],
            dst_ref=landed.at[origin, half],
            send_sem=send_sems.at[0],
            recv_sem=recv_sems.at[origin, half],
            device_id={"grp": neighbours[0]},
            device_id_type=MESH,
        ).wait_recv()

    ahead = 1 - 2 * core

    def phase(lines, half, dim):
        for k in (1, -1):
            for line in lines:
                origin = along(1 - dim, col, row, line)
                source = send_ref.at[half] if line == 0 else landed.at[origin, half]
                send(source, origin, half, along(dim, col, row, k))
        for line in lines:
            for k in (1, -1):
                arrive(along(dim, along(1 - dim, col, row, line) % width, along(1 - dim, col, row, line) // width, k), half)
        for line in lines:
            base = along(1 - dim, col, row, line)
            bc, br = base % width, base // width
            send(landed.at[along(dim, bc, br, -ahead), half], along(dim, bc, br, -ahead), half,
                 along(dim, col, row, ahead))
        for line in lines:
            base = along(1 - dim, col, row, line)
            arrive(along(dim, base % width, base // width, 2), half)

    phase([0], 0, 0)
    phase([0], 1, 1)
    phase([0, 1, -1, 2], 0, 1)
    phase([0, 1, -1, 2], 1, 0)
    for copy in sends:
        copy.wait_send()
    out_ref[...] = landed[...]


def grid_gather(x, width, collective_id):
    count = width * width
    x = x.reshape((2, x.shape[0] // 2) + x.shape[1:])
    gathered = pl.pallas_call(
        functools.partial(grid_kernel, width),
        out_shape=jax.ShapeDtypeStruct((count,) + x.shape, x.dtype),
        in_specs=[pl.BlockSpec(memory_space=pltpu.VMEM)],
        out_specs=pl.BlockSpec(memory_space=pltpu.VMEM),
        scratch_shapes=[
            pltpu.VMEM((count,) + x.shape, x.dtype),
            pltpu.SemaphoreType.DMA((2 * (count - 1),)),
            pltpu.SemaphoreType.DMA((count, 2)),
        ],
        compiler_params=pltpu.CompilerParams(collective_id=collective_id, has_side_effects=True),
    )(x)
    return gathered.reshape((count, x.shape[0] * x.shape[1]) + x.shape[2:])


def gather_hbm_kernel(axis, count, send_ref, out_ref, send_sems, recv_sems, local_sem):
    me = lax.axis_index(axis)
    barrier = pltpu.get_barrier_semaphore()
    for step in range(1, count):
        peer = lax.rem(me + step, count)
        pl.semaphore_signal(barrier, inc=1, device_id={axis: peer}, device_id_type=MESH)
    pl.semaphore_wait(barrier, count - 1)
    copies = []
    for step in range(1, count):
        peer = lax.rem(me + step, count)
        copy = pltpu.make_async_remote_copy(
            src_ref=send_ref,
            dst_ref=out_ref.at[me],
            send_sem=send_sems.at[step],
            recv_sem=recv_sems.at[step],
            device_id={axis: peer},
            device_id_type=MESH,
        )
        copy.start()
        copies.append(copy)
    local = pltpu.make_async_copy(send_ref, out_ref.at[me], local_sem)
    local.start()
    for copy in copies:
        copy.wait()
    local.wait()


def gather_hbm(x, axis, count, collective_id):
    return pl.pallas_call(
        functools.partial(gather_hbm_kernel, axis, count),
        out_shape=jax.ShapeDtypeStruct((count,) + x.shape, x.dtype),
        in_specs=[pl.BlockSpec(memory_space=pltpu.VMEM)],
        out_specs=pl.BlockSpec(memory_space=pl.ANY),
        scratch_shapes=[
            pltpu.SemaphoreType.DMA((count,)),
            pltpu.SemaphoreType.DMA((count,)),
            pltpu.SemaphoreType.DMA(()),
        ],
        compiler_params=pltpu.CompilerParams(collective_id=collective_id, has_side_effects=True),
    )(x)


def weights_gather_kernel(count, own_ref, for_partner_ref, out_ref, partner_rows,
                          send_sems, recv_sems, partner_sems, local_sems):
    me = lax.axis_index("grp")
    member = lax.axis_index("tp")
    partner = member + 1 - 2 * (member % 2)
    rows = own_ref.shape[0]
    barrier = pltpu.get_barrier_semaphore()
    pl.semaphore_signal(barrier, inc=1, device_id={"tp": partner}, device_id_type=MESH)
    for step in range(1, count):
        peer = lax.rem(me + step, count)
        pl.semaphore_signal(barrier, inc=1, device_id={"grp": peer}, device_id_type=MESH)
    pl.semaphore_wait(barrier, count)
    to_partner = pltpu.make_async_remote_copy(
        src_ref=for_partner_ref, dst_ref=partner_rows, send_sem=partner_sems.at[0],
        recv_sem=partner_sems.at[1], device_id={"tp": partner}, device_id_type=MESH,
    )
    to_partner.start()
    copies = []

    def spread(part, source, window):
        for step in range(1, count):
            peer = lax.rem(me + step, count)
            copy = pltpu.make_async_remote_copy(
                src_ref=source,
                dst_ref=out_ref.at[me, window],
                send_sem=send_sems.at[part, step],
                recv_sem=recv_sems.at[part, step],
                device_id={"grp": peer},
                device_id_type=MESH,
            )
            copy.start()
            copies.append(copy)
        local = pltpu.make_async_copy(source, out_ref.at[me, window], local_sems.at[part])
        local.start()
        copies.append(local)

    spread(0, own_ref, pl.ds(0, rows))
    to_partner.wait()
    spread(1, partner_rows, pl.ds(rows, partner_rows.shape[0]))
    for copy in copies:
        copy.wait()


def weights_gather(own, for_partner, count, collective_id):
    rows = own.shape[0] + for_partner.shape[0]
    return pl.pallas_call(
        functools.partial(weights_gather_kernel, count),
        out_shape=jax.ShapeDtypeStruct((count, rows) + own.shape[1:], own.dtype),
        in_specs=[pl.BlockSpec(memory_space=pltpu.VMEM)] * 2,
        out_specs=pl.BlockSpec(memory_space=pl.ANY),
        scratch_shapes=[
            pltpu.VMEM(for_partner.shape, for_partner.dtype),
            pltpu.SemaphoreType.DMA((2, count)),
            pltpu.SemaphoreType.DMA((2, count)),
            pltpu.SemaphoreType.DMA((2,)),
            pltpu.SemaphoreType.DMA((2,)),
        ],
        compiler_params=pltpu.CompilerParams(collective_id=collective_id, has_side_effects=True),
    )(own, for_partner)


def exchange_kernel(axis, count, scatter, send_ref, out_ref, landed, send_sems, recv_sems):
    me = lax.axis_index(axis)
    barrier = pltpu.get_barrier_semaphore()
    for step in range(1, count):
        peer = lax.rem(me + step, count)
        pl.semaphore_signal(barrier, inc=1, device_id={axis: peer}, device_id_type=MESH)
    pl.semaphore_wait(barrier, count - 1)
    copies = []
    for step in range(1, count):
        peer = lax.rem(me + step, count)
        source = send_ref.at[peer] if scatter else send_ref
        copy = pltpu.make_async_remote_copy(
            src_ref=source,
            dst_ref=landed.at[me],
            send_sem=send_sems.at[step],
            recv_sem=recv_sems.at[step],
            device_id={axis: peer},
            device_id_type=MESH,
        )
        copy.start()
        copies.append(copy)
    landed[me] = send_ref[me] if scatter else send_ref[...]
    for copy in copies:
        copy.wait()
    if scatter:
        width = landed.shape[-1]
        for source in range(count):
            out_ref[:, source * width:(source + 1) * width] = landed[source]
    else:
        out_ref[...] = landed[...]


def exchange(x, axis, count, scatter, collective_id):
    piece = x.shape[1:] if scatter else x.shape
    result = (piece[0], count * piece[1]) if scatter else (count,) + piece
    return pl.pallas_call(
        functools.partial(exchange_kernel, axis, count, scatter),
        out_shape=jax.ShapeDtypeStruct(result, x.dtype),
        in_specs=[pl.BlockSpec(memory_space=pltpu.VMEM)],
        out_specs=pl.BlockSpec(memory_space=pltpu.VMEM),
        scratch_shapes=[
            pltpu.VMEM((count,) + piece, x.dtype),
            pltpu.SemaphoreType.DMA((count,)),
            pltpu.SemaphoreType.DMA((count,)),
        ],
        compiler_params=pltpu.CompilerParams(collective_id=collective_id, has_side_effects=True),
    )(x)


def on_device(tokens, trainer_panels, panel_home, lengths):
    tp_count = lax.axis_size("tp")
    grp_count = lax.axis_size("grp")
    member_id = lax.axis_index("tp")
    kv_count = (panel_home.shape[0] - tp_count) // 2
    group_size = tp_count // kv_count
    head_dim = trainer_panels.shape[2]
    block_rows = trainer_panels.shape[1]
    half_rows = block_rows // 2
    seq_total = tokens.shape[0]

    return whole(trainer_panels, panel_home, tokens, lengths, tp_count // 2, grp_count, 4)


def solution(mesh):
    placed = (P("grp", None), P("tp", "grp", None), P(), P("grp", None))
    return jax.shard_map(
        on_device, mesh=mesh, in_specs=placed, out_specs=P(("grp", "tp"), None), check_vma=False
    )
```

```python
import functools

import jax
import jax.numpy as jnp
from jax import lax
from jax.experimental import pallas as pl
from jax.experimental.pallas import tpu as pltpu
from jax.sharding import PartitionSpec as P

MESH = pl.DeviceIdType.MESH


def ring_kernel(count, stride, chunks, send_ref, out_ref, landed, send_sems, recv_sems):
    me = lax.axis_index("tp")
    total = count * stride
    right, left = lax.rem(me + stride, total), lax.rem(me + total - stride, total)
    spot = me // stride
    barrier = pltpu.get_barrier_semaphore()
    for neighbour in (left, right):
        pl.semaphore_signal(barrier, inc=1, device_id={"tp": neighbour}, device_id_type=MESH)
    pl.semaphore_wait(barrier, 2)

    def incoming(origin, chunk):
        return pltpu.make_async_remote_copy(
            src_ref=send_ref.at[chunk],
            dst_ref=landed.at[origin, chunk],
            send_sem=send_sems.at[0, 0, 0],
            recv_sem=recv_sems.at[origin, chunk],
            device_id={"tp": right},
            device_id_type=MESH,
        )

    landed[spot] = send_ref[...]
    sends = []
    far_right, far_left = count // 2, (count - 1) // 2
    for step in range(1, far_right + 1):
        for chunk in range(chunks):
            streams = [(0, right, lax.rem(spot + count - (step - 1), count))]
            if step <= far_left:
                streams.append((1, left, lax.rem(spot + step - 1, count)))
            for way, target, origin in streams:
                if step > 1:
                    incoming(origin, chunk).wait_recv()
                source = send_ref.at[chunk] if step == 1 else landed.at[origin, chunk]
                copy = pltpu.make_async_remote_copy(
                    src_ref=source,
                    dst_ref=landed.at[origin, chunk],
                    send_sem=send_sems.at[way, step, chunk],
                    recv_sem=recv_sems.at[origin, chunk],
                    device_id={"tp": target},
                    device_id_type=MESH,
                )
                copy.start()
                sends.append(copy)
    for chunk in range(chunks):
        incoming(lax.rem(spot + count - far_right, count), chunk).wait_recv()
        incoming(lax.rem(spot + far_left, count), chunk).wait_recv()
    for copy in sends:
        copy.wait_send()
    out_ref[...] = landed[...]


def ring_gather(x, count, stride, chunks, collective_id):
    x = x.reshape((chunks, x.shape[0] // chunks) + x.shape[1:])
    gathered = pl.pallas_call(
        functools.partial(ring_kernel, count, stride, chunks),
        out_shape=jax.ShapeDtypeStruct((count,) + x.shape, x.dtype),
        in_specs=[pl.BlockSpec(memory_space=pltpu.VMEM)],
        out_specs=pl.BlockSpec(memory_space=pltpu.VMEM),
        scratch_shapes=[
            pltpu.VMEM((count,) + x.shape, x.dtype),
            pltpu.SemaphoreType.DMA((2, count // 2 + 1, chunks)),
            pltpu.SemaphoreType.DMA((count, chunks)),
        ],
        compiler_params=pltpu.CompilerParams(collective_id=collective_id, has_side_effects=True),
    )(x)
    return gathered.reshape((count * x.shape[0] * x.shape[1],) + x.shape[2:])


def chip_ring_kernel(count, groups, panels_ref, home_ref, out_ref, landed, send_sems, recv_sems,
                     own_ref, partner_ref, partner_rows, grp_send_sems, grp_recv_sems, partner_sems, local_sems,
                     greet=True):
    me = lax.axis_index("tp")
    here = lax.axis_index("grp")
    total = 2 * count
    core = me % 2
    partner = me + 1 - 2 * core
    right, left = lax.rem(me + 2, total), lax.rem(me + total - 2, total)
    spot = me // 2
    half = panels_ref.shape[1] // 2
    if greet:
        barrier = pltpu.get_barrier_semaphore()
        for neighbour in (left, right, partner):
            pl.semaphore_signal(barrier, inc=1, device_id={"tp": neighbour}, device_id_type=MESH)
        for step in range(1, groups):
            peer = lax.rem(here + step, groups)
            pl.semaphore_signal(barrier, inc=1, device_id={"grp": peer}, device_id_type=MESH)
        pl.semaphore_wait(barrier, 2 + groups)

    def rows_of(slot, which):
        return panels_ref.at[slot, pl.ds(pl.multiple_of(which * half, 16), half)]

    def incoming(origin, chunk):
        return pltpu.make_async_remote_copy(
            src_ref=rows_of(0, 0),
            dst_ref=landed.at[origin, chunk],
            send_sem=send_sems.at[0, 0, 0],
            recv_sem=recv_sems.at[origin, chunk],
            device_id={"tp": right},
            device_id_type=MESH,
        )

    sends = []

    def send(source, origin, chunk, sem, target):
        copy = pltpu.make_async_remote_copy(
            src_ref=source,
            dst_ref=landed.at[origin, chunk],
            send_sem=sem,
            recv_sem=recv_sems.at[origin, chunk],
            device_id={"tp": target},
            device_id_type=MESH,
        )
        copy.start()
        sends.append(copy)

    own = [2 * core + j for j in range(2)]
    theirs = [2 * (1 - core) + j for j in range(2)]
    for j in range(2):
        send(rows_of(j, 1 - core), spot, own[j], send_sems.at[0, 0, 1 + j], partner)
        landed[spot, own[j]] = rows_of(j, core)[...]
    far_right, far_left = count // 2, (count - 1) // 2
    first = [(rows_of(j, core), own[j]) for j in range(2)] + [(None, theirs[j]) for j in range(2)]
    for position, (source, chunk) in enumerate(first):
        if source is None:
            incoming(spot, chunk).wait_recv()
            source = landed.at[spot, chunk]
        send(source, spot, chunk, send_sems.at[0, 1, position], right)
        if far_left >= 1:
            send(source, spot, chunk, send_sems.at[1, 1, position], left)
    for step in range(2, far_right + 1):
        for chunk in range(4):
            streams = [(0, right, lax.rem(spot + count - (step - 1), count))]
            if step <= far_left:
                streams.append((1, left, lax.rem(spot + step - 1, count)))
            for way, target, origin in streams:
                incoming(origin, chunk).wait_recv()
                send(landed.at[origin, chunk], origin, chunk, send_sems.at[way, step, chunk], target)
    for chunk in range(4):
        incoming(lax.rem(spot + count - far_right, count), chunk).wait_recv()
        incoming(lax.rem(spot + far_left, count), chunk).wait_recv()
    if greet:
        for copy in sends:
            copy.wait_send()
    heads = total
    kv_heads = (home_ref.shape[0] - heads) // 2
    group = heads // kv_heads
    quarter = me % group
    kv_panel = heads + me // group + kv_heads * (quarter // 2)
    chip_slots = landed.shape[1]

    def block(panel):
        slot = home_ref[panel]
        return landed[slot // chip_slots, slot % chip_slots]

    own_ref[0:half] = block(me)
    own_ref[half:2 * half] = block(kv_panel)
    partner_ref[...] = block(partner)

    to_partner = pltpu.make_async_remote_copy(
        src_ref=partner_ref, dst_ref=partner_rows, send_sem=partner_sems.at[0],
        recv_sem=partner_sems.at[1], device_id={"tp": partner}, device_id_type=MESH,
    )
    to_partner.start()
    copies, local_copies = [], []

    def spread(part, source, window):
        for step in range(1, groups):
            peer = lax.rem(here + step, groups)
            copy = pltpu.make_async_remote_copy(
                src_ref=source,
                dst_ref=out_ref.at[here, window],
                send_sem=grp_send_sems.at[part, step],
                recv_sem=grp_recv_sems.at[part, step],
                device_id={"grp": peer},
                device_id_type=MESH,
            )
            copy.start()
            copies.append(copy)
        local = pltpu.make_async_copy(source, out_ref.at[here, window], local_sems.at[part])
        local.start()
        local_copies.append(local)

    spread(0, own_ref, pl.ds(0, 2 * half))
    to_partner.wait()
    spread(1, partner_rows, pl.ds(2 * half, half))
    for copy in local_copies:
        copy.wait()
    if greet:
        for copy in copies:
            copy.wait()
        return None
    windows = [(own_ref, pl.ds(0, 2 * half)), (partner_rows, pl.ds(2 * half, half))]

    def arrive(source):
        step = lax.rem(here + groups - source, groups)

        @pl.when(step != 0)
        def _():
            for part, (shape_ref, window) in enumerate(windows):
                pltpu.make_async_remote_copy(
                    src_ref=shape_ref,
                    dst_ref=out_ref.at[here, window],
                    send_sem=grp_send_sems.at[part, 0],
                    recv_sem=grp_recv_sems.at[part, step],
                    device_id={"grp": lax.rem(here + 1, groups)},
                    device_id_type=MESH,
                ).wait_recv()

    def finish():
        for copy in sends + copies:
            copy.wait_send()

    return arrive, finish


def chip_ring_gather(panels, home, count, groups, collective_id):
    slots, rows, width = panels.shape
    return pl.pallas_call(
        functools.partial(chip_ring_kernel, count, groups),
        out_shape=jax.ShapeDtypeStruct((groups, rows + rows // 2, width), panels.dtype),
        in_specs=[pl.BlockSpec(memory_space=pltpu.VMEM), pl.BlockSpec(memory_space=pltpu.SMEM)],
        out_specs=pl.BlockSpec(memory_space=pl.ANY),
        scratch_shapes=[
            pltpu.VMEM((count, 2 * slots, rows // 2, width), panels.dtype),
            pltpu.SemaphoreType.DMA((2, count // 2 + 1, 2 * slots)),
            pltpu.SemaphoreType.DMA((count, 2 * slots)),
            pltpu.VMEM((rows, width), panels.dtype),
            pltpu.VMEM((rows // 2, width), panels.dtype),
            pltpu.VMEM((rows // 2, width), panels.dtype),
            pltpu.SemaphoreType.DMA((2, groups)),
            pltpu.SemaphoreType.DMA((2, groups)),
            pltpu.SemaphoreType.DMA((2,)),
            pltpu.SemaphoreType.DMA((2,)),
        ],
        compiler_params=pltpu.CompilerParams(collective_id=collective_id, has_side_effects=True),
    )(panels, home)


def kv_share_kernel(part_ref, out_ref, partner_part, mine, theirs, send_sems, recv_sems):
    me = lax.axis_index("tp")
    partner = me + 1 - 2 * (me % 2)
    across = me + 2 - 4 * ((me // 2) % 2)
    barrier = pltpu.get_barrier_semaphore()
    for neighbour in (partner, across):
        pl.semaphore_signal(barrier, inc=1, device_id={"tp": neighbour}, device_id_type=MESH)
    pl.semaphore_wait(barrier, 2)
    first = pltpu.make_async_remote_copy(
        src_ref=part_ref, dst_ref=partner_part, send_sem=send_sems.at[0], recv_sem=recv_sems.at[0],
        device_id={"tp": partner}, device_id_type=MESH,
    )
    first.start()
    first.wait()
    mine[...] = (part_ref[...] + partner_part[...]).astype(mine.dtype)
    second = pltpu.make_async_remote_copy(
        src_ref=mine, dst_ref=theirs, send_sem=send_sems.at[1], recv_sem=recv_sems.at[1],
        device_id={"tp": across}, device_id_type=MESH,
    )
    second.start()
    second.wait()
    holds_k = (me % 4) < 2
    out_ref[0] = jnp.where(holds_k, mine[...], theirs[...])
    out_ref[1] = jnp.where(holds_k, theirs[...], mine[...])


def kv_share(part, collective_id):
    return pl.pallas_call(
        kv_share_kernel,
        out_shape=jax.ShapeDtypeStruct((2,) + part.shape, jnp.bfloat16),
        in_specs=[pl.BlockSpec(memory_space=pltpu.VMEM)],
        out_specs=pl.BlockSpec(memory_space=pltpu.VMEM),
        scratch_shapes=[
            pltpu.VMEM(part.shape, part.dtype),
            pltpu.VMEM(part.shape, jnp.bfloat16),
            pltpu.VMEM(part.shape, jnp.bfloat16),
            pltpu.SemaphoreType.DMA((2,)),
            pltpu.SemaphoreType.DMA((2,)),
        ],
        compiler_params=pltpu.CompilerParams(collective_id=collective_id, has_side_effects=True),
    )(part)


def tail_kernel(count, scale, tokens_ref, gathered_hbm, lengths_ref, out_ref,
                gathered, load_sem, part_ref, partner_part, mine, theirs, staged, landed, send_sems, recv_sems,
                greet=True, arrive=None):
    width = landed.shape[-1]
    me = lax.axis_index("tp")
    partner = me + 1 - 2 * (me % 2)
    across = me + 2 - 4 * ((me // 2) % 2)
    if greet:
        load = pltpu.make_async_copy(gathered_hbm, gathered, load_sem)
        load.start()
        barrier = pltpu.get_barrier_semaphore()
        for step in range(1, count):
            peer = lax.rem(me + step, count)
            pl.semaphore_signal(barrier, inc=1, device_id={"tp": peer}, device_id_type=MESH)
        load.wait()
    core = me % 2
    half = gathered.shape[1] // 3
    sources = gathered.shape[0]
    first_half = core == 0
    projected = jnp.zeros((tokens_ref.shape[0], 2 * width), jnp.float32)
    for pair in range(sources // 2):
        if arrive is not None:
            arrive(2 * pair)
            arrive(2 * pair + 1)
        q_parts, kv_parts = [], []
        for source in (2 * pair, 2 * pair + 1):
            here = gathered[source, 0:half]
            kv = gathered[source, half:2 * half]
            there = gathered[source, 2 * half:3 * half]
            zero = jnp.zeros_like(kv)
            q_parts.append(jnp.where(first_half, jnp.concatenate([here, there], axis=0),
                                     jnp.concatenate([there, here], axis=0)))
            kv_parts.append(jnp.where(first_half, jnp.concatenate([kv, zero], axis=0),
                                      jnp.concatenate([zero, kv], axis=0)))
        slab = jnp.concatenate(
            [jnp.concatenate(q_parts, axis=0), jnp.concatenate(kv_parts, axis=0)], axis=1
        )
        columns = slab.shape[0]
        projected = projected + jnp.dot(
            tokens_ref[:, pair * columns:(pair + 1) * columns], slab, preferred_element_type=jnp.float32
        )
    part_ref[...] = projected[:, width:]
    query = projected[:, :width].astype(jnp.bfloat16)
    if greet:
        pl.semaphore_wait(barrier, count - 1)
    first = pltpu.make_async_remote_copy(
        src_ref=part_ref, dst_ref=partner_part, send_sem=send_sems.at[0], recv_sem=recv_sems.at[0],
        device_id={"tp": partner}, device_id_type=MESH,
    )
    first.start()
    first.wait()
    mine[...] = (part_ref[...] + partner_part[...]).astype(mine.dtype)
    second = pltpu.make_async_remote_copy(
        src_ref=mine, dst_ref=theirs, send_sem=send_sems.at[1], recv_sem=recv_sems.at[1],
        device_id={"tp": across}, device_id_type=MESH,
    )
    second.start()
    second.wait()
    holds_k = (me % 4) < 2
    keys = jnp.where(holds_k, mine[...], theirs[...])
    values = jnp.where(holds_k, theirs[...], mine[...])

    seq = query.shape[0]
    rows = seq // count
    blocks = 4
    block_rows = seq // blocks
    col = lax.broadcasted_iota(jnp.int32, (block_rows, seq), 1)
    col_segment = jnp.zeros((block_rows, seq), jnp.int32)
    bounds = []
    bound = lengths_ref[0, 0] * 0
    for response in range(lengths_ref.shape[1]):
        bound = bound + lengths_ref[0, response]
        bounds.append(bound)
        col_segment = col_segment + (col >= bound).astype(jnp.int32)
    copies = []
    for block in range(blocks):
        first_row = block * block_rows
        scores = lax.dot_general(
            query[first_row:first_row + block_rows], keys, (((1,), (1,)), ((), ())),
            preferred_element_type=jnp.float32,
        ) * scale
        row = lax.broadcasted_iota(jnp.int32, (block_rows, seq), 0) + first_row
        row_segment = jnp.zeros((block_rows, seq), jnp.int32)
        for bound in bounds:
            row_segment = row_segment + (row >= bound).astype(jnp.int32)
        allowed = (row_segment == col_segment) & (col <= row)
        masked = jnp.where(allowed, scores, -jnp.inf)
        peak = jnp.max(masked, axis=1, keepdims=True)
        weights = jnp.exp(masked - peak)
        probs = (weights / jnp.sum(weights, axis=1, keepdims=True)).astype(jnp.bfloat16)
        context = jnp.dot(probs, values, preferred_element_type=jnp.float32)
        per_block = block_rows // rows
        for i in range(per_block):
            target = block * per_block + i
            staged[target] = context[i * rows:(i + 1) * rows]
        for i in range(per_block):
            target = block * per_block + i
            copy = pltpu.make_async_remote_copy(
                src_ref=staged.at[target],
                dst_ref=landed.at[me],
                send_sem=send_sems.at[2 + target],
                recv_sem=recv_sems.at[2 + me],
                device_id={"tp": target},
                device_id_type=MESH,
            )

            @pl.when(target != me)
            def _():
                copy.start()

            copies.append((target, copy))
    landed[me] = staged[me]
    for target, copy in copies:
        @pl.when(target != me)
        def _():
            copy.wait_send()
    for source in range(count):
        incoming = pltpu.make_async_remote_copy(
            src_ref=staged.at[source],
            dst_ref=landed.at[source],
            send_sem=send_sems.at[0],
            recv_sem=recv_sems.at[2 + source],
            device_id={"tp": partner},
            device_id_type=MESH,
        )

        @pl.when(source != me)
        def _():
            incoming.wait_recv()
    for source in range(count):
        out_ref[:, source * width:(source + 1) * width] = landed[source]


def tail(tokens, gathered, lengths, count, collective_id):
    seq, width = tokens.shape[0], gathered.shape[2]
    part = jax.ShapeDtypeStruct((seq, width), jnp.float32)
    rows = seq // count
    vmem = pl.BlockSpec(memory_space=pltpu.VMEM)
    return pl.pallas_call(
        functools.partial(tail_kernel, count, width ** (-0.5)),
        out_shape=jax.ShapeDtypeStruct((rows, count * width), jnp.float32),
        in_specs=[vmem, pl.BlockSpec(memory_space=pl.ANY), pl.BlockSpec(memory_space=pltpu.SMEM)],
        out_specs=vmem,
        scratch_shapes=[
            pltpu.VMEM(gathered.shape, gathered.dtype),
            pltpu.SemaphoreType.DMA(()),
            pltpu.VMEM(part.shape, part.dtype),
            pltpu.VMEM(part.shape, part.dtype),
            pltpu.VMEM(part.shape, jnp.bfloat16),
            pltpu.VMEM(part.shape, jnp.bfloat16),
            pltpu.VMEM((count, rows, width), jnp.float32),
            pltpu.VMEM((count, rows, width), jnp.float32),
            pltpu.SemaphoreType.DMA((count + 1,)),
            pltpu.SemaphoreType.DMA((count + 1,)),
        ],
        compiler_params=pltpu.CompilerParams(collective_id=collective_id, has_side_effects=True),
    )(tokens, gathered, lengths)


def whole_kernel(count, groups, scale, panels_ref, home_ref, tokens_ref, lengths_ref, out_ref, *scratch):
    ring_scratch, gathered, tail_scratch = scratch[:10], scratch[10], scratch[11:]
    me = lax.axis_index("tp")
    here = lax.axis_index("grp")
    total = 2 * count
    barrier = pltpu.get_barrier_semaphore()
    for step in range(1, total):
        peer = lax.rem(me + step, total)
        pl.semaphore_signal(barrier, inc=1, device_id={"tp": peer}, device_id_type=MESH)
    for step in range(1, groups):
        peer = lax.rem(here + step, groups)
        pl.semaphore_signal(barrier, inc=1, device_id={"grp": peer}, device_id_type=MESH)
    pl.semaphore_wait(barrier, total + groups - 2)
    arrive, finish = chip_ring_kernel(count, groups, panels_ref, home_ref, gathered, *ring_scratch, greet=False)
    tail_kernel(total, scale, tokens_ref, None, lengths_ref, out_ref, gathered, None, *tail_scratch, greet=False,
                arrive=arrive)
    finish()


def whole(panels, home, tokens, lengths, count, groups, collective_id):
    slots, rows, width = panels.shape
    seq = tokens.shape[0]
    total = 2 * count
    out_rows = seq // total
    part = (seq, width)
    vmem = pl.BlockSpec(memory_space=pltpu.VMEM)
    smem = pl.BlockSpec(memory_space=pltpu.SMEM)
    return pl.pallas_call(
        functools.partial(whole_kernel, count, groups, width ** (-0.5)),
        out_shape=jax.ShapeDtypeStruct((out_rows, total * width), jnp.float32),
        in_specs=[vmem, smem, vmem, smem],
        out_specs=vmem,
        scratch_shapes=[
            pltpu.VMEM((count, 2 * slots, rows // 2, width), panels.dtype),
            pltpu.SemaphoreType.DMA((2, count // 2 + 1, 2 * slots)),
            pltpu.SemaphoreType.DMA((count, 2 * slots)),
            pltpu.VMEM((rows, width), panels.dtype),
            pltpu.VMEM((rows // 2, width), panels.dtype),
            pltpu.VMEM((rows // 2, width), panels.dtype),
            pltpu.SemaphoreType.DMA((2, groups)),
            pltpu.SemaphoreType.DMA((2, groups)),
            pltpu.SemaphoreType.DMA((2,)),
            pltpu.SemaphoreType.DMA((2,)),
            pltpu.VMEM((groups, rows + rows // 2, width), panels.dtype),
            pltpu.VMEM(part, jnp.float32),
            pltpu.VMEM(part, jnp.float32),
            pltpu.VMEM(part, jnp.bfloat16),
            pltpu.VMEM(part, jnp.bfloat16),
            pltpu.VMEM((total, out_rows, width), jnp.float32),
            pltpu.VMEM((total, out_rows, width), jnp.float32),
            pltpu.SemaphoreType.DMA((total + 2,)),
            pltpu.SemaphoreType.DMA((total + 2,)),
        ],
        compiler_params=pltpu.CompilerParams(collective_id=collective_id, has_side_effects=True),
    )(panels, home, tokens, lengths)


def grid_kernel(width, send_ref, out_ref, landed, send_sems, recv_sems):
    me = lax.axis_index("grp")
    core = lax.axis_index("tp") % 2
    col, row = me % width, me // width

    def node(c, r):
        return lax.rem(r + width, width) * width + lax.rem(c + width, width)

    def along(dim, c, r, k):
        return node(c + k, r) if dim == 0 else node(c, r + k)

    barrier = pltpu.get_barrier_semaphore()
    neighbours = [node(col + 1, row), node(col - 1, row), node(col, row + 1), node(col, row - 1)]
    for neighbour in neighbours:
        pl.semaphore_signal(barrier, inc=1, device_id={"grp": neighbour}, device_id_type=MESH)
    pl.semaphore_wait(barrier, 4)

    landed[me] = send_ref[...]
    sends = []

    def send(source, origin, half, target):
        copy = pltpu.make_async_remote_copy(
            src_ref=source,
            dst_ref=landed.at[origin, half],
            send_sem=send_sems.at[len(sends)],
            recv_sem=recv_sems.at[origin, half],
            device_id={"grp": target},
            device_id_type=MESH,
        )
        copy.start()
        sends.append(copy)

    def arrive(origin, half):
        pltpu.make_async_remote_copy(
            src_ref=send_ref.at[half],
            dst_ref=landed.at[origin, half],
            send_sem=send_sems.at[0],
            recv_sem=recv_sems.at[origin, half],
            device_id={"grp": neighbours[0]},
            device_id_type=MESH,
        ).wait_recv()

    ahead = 1 - 2 * core

    def phase(lines, half, dim):
        for k in (1, -1):
            for line in lines:
                origin = along(1 - dim, col, row, line)
                source = send_ref.at[half] if line == 0 else landed.at[origin, half]
                send(source, origin, half, along(dim, col, row, k))
        for line in lines:
            for k in (1, -1):
                arrive(along(dim, along(1 - dim, col, row, line) % width, along(1 - dim, col, row, line) // width, k), half)
        for line in lines:
            base = along(1 - dim, col, row, line)
            bc, br = base % width, base // width
            send(landed.at[along(dim, bc, br, -ahead), half], along(dim, bc, br, -ahead), half,
                 along(dim, col, row, ahead))
        for line in lines:
            base = along(1 - dim, col, row, line)
            arrive(along(dim, base % width, base // width, 2), half)

    phase([0], 0, 0)
    phase([0], 1, 1)
    phase([0, 1, -1, 2], 0, 1)
    phase([0, 1, -1, 2], 1, 0)
    for copy in sends:
        copy.wait_send()
    out_ref[...] = landed[...]


def grid_gather(x, width, collective_id):
    count = width * width
    x = x.reshape((2, x.shape[0] // 2) + x.shape[1:])
    gathered = pl.pallas_call(
        functools.partial(grid_kernel, width),
        out_shape=jax.ShapeDtypeStruct((count,) + x.shape, x.dtype),
        in_specs=[pl.BlockSpec(memory_space=pltpu.VMEM)],
        out_specs=pl.BlockSpec(memory_space=pltpu.VMEM),
        scratch_shapes=[
            pltpu.VMEM((count,) + x.shape, x.dtype),
            pltpu.SemaphoreType.DMA((2 * (count - 1),)),
            pltpu.SemaphoreType.DMA((count, 2)),
        ],
        compiler_params=pltpu.CompilerParams(collective_id=collective_id, has_side_effects=True),
    )(x)
    return gathered.reshape((count, x.shape[0] * x.shape[1]) + x.shape[2:])


def gather_hbm_kernel(axis, count, send_ref, out_ref, send_sems, recv_sems, local_sem):
    me = lax.axis_index(axis)
    barrier = pltpu.get_barrier_semaphore()
    for step in range(1, count):
        peer = lax.rem(me + step, count)
        pl.semaphore_signal(barrier, inc=1, device_id={axis: peer}, device_id_type=MESH)
    pl.semaphore_wait(barrier, count - 1)
    copies = []
    for step in range(1, count):
        peer = lax.rem(me + step, count)
        copy = pltpu.make_async_remote_copy(
            src_ref=send_ref,
            dst_ref=out_ref.at[me],
            send_sem=send_sems.at[step],
            recv_sem=recv_sems.at[step],
            device_id={axis: peer},
            device_id_type=MESH,
        )
        copy.start()
        copies.append(copy)
    local = pltpu.make_async_copy(send_ref, out_ref.at[me], local_sem)
    local.start()
    for copy in copies:
        copy.wait()
    local.wait()


def gather_hbm(x, axis, count, collective_id):
    return pl.pallas_call(
        functools.partial(gather_hbm_kernel, axis, count),
        out_shape=jax.ShapeDtypeStruct((count,) + x.shape, x.dtype),
        in_specs=[pl.BlockSpec(memory_space=pltpu.VMEM)],
        out_specs=pl.BlockSpec(memory_space=pl.ANY),
        scratch_shapes=[
            pltpu.SemaphoreType.DMA((count,)),
            pltpu.SemaphoreType.DMA((count,)),
            pltpu.SemaphoreType.DMA(()),
        ],
        compiler_params=pltpu.CompilerParams(collective_id=collective_id, has_side_effects=True),
    )(x)


def weights_gather_kernel(count, own_ref, for_partner_ref, out_ref, partner_rows,
                          send_sems, recv_sems, partner_sems, local_sems):
    me = lax.axis_index("grp")
    member = lax.axis_index("tp")
    partner = member + 1 - 2 * (member % 2)
    rows = own_ref.shape[0]
    barrier = pltpu.get_barrier_semaphore()
    pl.semaphore_signal(barrier, inc=1, device_id={"tp": partner}, device_id_type=MESH)
    for step in range(1, count):
        peer = lax.rem(me + step, count)
        pl.semaphore_signal(barrier, inc=1, device_id={"grp": peer}, device_id_type=MESH)
    pl.semaphore_wait(barrier, count)
    to_partner = pltpu.make_async_remote_copy(
        src_ref=for_partner_ref, dst_ref=partner_rows, send_sem=partner_sems.at[0],
        recv_sem=partner_sems.at[1], device_id={"tp": partner}, device_id_type=MESH,
    )
    to_partner.start()
    copies = []

    def spread(part, source, window):
        for step in range(1, count):
            peer = lax.rem(me + step, count)
            copy = pltpu.make_async_remote_copy(
                src_ref=source,
                dst_ref=out_ref.at[me, window],
                send_sem=send_sems.at[part, step],
                recv_sem=recv_sems.at[part, step],
                device_id={"grp": peer},
                device_id_type=MESH,
            )
            copy.start()
            copies.append(copy)
        local = pltpu.make_async_copy(source, out_ref.at[me, window], local_sems.at[part])
        local.start()
        copies.append(local)

    spread(0, own_ref, pl.ds(0, rows))
    to_partner.wait()
    spread(1, partner_rows, pl.ds(rows, partner_rows.shape[0]))
    for copy in copies:
        copy.wait()


def weights_gather(own, for_partner, count, collective_id):
    rows = own.shape[0] + for_partner.shape[0]
    return pl.pallas_call(
        functools.partial(weights_gather_kernel, count),
        out_shape=jax.ShapeDtypeStruct((count, rows) + own.shape[1:], own.dtype),
        in_specs=[pl.BlockSpec(memory_space=pltpu.VMEM)] * 2,
        out_specs=pl.BlockSpec(memory_space=pl.ANY),
        scratch_shapes=[
            pltpu.VMEM(for_partner.shape, for_partner.dtype),
            pltpu.SemaphoreType.DMA((2, count)),
            pltpu.SemaphoreType.DMA((2, count)),
            pltpu.SemaphoreType.DMA((2,)),
            pltpu.SemaphoreType.DMA((2,)),
        ],
        compiler_params=pltpu.CompilerParams(collective_id=collective_id, has_side_effects=True),
    )(own, for_partner)


def exchange_kernel(axis, count, scatter, send_ref, out_ref, landed, send_sems, recv_sems):
    me = lax.axis_index(axis)
    barrier = pltpu.get_barrier_semaphore()
    for step in range(1, count):
        peer = lax.rem(me + step, count)
        pl.semaphore_signal(barrier, inc=1, device_id={axis: peer}, device_id_type=MESH)
    pl.semaphore_wait(barrier, count - 1)
    copies = []
    for step in range(1, count):
        peer = lax.rem(me + step, count)
        source = send_ref.at[peer] if scatter else send_ref
        copy = pltpu.make_async_remote_copy(
            src_ref=source,
            dst_ref=landed.at[me],
            send_sem=send_sems.at[step],
            recv_sem=recv_sems.at[step],
            device_id={axis: peer},
            device_id_type=MESH,
        )
        copy.start()
        copies.append(copy)
    landed[me] = send_ref[me] if scatter else send_ref[...]
    for copy in copies:
        copy.wait()
    if scatter:
        width = landed.shape[-1]
        for source in range(count):
            out_ref[:, source * width:(source + 1) * width] = landed[source]
    else:
        out_ref[...] = landed[...]


def exchange(x, axis, count, scatter, collective_id):
    piece = x.shape[1:] if scatter else x.shape
    result = (piece[0], count * piece[1]) if scatter else (count,) + piece
    return pl.pallas_call(
        functools.partial(exchange_kernel, axis, count, scatter),
        out_shape=jax.ShapeDtypeStruct(result, x.dtype),
        in_specs=[pl.BlockSpec(memory_space=pltpu.VMEM)],
        out_specs=pl.BlockSpec(memory_space=pltpu.VMEM),
        scratch_shapes=[
            pltpu.VMEM((count,) + piece, x.dtype),
            pltpu.SemaphoreType.DMA((count,)),
            pltpu.SemaphoreType.DMA((count,)),
        ],
        compiler_params=pltpu.CompilerParams(collective_id=collective_id, has_side_effects=True),
    )(x)


def on_device(tokens, trainer_panels, panel_home, lengths):
    tp_count = lax.axis_size("tp")
    grp_count = lax.axis_size("grp")
    member_id = lax.axis_index("tp")
    kv_count = (panel_home.shape[0] - tp_count) // 2
    group_size = tp_count // kv_count
    head_dim = trainer_panels.shape[2]
    block_rows = trainer_panels.shape[1]
    half_rows = block_rows // 2
    seq_total = tokens.shape[0]

    return whole(trainer_panels, panel_home, tokens, lengths, tp_count // 2, grp_count, 4)


def solution(mesh):
    placed = (P("grp", None), P("tp", "grp", None), P(), P("grp", None))
    return jax.shard_map(
        on_device, mesh=mesh, in_specs=placed, out_specs=P(("grp", "tp"), None), check_vma=False
    )
```
